256 devices in a mesh: lon: 16 (over y, x_lo, core), lat: 16 (over x_hi, z).
Axes of the slice: x: 4 (x_hi: 2, x_lo: 2; x = x_hi * 2 + x_lo), y: 4, z: 8, core: 2. Of those that a mesh axis runs over, the one named last changes fastest.
Arguments:
- eastbound_current: float32 [32, 512, 4096], P(None, 'lat', 'lon'), may hold values from -3 to 3
- poleward_current: float32 [32, 512, 4096], P(None, 'lat', 'lon'), may hold values from -3 to 3
- warmth_excess: float32 [32, 512, 4096], P(None, 'lat', 'lon'), may hold values from -5 to 5
- saltiness_excess: float32 [32, 512, 4096], P(None, 'lat', 'lon'), may hold values from -5 to 5
- water_indicator: int32 [32, 512, 4096], P(None, 'lat', 'lon'), may hold values 0 or 1
- column_layer_count: int32 [512, 4096], P('lat', 'lon'), may hold values from 1 to 32
Outputs:
- east_next: float32 [32, 512, 4096], P(None, 'lat', 'lon')
- north_next: float32 [32, 512, 4096], P(None, 'lat', 'lon')
- temp_next: float32 [32, 512, 4096], P(None, 'lat', 'lon')
- salt_next: float32 [32, 512, 4096], P(None, 'lat', 'lon')
The draws below stay inside these ranges and needn't reach their ends.
All inputs are finite; a program needn't handle non-finite values. No bound on the sum of `water_indicator` on one device may be relied on, other than what follows from the above.
Results may differ from the reference program's by a relative error of at most 0.00002.
Values sent between devices are 32-bit elements; how exact they have to be, the bound alone decides.
A program may use at most 128 MiB of HBM per device.

```python
import jax
import jax.numpy as jnp

CY = 32
VERTICAL_LAYERS = 32
EASTWARD_CELLS = 4096
NORTHWARD_CELLS = 512
N_LAT = 16


def with_ends(entries, rng, least, high):
    shape = entries.shape
    index_at = [jax.random.randint(jax.random.fold_in(rng, axis), (), 0, shape[axis]) for axis in range(len(shape))]
    entries = entries.at[tuple(index_at)].set(least)
    longest = shape.index(max(shape))
    index_at[longest] = (index_at[longest] + 1) % shape[longest]
    return entries.at[tuple(index_at)].set(high)


def block_scale(rng, extent, pieces, smallest, high):
    def one(axis_at, shards_of):
        steps = jax.random.uniform(jax.random.fold_in(jax.random.fold_in(rng, 6), axis_at), (shards_of,), jnp.float32, smallest / len(pieces), high / len(pieces))
        return jnp.repeat(jnp.exp(steps), extent[axis_at] // shards_of).reshape((-1,) + (1,) * (len(extent) - axis_at - 1))

    loudness = one(*pieces[0])
    for cut in pieces[1:]:
        loudness = loudness * one(*cut)
    return loudness


def scatter_about(rng, shape, scale, reach, pieces=(), kind=jnp.bfloat16):
    entries = scale * jax.random.normal(rng, shape, jnp.float32)
    if pieces:
        entries = entries * block_scale(rng, shape, pieces, -0.22, 0.18)
    return jnp.clip(entries, -reach, reach).astype(kind)


def setup_inputs(seed: int = 0) -> dict:
    splits = jax.random.split(jax.random.key(seed), 7)
    eastbound_current = scatter_about(splits[0], (VERTICAL_LAYERS, NORTHWARD_CELLS, EASTWARD_CELLS), 0.5, 3.0, ((1, 16), (2, 16)), jnp.float32)
    poleward_current = scatter_about(splits[1], (VERTICAL_LAYERS, NORTHWARD_CELLS, EASTWARD_CELLS), 0.5, 3.0, ((1, 16), (2, 16)), jnp.float32)
    warmth_excess = scatter_about(splits[2], (VERTICAL_LAYERS, NORTHWARD_CELLS, EASTWARD_CELLS), 1.0, 5.0, ((1, 16), (2, 16)), jnp.float32)
    saltiness_excess = scatter_about(splits[3], (VERTICAL_LAYERS, NORTHWARD_CELLS, EASTWARD_CELLS), 1.0, 5.0, ((1, 16), (2, 16)), jnp.float32)
    water_indicator = with_ends((jax.random.randint(splits[4], (VERTICAL_LAYERS, NORTHWARD_CELLS, EASTWARD_CELLS), 0, 5) < 4).astype(jnp.int32), jax.random.fold_in(splits[4], 1), 0, 1)
    column_layer_count = with_ends(jax.random.randint(splits[5], (NORTHWARD_CELLS, EASTWARD_CELLS), 1, VERTICAL_LAYERS + 1), jax.random.fold_in(splits[5], 1), 1, VERTICAL_LAYERS).astype(jnp.int32)
    return dict(eastbound_current=eastbound_current, poleward_current=poleward_current, warmth_excess=warmth_excess, saltiness_excess=saltiness_excess, water_indicator=water_indicator, column_layer_count=column_layer_count)


time_step = 0.2
lateral_diff = 0.1
vertical_diff = 0.5
pressure_coef = 0.1
drag_coef = 2.0
coriolis_max = 1.0
level_depth = 100.0
thermal_expand = 0.1655
haline_contract = 0.76554
cabbel_temp = 0.05952
cabbel_salt = 0.00054914
cabbel_mixed = 0.0024341
thermo_temp = 0.0001497
thermo_salt = 0.00001109


def view_at(field, lat_step, lon_step):
    rows = field.shape[1] - 2
    cols = field.shape[2] - 2
    return field[:, 1 + lat_step:1 + lat_step + rows, 1 + lon_step:1 + lon_step + cols]


def column_flux(centre, mixing):
    between = -vertical_diff * mixing * (centre[1:] - centre[:-1])
    surface = jnp.zeros_like(centre[:1])
    above = jnp.concatenate([surface, between], axis=0)
    below = jnp.concatenate([between, surface], axis=0)
    return above - below


def advance(extended, column_layer_count, row_start, total_rows):
    eastward = extended[0]
    northward = extended[1]
    temper = extended[2]
    saline = extended[3]
    wet = extended[4]
    levels = extended.shape[1]
    rows = extended.shape[2] - 2
    level_index = jnp.arange(levels, dtype=jnp.int32)[:, None, None]
    wet_here = view_at(wet, 0, 0)
    mask_east = wet_here * view_at(wet, 0, 1)
    mask_west = view_at(wet, 0, -1) * wet_here
    mask_north = wet_here * view_at(wet, 1, 0)
    mask_south = view_at(wet, -1, 0) * wet_here
    mixing = wet_here[:-1] * wet_here[1:] * (level_index[1:] < column_layer_count[None]).astype(jnp.float32)
    bottom = (level_index == column_layer_count[None] - 1).astype(jnp.float32)
    depth = (level_index.astype(jnp.float32) + 0.5) * level_depth
    density = (-thermal_expand * (1.0 + 0.5 * cabbel_temp * temper + thermo_temp * depth) * temper
               + haline_contract * (1.0 - 0.5 * cabbel_salt * saline - thermo_salt * depth) * saline
               - cabbel_mixed * temper * saline)
    pressure = jnp.cumsum(wet * density, axis=0)
    row_index = (row_start + jnp.arange(rows, dtype=jnp.int32)).astype(jnp.float32)[None, :, None]
    coriolis_t = coriolis_max * (2.0 * (row_index + 0.5) / total_rows - 1.0)
    coriolis_v = coriolis_max * (2.0 * (row_index + 1.0) / total_rows - 1.0)

    def tracer(field):
        centre = view_at(field, 0, 0)
        east_side = view_at(field, 0, 1)
        west_side = view_at(field, 0, -1)
        north_side = view_at(field, 1, 0)
        south_side = view_at(field, -1, 0)
        flux_east = mask_east * (view_at(eastward, 0, 0) * (centre + east_side) * 0.5 - lateral_diff * (east_side - centre))
        flux_west = mask_west * (view_at(eastward, 0, -1) * (west_side + centre) * 0.5 - lateral_diff * (centre - west_side))
        flux_north = mask_north * (view_at(northward, 0, 0) * (centre + north_side) * 0.5 - lateral_diff * (north_side - centre))
        flux_south = mask_south * (view_at(northward, -1, 0) * (south_side + centre) * 0.5 - lateral_diff * (centre - south_side))
        tendency = (flux_west - flux_east) + (flux_south - flux_north) + column_flux(centre, mixing)
        return wet_here * (centre + time_step * tendency)

    east_here = view_at(eastward, 0, 0)
    north_here = view_at(northward, 0, 0)
    corner_ne = wet_here * view_at(wet, 0, 1) * view_at(wet, 1, 0) * view_at(wet, 1, 1)
    corner_se = view_at(wet, -1, 0) * view_at(wet, -1, 1) * wet_here * view_at(wet, 0, 1)
    corner_nw = view_at(wet, 0, -1) * wet_here * view_at(wet, 1, -1) * view_at(wet, 1, 0)

    cell_east = view_at(wet, 0, 1) * (((east_here + view_at(eastward, 0, 1)) * 0.5) ** 2
                                     - lateral_diff * (view_at(eastward, 0, 1) - east_here))
    cell_west = wet_here * (((view_at(eastward, 0, -1) + east_here) * 0.5) ** 2
                           - lateral_diff * (east_here - view_at(eastward, 0, -1)))
    product_ne = (north_here + view_at(northward, 0, 1)) * 0.5 * (east_here + view_at(eastward, 1, 0)) * 0.5
    product_se = (view_at(northward, -1, 0) + view_at(northward, -1, 1)) * 0.5 * (view_at(eastward, -1, 0) + east_here) * 0.5
    product_nw = (view_at(eastward, 0, -1) + view_at(eastward, 1, -1)) * 0.5 * (view_at(northward, 0, -1) + north_here) * 0.5
    shear_north = corner_ne * (product_ne - lateral_diff * (view_at(eastward, 1, 0) - east_here))
    shear_south = corner_se * (product_se - lateral_diff * (east_here - view_at(eastward, -1, 0)))
    north_mean = (north_here + view_at(northward, 0, 1) + view_at(northward, -1, 0) + view_at(northward, -1, 1)) * 0.25
    east_tend = ((cell_west - cell_east) + (shear_south - shear_north) + coriolis_t * north_mean
                 - pressure_coef * (view_at(pressure, 0, 1) - view_at(pressure, 0, 0))
                 + column_flux(east_here, mixing) - drag_coef * bottom * east_here)
    east_next = mask_east * (east_here + time_step * east_tend)

    cell_north = view_at(wet, 1, 0) * (((north_here + view_at(northward, 1, 0)) * 0.5) ** 2
                                      - lateral_diff * (view_at(northward, 1, 0) - north_here))
    cell_south = wet_here * (((view_at(northward, -1, 0) + north_here) * 0.5) ** 2
                            - lateral_diff * (north_here - view_at(northward, -1, 0)))
    stress_east = corner_ne * (product_ne - lateral_diff * (view_at(northward, 0, 1) - north_here))
    stress_west = corner_nw * (product_nw - lateral_diff * (north_here - view_at(northward, 0, -1)))
    east_mean = (east_here + view_at(eastward, 0, -1) + view_at(eastward, 1, 0) + view_at(eastward, 1, -1)) * 0.25
    north_tend = ((stress_west - stress_east) + (cell_south - cell_north) - coriolis_v * east_mean
                  - pressure_coef * (view_at(pressure, 1, 0) - view_at(pressure, 0, 0))
                  + column_flux(north_here, mixing) - drag_coef * bottom * north_here)
    north_next = mask_north * (north_here + time_step * north_tend)
    return east_next, north_next, tracer(temper), tracer(saline)


def extend_all(tracer_bundle):
    sign = jnp.array([-1.0, -1.0, 1.0, 1.0, 1.0], dtype=jnp.float32)[:, None, None, None]
    widened = jnp.concatenate([tracer_bundle[..., -1:], tracer_bundle, tracer_bundle[..., :1]], axis=3)
    northern = sign * widened[:, :, -1:, ::-1]
    southern = jnp.zeros_like(northern)
    return jnp.concatenate([southern, widened, northern], axis=2)


def reference(eastbound_current, poleward_current, warmth_excess, saltiness_excess, water_indicator, column_layer_count):
    tracer_bundle = jnp.stack([eastbound_current, poleward_current, warmth_excess, saltiness_excess, water_indicator.astype(jnp.float32)])
    extended = extend_all(tracer_bundle)
    east_parts = []
    north_parts = []
    temp_parts = []
    salt_parts = []
    for block in range(N_LAT):
        start = block * CY
        results = advance(extended[:, :, start:start + CY + 2, :], column_layer_count[start:start + CY], start, NORTHWARD_CELLS)
        east_parts.append(results[0])
        north_parts.append(results[1])
        temp_parts.append(results[2])
        salt_parts.append(results[3])
    return (jnp.concatenate(east_parts, axis=1), jnp.concatenate(north_parts, axis=1),
            jnp.concatenate(temp_parts, axis=1), jnp.concatenate(salt_parts, axis=1))
```

```python
import jax
import jax.numpy as jnp
from jax import lax
from jax.sharding import PartitionSpec as P

time_step = 0.2
lateral_diff = 0.1
vertical_diff = 0.5
pressure_coef = 0.1
drag_coef = 2.0
coriolis_max = 1.0
level_depth = 100.0
thermal_expand = 0.1655
haline_contract = 0.76554
cabbel_temp = 0.05952
cabbel_salt = 0.00054914
cabbel_mixed = 0.0024341
thermo_temp = 0.0001497
thermo_salt = 1.109e-05


def view_at(field, lat_step, lon_step):
    rows = field.shape[1] - 2
    cols = field.shape[2] - 2
    return field[:, 1 + lat_step : 1 + lat_step + rows, 1 + lon_step : 1 + lon_step + cols]


def column_flux(centre, mixing):
    between = -vertical_diff * mixing * (centre[1:] - centre[:-1])
    surface = jnp.zeros_like(centre[:1])
    above = jnp.concatenate([surface, between], axis=0)
    below = jnp.concatenate([between, surface], axis=0)
    return above - below


def advance(extended, column_layer_count, row_start, total_rows):
    eastward = extended[0]
    northward = extended[1]
    temper = extended[2]
    saline = extended[3]
    wet = extended[4]
    levels = extended.shape[1]
    rows = extended.shape[2] - 2
    level_index = jnp.arange(levels, dtype=jnp.int32)[:, None, None]
    wet_here = view_at(wet, 0, 0)
    mask_east = wet_here * view_at(wet, 0, 1)
    mask_west = view_at(wet, 0, -1) * wet_here
    mask_north = wet_here * view_at(wet, 1, 0)
    mask_south = view_at(wet, -1, 0) * wet_here
    mixing = (
        wet_here[:-1]
        * wet_here[1:]
        * (level_index[1:] < column_layer_count[None]).astype(jnp.float32)
    )
    bottom = (level_index == column_layer_count[None] - 1).astype(jnp.float32)
    depth = (level_index.astype(jnp.float32) + 0.5) * level_depth
    density = (
        -thermal_expand * (1.0 + 0.5 * cabbel_temp * temper + thermo_temp * depth) * temper
        + haline_contract * (1.0 - 0.5 * cabbel_salt * saline - thermo_salt * depth) * saline
        - cabbel_mixed * temper * saline
    )
    pressure = jnp.cumsum(wet * density, axis=0)
    row_index = (row_start + jnp.arange(rows, dtype=jnp.int32)).astype(jnp.float32)[None, :, None]
    coriolis_t = coriolis_max * (2.0 * (row_index + 0.5) / total_rows - 1.0)
    coriolis_v = coriolis_max * (2.0 * (row_index + 1.0) / total_rows - 1.0)

    def tracer(field):
        centre = view_at(field, 0, 0)
        east_side = view_at(field, 0, 1)
        west_side = view_at(field, 0, -1)
        north_side = view_at(field, 1, 0)
        south_side = view_at(field, -1, 0)
        flux_east = mask_east * (
            view_at(eastward, 0, 0) * (centre + east_side) * 0.5
            - lateral_diff * (east_side - centre)
        )
        flux_west = mask_west * (
            view_at(eastward, 0, -1) * (west_side + centre) * 0.5
            - lateral_diff * (centre - west_side)
        )
        flux_north = mask_north * (
            view_at(northward, 0, 0) * (centre + north_side) * 0.5
            - lateral_diff * (north_side - centre)
        )
        flux_south = mask_south * (
            view_at(northward, -1, 0) * (south_side + centre) * 0.5
            - lateral_diff * (centre - south_side)
        )
        tendency = flux_west - flux_east + (flux_south - flux_north) + column_flux(centre, mixing)
        return wet_here * (centre + time_step * tendency)

    east_here = view_at(eastward, 0, 0)
    north_here = view_at(northward, 0, 0)
    corner_ne = wet_here * view_at(wet, 0, 1) * view_at(wet, 1, 0) * view_at(wet, 1, 1)
    corner_se = view_at(wet, -1, 0) * view_at(wet, -1, 1) * wet_here * view_at(wet, 0, 1)
    corner_nw = view_at(wet, 0, -1) * wet_here * view_at(wet, 1, -1) * view_at(wet, 1, 0)
    cell_east = view_at(wet, 0, 1) * (
        ((east_here + view_at(eastward, 0, 1)) * 0.5) ** 2
        - lateral_diff * (view_at(eastward, 0, 1) - east_here)
    )
    cell_west = wet_here * (
        ((view_at(eastward, 0, -1) + east_here) * 0.5) ** 2
        - lateral_diff * (east_here - view_at(eastward, 0, -1))
    )
    product_ne = (
        (north_here + view_at(northward, 0, 1)) * 0.5 * (east_here + view_at(eastward, 1, 0)) * 0.5
    )
    product_se = (
        (view_at(northward, -1, 0) + view_at(northward, -1, 1))
        * 0.5
        * (view_at(eastward, -1, 0) + east_here)
        * 0.5
    )
    product_nw = (
        (view_at(eastward, 0, -1) + view_at(eastward, 1, -1))
        * 0.5
        * (view_at(northward, 0, -1) + north_here)
        * 0.5
    )
    shear_north = corner_ne * (product_ne - lateral_diff * (view_at(eastward, 1, 0) - east_here))
    shear_south = corner_se * (product_se - lateral_diff * (east_here - view_at(eastward, -1, 0)))
    north_mean = (
        north_here
        + view_at(northward, 0, 1)
        + view_at(northward, -1, 0)
        + view_at(northward, -1, 1)
    ) * 0.25
    east_tend = (
        cell_west
        - cell_east
        + (shear_south - shear_north)
        + coriolis_t * north_mean
        - pressure_coef * (view_at(pressure, 0, 1) - view_at(pressure, 0, 0))
        + column_flux(east_here, mixing)
        - drag_coef * bottom * east_here
    )
    east_next = mask_east * (east_here + time_step * east_tend)
    cell_north = view_at(wet, 1, 0) * (
        ((north_here + view_at(northward, 1, 0)) * 0.5) ** 2
        - lateral_diff * (view_at(northward, 1, 0) - north_here)
    )
    cell_south = wet_here * (
        ((view_at(northward, -1, 0) + north_here) * 0.5) ** 2
        - lateral_diff * (north_here - view_at(northward, -1, 0))
    )
    stress_east = corner_ne * (product_ne - lateral_diff * (view_at(northward, 0, 1) - north_here))
    stress_west = corner_nw * (product_nw - lateral_diff * (north_here - view_at(northward, 0, -1)))
    east_mean = (
        east_here + view_at(eastward, 0, -1) + view_at(eastward, 1, 0) + view_at(eastward, 1, -1)
    ) * 0.25
    north_tend = (
        stress_west
        - stress_east
        + (cell_south - cell_north)
        - coriolis_v * east_mean
        - pressure_coef * (view_at(pressure, 1, 0) - view_at(pressure, 0, 0))
        + column_flux(north_here, mixing)
        - drag_coef * bottom * north_here
    )
    north_next = mask_north * (north_here + time_step * north_tend)
    return (east_next, north_next, tracer(temper), tracer(saline))


def shift(value, mapping):
    lat_size = lax.axis_size("lat")
    lon_size = lax.axis_size("lon")
    pairs = []
    for a in range(lat_size):
        for b in range(lon_size):
            target = mapping(a, b, lat_size, lon_size)
            if target is not None:
                pairs.append((b * lat_size + a, target[1] * lat_size + target[0]))
    return lax.ppermute(value, ("lon", "lat"), pairs)


def per_device(
    eastbound_current,
    poleward_current,
    warmth_excess,
    saltiness_excess,
    water_indicator,
    column_layer_count,
):
    fields = jnp.stack(
        (
            eastbound_current,
            poleward_current,
            warmth_excess,
            saltiness_excess,
            water_indicator.astype(jnp.float32),
        )
    )
    top = fields[:, :, -1, :]
    bottom = fields[:, :, 0, :]
    west_col = fields[:, :, :, 0]
    east_col = fields[:, :, :, -1]

    def east_of(a, b, na, nl):
        return (a, (b + 1) % nl)

    def west_of(a, b, na, nl):
        return (a, (b - 1) % nl)

    def north_of(a, b, na, nl):
        return (a + 1, b) if a + 1 < na else None

    def south_of(a, b, na, nl):
        return (a - 1, b) if a > 0 else None

    def north_east(a, b, na, nl):
        return (a + 1, (b + 1) % nl) if a + 1 < na else None

    def north_west(a, b, na, nl):
        return (a + 1, (b - 1) % nl) if a + 1 < na else None

    def south_east(a, b, na, nl):
        return (a - 1, (b + 1) % nl) if a > 0 else None

    def south_west(a, b, na, nl):
        return (a - 1, (b - 1) % nl) if a > 0 else None

    def mirror(a, b, na, nl):
        return (a, nl - 1 - b) if a == na - 1 else None

    def mirror_left(a, b, na, nl):
        return (a, (nl - b) % nl) if a == na - 1 else None

    def mirror_right(a, b, na, nl):
        return (a, (nl - 2 - b) % nl) if a == na - 1 else None

    halo_west = shift(east_col, east_of)
    halo_east = shift(west_col, west_of)
    halo_south = shift(top, north_of)
    halo_north = shift(bottom, south_of)
    corner_sw = shift(top[:, :, -1:], north_east)
    corner_se = shift(top[:, :, :1], north_west)
    corner_nw = shift(bottom[:, :, -1:], south_east)
    corner_ne = shift(bottom[:, :, :1], south_west)
    fold_row = shift(top, mirror)
    fold_left = shift(top[:, :, :1], mirror_left)
    fold_right = shift(top[:, :, -1:], mirror_right)

    sign = jnp.array([-1.0, -1.0, 1.0, 1.0, 1.0], dtype=jnp.float32)[:, None, None]
    ghost = sign * jnp.concatenate([fold_left, fold_row[:, :, ::-1], fold_right], axis=2)
    north_row = jnp.concatenate([corner_nw, halo_north, corner_ne], axis=2)
    is_top = lax.axis_index("lat") == lax.axis_size("lat") - 1
    north_row = jnp.where(is_top, ghost, north_row)
    south_row = jnp.concatenate([corner_sw, halo_south, corner_se], axis=2)
    middle = jnp.concatenate([halo_west[..., None], fields, halo_east[..., None]], axis=3)
    extended = jnp.concatenate([south_row[:, :, None, :], middle, north_row[:, :, None, :]], axis=2)
    rows = eastbound_current.shape[1]
    row_start = lax.axis_index("lat") * rows
    total_rows = rows * lax.axis_size("lat")
    return advance(extended, column_layer_count, row_start, total_rows)


def solution(mesh):
    placed = (
        P(None, "lat", "lon"),
        P(None, "lat", "lon"),
        P(None, "lat", "lon"),
        P(None, "lat", "lon"),
        P(None, "lat", "lon"),
        P("lat", "lon"),
    )
    return jax.shard_map(
        per_device,
        mesh=mesh,
        in_specs=placed,
        out_specs=(
            P(None, "lat", "lon"),
            P(None, "lat", "lon"),
            P(None, "lat", "lon"),
            P(None, "lat", "lon"),
        ),
        check_vma=False,
    )
```

```python
import jax
import jax.numpy as jnp
from jax import lax
from jax.experimental import pallas as pl
from jax.experimental.pallas import tpu as pltpu
from jax.sharding import PartitionSpec as P

time_step = 0.2
lateral_diff = 0.1
vertical_diff = 0.5
pressure_coef = 0.1
drag_coef = 2.0
coriolis_max = 1.0
level_depth = 100.0
thermal_expand = 0.1655
haline_contract = 0.76554
cabbel_temp = 0.05952
cabbel_salt = 0.00054914
cabbel_mixed = 0.0024341
thermo_temp = 0.0001497
thermo_salt = 1.109e-05


def view_at(field, lat_step, lon_step):
    rows = field.shape[1] - 2
    cols = field.shape[2] - 2
    return field[:, 1 + lat_step : 1 + lat_step + rows, 1 + lon_step : 1 + lon_step + cols]


def column_flux(centre, mixing):
    between = -vertical_diff * mixing * (centre[1:] - centre[:-1])
    surface = jnp.zeros_like(centre[:1])
    above = jnp.concatenate([surface, between], axis=0)
    below = jnp.concatenate([between, surface], axis=0)
    return above - below


def advance(extended, column_layer_count, row_start, total_rows):
    eastward = extended[0]
    northward = extended[1]
    temper = extended[2]
    saline = extended[3]
    wet = extended[4]
    levels = extended.shape[1]
    rows = extended.shape[2] - 2
    level_index = jnp.arange(levels, dtype=jnp.int32)[:, None, None]
    wet_here = view_at(wet, 0, 0)
    mask_east = wet_here * view_at(wet, 0, 1)
    mask_west = view_at(wet, 0, -1) * wet_here
    mask_north = wet_here * view_at(wet, 1, 0)
    mask_south = view_at(wet, -1, 0) * wet_here
    mixing = (
        wet_here[:-1]
        * wet_here[1:]
        * (level_index[1:] < column_layer_count[None]).astype(jnp.float32)
    )
    bottom = (level_index == column_layer_count[None] - 1).astype(jnp.float32)
    depth = (level_index.astype(jnp.float32) + 0.5) * level_depth
    density = (
        -thermal_expand * (1.0 + 0.5 * cabbel_temp * temper + thermo_temp * depth) * temper
        + haline_contract * (1.0 - 0.5 * cabbel_salt * saline - thermo_salt * depth) * saline
        - cabbel_mixed * temper * saline
    )
    pressure = jnp.cumsum(wet * density, axis=0)
    row_index = (row_start + jnp.arange(rows, dtype=jnp.int32)).astype(jnp.float32)[None, :, None]
    coriolis_t = coriolis_max * (2.0 * (row_index + 0.5) / total_rows - 1.0)
    coriolis_v = coriolis_max * (2.0 * (row_index + 1.0) / total_rows - 1.0)

    def tracer(field):
        centre = view_at(field, 0, 0)
        east_side = view_at(field, 0, 1)
        west_side = view_at(field, 0, -1)
        north_side = view_at(field, 1, 0)
        south_side = view_at(field, -1, 0)
        flux_east = mask_east * (
            view_at(eastward, 0, 0) * (centre + east_side) * 0.5
            - lateral_diff * (east_side - centre)
        )
        flux_west = mask_west * (
            view_at(eastward, 0, -1) * (west_side + centre) * 0.5
            - lateral_diff * (centre - west_side)
        )
        flux_north = mask_north * (
            view_at(northward, 0, 0) * (centre + north_side) * 0.5
            - lateral_diff * (north_side - centre)
        )
        flux_south = mask_south * (
            view_at(northward, -1, 0) * (south_side + centre) * 0.5
            - lateral_diff * (centre - south_side)
        )
        tendency = flux_west - flux_east + (flux_south - flux_north) + column_flux(centre, mixing)
        return wet_here * (centre + time_step * tendency)

    east_here = view_at(eastward, 0, 0)
    north_here = view_at(northward, 0, 0)
    corner_ne = wet_here * view_at(wet, 0, 1) * view_at(wet, 1, 0) * view_at(wet, 1, 1)
    corner_se = view_at(wet, -1, 0) * view_at(wet, -1, 1) * wet_here * view_at(wet, 0, 1)
    corner_nw = view_at(wet, 0, -1) * wet_here * view_at(wet, 1, -1) * view_at(wet, 1, 0)
    cell_east = view_at(wet, 0, 1) * (
        ((east_here + view_at(eastward, 0, 1)) * 0.5) ** 2
        - lateral_diff * (view_at(eastward, 0, 1) - east_here)
    )
    cell_west = wet_here * (
        ((view_at(eastward, 0, -1) + east_here) * 0.5) ** 2
        - lateral_diff * (east_here - view_at(eastward, 0, -1))
    )
    product_ne = (
        (north_here + view_at(northward, 0, 1)) * 0.5 * (east_here + view_at(eastward, 1, 0)) * 0.5
    )
    product_se = (
        (view_at(northward, -1, 0) + view_at(northward, -1, 1))
        * 0.5
        * (view_at(eastward, -1, 0) + east_here)
        * 0.5
    )
    product_nw = (
        (view_at(eastward, 0, -1) + view_at(eastward, 1, -1))
        * 0.5
        * (view_at(northward, 0, -1) + north_here)
        * 0.5
    )
    shear_north = corner_ne * (product_ne - lateral_diff * (view_at(eastward, 1, 0) - east_here))
    shear_south = corner_se * (product_se - lateral_diff * (east_here - view_at(eastward, -1, 0)))
    north_mean = (
        north_here
        + view_at(northward, 0, 1)
        + view_at(northward, -1, 0)
        + view_at(northward, -1, 1)
    ) * 0.25
    east_tend = (
        cell_west
        - cell_east
        + (shear_south - shear_north)
        + coriolis_t * north_mean
        - pressure_coef * (view_at(pressure, 0, 1) - view_at(pressure, 0, 0))
        + column_flux(east_here, mixing)
        - drag_coef * bottom * east_here
    )
    east_next = mask_east * (east_here + time_step * east_tend)
    cell_north = view_at(wet, 1, 0) * (
        ((north_here + view_at(northward, 1, 0)) * 0.5) ** 2
        - lateral_diff * (view_at(northward, 1, 0) - north_here)
    )
    cell_south = wet_here * (
        ((view_at(northward, -1, 0) + north_here) * 0.5) ** 2
        - lateral_diff * (north_here - view_at(northward, -1, 0))
    )
    stress_east = corner_ne * (product_ne - lateral_diff * (view_at(northward, 0, 1) - north_here))
    stress_west = corner_nw * (product_nw - lateral_diff * (north_here - view_at(northward, 0, -1)))
    east_mean = (
        east_here + view_at(eastward, 0, -1) + view_at(eastward, 1, 0) + view_at(eastward, 1, -1)
    ) * 0.25
    north_tend = (
        stress_west
        - stress_east
        + (cell_south - cell_north)
        - coriolis_v * east_mean
        - pressure_coef * (view_at(pressure, 1, 0) - view_at(pressure, 0, 0))
        + column_flux(north_here, mixing)
        - drag_coef * bottom * north_here
    )
    north_next = mask_north * (north_here + time_step * north_tend)
    return (east_next, north_next, tracer(temper), tracer(saline))


def shift(value, mapping):
    lat_size = lax.axis_size("lat")
    lon_size = lax.axis_size("lon")
    pairs = []
    for a in range(lat_size):
        for b in range(lon_size):
            target = mapping(a, b, lat_size, lon_size)
            if target is not None:
                pairs.append((b * lat_size + a, target[1] * lat_size + target[0]))
    return lax.ppermute(value, ("lon", "lat"), pairs)


def stencil_kernel(
    cor_ref, u_ref, v_ref, t_ref, s_ref, wet_ref, clc_ref, rows_ref, cols_ref,
    east_ref, north_ref, temp_ref, salt_ref,
):
    levels, rows, cols = u_ref.shape
    fields = 5
    lane = lax.broadcasted_iota(jnp.int32, (rows, cols), 1)
    sub = lax.broadcasted_iota(jnp.int32, (rows, cols), 0)
    at_east = lane == cols - 1
    at_west = lane == 0
    at_north = sub == rows - 1
    at_south = sub == 0
    cor_t = cor_ref[0]
    cor_v = cor_ref[1]
    count = clc_ref[...]

    def east(x, col):
        return jnp.where(at_east, col, pltpu.roll(x, cols - 1, 1))

    def west(x, col):
        return jnp.where(at_west, col, pltpu.roll(x, 1, 1))

    def north(x, row):
        return jnp.where(at_north, row, pltpu.roll(x, rows - 1, 0))

    def south(x, row):
        return jnp.where(at_south, row, pltpu.roll(x, 1, 0))

    def body(k, carry):
        pres, pres_e, pres_n = carry
        km = jnp.maximum(k - 1, 0)
        kp = jnp.minimum(k + 1, levels - 1)

        def row(variant, field):
            return rows_ref[variant * fields + field, pl.ds(k, 1), :]

        def col(field):
            pair = cols_ref[field, k]
            return pair[:, 0:1], pair[:, 1:2]

        w = wet_ref[k].astype(jnp.float32)
        w_above = wet_ref[km].astype(jnp.float32)
        w_below = wet_ref[kp].astype(jnp.float32)
        w_wc, w_ec = col(4)
        w_e = east(w, w_ec)
        w_w = west(w, w_wc)
        w_n = north(w, row(0, 4))
        w_s = south(w, row(3, 4))
        w_ne = north(w_e, row(1, 4))
        w_se = south(w_e, row(4, 4))
        w_nw = north(w_w, row(2, 4))
        mask_east = w * w_e
        mask_west = w_w * w
        mask_north = w * w_n
        mask_south = w_s * w
        mix_below = jnp.where(
            k < levels - 1, w * w_below * (k + 1 < count).astype(jnp.float32), 0.0
        )
        mix_above = jnp.where(k > 0, w_above * w * (k < count).astype(jnp.float32), 0.0)
        bottom = (k == count - 1).astype(jnp.float32)

        def column(ref, centre):
            upper = ref[km]
            lower = ref[kp]
            above = -vertical_diff * mix_above * (centre - upper)
            below = -vertical_diff * mix_below * (lower - centre)
            return above - below

        depth = (k.astype(jnp.float32) + 0.5) * level_depth

        def density(temper, saline):
            return (
                -thermal_expand * (1.0 + 0.5 * cabbel_temp * temper + thermo_temp * depth) * temper
                + haline_contract * (1.0 - 0.5 * cabbel_salt * saline - thermo_salt * depth) * saline
                - cabbel_mixed * temper * saline
            )

        tc = t_ref[k]
        sc = s_ref[k]
        t_wc, t_ec = col(2)
        s_wc, s_ec = col(3)
        pres = pres + w * density(tc, sc)
        pres_e = pres_e + w_ec * density(t_ec, s_ec)
        pres_n = pres_n + row(0, 4) * density(row(0, 2), row(0, 3))
        p_e = east(pres, pres_e)
        p_n = north(pres, pres_n)

        uc = u_ref[k]
        u_wc, u_ec = col(0)
        u_e = east(uc, u_ec)
        u_w = west(uc, u_wc)
        u_n = north(uc, row(0, 0))
        u_s = south(uc, row(3, 0))
        u_nw = north(u_w, row(2, 0))
        vc = v_ref[k]
        v_wc, v_ec = col(1)
        v_e = east(vc, v_ec)
        v_w = west(vc, v_wc)
        v_n = north(vc, row(0, 1))
        v_s = south(vc, row(3, 1))
        v_se = south(v_e, row(4, 1))

        def tracer(ref, centre, field, wcol, ecol):
            east_side = east(centre, ecol)
            west_side = west(centre, wcol)
            north_side = north(centre, row(0, field))
            south_side = south(centre, row(3, field))
            flux_east = mask_east * (
                uc * (centre + east_side) * 0.5 - lateral_diff * (east_side - centre)
            )
            flux_west = mask_west * (
                u_w * (west_side + centre) * 0.5 - lateral_diff * (centre - west_side)
            )
            flux_north = mask_north * (
                vc * (centre + north_side) * 0.5 - lateral_diff * (north_side - centre)
            )
            flux_south = mask_south * (
                v_s * (south_side + centre) * 0.5 - lateral_diff * (centre - south_side)
            )
            tendency = (
                flux_west - flux_east + (flux_south - flux_north) + column(ref, centre)
            )
            return w * (centre + time_step * tendency)

        temp_ref[k] = tracer(t_ref, tc, 2, t_wc, t_ec)
        salt_ref[k] = tracer(s_ref, sc, 3, s_wc, s_ec)

        corner_ne = w * w_e * w_n * w_ne
        corner_se = w_s * w_se * w * w_e
        corner_nw = w_w * w * w_nw * w_n
        half_e = (uc + u_e) * 0.5
        cell_east = w_e * (half_e * half_e - lateral_diff * (u_e - uc))
        half_w = (u_w + uc) * 0.5
        cell_west = w * (half_w * half_w - lateral_diff * (uc - u_w))
        product_ne = (vc + v_e) * 0.5 * (uc + u_n) * 0.5
        product_se = (v_s + v_se) * 0.5 * (u_s + uc) * 0.5
        product_nw = (u_w + u_nw) * 0.5 * (v_w + vc) * 0.5
        shear_north = corner_ne * (product_ne - lateral_diff * (u_n - uc))
        shear_south = corner_se * (product_se - lateral_diff * (uc - u_s))
        north_mean = (vc + v_e + v_s + v_se) * 0.25
        east_tend = (
            cell_west
            - cell_east
            + (shear_south - shear_north)
            + cor_t * north_mean
            - pressure_coef * (p_e - pres)
            + column(u_ref, uc)
            - drag_coef * bottom * uc
        )
        east_ref[k] = mask_east * (uc + time_step * east_tend)
        half_n = (vc + v_n) * 0.5
        cell_north = w_n * (half_n * half_n - lateral_diff * (v_n - vc))
        half_s = (v_s + vc) * 0.5
        cell_south = w * (half_s * half_s - lateral_diff * (vc - v_s))
        stress_east = corner_ne * (product_ne - lateral_diff * (v_e - vc))
        stress_west = corner_nw * (product_nw - lateral_diff * (vc - v_w))
        east_mean = (uc + u_w + u_n + u_nw) * 0.25
        north_tend = (
            stress_west
            - stress_east
            + (cell_south - cell_north)
            - cor_v * east_mean
            - pressure_coef * (p_n - pres)
            + column(v_ref, vc)
            - drag_coef * bottom * vc
        )
        north_ref[k] = mask_north * (vc + time_step * north_tend)
        return pres, pres_e, pres_n

    init = (
        jnp.zeros((rows, cols), jnp.float32),
        jnp.zeros((rows, 1), jnp.float32),
        jnp.zeros((1, cols), jnp.float32),
    )
    lax.fori_loop(0, levels, body, init)


def per_device(
    eastbound_current,
    poleward_current,
    warmth_excess,
    saltiness_excess,
    water_indicator,
    column_layer_count,
):
    inputs = (
        eastbound_current,
        poleward_current,
        warmth_excess,
        saltiness_excess,
        water_indicator,
    )

    def edge(pick):
        return jnp.stack([pick(field).astype(jnp.float32) for field in inputs])

    top = edge(lambda f: f[:, -1, :])
    bottom = edge(lambda f: f[:, 0, :])
    west_col = edge(lambda f: f[:, :, 0])
    east_col = edge(lambda f: f[:, :, -1])

    def east_of(a, b, na, nl):
        return (a, (b + 1) % nl)

    def west_of(a, b, na, nl):
        return (a, (b - 1) % nl)

    def north_of(a, b, na, nl):
        return (a + 1, b) if a + 1 < na else None

    def south_of(a, b, na, nl):
        return (a - 1, b) if a > 0 else None

    def north_east(a, b, na, nl):
        return (a + 1, (b + 1) % nl) if a + 1 < na else None

    def north_west(a, b, na, nl):
        return (a + 1, (b - 1) % nl) if a + 1 < na else None

    def south_east(a, b, na, nl):
        return (a - 1, (b + 1) % nl) if a > 0 else None

    def south_west(a, b, na, nl):
        return (a - 1, (b - 1) % nl) if a > 0 else None

    def mirror(a, b, na, nl):
        return (a, nl - 1 - b) if a == na - 1 else None

    def mirror_left(a, b, na, nl):
        return (a, (nl - b) % nl) if a == na - 1 else None

    def mirror_right(a, b, na, nl):
        return (a, (nl - 2 - b) % nl) if a == na - 1 else None

    halo_west = shift(east_col, east_of)
    halo_east = shift(west_col, west_of)
    halo_south = shift(top, north_of)
    halo_north = shift(bottom, south_of)
    corner_sw = shift(top[:, :, -1:], north_east)
    corner_se = shift(top[:, :, :1], north_west)
    corner_nw = shift(bottom[:, :, -1:], south_east)
    corner_ne = shift(bottom[:, :, :1], south_west)
    fold_row = shift(top, mirror)
    fold_left = shift(top[:, :, :1], mirror_left)
    fold_right = shift(top[:, :, -1:], mirror_right)

    sign = jnp.array([-1.0, -1.0, 1.0, 1.0, 1.0], dtype=jnp.float32)[:, None, None]
    ghost = sign * jnp.concatenate([fold_left, fold_row[:, :, ::-1], fold_right], axis=2)
    north_row = jnp.concatenate([corner_nw, halo_north, corner_ne], axis=2)
    is_top = lax.axis_index("lat") == lax.axis_size("lat") - 1
    north_row = jnp.where(is_top, ghost, north_row)
    south_row = jnp.concatenate([corner_sw, halo_south, corner_se], axis=2)
    width = top.shape[2]
    halo_rows = jnp.stack(
        [
            north_row[:, :, 1 : width + 1],
            north_row[:, :, 2 : width + 2],
            north_row[:, :, 0:width],
            south_row[:, :, 1 : width + 1],
            south_row[:, :, 2 : width + 2],
            south_row[:, :, 0:width],
        ]
    )
    halo_rows = halo_rows.reshape((-1,) + halo_rows.shape[2:])
    halo_cols = jnp.stack([halo_west, halo_east], axis=-1)

    levels, rows, cols = eastbound_current.shape
    row_start = lax.axis_index("lat") * rows
    total_rows = rows * lax.axis_size("lat")
    row_index = (row_start + jnp.arange(rows, dtype=jnp.int32)).astype(jnp.float32)[:, None]
    coriolis_t = coriolis_max * (2.0 * (row_index + 0.5) / total_rows - 1.0)
    coriolis_v = coriolis_max * (2.0 * (row_index + 1.0) / total_rows - 1.0)
    coriolis = jnp.broadcast_to(jnp.stack([coriolis_t, coriolis_v]), (2, rows, cols))

    block = jax.ShapeDtypeStruct((levels, rows, cols), jnp.float32)
    return pl.pallas_call(
        stencil_kernel,
        out_shape=(block, block, block, block),
    )(
        coriolis,
        eastbound_current,
        poleward_current,
        warmth_excess,
        saltiness_excess,
        water_indicator,
        column_layer_count,
        halo_rows,
        halo_cols,
    )


def solution(mesh):
    placed = (
        P(None, "lat", "lon"),
        P(None, "lat", "lon"),
        P(None, "lat", "lon"),
        P(None, "lat", "lon"),
        P(None, "lat", "lon"),
        P("lat", "lon"),
    )
    return jax.shard_map(
        per_device,
        mesh=mesh,
        in_specs=placed,
        out_specs=(
            P(None, "lat", "lon"),
            P(None, "lat", "lon"),
            P(None, "lat", "lon"),
            P(None, "lat", "lon"),
        ),
        check_vma=False,
    )
```

```python
import jax
import jax.numpy as jnp
from jax import lax
from jax.experimental import pallas as pl
from jax.experimental.pallas import tpu as pltpu
from jax.sharding import PartitionSpec as P

time_step = 0.2
lateral_diff = 0.1
vertical_diff = 0.5
pressure_coef = 0.1
drag_coef = 2.0
coriolis_max = 1.0
level_depth = 100.0
thermal_expand = 0.1655
haline_contract = 0.76554
cabbel_temp = 0.05952
cabbel_salt = 0.00054914
cabbel_mixed = 0.0024341
thermo_temp = 0.0001497
thermo_salt = 1.109e-05


def view_at(field, lat_step, lon_step):
    rows = field.shape[1] - 2
    cols = field.shape[2] - 2
    return field[:, 1 + lat_step : 1 + lat_step + rows, 1 + lon_step : 1 + lon_step + cols]


def column_flux(centre, mixing):
    between = -vertical_diff * mixing * (centre[1:] - centre[:-1])
    surface = jnp.zeros_like(centre[:1])
    above = jnp.concatenate([surface, between], axis=0)
    below = jnp.concatenate([between, surface], axis=0)
    return above - below


def advance(extended, column_layer_count, row_start, total_rows):
    eastward = extended[0]
    northward = extended[1]
    temper = extended[2]
    saline = extended[3]
    wet = extended[4]
    levels = extended.shape[1]
    rows = extended.shape[2] - 2
    level_index = jnp.arange(levels, dtype=jnp.int32)[:, None, None]
    wet_here = view_at(wet, 0, 0)
    mask_east = wet_here * view_at(wet, 0, 1)
    mask_west = view_at(wet, 0, -1) * wet_here
    mask_north = wet_here * view_at(wet, 1, 0)
    mask_south = view_at(wet, -1, 0) * wet_here
    mixing = (
        wet_here[:-1]
        * wet_here[1:]
        * (level_index[1:] < column_layer_count[None]).astype(jnp.float32)
    )
    bottom = (level_index == column_layer_count[None] - 1).astype(jnp.float32)
    depth = (level_index.astype(jnp.float32) + 0.5) * level_depth
    density = (
        -thermal_expand * (1.0 + 0.5 * cabbel_temp * temper + thermo_temp * depth) * temper
        + haline_contract * (1.0 - 0.5 * cabbel_salt * saline - thermo_salt * depth) * saline
        - cabbel_mixed * temper * saline
    )
    pressure = jnp.cumsum(wet * density, axis=0)
    row_index = (row_start + jnp.arange(rows, dtype=jnp.int32)).astype(jnp.float32)[None, :, None]
    coriolis_t = coriolis_max * (2.0 * (row_index + 0.5) / total_rows - 1.0)
    coriolis_v = coriolis_max * (2.0 * (row_index + 1.0) / total_rows - 1.0)

    def tracer(field):
        centre = view_at(field, 0, 0)
        east_side = view_at(field, 0, 1)
        west_side = view_at(field, 0, -1)
        north_side = view_at(field, 1, 0)
        south_side = view_at(field, -1, 0)
        flux_east = mask_east * (
            view_at(eastward, 0, 0) * (centre + east_side) * 0.5
            - lateral_diff * (east_side - centre)
        )
        flux_west = mask_west * (
            view_at(eastward, 0, -1) * (west_side + centre) * 0.5
            - lateral_diff * (centre - west_side)
        )
        flux_north = mask_north * (
            view_at(northward, 0, 0) * (centre + north_side) * 0.5
            - lateral_diff * (north_side - centre)
        )
        flux_south = mask_south * (
            view_at(northward, -1, 0) * (south_side + centre) * 0.5
            - lateral_diff * (centre - south_side)
        )
        tendency = flux_west - flux_east + (flux_south - flux_north) + column_flux(centre, mixing)
        return wet_here * (centre + time_step * tendency)

    east_here = view_at(eastward, 0, 0)
    north_here = view_at(northward, 0, 0)
    corner_ne = wet_here * view_at(wet, 0, 1) * view_at(wet, 1, 0) * view_at(wet, 1, 1)
    corner_se = view_at(wet, -1, 0) * view_at(wet, -1, 1) * wet_here * view_at(wet, 0, 1)
    corner_nw = view_at(wet, 0, -1) * wet_here * view_at(wet, 1, -1) * view_at(wet, 1, 0)
    cell_east = view_at(wet, 0, 1) * (
        ((east_here + view_at(eastward, 0, 1)) * 0.5) ** 2
        - lateral_diff * (view_at(eastward, 0, 1) - east_here)
    )
    cell_west = wet_here * (
        ((view_at(eastward, 0, -1) + east_here) * 0.5) ** 2
        - lateral_diff * (east_here - view_at(eastward, 0, -1))
    )
    product_ne = (
        (north_here + view_at(northward, 0, 1)) * 0.5 * (east_here + view_at(eastward, 1, 0)) * 0.5
    )
    product_se = (
        (view_at(northward, -1, 0) + view_at(northward, -1, 1))
        * 0.5
        * (view_at(eastward, -1, 0) + east_here)
        * 0.5
    )
    product_nw = (
        (view_at(eastward, 0, -1) + view_at(eastward, 1, -1))
        * 0.5
        * (view_at(northward, 0, -1) + north_here)
        * 0.5
    )
    shear_north = corner_ne * (product_ne - lateral_diff * (view_at(eastward, 1, 0) - east_here))
    shear_south = corner_se * (product_se - lateral_diff * (east_here - view_at(eastward, -1, 0)))
    north_mean = (
        north_here
        + view_at(northward, 0, 1)
        + view_at(northward, -1, 0)
        + view_at(northward, -1, 1)
    ) * 0.25
    east_tend = (
        cell_west
        - cell_east
        + (shear_south - shear_north)
        + coriolis_t * north_mean
        - pressure_coef * (view_at(pressure, 0, 1) - view_at(pressure, 0, 0))
        + column_flux(east_here, mixing)
        - drag_coef * bottom * east_here
    )
    east_next = mask_east * (east_here + time_step * east_tend)
    cell_north = view_at(wet, 1, 0) * (
        ((north_here + view_at(northward, 1, 0)) * 0.5) ** 2
        - lateral_diff * (view_at(northward, 1, 0) - north_here)
    )
    cell_south = wet_here * (
        ((view_at(northward, -1, 0) + north_here) * 0.5) ** 2
        - lateral_diff * (north_here - view_at(northward, -1, 0))
    )
    stress_east = corner_ne * (product_ne - lateral_diff * (view_at(northward, 0, 1) - north_here))
    stress_west = corner_nw * (product_nw - lateral_diff * (north_here - view_at(northward, 0, -1)))
    east_mean = (
        east_here + view_at(eastward, 0, -1) + view_at(eastward, 1, 0) + view_at(eastward, 1, -1)
    ) * 0.25
    north_tend = (
        stress_west
        - stress_east
        + (cell_south - cell_north)
        - coriolis_v * east_mean
        - pressure_coef * (view_at(pressure, 1, 0) - view_at(pressure, 0, 0))
        + column_flux(north_here, mixing)
        - drag_coef * bottom * north_here
    )
    north_next = mask_north * (north_here + time_step * north_tend)
    return (east_next, north_next, tracer(temper), tracer(saline))


def shift(value, mapping):
    lat_size = lax.axis_size("lat")
    lon_size = lax.axis_size("lon")
    pairs = []
    for a in range(lat_size):
        for b in range(lon_size):
            target = mapping(a, b, lat_size, lon_size)
            if target is not None:
                pairs.append((b * lat_size + a, target[1] * lat_size + target[0]))
    return lax.ppermute(value, ("lon", "lat"), pairs)


def stencil_kernel(
    cor_ref, u_ref, v_ref, t_ref, s_ref, wet_ref, clc_ref, rows_ref, cols_ref,
    east_ref, north_ref, temp_ref, salt_ref,
):
    levels, rows, cols = u_ref.shape
    fields = 5
    lane = lax.broadcasted_iota(jnp.int32, (rows, cols), 1)
    sub = lax.broadcasted_iota(jnp.int32, (rows, cols), 0)
    at_east = lane == cols - 1
    at_west = lane == 0
    at_north = sub == rows - 1
    at_south = sub == 0
    cor_t = cor_ref[0]
    cor_v = cor_ref[1]
    count = clc_ref[...]

    def east(x, col):
        return jnp.where(at_east, col, pltpu.roll(x, cols - 1, 1))

    def west(x, col):
        return jnp.where(at_west, col, pltpu.roll(x, 1, 1))

    def north(x, row):
        return jnp.where(at_north, row, pltpu.roll(x, rows - 1, 0))

    def south(x, row):
        return jnp.where(at_south, row, pltpu.roll(x, 1, 0))

    def body(k, carry):
        pres, pres_e, pres_n = carry
        km = jnp.maximum(k - 1, 0)
        kp = jnp.minimum(k + 1, levels - 1)

        def row(variant, field):
            return rows_ref[variant * fields + field, pl.ds(k, 1), :]

        def col(field):
            pair = cols_ref[field, k]
            return pair[:, 0:1], pair[:, 1:2]

        w = wet_ref[k].astype(jnp.float32)
        w_above = wet_ref[km].astype(jnp.float32)
        w_below = wet_ref[kp].astype(jnp.float32)
        w_wc, w_ec = col(4)
        w_e = east(w, w_ec)
        w_w = west(w, w_wc)
        w_n = north(w, row(0, 4))
        w_s = south(w, row(3, 4))
        w_ne = north(w_e, row(1, 4))
        w_se = south(w_e, row(4, 4))
        w_nw = north(w_w, row(2, 4))
        mask_east = w * w_e
        mask_west = w_w * w
        mask_north = w * w_n
        mask_south = w_s * w
        mix_below = jnp.where(
            k < levels - 1, w * w_below * (k + 1 < count).astype(jnp.float32), 0.0
        )
        mix_above = jnp.where(k > 0, w_above * w * (k < count).astype(jnp.float32), 0.0)
        bottom = (k == count - 1).astype(jnp.float32)

        def column(ref, centre):
            upper = ref[km]
            lower = ref[kp]
            above = -vertical_diff * mix_above * (centre - upper)
            below = -vertical_diff * mix_below * (lower - centre)
            return above - below

        depth = (k.astype(jnp.float32) + 0.5) * level_depth

        def density(temper, saline):
            return (
                -thermal_expand * (1.0 + 0.5 * cabbel_temp * temper + thermo_temp * depth) * temper
                + haline_contract * (1.0 - 0.5 * cabbel_salt * saline - thermo_salt * depth) * saline
                - cabbel_mixed * temper * saline
            )

        tc = t_ref[k]
        sc = s_ref[k]
        t_wc, t_ec = col(2)
        s_wc, s_ec = col(3)
        pres = pres + w * density(tc, sc)
        pres_e = pres_e + w_ec * density(t_ec, s_ec)
        pres_n = pres_n + row(0, 4) * density(row(0, 2), row(0, 3))
        p_e = east(pres, pres_e)
        p_n = north(pres, pres_n)

        uc = u_ref[k]
        u_wc, u_ec = col(0)
        u_e = east(uc, u_ec)
        u_w = west(uc, u_wc)
        u_n = north(uc, row(0, 0))
        u_s = south(uc, row(3, 0))
        u_nw = north(u_w, row(2, 0))
        vc = v_ref[k]
        v_wc, v_ec = col(1)
        v_e = east(vc, v_ec)
        v_w = west(vc, v_wc)
        v_n = north(vc, row(0, 1))
        v_s = south(vc, row(3, 1))
        v_se = south(v_e, row(4, 1))

        def tracer(ref, centre, field, wcol, ecol):
            east_side = east(centre, ecol)
            west_side = west(centre, wcol)
            north_side = north(centre, row(0, field))
            south_side = south(centre, row(3, field))
            flux_east = mask_east * (
                uc * (centre + east_side) * 0.5 - lateral_diff * (east_side - centre)
            )
            flux_west = mask_west * (
                u_w * (west_side + centre) * 0.5 - lateral_diff * (centre - west_side)
            )
            flux_north = mask_north * (
                vc * (centre + north_side) * 0.5 - lateral_diff * (north_side - centre)
            )
            flux_south = mask_south * (
                v_s * (south_side + centre) * 0.5 - lateral_diff * (centre - south_side)
            )
            tendency = (
                flux_west - flux_east + (flux_south - flux_north) + column(ref, centre)
            )
            return w * (centre + time_step * tendency)

        temp_ref[k] = tracer(t_ref, tc, 2, t_wc, t_ec)
        salt_ref[k] = tracer(s_ref, sc, 3, s_wc, s_ec)

        corner_ne = w * w_e * w_n * w_ne
        corner_se = w_s * w_se * w * w_e
        corner_nw = w_w * w * w_nw * w_n
        half_e = (uc + u_e) * 0.5
        cell_east = w_e * (half_e * half_e - lateral_diff * (u_e - uc))
        half_w = (u_w + uc) * 0.5
        cell_west = w * (half_w * half_w - lateral_diff * (uc - u_w))
        product_ne = (vc + v_e) * 0.5 * (uc + u_n) * 0.5
        product_se = (v_s + v_se) * 0.5 * (u_s + uc) * 0.5
        product_nw = (u_w + u_nw) * 0.5 * (v_w + vc) * 0.5
        shear_north = corner_ne * (product_ne - lateral_diff * (u_n - uc))
        shear_south = corner_se * (product_se - lateral_diff * (uc - u_s))
        north_mean = (vc + v_e + v_s + v_se) * 0.25
        east_tend = (
            cell_west
            - cell_east
            + (shear_south - shear_north)
            + cor_t * north_mean
            - pressure_coef * (p_e - pres)
            + column(u_ref, uc)
            - drag_coef * bottom * uc
        )
        east_ref[k] = mask_east * (uc + time_step * east_tend)
        half_n = (vc + v_n) * 0.5
        cell_north = w_n * (half_n * half_n - lateral_diff * (v_n - vc))
        half_s = (v_s + vc) * 0.5
        cell_south = w * (half_s * half_s - lateral_diff * (vc - v_s))
        stress_east = corner_ne * (product_ne - lateral_diff * (v_e - vc))
        stress_west = corner_nw * (product_nw - lateral_diff * (vc - v_w))
        east_mean = (uc + u_w + u_n + u_nw) * 0.25
        north_tend = (
            stress_west
            - stress_east
            + (cell_south - cell_north)
            - cor_v * east_mean
            - pressure_coef * (p_n - pres)
            + column(v_ref, vc)
            - drag_coef * bottom * vc
        )
        north_ref[k] = mask_north * (vc + time_step * north_tend)
        return pres, pres_e, pres_n

    init = (
        jnp.zeros((rows, cols), jnp.float32),
        jnp.zeros((rows, 1), jnp.float32),
        jnp.zeros((1, cols), jnp.float32),
    )
    lax.fori_loop(0, levels, body, init)


def per_device(
    eastbound_current,
    poleward_current,
    warmth_excess,
    saltiness_excess,
    water_indicator,
    column_layer_count,
):
    inputs = (
        eastbound_current,
        poleward_current,
        warmth_excess,
        saltiness_excess,
        water_indicator,
    )

    def edge(pick):
        return jnp.stack([pick(field).astype(jnp.float32) for field in inputs])

    top = edge(lambda f: f[:, -1, :])
    bottom = edge(lambda f: f[:, 0, :])
    west_col = edge(lambda f: f[:, :, 0])
    east_col = edge(lambda f: f[:, :, -1])

    def east_of(a, b, na, nl):
        return (a, (b + 1) % nl)

    def west_of(a, b, na, nl):
        return (a, (b - 1) % nl)

    def north_of(a, b, na, nl):
        return (a + 1, b) if a + 1 < na else None

    def south_of(a, b, na, nl):
        return (a - 1, b) if a > 0 else None

    def mirror(a, b, na, nl):
        return (a, nl - 1 - b) if a == na - 1 else None

    halo_south = shift(top, north_of)
    halo_north = shift(bottom, south_of)
    fold_row = shift(top, mirror)
    sign = jnp.array([-1.0, -1.0, 1.0, 1.0, 1.0], dtype=jnp.float32)[:, None, None]
    is_top = lax.axis_index("lat") == lax.axis_size("lat") - 1
    halo_north = jnp.where(is_top, sign * fold_row[:, :, ::-1], halo_north)
    west_tall = jnp.concatenate(
        [halo_south[:, :, None, 0], west_col, halo_north[:, :, None, 0]], axis=2
    )
    east_tall = jnp.concatenate(
        [halo_south[:, :, None, -1], east_col, halo_north[:, :, None, -1]], axis=2
    )
    halo_west = shift(east_tall, east_of)
    halo_east = shift(west_tall, west_of)
    north_row = jnp.concatenate(
        [halo_west[:, :, -1:], halo_north, halo_east[:, :, -1:]], axis=2
    )
    south_row = jnp.concatenate([halo_west[:, :, :1], halo_south, halo_east[:, :, :1]], axis=2)
    width = top.shape[2]
    halo_rows = jnp.stack(
        [
            north_row[:, :, 1 : width + 1],
            north_row[:, :, 2 : width + 2],
            north_row[:, :, 0:width],
            south_row[:, :, 1 : width + 1],
            south_row[:, :, 2 : width + 2],
            south_row[:, :, 0:width],
        ]
    )
    halo_rows = halo_rows.reshape((-1,) + halo_rows.shape[2:])
    halo_cols = jnp.stack([halo_west[:, :, 1:-1], halo_east[:, :, 1:-1]], axis=-1)

    levels, rows, cols = eastbound_current.shape
    row_start = lax.axis_index("lat") * rows
    total_rows = rows * lax.axis_size("lat")
    row_index = (row_start + jnp.arange(rows, dtype=jnp.int32)).astype(jnp.float32)[:, None]
    coriolis_t = coriolis_max * (2.0 * (row_index + 0.5) / total_rows - 1.0)
    coriolis_v = coriolis_max * (2.0 * (row_index + 1.0) / total_rows - 1.0)
    coriolis = jnp.broadcast_to(jnp.stack([coriolis_t, coriolis_v]), (2, rows, cols))

    block = jax.ShapeDtypeStruct((levels, rows, cols), jnp.float32)
    return pl.pallas_call(
        stencil_kernel,
        out_shape=(block, block, block, block),
    )(
        coriolis,
        eastbound_current,
        poleward_current,
        warmth_excess,
        saltiness_excess,
        water_indicator,
        column_layer_count,
        halo_rows,
        halo_cols,
    )


def solution(mesh):
    placed = (
        P(None, "lat", "lon"),
        P(None, "lat", "lon"),
        P(None, "lat", "lon"),
        P(None, "lat", "lon"),
        P(None, "lat", "lon"),
        P("lat", "lon"),
    )
    return jax.shard_map(
        per_device,
        mesh=mesh,
        in_specs=placed,
        out_specs=(
            P(None, "lat", "lon"),
            P(None, "lat", "lon"),
            P(None, "lat", "lon"),
            P(None, "lat", "lon"),
        ),
        check_vma=False,
    )
```

```python
import jax
import jax.numpy as jnp
from jax import lax
from jax.experimental import pallas as pl
from jax.experimental.pallas import tpu as pltpu
from jax.sharding import PartitionSpec as P

time_step = 0.2
lateral_diff = 0.1
vertical_diff = 0.5
pressure_coef = 0.1
drag_coef = 2.0
coriolis_max = 1.0
level_depth = 100.0
thermal_expand = 0.1655
haline_contract = 0.76554
cabbel_temp = 0.05952
cabbel_salt = 0.00054914
cabbel_mixed = 0.0024341
thermo_temp = 0.0001497
thermo_salt = 1.109e-05


def view_at(field, lat_step, lon_step):
    rows = field.shape[1] - 2
    cols = field.shape[2] - 2
    return field[:, 1 + lat_step : 1 + lat_step + rows, 1 + lon_step : 1 + lon_step + cols]


def column_flux(centre, mixing):
    between = -vertical_diff * mixing * (centre[1:] - centre[:-1])
    surface = jnp.zeros_like(centre[:1])
    above = jnp.concatenate([surface, between], axis=0)
    below = jnp.concatenate([between, surface], axis=0)
    return above - below


def advance(extended, column_layer_count, row_start, total_rows):
    eastward = extended[0]
    northward = extended[1]
    temper = extended[2]
    saline = extended[3]
    wet = extended[4]
    levels = extended.shape[1]
    rows = extended.shape[2] - 2
    level_index = jnp.arange(levels, dtype=jnp.int32)[:, None, None]
    wet_here = view_at(wet, 0, 0)
    mask_east = wet_here * view_at(wet, 0, 1)
    mask_west = view_at(wet, 0, -1) * wet_here
    mask_north = wet_here * view_at(wet, 1, 0)
    mask_south = view_at(wet, -1, 0) * wet_here
    mixing = (
        wet_here[:-1]
        * wet_here[1:]
        * (level_index[1:] < column_layer_count[None]).astype(jnp.float32)
    )
    bottom = (level_index == column_layer_count[None] - 1).astype(jnp.float32)
    depth = (level_index.astype(jnp.float32) + 0.5) * level_depth
    density = (
        -thermal_expand * (1.0 + 0.5 * cabbel_temp * temper + thermo_temp * depth) * temper
        + haline_contract * (1.0 - 0.5 * cabbel_salt * saline - thermo_salt * depth) * saline
        - cabbel_mixed * temper * saline
    )
    pressure = jnp.cumsum(wet * density, axis=0)
    row_index = (row_start + jnp.arange(rows, dtype=jnp.int32)).astype(jnp.float32)[None, :, None]
    coriolis_t = coriolis_max * (2.0 * (row_index + 0.5) / total_rows - 1.0)
    coriolis_v = coriolis_max * (2.0 * (row_index + 1.0) / total_rows - 1.0)

    def tracer(field):
        centre = view_at(field, 0, 0)
        east_side = view_at(field, 0, 1)
        west_side = view_at(field, 0, -1)
        north_side = view_at(field, 1, 0)
        south_side = view_at(field, -1, 0)
        flux_east = mask_east * (
            view_at(eastward, 0, 0) * (centre + east_side) * 0.5
            - lateral_diff * (east_side - centre)
        )
        flux_west = mask_west * (
            view_at(eastward, 0, -1) * (west_side + centre) * 0.5
            - lateral_diff * (centre - west_side)
        )
        flux_north = mask_north * (
            view_at(northward, 0, 0) * (centre + north_side) * 0.5
            - lateral_diff * (north_side - centre)
        )
        flux_south = mask_south * (
            view_at(northward, -1, 0) * (south_side + centre) * 0.5
            - lateral_diff * (centre - south_side)
        )
        tendency = flux_west - flux_east + (flux_south - flux_north) + column_flux(centre, mixing)
        return wet_here * (centre + time_step * tendency)

    east_here = view_at(eastward, 0, 0)
    north_here = view_at(northward, 0, 0)
    corner_ne = wet_here * view_at(wet, 0, 1) * view_at(wet, 1, 0) * view_at(wet, 1, 1)
    corner_se = view_at(wet, -1, 0) * view_at(wet, -1, 1) * wet_here * view_at(wet, 0, 1)
    corner_nw = view_at(wet, 0, -1) * wet_here * view_at(wet, 1, -1) * view_at(wet, 1, 0)
    cell_east = view_at(wet, 0, 1) * (
        ((east_here + view_at(eastward, 0, 1)) * 0.5) ** 2
        - lateral_diff * (view_at(eastward, 0, 1) - east_here)
    )
    cell_west = wet_here * (
        ((view_at(eastward, 0, -1) + east_here) * 0.5) ** 2
        - lateral_diff * (east_here - view_at(eastward, 0, -1))
    )
    product_ne = (
        (north_here + view_at(northward, 0, 1)) * 0.5 * (east_here + view_at(eastward, 1, 0)) * 0.5
    )
    product_se = (
        (view_at(northward, -1, 0) + view_at(northward, -1, 1))
        * 0.5
        * (view_at(eastward, -1, 0) + east_here)
        * 0.5
    )
    product_nw = (
        (view_at(eastward, 0, -1) + view_at(eastward, 1, -1))
        * 0.5
        * (view_at(northward, 0, -1) + north_here)
        * 0.5
    )
    shear_north = corner_ne * (product_ne - lateral_diff * (view_at(eastward, 1, 0) - east_here))
    shear_south = corner_se * (product_se - lateral_diff * (east_here - view_at(eastward, -1, 0)))
    north_mean = (
        north_here
        + view_at(northward, 0, 1)
        + view_at(northward, -1, 0)
        + view_at(northward, -1, 1)
    ) * 0.25
    east_tend = (
        cell_west
        - cell_east
        + (shear_south - shear_north)
        + coriolis_t * north_mean
        - pressure_coef * (view_at(pressure, 0, 1) - view_at(pressure, 0, 0))
        + column_flux(east_here, mixing)
        - drag_coef * bottom * east_here
    )
    east_next = mask_east * (east_here + time_step * east_tend)
    cell_north = view_at(wet, 1, 0) * (
        ((north_here + view_at(northward, 1, 0)) * 0.5) ** 2
        - lateral_diff * (view_at(northward, 1, 0) - north_here)
    )
    cell_south = wet_here * (
        ((view_at(northward, -1, 0) + north_here) * 0.5) ** 2
        - lateral_diff * (north_here - view_at(northward, -1, 0))
    )
    stress_east = corner_ne * (product_ne - lateral_diff * (view_at(northward, 0, 1) - north_here))
    stress_west = corner_nw * (product_nw - lateral_diff * (north_here - view_at(northward, 0, -1)))
    east_mean = (
        east_here + view_at(eastward, 0, -1) + view_at(eastward, 1, 0) + view_at(eastward, 1, -1)
    ) * 0.25
    north_tend = (
        stress_west
        - stress_east
        + (cell_south - cell_north)
        - coriolis_v * east_mean
        - pressure_coef * (view_at(pressure, 1, 0) - view_at(pressure, 0, 0))
        + column_flux(north_here, mixing)
        - drag_coef * bottom * north_here
    )
    north_next = mask_north * (north_here + time_step * north_tend)
    return (east_next, north_next, tracer(temper), tracer(saline))


def shift(value, mapping):
    lat_size = lax.axis_size("lat")
    lon_size = lax.axis_size("lon")
    pairs = []
    for a in range(lat_size):
        for b in range(lon_size):
            target = mapping(a, b, lat_size, lon_size)
            if target is not None:
                pairs.append((b * lat_size + a, target[1] * lat_size + target[0]))
    return lax.ppermute(value, ("lon", "lat"), pairs)


def edge_kernel(*refs):
    fields = len(refs) - 4
    sources = refs[:fields]
    top_ref, bottom_ref, west_ref, east_ref = refs[fields:]
    levels, rows, cols = sources[0].shape
    lane = lax.broadcasted_iota(jnp.int32, (rows, levels), 1)
    for field, source in enumerate(sources):

        def body(k, carry):
            west, east = carry
            x = source[k].astype(jnp.float32)
            top_ref[field, pl.ds(k, 1), :] = x[rows - 1 : rows, :]
            bottom_ref[field, pl.ds(k, 1), :] = x[0:1, :]
            west = jnp.where(lane == k, x[:, 0:1], west)
            east = jnp.where(lane == k, x[:, cols - 1 : cols], east)
            return west, east

        zero = jnp.zeros((rows, levels), jnp.float32)
        west, east = lax.fori_loop(0, levels, body, (zero, zero))
        west_ref[field] = west
        east_ref[field] = east


def stencil_kernel(
    cor_ref, u_ref, v_ref, t_ref, s_ref, wet_ref, clc_ref, rn_ref, rs_ref, tw_ref, te_ref,
    east_ref, north_ref, temp_ref, salt_ref,
):
    levels, rows, cols = u_ref.shape
    fields = 5
    lane = lax.broadcasted_iota(jnp.int32, (rows, cols), 1)
    sub = lax.broadcasted_iota(jnp.int32, (rows, cols), 0)
    at_east = lane == cols - 1
    at_west = lane == 0
    at_north = sub == rows - 1
    at_south = sub == 0
    row_lane = lax.broadcasted_iota(jnp.int32, (1, cols), 1)
    row_east = row_lane == cols - 1
    row_west = row_lane == 0
    pick = lax.broadcasted_iota(jnp.int32, (levels, cols), 0)
    cor_t = cor_ref[0]
    cor_v = cor_ref[1]
    count = clc_ref[...]

    def east(x, col):
        return jnp.where(at_east, col, pltpu.roll(x, cols - 1, 1))

    def west(x, col):
        return jnp.where(at_west, col, pltpu.roll(x, 1, 1))

    def north(x, row):
        return jnp.where(at_north, row, pltpu.roll(x, rows - 1, 0))

    def south(x, row):
        return jnp.where(at_south, row, pltpu.roll(x, 1, 0))

    def body(k, carry):
        pres, pres_e, pres_n = carry
        km = jnp.maximum(k - 1, 0)
        kp = jnp.minimum(k + 1, levels - 1)

        onehot = (pick == k).astype(jnp.float32)
        spread = {}

        def tall(field):
            if field not in spread:
                spread[field] = tuple(
                    jnp.dot(
                        ref[field],
                        onehot,
                        precision=lax.Precision.HIGHEST,
                        preferred_element_type=jnp.float32,
                    )
                    for ref in (tw_ref, te_ref)
                )
            return spread[field]

        def row(variant, field):
            west_t, east_t = tall(field)
            if variant == 0:
                return rn_ref[field, pl.ds(k, 1), :]
            if variant == 3:
                return rs_ref[field, pl.ds(k, 1), :]
            if variant == 1:
                return jnp.where(row_east, east_t[rows + 1 : rows + 2], pltpu.roll(row(0, field), cols - 1, 1))
            if variant == 2:
                return jnp.where(row_west, west_t[rows + 1 : rows + 2], pltpu.roll(row(0, field), 1, 1))
            return jnp.where(row_east, east_t[rows : rows + 1], pltpu.roll(row(3, field), cols - 1, 1))

        def col(field):
            west_t, east_t = tall(field)
            return west_t[0:rows], east_t[0:rows]

        w = wet_ref[k].astype(jnp.float32)
        w_above = wet_ref[km].astype(jnp.float32)
        w_below = wet_ref[kp].astype(jnp.float32)
        w_wc, w_ec = col(4)
        w_e = east(w, w_ec)
        w_w = west(w, w_wc)
        w_n = north(w, row(0, 4))
        w_s = south(w, row(3, 4))
        w_ne = north(w_e, row(1, 4))
        w_se = south(w_e, row(4, 4))
        w_nw = north(w_w, row(2, 4))
        mask_east = w * w_e
        mask_west = w_w * w
        mask_north = w * w_n
        mask_south = w_s * w
        mix_below = jnp.where(
            k < levels - 1, w * w_below * (k + 1 < count).astype(jnp.float32), 0.0
        )
        mix_above = jnp.where(k > 0, w_above * w * (k < count).astype(jnp.float32), 0.0)
        bottom = (k == count - 1).astype(jnp.float32)

        def column(ref, centre):
            upper = ref[km]
            lower = ref[kp]
            above = -vertical_diff * mix_above * (centre - upper)
            below = -vertical_diff * mix_below * (lower - centre)
            return above - below

        depth = (k.astype(jnp.float32) + 0.5) * level_depth

        def density(temper, saline):
            return (
                -thermal_expand * (1.0 + 0.5 * cabbel_temp * temper + thermo_temp * depth) * temper
                + haline_contract * (1.0 - 0.5 * cabbel_salt * saline - thermo_salt * depth) * saline
                - cabbel_mixed * temper * saline
            )

        tc = t_ref[k]
        sc = s_ref[k]
        t_wc, t_ec = col(2)
        s_wc, s_ec = col(3)
        pres = pres + w * density(tc, sc)
        pres_e = pres_e + w_ec * density(t_ec, s_ec)
        pres_n = pres_n + row(0, 4) * density(row(0, 2), row(0, 3))
        p_e = east(pres, pres_e)
        p_n = north(pres, pres_n)

        uc = u_ref[k]
        u_wc, u_ec = col(0)
        u_e = east(uc, u_ec)
        u_w = west(uc, u_wc)
        u_n = north(uc, row(0, 0))
        u_s = south(uc, row(3, 0))
        u_nw = north(u_w, row(2, 0))
        vc = v_ref[k]
        v_wc, v_ec = col(1)
        v_e = east(vc, v_ec)
        v_w = west(vc, v_wc)
        v_n = north(vc, row(0, 1))
        v_s = south(vc, row(3, 1))
        v_se = south(v_e, row(4, 1))

        def tracer(ref, centre, field, wcol, ecol):
            east_side = east(centre, ecol)
            west_side = west(centre, wcol)
            north_side = north(centre, row(0, field))
            south_side = south(centre, row(3, field))
            flux_east = mask_east * (
                uc * (centre + east_side) * 0.5 - lateral_diff * (east_side - centre)
            )
            flux_west = mask_west * (
                u_w * (west_side + centre) * 0.5 - lateral_diff * (centre - west_side)
            )
            flux_north = mask_north * (
                vc * (centre + north_side) * 0.5 - lateral_diff * (north_side - centre)
            )
            flux_south = mask_south * (
                v_s * (south_side + centre) * 0.5 - lateral_diff * (centre - south_side)
            )
            tendency = (
                flux_west - flux_east + (flux_south - flux_north) + column(ref, centre)
            )
            return w * (centre + time_step * tendency)

        temp_ref[k] = tracer(t_ref, tc, 2, t_wc, t_ec)
        salt_ref[k] = tracer(s_ref, sc, 3, s_wc, s_ec)

        corner_ne = w * w_e * w_n * w_ne
        corner_se = w_s * w_se * w * w_e
        corner_nw = w_w * w * w_nw * w_n
        half_e = (uc + u_e) * 0.5
        cell_east = w_e * (half_e * half_e - lateral_diff * (u_e - uc))
        half_w = (u_w + uc) * 0.5
        cell_west = w * (half_w * half_w - lateral_diff * (uc - u_w))
        product_ne = (vc + v_e) * 0.5 * (uc + u_n) * 0.5
        product_se = (v_s + v_se) * 0.5 * (u_s + uc) * 0.5
        product_nw = (u_w + u_nw) * 0.5 * (v_w + vc) * 0.5
        shear_north = corner_ne * (product_ne - lateral_diff * (u_n - uc))
        shear_south = corner_se * (product_se - lateral_diff * (uc - u_s))
        north_mean = (vc + v_e + v_s + v_se) * 0.25
        east_tend = (
            cell_west
            - cell_east
            + (shear_south - shear_north)
            + cor_t * north_mean
            - pressure_coef * (p_e - pres)
            + column(u_ref, uc)
            - drag_coef * bottom * uc
        )
        east_ref[k] = mask_east * (uc + time_step * east_tend)
        half_n = (vc + v_n) * 0.5
        cell_north = w_n * (half_n * half_n - lateral_diff * (v_n - vc))
        half_s = (v_s + vc) * 0.5
        cell_south = w * (half_s * half_s - lateral_diff * (vc - v_s))
        stress_east = corner_ne * (product_ne - lateral_diff * (v_e - vc))
        stress_west = corner_nw * (product_nw - lateral_diff * (vc - v_w))
        east_mean = (uc + u_w + u_n + u_nw) * 0.25
        north_tend = (
            stress_west
            - stress_east
            + (cell_south - cell_north)
            - cor_v * east_mean
            - pressure_coef * (p_n - pres)
            + column(v_ref, vc)
            - drag_coef * bottom * vc
        )
        north_ref[k] = mask_north * (vc + time_step * north_tend)
        return pres, pres_e, pres_n

    init = (
        jnp.zeros((rows, cols), jnp.float32),
        jnp.zeros((rows, cols), jnp.float32),
        jnp.zeros((1, cols), jnp.float32),
    )
    lax.fori_loop(0, levels, body, init)


def per_device(
    eastbound_current,
    poleward_current,
    warmth_excess,
    saltiness_excess,
    water_indicator,
    column_layer_count,
):
    inputs = (
        eastbound_current,
        poleward_current,
        warmth_excess,
        saltiness_excess,
        water_indicator,
    )

    levels, rows, cols = eastbound_current.shape
    fields = len(inputs)
    top, bottom, west_col, east_col = pl.pallas_call(
        edge_kernel,
        out_shape=(
            jax.ShapeDtypeStruct((fields, levels, cols), jnp.float32),
            jax.ShapeDtypeStruct((fields, levels, cols), jnp.float32),
            jax.ShapeDtypeStruct((fields, rows, levels), jnp.float32),
            jax.ShapeDtypeStruct((fields, rows, levels), jnp.float32),
        ),
    )(*inputs)

    def east_of(a, b, na, nl):
        return (a, (b + 1) % nl)

    def west_of(a, b, na, nl):
        return (a, (b - 1) % nl)

    def north_of(a, b, na, nl):
        return (a + 1, b) if a + 1 < na else None

    def south_of(a, b, na, nl):
        return (a - 1, b) if a > 0 else None

    def mirror(a, b, na, nl):
        return (a, nl - 1 - b) if a == na - 1 else None

    halo_south = shift(top, north_of)
    halo_north = shift(bottom, south_of)
    fold_row = shift(top, mirror)
    sign = jnp.array([-1.0, -1.0, 1.0, 1.0, 1.0], dtype=jnp.float32)[:, None, None]
    is_top = lax.axis_index("lat") == lax.axis_size("lat") - 1
    halo_north = jnp.where(is_top, sign * fold_row[:, :, ::-1], halo_north)
    pad = jnp.zeros((fields, 6, levels), jnp.float32)
    west_tall = jnp.concatenate(
        [west_col, halo_south[:, None, :, 0], halo_north[:, None, :, 0], pad], axis=1
    )
    east_tall = jnp.concatenate(
        [east_col, halo_south[:, None, :, -1], halo_north[:, None, :, -1], pad], axis=1
    )
    halo_west = shift(east_tall, east_of)
    halo_east = shift(west_tall, west_of)

    row_start = lax.axis_index("lat") * rows
    total_rows = rows * lax.axis_size("lat")
    row_index = (row_start + jnp.arange(rows, dtype=jnp.int32)).astype(jnp.float32)[:, None]
    coriolis_t = coriolis_max * (2.0 * (row_index + 0.5) / total_rows - 1.0)
    coriolis_v = coriolis_max * (2.0 * (row_index + 1.0) / total_rows - 1.0)
    coriolis = jnp.broadcast_to(jnp.stack([coriolis_t, coriolis_v]), (2, rows, cols))

    block = jax.ShapeDtypeStruct((levels, rows, cols), jnp.float32)
    return pl.pallas_call(
        stencil_kernel,
        out_shape=(block, block, block, block),
    )(
        coriolis,
        eastbound_current,
        poleward_current,
        warmth_excess,
        saltiness_excess,
        water_indicator,
        column_layer_count,
        halo_north,
        halo_south,
        halo_west,
        halo_east,
    )


def solution(mesh):
    placed = (
        P(None, "lat", "lon"),
        P(None, "lat", "lon"),
        P(None, "lat", "lon"),
        P(None, "lat", "lon"),
        P(None, "lat", "lon"),
        P("lat", "lon"),
    )
    return jax.shard_map(
        per_device,
        mesh=mesh,
        in_specs=placed,
        out_specs=(
            P(None, "lat", "lon"),
            P(None, "lat", "lon"),
            P(None, "lat", "lon"),
            P(None, "lat", "lon"),
        ),
        check_vma=False,
    )
```

```python
import jax
import jax.numpy as jnp
from jax import lax
from jax.experimental import pallas as pl
from jax.experimental.pallas import tpu as pltpu
from jax.sharding import PartitionSpec as P

time_step = 0.2
lateral_diff = 0.1
vertical_diff = 0.5
pressure_coef = 0.1
drag_coef = 2.0
coriolis_max = 1.0
level_depth = 100.0
thermal_expand = 0.1655
haline_contract = 0.76554
cabbel_temp = 0.05952
cabbel_salt = 0.00054914
cabbel_mixed = 0.0024341
thermo_temp = 0.0001497
thermo_salt = 1.109e-05


def view_at(field, lat_step, lon_step):
    rows = field.shape[1] - 2
    cols = field.shape[2] - 2
    return field[:, 1 + lat_step : 1 + lat_step + rows, 1 + lon_step : 1 + lon_step + cols]


def column_flux(centre, mixing):
    between = -vertical_diff * mixing * (centre[1:] - centre[:-1])
    surface = jnp.zeros_like(centre[:1])
    above = jnp.concatenate([surface, between], axis=0)
    below = jnp.concatenate([between, surface], axis=0)
    return above - below


def advance(extended, column_layer_count, row_start, total_rows):
    eastward = extended[0]
    northward = extended[1]
    temper = extended[2]
    saline = extended[3]
    wet = extended[4]
    levels = extended.shape[1]
    rows = extended.shape[2] - 2
    level_index = jnp.arange(levels, dtype=jnp.int32)[:, None, None]
    wet_here = view_at(wet, 0, 0)
    mask_east = wet_here * view_at(wet, 0, 1)
    mask_west = view_at(wet, 0, -1) * wet_here
    mask_north = wet_here * view_at(wet, 1, 0)
    mask_south = view_at(wet, -1, 0) * wet_here
    mixing = (
        wet_here[:-1]
        * wet_here[1:]
        * (level_index[1:] < column_layer_count[None]).astype(jnp.float32)
    )
    bottom = (level_index == column_layer_count[None] - 1).astype(jnp.float32)
    depth = (level_index.astype(jnp.float32) + 0.5) * level_depth
    density = (
        -thermal_expand * (1.0 + 0.5 * cabbel_temp * temper + thermo_temp * depth) * temper
        + haline_contract * (1.0 - 0.5 * cabbel_salt * saline - thermo_salt * depth) * saline
        - cabbel_mixed * temper * saline
    )
    pressure = jnp.cumsum(wet * density, axis=0)
    row_index = (row_start + jnp.arange(rows, dtype=jnp.int32)).astype(jnp.float32)[None, :, None]
    coriolis_t = coriolis_max * (2.0 * (row_index + 0.5) / total_rows - 1.0)
    coriolis_v = coriolis_max * (2.0 * (row_index + 1.0) / total_rows - 1.0)

    def tracer(field):
        centre = view_at(field, 0, 0)
        east_side = view_at(field, 0, 1)
        west_side = view_at(field, 0, -1)
        north_side = view_at(field, 1, 0)
        south_side = view_at(field, -1, 0)
        flux_east = mask_east * (
            view_at(eastward, 0, 0) * (centre + east_side) * 0.5
            - lateral_diff * (east_side - centre)
        )
        flux_west = mask_west * (
            view_at(eastward, 0, -1) * (west_side + centre) * 0.5
            - lateral_diff * (centre - west_side)
        )
        flux_north = mask_north * (
            view_at(northward, 0, 0) * (centre + north_side) * 0.5
            - lateral_diff * (north_side - centre)
        )
        flux_south = mask_south * (
            view_at(northward, -1, 0) * (south_side + centre) * 0.5
            - lateral_diff * (centre - south_side)
        )
        tendency = flux_west - flux_east + (flux_south - flux_north) + column_flux(centre, mixing)
        return wet_here * (centre + time_step * tendency)

    east_here = view_at(eastward, 0, 0)
    north_here = view_at(northward, 0, 0)
    corner_ne = wet_here * view_at(wet, 0, 1) * view_at(wet, 1, 0) * view_at(wet, 1, 1)
    corner_se = view_at(wet, -1, 0) * view_at(wet, -1, 1) * wet_here * view_at(wet, 0, 1)
    corner_nw = view_at(wet, 0, -1) * wet_here * view_at(wet, 1, -1) * view_at(wet, 1, 0)
    cell_east = view_at(wet, 0, 1) * (
        ((east_here + view_at(eastward, 0, 1)) * 0.5) ** 2
        - lateral_diff * (view_at(eastward, 0, 1) - east_here)
    )
    cell_west = wet_here * (
        ((view_at(eastward, 0, -1) + east_here) * 0.5) ** 2
        - lateral_diff * (east_here - view_at(eastward, 0, -1))
    )
    product_ne = (
        (north_here + view_at(northward, 0, 1)) * 0.5 * (east_here + view_at(eastward, 1, 0)) * 0.5
    )
    product_se = (
        (view_at(northward, -1, 0) + view_at(northward, -1, 1))
        * 0.5
        * (view_at(eastward, -1, 0) + east_here)
        * 0.5
    )
    product_nw = (
        (view_at(eastward, 0, -1) + view_at(eastward, 1, -1))
        * 0.5
        * (view_at(northward, 0, -1) + north_here)
        * 0.5
    )
    shear_north = corner_ne * (product_ne - lateral_diff * (view_at(eastward, 1, 0) - east_here))
    shear_south = corner_se * (product_se - lateral_diff * (east_here - view_at(eastward, -1, 0)))
    north_mean = (
        north_here
        + view_at(northward, 0, 1)
        + view_at(northward, -1, 0)
        + view_at(northward, -1, 1)
    ) * 0.25
    east_tend = (
        cell_west
        - cell_east
        + (shear_south - shear_north)
        + coriolis_t * north_mean
        - pressure_coef * (view_at(pressure, 0, 1) - view_at(pressure, 0, 0))
        + column_flux(east_here, mixing)
        - drag_coef * bottom * east_here
    )
    east_next = mask_east * (east_here + time_step * east_tend)
    cell_north = view_at(wet, 1, 0) * (
        ((north_here + view_at(northward, 1, 0)) * 0.5) ** 2
        - lateral_diff * (view_at(northward, 1, 0) - north_here)
    )
    cell_south = wet_here * (
        ((view_at(northward, -1, 0) + north_here) * 0.5) ** 2
        - lateral_diff * (north_here - view_at(northward, -1, 0))
    )
    stress_east = corner_ne * (product_ne - lateral_diff * (view_at(northward, 0, 1) - north_here))
    stress_west = corner_nw * (product_nw - lateral_diff * (north_here - view_at(northward, 0, -1)))
    east_mean = (
        east_here + view_at(eastward, 0, -1) + view_at(eastward, 1, 0) + view_at(eastward, 1, -1)
    ) * 0.25
    north_tend = (
        stress_west
        - stress_east
        + (cell_south - cell_north)
        - coriolis_v * east_mean
        - pressure_coef * (view_at(pressure, 1, 0) - view_at(pressure, 0, 0))
        + column_flux(north_here, mixing)
        - drag_coef * bottom * north_here
    )
    north_next = mask_north * (north_here + time_step * north_tend)
    return (east_next, north_next, tracer(temper), tracer(saline))


def shift(value, mapping):
    lat_size = lax.axis_size("lat")
    lon_size = lax.axis_size("lon")
    pairs = []
    for a in range(lat_size):
        for b in range(lon_size):
            target = mapping(a, b, lat_size, lon_size)
            if target is not None:
                pairs.append((b * lat_size + a, target[1] * lat_size + target[0]))
    return lax.ppermute(value, ("lon", "lat"), pairs)


def edge_kernel(*refs):
    fields = len(refs) - 4
    sources = refs[:fields]
    top_ref, bottom_ref, west_ref, east_ref = refs[fields:]
    chunk, rows, cols = sources[0].shape
    levels = west_ref.shape[2]
    step = pl.program_id(0)
    lane = lax.broadcasted_iota(jnp.int32, (rows, levels), 1)

    @pl.when(step == 0)
    def _():
        west_ref[...] = jnp.zeros(west_ref.shape, jnp.float32)
        east_ref[...] = jnp.zeros(east_ref.shape, jnp.float32)

    for field, source in enumerate(sources):
        west = west_ref[field]
        east = east_ref[field]
        for r in range(chunk):
            x = source[r].astype(jnp.float32)
            top_ref[field, r : r + 1, :] = x[rows - 1 : rows, :]
            bottom_ref[field, r : r + 1, :] = x[0:1, :]
            here = lane == step * chunk + r
            west = jnp.where(here, x[:, 0:1], west)
            east = jnp.where(here, x[:, cols - 1 : cols], east)
        west_ref[field] = west
        east_ref[field] = east


def stencil_kernel(
    cor_ref, u_ref, v_ref, t_ref, s_ref, wet_ref, clc_ref, rn_ref, rs_ref, tw_ref, te_ref,
    east_ref, north_ref, temp_ref, salt_ref,
):
    levels, rows, cols = u_ref.shape
    fields = 5
    lane = lax.broadcasted_iota(jnp.int32, (rows, cols), 1)
    sub = lax.broadcasted_iota(jnp.int32, (rows, cols), 0)
    at_east = lane == cols - 1
    at_west = lane == 0
    at_north = sub == rows - 1
    at_south = sub == 0
    row_lane = lax.broadcasted_iota(jnp.int32, (1, cols), 1)
    row_east = row_lane == cols - 1
    row_west = row_lane == 0
    pick = lax.broadcasted_iota(jnp.int32, (levels, cols), 0)
    cor_t = cor_ref[0]
    cor_v = cor_ref[1]
    count = clc_ref[...]

    def east(x, col):
        return jnp.where(at_east, col, pltpu.roll(x, cols - 1, 1))

    def west(x, col):
        return jnp.where(at_west, col, pltpu.roll(x, 1, 1))

    def north(x, row):
        return jnp.where(at_north, row, pltpu.roll(x, rows - 1, 0))

    def south(x, row):
        return jnp.where(at_south, row, pltpu.roll(x, 1, 0))

    def body(k, carry):
        pres, pres_e, pres_n = carry
        km = jnp.maximum(k - 1, 0)
        kp = jnp.minimum(k + 1, levels - 1)

        onehot = (pick == k).astype(jnp.float32)
        spread = {}

        def tall(field):
            if field not in spread:
                spread[field] = tuple(
                    jnp.dot(
                        ref[field],
                        onehot,
                        precision=lax.Precision.HIGHEST,
                        preferred_element_type=jnp.float32,
                    )
                    for ref in (tw_ref, te_ref)
                )
            return spread[field]

        def row(variant, field):
            west_t, east_t = tall(field)
            if variant == 0:
                return rn_ref[field, pl.ds(k, 1), :]
            if variant == 3:
                return rs_ref[field, pl.ds(k, 1), :]
            if variant == 1:
                return jnp.where(row_east, east_t[rows + 1 : rows + 2], pltpu.roll(row(0, field), cols - 1, 1))
            if variant == 2:
                return jnp.where(row_west, west_t[rows + 1 : rows + 2], pltpu.roll(row(0, field), 1, 1))
            return jnp.where(row_east, east_t[rows : rows + 1], pltpu.roll(row(3, field), cols - 1, 1))

        def col(field):
            west_t, east_t = tall(field)
            return west_t[0:rows], east_t[0:rows]

        w = wet_ref[k].astype(jnp.float32)
        w_above = wet_ref[km].astype(jnp.float32)
        w_below = wet_ref[kp].astype(jnp.float32)
        w_wc, w_ec = col(4)
        w_e = east(w, w_ec)
        w_w = west(w, w_wc)
        w_n = north(w, row(0, 4))
        w_s = south(w, row(3, 4))
        w_ne = north(w_e, row(1, 4))
        w_se = south(w_e, row(4, 4))
        w_nw = north(w_w, row(2, 4))
        mask_east = w * w_e
        mask_west = w_w * w
        mask_north = w * w_n
        mask_south = w_s * w
        mix_below = jnp.where(
            k < levels - 1, w * w_below * (k + 1 < count).astype(jnp.float32), 0.0
        )
        mix_above = jnp.where(k > 0, w_above * w * (k < count).astype(jnp.float32), 0.0)
        bottom = (k == count - 1).astype(jnp.float32)

        def column(ref, centre):
            upper = ref[km]
            lower = ref[kp]
            above = -vertical_diff * mix_above * (centre - upper)
            below = -vertical_diff * mix_below * (lower - centre)
            return above - below

        depth = (k.astype(jnp.float32) + 0.5) * level_depth

        def density(temper, saline):
            return (
                -thermal_expand * (1.0 + 0.5 * cabbel_temp * temper + thermo_temp * depth) * temper
                + haline_contract * (1.0 - 0.5 * cabbel_salt * saline - thermo_salt * depth) * saline
                - cabbel_mixed * temper * saline
            )

        tc = t_ref[k]
        sc = s_ref[k]
        t_wc, t_ec = col(2)
        s_wc, s_ec = col(3)
        pres = pres + w * density(tc, sc)
        pres_e = pres_e + w_ec * density(t_ec, s_ec)
        pres_n = pres_n + row(0, 4) * density(row(0, 2), row(0, 3))
        p_e = east(pres, pres_e)
        p_n = north(pres, pres_n)

        uc = u_ref[k]
        u_wc, u_ec = col(0)
        u_e = east(uc, u_ec)
        u_w = west(uc, u_wc)
        u_n = north(uc, row(0, 0))
        u_s = south(uc, row(3, 0))
        u_nw = north(u_w, row(2, 0))
        vc = v_ref[k]
        v_wc, v_ec = col(1)
        v_e = east(vc, v_ec)
        v_w = west(vc, v_wc)
        v_n = north(vc, row(0, 1))
        v_s = south(vc, row(3, 1))
        v_se = south(v_e, row(4, 1))

        def tracer(ref, centre, field, wcol, ecol):
            east_side = east(centre, ecol)
            west_side = west(centre, wcol)
            north_side = north(centre, row(0, field))
            south_side = south(centre, row(3, field))
            flux_east = mask_east * (
                uc * (centre + east_side) * 0.5 - lateral_diff * (east_side - centre)
            )
            flux_west = mask_west * (
                u_w * (west_side + centre) * 0.5 - lateral_diff * (centre - west_side)
            )
            flux_north = mask_north * (
                vc * (centre + north_side) * 0.5 - lateral_diff * (north_side - centre)
            )
            flux_south = mask_south * (
                v_s * (south_side + centre) * 0.5 - lateral_diff * (centre - south_side)
            )
            tendency = (
                flux_west - flux_east + (flux_south - flux_north) + column(ref, centre)
            )
            return w * (centre + time_step * tendency)

        temp_ref[k] = tracer(t_ref, tc, 2, t_wc, t_ec)
        salt_ref[k] = tracer(s_ref, sc, 3, s_wc, s_ec)

        corner_ne = w * w_e * w_n * w_ne
        corner_se = w_s * w_se * w * w_e
        corner_nw = w_w * w * w_nw * w_n
        half_e = (uc + u_e) * 0.5
        cell_east = w_e * (half_e * half_e - lateral_diff * (u_e - uc))
        half_w = (u_w + uc) * 0.5
        cell_west = w * (half_w * half_w - lateral_diff * (uc - u_w))
        product_ne = (vc + v_e) * 0.5 * (uc + u_n) * 0.5
        product_se = (v_s + v_se) * 0.5 * (u_s + uc) * 0.5
        product_nw = (u_w + u_nw) * 0.5 * (v_w + vc) * 0.5
        shear_north = corner_ne * (product_ne - lateral_diff * (u_n - uc))
        shear_south = corner_se * (product_se - lateral_diff * (uc - u_s))
        north_mean = (vc + v_e + v_s + v_se) * 0.25
        east_tend = (
            cell_west
            - cell_east
            + (shear_south - shear_north)
            + cor_t * north_mean
            - pressure_coef * (p_e - pres)
            + column(u_ref, uc)
            - drag_coef * bottom * uc
        )
        east_ref[k] = mask_east * (uc + time_step * east_tend)
        half_n = (vc + v_n) * 0.5
        cell_north = w_n * (half_n * half_n - lateral_diff * (v_n - vc))
        half_s = (v_s + vc) * 0.5
        cell_south = w * (half_s * half_s - lateral_diff * (vc - v_s))
        stress_east = corner_ne * (product_ne - lateral_diff * (v_e - vc))
        stress_west = corner_nw * (product_nw - lateral_diff * (vc - v_w))
        east_mean = (uc + u_w + u_n + u_nw) * 0.25
        north_tend = (
            stress_west
            - stress_east
            + (cell_south - cell_north)
            - cor_v * east_mean
            - pressure_coef * (p_n - pres)
            + column(v_ref, vc)
            - drag_coef * bottom * vc
        )
        north_ref[k] = mask_north * (vc + time_step * north_tend)
        return pres, pres_e, pres_n

    init = (
        jnp.zeros((rows, cols), jnp.float32),
        jnp.zeros((rows, cols), jnp.float32),
        jnp.zeros((1, cols), jnp.float32),
    )
    lax.fori_loop(0, levels, body, init)


def per_device(
    eastbound_current,
    poleward_current,
    warmth_excess,
    saltiness_excess,
    water_indicator,
    column_layer_count,
):
    inputs = (
        eastbound_current,
        poleward_current,
        warmth_excess,
        saltiness_excess,
        water_indicator,
    )

    levels, rows, cols = eastbound_current.shape
    fields = len(inputs)
    chunk = 8 if levels % 8 == 0 else levels
    row_block = pl.BlockSpec((fields, chunk, cols), lambda c: (0, c, 0))
    col_block = pl.BlockSpec((fields, rows, levels), lambda c: (0, 0, 0))
    top, bottom, west_col, east_col = pl.pallas_call(
        edge_kernel,
        grid=(levels // chunk,),
        in_specs=[pl.BlockSpec((chunk, rows, cols), lambda c: (c, 0, 0))] * fields,
        out_specs=(row_block, row_block, col_block, col_block),
        out_shape=(
            jax.ShapeDtypeStruct((fields, levels, cols), jnp.float32),
            jax.ShapeDtypeStruct((fields, levels, cols), jnp.float32),
            jax.ShapeDtypeStruct((fields, rows, levels), jnp.float32),
            jax.ShapeDtypeStruct((fields, rows, levels), jnp.float32),
        ),
    )(*inputs)

    def east_of(a, b, na, nl):
        return (a, (b + 1) % nl)

    def west_of(a, b, na, nl):
        return (a, (b - 1) % nl)

    def north_of(a, b, na, nl):
        return (a + 1, b) if a + 1 < na else None

    def south_of(a, b, na, nl):
        return (a - 1, b) if a > 0 else None

    def mirror(a, b, na, nl):
        return (a, nl - 1 - b) if a == na - 1 else None

    halo_south = shift(top, north_of)
    halo_north = shift(bottom, south_of)
    fold_row = shift(top, mirror)
    sign = jnp.array([-1.0, -1.0, 1.0, 1.0, 1.0], dtype=jnp.float32)[:, None, None]
    is_top = lax.axis_index("lat") == lax.axis_size("lat") - 1
    halo_north = jnp.where(is_top, sign * fold_row[:, :, ::-1], halo_north)
    pad = jnp.zeros((fields, 6, levels), jnp.float32)
    west_tall = jnp.concatenate(
        [west_col, halo_south[:, None, :, 0], halo_north[:, None, :, 0], pad], axis=1
    )
    east_tall = jnp.concatenate(
        [east_col, halo_south[:, None, :, -1], halo_north[:, None, :, -1], pad], axis=1
    )
    halo_west = shift(east_tall, east_of)
    halo_east = shift(west_tall, west_of)

    row_start = lax.axis_index("lat") * rows
    total_rows = rows * lax.axis_size("lat")
    row_index = (row_start + jnp.arange(rows, dtype=jnp.int32)).astype(jnp.float32)[:, None]
    coriolis_t = coriolis_max * (2.0 * (row_index + 0.5) / total_rows - 1.0)
    coriolis_v = coriolis_max * (2.0 * (row_index + 1.0) / total_rows - 1.0)
    coriolis = jnp.broadcast_to(jnp.stack([coriolis_t, coriolis_v]), (2, rows, cols))

    block = jax.ShapeDtypeStruct((levels, rows, cols), jnp.float32)
    return pl.pallas_call(
        stencil_kernel,
        out_shape=(block, block, block, block),
    )(
        coriolis,
        eastbound_current,
        poleward_current,
        warmth_excess,
        saltiness_excess,
        water_indicator,
        column_layer_count,
        halo_north,
        halo_south,
        halo_west,
        halo_east,
    )


def solution(mesh):
    placed = (
        P(None, "lat", "lon"),
        P(None, "lat", "lon"),
        P(None, "lat", "lon"),
        P(None, "lat", "lon"),
        P(None, "lat", "lon"),
        P("lat", "lon"),
    )
    return jax.shard_map(
        per_device,
        mesh=mesh,
        in_specs=placed,
        out_specs=(
            P(None, "lat", "lon"),
            P(None, "lat", "lon"),
            P(None, "lat", "lon"),
            P(None, "lat", "lon"),
        ),
        check_vma=False,
    )
```

```python
import jax
import jax.numpy as jnp
from jax import lax
from jax.experimental import pallas as pl
from jax.experimental.pallas import tpu as pltpu
from jax.sharding import PartitionSpec as P

time_step = 0.2
lateral_diff = 0.1
vertical_diff = 0.5
pressure_coef = 0.1
drag_coef = 2.0
coriolis_max = 1.0
level_depth = 100.0
thermal_expand = 0.1655
haline_contract = 0.76554
cabbel_temp = 0.05952
cabbel_salt = 0.00054914
cabbel_mixed = 0.0024341
thermo_temp = 0.0001497
thermo_salt = 1.109e-05


def view_at(field, lat_step, lon_step):
    rows = field.shape[1] - 2
    cols = field.shape[2] - 2
    return field[:, 1 + lat_step : 1 + lat_step + rows, 1 + lon_step : 1 + lon_step + cols]


def column_flux(centre, mixing):
    between = -vertical_diff * mixing * (centre[1:] - centre[:-1])
    surface = jnp.zeros_like(centre[:1])
    above = jnp.concatenate([surface, between], axis=0)
    below = jnp.concatenate([between, surface], axis=0)
    return above - below


def advance(extended, column_layer_count, row_start, total_rows):
    eastward = extended[0]
    northward = extended[1]
    temper = extended[2]
    saline = extended[3]
    wet = extended[4]
    levels = extended.shape[1]
    rows = extended.shape[2] - 2
    level_index = jnp.arange(levels, dtype=jnp.int32)[:, None, None]
    wet_here = view_at(wet, 0, 0)
    mask_east = wet_here * view_at(wet, 0, 1)
    mask_west = view_at(wet, 0, -1) * wet_here
    mask_north = wet_here * view_at(wet, 1, 0)
    mask_south = view_at(wet, -1, 0) * wet_here
    mixing = (
        wet_here[:-1]
        * wet_here[1:]
        * (level_index[1:] < column_layer_count[None]).astype(jnp.float32)
    )
    bottom = (level_index == column_layer_count[None] - 1).astype(jnp.float32)
    depth = (level_index.astype(jnp.float32) + 0.5) * level_depth
    density = (
        -thermal_expand * (1.0 + 0.5 * cabbel_temp * temper + thermo_temp * depth) * temper
        + haline_contract * (1.0 - 0.5 * cabbel_salt * saline - thermo_salt * depth) * saline
        - cabbel_mixed * temper * saline
    )
    pressure = jnp.cumsum(wet * density, axis=0)
    row_index = (row_start + jnp.arange(rows, dtype=jnp.int32)).astype(jnp.float32)[None, :, None]
    coriolis_t = coriolis_max * (2.0 * (row_index + 0.5) / total_rows - 1.0)
    coriolis_v = coriolis_max * (2.0 * (row_index + 1.0) / total_rows - 1.0)

    def tracer(field):
        centre = view_at(field, 0, 0)
        east_side = view_at(field, 0, 1)
        west_side = view_at(field, 0, -1)
        north_side = view_at(field, 1, 0)
        south_side = view_at(field, -1, 0)
        flux_east = mask_east * (
            view_at(eastward, 0, 0) * (centre + east_side) * 0.5
            - lateral_diff * (east_side - centre)
        )
        flux_west = mask_west * (
            view_at(eastward, 0, -1) * (west_side + centre) * 0.5
            - lateral_diff * (centre - west_side)
        )
        flux_north = mask_north * (
            view_at(northward, 0, 0) * (centre + north_side) * 0.5
            - lateral_diff * (north_side - centre)
        )
        flux_south = mask_south * (
            view_at(northward, -1, 0) * (south_side + centre) * 0.5
            - lateral_diff * (centre - south_side)
        )
        tendency = flux_west - flux_east + (flux_south - flux_north) + column_flux(centre, mixing)
        return wet_here * (centre + time_step * tendency)

    east_here = view_at(eastward, 0, 0)
    north_here = view_at(northward, 0, 0)
    corner_ne = wet_here * view_at(wet, 0, 1) * view_at(wet, 1, 0) * view_at(wet, 1, 1)
    corner_se = view_at(wet, -1, 0) * view_at(wet, -1, 1) * wet_here * view_at(wet, 0, 1)
    corner_nw = view_at(wet, 0, -1) * wet_here * view_at(wet, 1, -1) * view_at(wet, 1, 0)
    cell_east = view_at(wet, 0, 1) * (
        ((east_here + view_at(eastward, 0, 1)) * 0.5) ** 2
        - lateral_diff * (view_at(eastward, 0, 1) - east_here)
    )
    cell_west = wet_here * (
        ((view_at(eastward, 0, -1) + east_here) * 0.5) ** 2
        - lateral_diff * (east_here - view_at(eastward, 0, -1))
    )
    product_ne = (
        (north_here + view_at(northward, 0, 1)) * 0.5 * (east_here + view_at(eastward, 1, 0)) * 0.5
    )
    product_se = (
        (view_at(northward, -1, 0) + view_at(northward, -1, 1))
        * 0.5
        * (view_at(eastward, -1, 0) + east_here)
        * 0.5
    )
    product_nw = (
        (view_at(eastward, 0, -1) + view_at(eastward, 1, -1))
        * 0.5
        * (view_at(northward, 0, -1) + north_here)
        * 0.5
    )
    shear_north = corner_ne * (product_ne - lateral_diff * (view_at(eastward, 1, 0) - east_here))
    shear_south = corner_se * (product_se - lateral_diff * (east_here - view_at(eastward, -1, 0)))
    north_mean = (
        north_here
        + view_at(northward, 0, 1)
        + view_at(northward, -1, 0)
        + view_at(northward, -1, 1)
    ) * 0.25
    east_tend = (
        cell_west
        - cell_east
        + (shear_south - shear_north)
        + coriolis_t * north_mean
        - pressure_coef * (view_at(pressure, 0, 1) - view_at(pressure, 0, 0))
        + column_flux(east_here, mixing)
        - drag_coef * bottom * east_here
    )
    east_next = mask_east * (east_here + time_step * east_tend)
    cell_north = view_at(wet, 1, 0) * (
        ((north_here + view_at(northward, 1, 0)) * 0.5) ** 2
        - lateral_diff * (view_at(northward, 1, 0) - north_here)
    )
    cell_south = wet_here * (
        ((view_at(northward, -1, 0) + north_here) * 0.5) ** 2
        - lateral_diff * (north_here - view_at(northward, -1, 0))
    )
    stress_east = corner_ne * (product_ne - lateral_diff * (view_at(northward, 0, 1) - north_here))
    stress_west = corner_nw * (product_nw - lateral_diff * (north_here - view_at(northward, 0, -1)))
    east_mean = (
        east_here + view_at(eastward, 0, -1) + view_at(eastward, 1, 0) + view_at(eastward, 1, -1)
    ) * 0.25
    north_tend = (
        stress_west
        - stress_east
        + (cell_south - cell_north)
        - coriolis_v * east_mean
        - pressure_coef * (view_at(pressure, 1, 0) - view_at(pressure, 0, 0))
        + column_flux(north_here, mixing)
        - drag_coef * bottom * north_here
    )
    north_next = mask_north * (north_here + time_step * north_tend)
    return (east_next, north_next, tracer(temper), tracer(saline))


def shift(value, mapping):
    lat_size = lax.axis_size("lat")
    lon_size = lax.axis_size("lon")
    pairs = []
    for a in range(lat_size):
        for b in range(lon_size):
            target = mapping(a, b, lat_size, lon_size)
            if target is not None:
                pairs.append((b * lat_size + a, target[1] * lat_size + target[0]))
    return lax.ppermute(value, ("lon", "lat"), pairs)


def edge_kernel(*refs):
    fields = len(refs) - 4
    sources = refs[:fields]
    top_ref, bottom_ref, west_ref, east_ref = refs[fields:]
    chunk, rows, cols = sources[0].shape
    levels = west_ref.shape[2]
    step = pl.program_id(0)
    lane = lax.broadcasted_iota(jnp.int32, (rows, levels), 1)

    @pl.when(step == 0)
    def _():
        west_ref[...] = jnp.zeros(west_ref.shape, jnp.float32)
        east_ref[...] = jnp.zeros(east_ref.shape, jnp.float32)

    for field, source in enumerate(sources):
        west = west_ref[field]
        east = east_ref[field]
        for r in range(chunk):
            x = source[r].astype(jnp.float32)
            top_ref[field, r : r + 1, :] = x[rows - 1 : rows, :]
            bottom_ref[field, r : r + 1, :] = x[0:1, :]
            here = lane == step * chunk + r
            west = jnp.where(here, x[:, 0:1], west)
            east = jnp.where(here, x[:, cols - 1 : cols], east)
        west_ref[field] = west
        east_ref[field] = east


def stencil_kernel(
    cor_ref, u_ref, v_ref, t_ref, s_ref, wet_ref, ua_ref, va_ref, ta_ref, sa_ref, wa_ref,
    ub_ref, vb_ref, tb_ref, sb_ref, wb_ref, clc_ref, rn_ref, rs_ref, tw_ref, te_ref,
    east_ref, north_ref, temp_ref, salt_ref, p_ref, pe_ref, pn_ref,
):
    chunk, rows, cols = u_ref.shape
    levels = tw_ref.shape[2]
    step = pl.program_id(0)
    near = {
        id(u_ref): (ua_ref, ub_ref),
        id(v_ref): (va_ref, vb_ref),
        id(t_ref): (ta_ref, tb_ref),
        id(s_ref): (sa_ref, sb_ref),
        id(wet_ref): (wa_ref, wb_ref),
    }

    def level(ref, r, offset):
        above, below = near[id(ref)]
        if offset < 0:
            return jnp.where(r == 0, above[0], ref[jnp.maximum(r - 1, 0)])
        return jnp.where(r == chunk - 1, below[0], ref[jnp.minimum(r + 1, chunk - 1)])

    @pl.when(step == 0)
    def _():
        p_ref[...] = jnp.zeros(p_ref.shape, jnp.float32)
        pe_ref[...] = jnp.zeros(pe_ref.shape, jnp.float32)
        pn_ref[...] = jnp.zeros(pn_ref.shape, jnp.float32)

    fields = 5
    lane = lax.broadcasted_iota(jnp.int32, (rows, cols), 1)
    sub = lax.broadcasted_iota(jnp.int32, (rows, cols), 0)
    at_east = lane == cols - 1
    at_west = lane == 0
    at_north = sub == rows - 1
    at_south = sub == 0
    row_lane = lax.broadcasted_iota(jnp.int32, (1, cols), 1)
    row_east = row_lane == cols - 1
    row_west = row_lane == 0
    pick = lax.broadcasted_iota(jnp.int32, (levels, cols), 0)
    cor_t = cor_ref[0]
    cor_v = cor_ref[1]
    count = clc_ref[...]

    def east(x, col):
        return jnp.where(at_east, col, pltpu.roll(x, cols - 1, 1))

    def west(x, col):
        return jnp.where(at_west, col, pltpu.roll(x, 1, 1))

    def north(x, row):
        return jnp.where(at_north, row, pltpu.roll(x, rows - 1, 0))

    def south(x, row):
        return jnp.where(at_south, row, pltpu.roll(x, 1, 0))

    def body(r, carry):
        pres, pres_e, pres_n = carry
        k = step * chunk + r

        onehot = (pick == k).astype(jnp.float32)
        spread = {}

        def tall(field):
            if field not in spread:
                spread[field] = tuple(
                    jnp.dot(
                        ref[field],
                        onehot,
                        precision=lax.Precision.HIGHEST,
                        preferred_element_type=jnp.float32,
                    )
                    for ref in (tw_ref, te_ref)
                )
            return spread[field]

        def row(variant, field):
            west_t, east_t = tall(field)
            if variant == 0:
                return rn_ref[field, pl.ds(r, 1), :]
            if variant == 3:
                return rs_ref[field, pl.ds(r, 1), :]
            if variant == 1:
                return jnp.where(row_east, east_t[rows + 1 : rows + 2], pltpu.roll(row(0, field), cols - 1, 1))
            if variant == 2:
                return jnp.where(row_west, west_t[rows + 1 : rows + 2], pltpu.roll(row(0, field), 1, 1))
            return jnp.where(row_east, east_t[rows : rows + 1], pltpu.roll(row(3, field), cols - 1, 1))

        def col(field):
            west_t, east_t = tall(field)
            return west_t[0:rows], east_t[0:rows]

        w = wet_ref[r].astype(jnp.float32)
        w_above = level(wet_ref, r, -1).astype(jnp.float32)
        w_below = level(wet_ref, r, 1).astype(jnp.float32)
        w_wc, w_ec = col(4)
        w_e = east(w, w_ec)
        w_w = west(w, w_wc)
        w_n = north(w, row(0, 4))
        w_s = south(w, row(3, 4))
        w_ne = north(w_e, row(1, 4))
        w_se = south(w_e, row(4, 4))
        w_nw = north(w_w, row(2, 4))
        mask_east = w * w_e
        mask_west = w_w * w
        mask_north = w * w_n
        mask_south = w_s * w
        mix_below = jnp.where(
            k < levels - 1, w * w_below * (k + 1 < count).astype(jnp.float32), 0.0
        )
        mix_above = jnp.where(k > 0, w_above * w * (k < count).astype(jnp.float32), 0.0)
        bottom = (k == count - 1).astype(jnp.float32)

        def column(ref, centre):
            upper = level(ref, r, -1)
            lower = level(ref, r, 1)
            above = -vertical_diff * mix_above * (centre - upper)
            below = -vertical_diff * mix_below * (lower - centre)
            return above - below

        depth = (k.astype(jnp.float32) + 0.5) * level_depth

        def density(temper, saline):
            return (
                -thermal_expand * (1.0 + 0.5 * cabbel_temp * temper + thermo_temp * depth) * temper
                + haline_contract * (1.0 - 0.5 * cabbel_salt * saline - thermo_salt * depth) * saline
                - cabbel_mixed * temper * saline
            )

        tc = t_ref[r]
        sc = s_ref[r]
        t_wc, t_ec = col(2)
        s_wc, s_ec = col(3)
        pres = pres + w * density(tc, sc)
        pres_e = pres_e + w_ec * density(t_ec, s_ec)
        pres_n = pres_n + row(0, 4) * density(row(0, 2), row(0, 3))
        p_e = east(pres, pres_e)
        p_n = north(pres, pres_n)

        uc = u_ref[r]
        u_wc, u_ec = col(0)
        u_e = east(uc, u_ec)
        u_w = west(uc, u_wc)
        u_n = north(uc, row(0, 0))
        u_s = south(uc, row(3, 0))
        u_nw = north(u_w, row(2, 0))
        vc = v_ref[r]
        v_wc, v_ec = col(1)
        v_e = east(vc, v_ec)
        v_w = west(vc, v_wc)
        v_n = north(vc, row(0, 1))
        v_s = south(vc, row(3, 1))
        v_se = south(v_e, row(4, 1))

        def tracer(ref, centre, field, wcol, ecol):
            east_side = east(centre, ecol)
            west_side = west(centre, wcol)
            north_side = north(centre, row(0, field))
            south_side = south(centre, row(3, field))
            flux_east = mask_east * (
                uc * (centre + east_side) * 0.5 - lateral_diff * (east_side - centre)
            )
            flux_west = mask_west * (
                u_w * (west_side + centre) * 0.5 - lateral_diff * (centre - west_side)
            )
            flux_north = mask_north * (
                vc * (centre + north_side) * 0.5 - lateral_diff * (north_side - centre)
            )
            flux_south = mask_south * (
                v_s * (south_side + centre) * 0.5 - lateral_diff * (centre - south_side)
            )
            tendency = (
                flux_west - flux_east + (flux_south - flux_north) + column(ref, centre)
            )
            return w * (centre + time_step * tendency)

        temp_ref[r] = tracer(t_ref, tc, 2, t_wc, t_ec)
        salt_ref[r] = tracer(s_ref, sc, 3, s_wc, s_ec)

        corner_ne = w * w_e * w_n * w_ne
        corner_se = w_s * w_se * w * w_e
        corner_nw = w_w * w * w_nw * w_n
        half_e = (uc + u_e) * 0.5
        cell_east = w_e * (half_e * half_e - lateral_diff * (u_e - uc))
        half_w = (u_w + uc) * 0.5
        cell_west = w * (half_w * half_w - lateral_diff * (uc - u_w))
        product_ne = (vc + v_e) * 0.5 * (uc + u_n) * 0.5
        product_se = (v_s + v_se) * 0.5 * (u_s + uc) * 0.5
        product_nw = (u_w + u_nw) * 0.5 * (v_w + vc) * 0.5
        shear_north = corner_ne * (product_ne - lateral_diff * (u_n - uc))
        shear_south = corner_se * (product_se - lateral_diff * (uc - u_s))
        north_mean = (vc + v_e + v_s + v_se) * 0.25
        east_tend = (
            cell_west
            - cell_east
            + (shear_south - shear_north)
            + cor_t * north_mean
            - pressure_coef * (p_e - pres)
            + column(u_ref, uc)
            - drag_coef * bottom * uc
        )
        east_ref[r] = mask_east * (uc + time_step * east_tend)
        half_n = (vc + v_n) * 0.5
        cell_north = w_n * (half_n * half_n - lateral_diff * (v_n - vc))
        half_s = (v_s + vc) * 0.5
        cell_south = w * (half_s * half_s - lateral_diff * (vc - v_s))
        stress_east = corner_ne * (product_ne - lateral_diff * (v_e - vc))
        stress_west = corner_nw * (product_nw - lateral_diff * (vc - v_w))
        east_mean = (uc + u_w + u_n + u_nw) * 0.25
        north_tend = (
            stress_west
            - stress_east
            + (cell_south - cell_north)
            - cor_v * east_mean
            - pressure_coef * (p_n - pres)
            + column(v_ref, vc)
            - drag_coef * bottom * vc
        )
        north_ref[r] = mask_north * (vc + time_step * north_tend)
        return pres, pres_e, pres_n

    init = (p_ref[...], pe_ref[...], pn_ref[...])
    pres, pres_e, pres_n = lax.fori_loop(0, chunk, body, init)
    p_ref[...] = pres
    pe_ref[...] = pres_e
    pn_ref[...] = pres_n


def per_device(
    eastbound_current,
    poleward_current,
    warmth_excess,
    saltiness_excess,
    water_indicator,
    column_layer_count,
):
    inputs = (
        eastbound_current,
        poleward_current,
        warmth_excess,
        saltiness_excess,
        water_indicator,
    )

    levels, rows, cols = eastbound_current.shape
    fields = len(inputs)
    chunk = 8 if levels % 8 == 0 else levels
    row_block = pl.BlockSpec((fields, chunk, cols), lambda c: (0, c, 0))
    col_block = pl.BlockSpec((fields, rows, levels), lambda c: (0, 0, 0))
    top, bottom, west_col, east_col = pl.pallas_call(
        edge_kernel,
        grid=(levels // chunk,),
        in_specs=[pl.BlockSpec((chunk, rows, cols), lambda c: (c, 0, 0))] * fields,
        out_specs=(row_block, row_block, col_block, col_block),
        out_shape=(
            jax.ShapeDtypeStruct((fields, levels, cols), jnp.float32),
            jax.ShapeDtypeStruct((fields, levels, cols), jnp.float32),
            jax.ShapeDtypeStruct((fields, rows, levels), jnp.float32),
            jax.ShapeDtypeStruct((fields, rows, levels), jnp.float32),
        ),
    )(*inputs)

    def east_of(a, b, na, nl):
        return (a, (b + 1) % nl)

    def west_of(a, b, na, nl):
        return (a, (b - 1) % nl)

    def north_of(a, b, na, nl):
        return (a + 1, b) if a + 1 < na else None

    def south_of(a, b, na, nl):
        return (a - 1, b) if a > 0 else None

    def mirror(a, b, na, nl):
        return (a, nl - 1 - b) if a == na - 1 else None

    halo_south = shift(top, north_of)
    halo_north = shift(bottom, south_of)
    fold_row = shift(top, mirror)
    sign = jnp.array([-1.0, -1.0, 1.0, 1.0, 1.0], dtype=jnp.float32)[:, None, None]
    is_top = lax.axis_index("lat") == lax.axis_size("lat") - 1
    halo_north = jnp.where(is_top, sign * fold_row[:, :, ::-1], halo_north)
    pad = jnp.zeros((fields, 6, levels), jnp.float32)
    west_tall = jnp.concatenate(
        [west_col, halo_south[:, None, :, 0], halo_north[:, None, :, 0], pad], axis=1
    )
    east_tall = jnp.concatenate(
        [east_col, halo_south[:, None, :, -1], halo_north[:, None, :, -1], pad], axis=1
    )
    halo_west = shift(east_tall, east_of)
    halo_east = shift(west_tall, west_of)

    row_start = lax.axis_index("lat") * rows
    total_rows = rows * lax.axis_size("lat")
    row_index = (row_start + jnp.arange(rows, dtype=jnp.int32)).astype(jnp.float32)[:, None]
    coriolis_t = coriolis_max * (2.0 * (row_index + 0.5) / total_rows - 1.0)
    coriolis_v = coriolis_max * (2.0 * (row_index + 1.0) / total_rows - 1.0)
    coriolis = jnp.broadcast_to(jnp.stack([coriolis_t, coriolis_v]), (2, rows, cols))

    block = jax.ShapeDtypeStruct((levels, rows, cols), jnp.float32)
    main = pl.BlockSpec((chunk, rows, cols), lambda c: (c, 0, 0))
    above = pl.BlockSpec((1, rows, cols), lambda c: (jnp.maximum(c * chunk - 1, 0), 0, 0))
    below = pl.BlockSpec(
        (1, rows, cols), lambda c: (jnp.minimum(c * chunk + chunk, levels - 1), 0, 0)
    )

    def whole(shape):
        return pl.BlockSpec(shape, lambda c: (0,) * len(shape))

    halo_row = pl.BlockSpec((fields, chunk, cols), lambda c: (0, c, 0))
    return pl.pallas_call(
        stencil_kernel,
        grid=(levels // chunk,),
        in_specs=[whole((2, rows, cols))]
        + [main] * fields
        + [above] * fields
        + [below] * fields
        + [whole((rows, cols)), halo_row, halo_row, whole(halo_west.shape), whole(halo_east.shape)],
        out_specs=(main, main, main, main),
        out_shape=(block, block, block, block),
        scratch_shapes=[
            pltpu.VMEM((rows, cols), jnp.float32),
            pltpu.VMEM((rows, cols), jnp.float32),
            pltpu.VMEM((1, cols), jnp.float32),
        ],
    )(
        coriolis,
        *inputs,
        *inputs,
        *inputs,
        column_layer_count,
        halo_north,
        halo_south,
        halo_west,
        halo_east,
    )


def solution(mesh):
    placed = (
        P(None, "lat", "lon"),
        P(None, "lat", "lon"),
        P(None, "lat", "lon"),
        P(None, "lat", "lon"),
        P(None, "lat", "lon"),
        P("lat", "lon"),
    )
    return jax.shard_map(
        per_device,
        mesh=mesh,
        in_specs=placed,
        out_specs=(
            P(None, "lat", "lon"),
            P(None, "lat", "lon"),
            P(None, "lat", "lon"),
            P(None, "lat", "lon"),
        ),
        check_vma=False,
    )
```

```python
import jax
import jax.numpy as jnp
from jax import lax
from jax.experimental import pallas as pl
from jax.experimental.pallas import tpu as pltpu
from jax.sharding import PartitionSpec as P

time_step = 0.2
lateral_diff = 0.1
vertical_diff = 0.5
pressure_coef = 0.1
drag_coef = 2.0
coriolis_max = 1.0
level_depth = 100.0
thermal_expand = 0.1655
haline_contract = 0.76554
cabbel_temp = 0.05952
cabbel_salt = 0.00054914
cabbel_mixed = 0.0024341
thermo_temp = 0.0001497
thermo_salt = 1.109e-05


def view_at(field, lat_step, lon_step):
    rows = field.shape[1] - 2
    cols = field.shape[2] - 2
    return field[:, 1 + lat_step : 1 + lat_step + rows, 1 + lon_step : 1 + lon_step + cols]


def column_flux(centre, mixing):
    between = -vertical_diff * mixing * (centre[1:] - centre[:-1])
    surface = jnp.zeros_like(centre[:1])
    above = jnp.concatenate([surface, between], axis=0)
    below = jnp.concatenate([between, surface], axis=0)
    return above - below


def advance(extended, column_layer_count, row_start, total_rows):
    eastward = extended[0]
    northward = extended[1]
    temper = extended[2]
    saline = extended[3]
    wet = extended[4]
    levels = extended.shape[1]
    rows = extended.shape[2] - 2
    level_index = jnp.arange(levels, dtype=jnp.int32)[:, None, None]
    wet_here = view_at(wet, 0, 0)
    mask_east = wet_here * view_at(wet, 0, 1)
    mask_west = view_at(wet, 0, -1) * wet_here
    mask_north = wet_here * view_at(wet, 1, 0)
    mask_south = view_at(wet, -1, 0) * wet_here
    mixing = (
        wet_here[:-1]
        * wet_here[1:]
        * (level_index[1:] < column_layer_count[None]).astype(jnp.float32)
    )
    bottom = (level_index == column_layer_count[None] - 1).astype(jnp.float32)
    depth = (level_index.astype(jnp.float32) + 0.5) * level_depth
    density = (
        -thermal_expand * (1.0 + 0.5 * cabbel_temp * temper + thermo_temp * depth) * temper
        + haline_contract * (1.0 - 0.5 * cabbel_salt * saline - thermo_salt * depth) * saline
        - cabbel_mixed * temper * saline
    )
    pressure = jnp.cumsum(wet * density, axis=0)
    row_index = (row_start + jnp.arange(rows, dtype=jnp.int32)).astype(jnp.float32)[None, :, None]
    coriolis_t = coriolis_max * (2.0 * (row_index + 0.5) / total_rows - 1.0)
    coriolis_v = coriolis_max * (2.0 * (row_index + 1.0) / total_rows - 1.0)

    def tracer(field):
        centre = view_at(field, 0, 0)
        east_side = view_at(field, 0, 1)
        west_side = view_at(field, 0, -1)
        north_side = view_at(field, 1, 0)
        south_side = view_at(field, -1, 0)
        flux_east = mask_east * (
            view_at(eastward, 0, 0) * (centre + east_side) * 0.5
            - lateral_diff * (east_side - centre)
        )
        flux_west = mask_west * (
            view_at(eastward, 0, -1) * (west_side + centre) * 0.5
            - lateral_diff * (centre - west_side)
        )
        flux_north = mask_north * (
            view_at(northward, 0, 0) * (centre + north_side) * 0.5
            - lateral_diff * (north_side - centre)
        )
        flux_south = mask_south * (
            view_at(northward, -1, 0) * (south_side + centre) * 0.5
            - lateral_diff * (centre - south_side)
        )
        tendency = flux_west - flux_east + (flux_south - flux_north) + column_flux(centre, mixing)
        return wet_here * (centre + time_step * tendency)

    east_here = view_at(eastward, 0, 0)
    north_here = view_at(northward, 0, 0)
    corner_ne = wet_here * view_at(wet, 0, 1) * view_at(wet, 1, 0) * view_at(wet, 1, 1)
    corner_se = view_at(wet, -1, 0) * view_at(wet, -1, 1) * wet_here * view_at(wet, 0, 1)
    corner_nw = view_at(wet, 0, -1) * wet_here * view_at(wet, 1, -1) * view_at(wet, 1, 0)
    cell_east = view_at(wet, 0, 1) * (
        ((east_here + view_at(eastward, 0, 1)) * 0.5) ** 2
        - lateral_diff * (view_at(eastward, 0, 1) - east_here)
    )
    cell_west = wet_here * (
        ((view_at(eastward, 0, -1) + east_here) * 0.5) ** 2
        - lateral_diff * (east_here - view_at(eastward, 0, -1))
    )
    product_ne = (
        (north_here + view_at(northward, 0, 1)) * 0.5 * (east_here + view_at(eastward, 1, 0)) * 0.5
    )
    product_se = (
        (view_at(northward, -1, 0) + view_at(northward, -1, 1))
        * 0.5
        * (view_at(eastward, -1, 0) + east_here)
        * 0.5
    )
    product_nw = (
        (view_at(eastward, 0, -1) + view_at(eastward, 1, -1))
        * 0.5
        * (view_at(northward, 0, -1) + north_here)
        * 0.5
    )
    shear_north = corner_ne * (product_ne - lateral_diff * (view_at(eastward, 1, 0) - east_here))
    shear_south = corner_se * (product_se - lateral_diff * (east_here - view_at(eastward, -1, 0)))
    north_mean = (
        north_here
        + view_at(northward, 0, 1)
        + view_at(northward, -1, 0)
        + view_at(northward, -1, 1)
    ) * 0.25
    east_tend = (
        cell_west
        - cell_east
        + (shear_south - shear_north)
        + coriolis_t * north_mean
        - pressure_coef * (view_at(pressure, 0, 1) - view_at(pressure, 0, 0))
        + column_flux(east_here, mixing)
        - drag_coef * bottom * east_here
    )
    east_next = mask_east * (east_here + time_step * east_tend)
    cell_north = view_at(wet, 1, 0) * (
        ((north_here + view_at(northward, 1, 0)) * 0.5) ** 2
        - lateral_diff * (view_at(northward, 1, 0) - north_here)
    )
    cell_south = wet_here * (
        ((view_at(northward, -1, 0) + north_here) * 0.5) ** 2
        - lateral_diff * (north_here - view_at(northward, -1, 0))
    )
    stress_east = corner_ne * (product_ne - lateral_diff * (view_at(northward, 0, 1) - north_here))
    stress_west = corner_nw * (product_nw - lateral_diff * (north_here - view_at(northward, 0, -1)))
    east_mean = (
        east_here + view_at(eastward, 0, -1) + view_at(eastward, 1, 0) + view_at(eastward, 1, -1)
    ) * 0.25
    north_tend = (
        stress_west
        - stress_east
        + (cell_south - cell_north)
        - coriolis_v * east_mean
        - pressure_coef * (view_at(pressure, 1, 0) - view_at(pressure, 0, 0))
        + column_flux(north_here, mixing)
        - drag_coef * bottom * north_here
    )
    north_next = mask_north * (north_here + time_step * north_tend)
    return (east_next, north_next, tracer(temper), tracer(saline))


def shift(value, mapping):
    lat_size = lax.axis_size("lat")
    lon_size = lax.axis_size("lon")
    pairs = []
    for a in range(lat_size):
        for b in range(lon_size):
            target = mapping(a, b, lat_size, lon_size)
            if target is not None:
                pairs.append((b * lat_size + a, target[1] * lat_size + target[0]))
    return lax.ppermute(value, ("lon", "lat"), pairs)


def edge_kernel(*refs):
    fields = len(refs) - 4
    sources = refs[:fields]
    top_ref, bottom_ref, west_ref, east_ref = refs[fields:]
    chunk, rows, cols = sources[0].shape
    levels = west_ref.shape[2]
    step = pl.program_id(0)
    lane = lax.broadcasted_iota(jnp.int32, (rows, levels), 1)

    @pl.when(step == 0)
    def _():
        west_ref[...] = jnp.zeros(west_ref.shape, jnp.float32)
        east_ref[...] = jnp.zeros(east_ref.shape, jnp.float32)

    for field, source in enumerate(sources):
        west = west_ref[field]
        east = east_ref[field]
        for r in range(chunk):
            x = source[r].astype(jnp.float32)
            top_ref[field, r : r + 1, :] = x[rows - 1 : rows, :]
            bottom_ref[field, r : r + 1, :] = x[0:1, :]
            here = lane == step * chunk + r
            west = jnp.where(here, x[:, 0:1], west)
            east = jnp.where(here, x[:, cols - 1 : cols], east)
        west_ref[field] = west
        east_ref[field] = east


def stencil_kernel(
    cor_ref, u_ref, v_ref, t_ref, s_ref, wet_ref, ua_ref, va_ref, ta_ref, sa_ref, wa_ref,
    ub_ref, vb_ref, tb_ref, sb_ref, wb_ref, clc_ref, rn_ref, rs_ref, tw_ref, te_ref,
    east_ref, north_ref, temp_ref, salt_ref, p_ref, pe_ref, pn_ref,
):
    chunk, rows, cols = u_ref.shape
    levels = tw_ref.shape[1]
    step = pl.program_id(0)
    near = {
        id(u_ref): (ua_ref, ub_ref),
        id(v_ref): (va_ref, vb_ref),
        id(t_ref): (ta_ref, tb_ref),
        id(s_ref): (sa_ref, sb_ref),
        id(wet_ref): (wa_ref, wb_ref),
    }

    def level(ref, r, offset):
        above, below = near[id(ref)]
        if offset < 0:
            return jnp.where(r == 0, above[0], ref[jnp.maximum(r - 1, 0)])
        return jnp.where(r == chunk - 1, below[0], ref[jnp.minimum(r + 1, chunk - 1)])

    @pl.when(step == 0)
    def _():
        p_ref[...] = jnp.zeros(p_ref.shape, jnp.float32)
        pe_ref[...] = jnp.zeros(pe_ref.shape, jnp.float32)
        pn_ref[...] = jnp.zeros(pn_ref.shape, jnp.float32)

    fields = 5
    lane = lax.broadcasted_iota(jnp.int32, (rows, cols), 1)
    sub = lax.broadcasted_iota(jnp.int32, (rows, cols), 0)
    at_east = lane == cols - 1
    at_west = lane == 0
    at_north = sub == rows - 1
    at_south = sub == 0
    row_lane = lax.broadcasted_iota(jnp.int32, (1, cols), 1)
    row_east = row_lane == cols - 1
    row_west = row_lane == 0
    pick = lax.broadcasted_iota(jnp.int32, (levels, cols), 0)
    cor_t = cor_ref[0]
    cor_v = cor_ref[1]
    count = clc_ref[...]

    def east(x, col):
        return jnp.where(at_east, col, pltpu.roll(x, cols - 1, 1))

    def west(x, col):
        return jnp.where(at_west, col, pltpu.roll(x, 1, 1))

    def north(x, row):
        return jnp.where(at_north, row, pltpu.roll(x, rows - 1, 0))

    def south(x, row):
        return jnp.where(at_south, row, pltpu.roll(x, 1, 0))

    def body(r, carry):
        pres, pres_e, pres_n = carry
        k = step * chunk + r

        onehot = (pick == k).astype(jnp.float32)
        spread = {}

        def tall(field):
            if not spread:
                for ref in (tw_ref, te_ref):
                    spread[id(ref)] = jnp.dot(
                        ref[...],
                        onehot,
                        precision=lax.Precision.HIGHEST,
                        preferred_element_type=jnp.float32,
                    )
            span = tw_ref.shape[0] // fields
            return tuple(
                spread[id(ref)][field * span : (field + 1) * span] for ref in (tw_ref, te_ref)
            )

        def row(variant, field):
            west_t, east_t = tall(field)
            if variant == 0:
                return rn_ref[field, pl.ds(r, 1), :]
            if variant == 3:
                return rs_ref[field, pl.ds(r, 1), :]
            if variant == 1:
                return jnp.where(row_east, east_t[rows + 1 : rows + 2], pltpu.roll(row(0, field), cols - 1, 1))
            if variant == 2:
                return jnp.where(row_west, west_t[rows + 1 : rows + 2], pltpu.roll(row(0, field), 1, 1))
            return jnp.where(row_east, east_t[rows : rows + 1], pltpu.roll(row(3, field), cols - 1, 1))

        def col(field):
            west_t, east_t = tall(field)
            return west_t[0:rows], east_t[0:rows]

        w = wet_ref[r].astype(jnp.float32)
        w_above = level(wet_ref, r, -1).astype(jnp.float32)
        w_below = level(wet_ref, r, 1).astype(jnp.float32)
        w_wc, w_ec = col(4)
        w_e = east(w, w_ec)
        w_w = west(w, w_wc)
        w_n = north(w, row(0, 4))
        w_s = south(w, row(3, 4))
        w_ne = north(w_e, row(1, 4))
        w_se = south(w_e, row(4, 4))
        w_nw = north(w_w, row(2, 4))
        mask_east = w * w_e
        mask_west = w_w * w
        mask_north = w * w_n
        mask_south = w_s * w
        mix_below = jnp.where(
            k < levels - 1, w * w_below * (k + 1 < count).astype(jnp.float32), 0.0
        )
        mix_above = jnp.where(k > 0, w_above * w * (k < count).astype(jnp.float32), 0.0)
        bottom = (k == count - 1).astype(jnp.float32)

        def column(ref, centre):
            upper = level(ref, r, -1)
            lower = level(ref, r, 1)
            above = -vertical_diff * mix_above * (centre - upper)
            below = -vertical_diff * mix_below * (lower - centre)
            return above - below

        depth = (k.astype(jnp.float32) + 0.5) * level_depth

        def density(temper, saline):
            return (
                -thermal_expand * (1.0 + 0.5 * cabbel_temp * temper + thermo_temp * depth) * temper
                + haline_contract * (1.0 - 0.5 * cabbel_salt * saline - thermo_salt * depth) * saline
                - cabbel_mixed * temper * saline
            )

        tc = t_ref[r]
        sc = s_ref[r]
        t_wc, t_ec = col(2)
        s_wc, s_ec = col(3)
        pres = pres + w * density(tc, sc)
        pres_e = pres_e + w_ec * density(t_ec, s_ec)
        pres_n = pres_n + row(0, 4) * density(row(0, 2), row(0, 3))
        p_e = east(pres, pres_e)
        p_n = north(pres, pres_n)

        uc = u_ref[r]
        u_wc, u_ec = col(0)
        u_e = east(uc, u_ec)
        u_w = west(uc, u_wc)
        u_n = north(uc, row(0, 0))
        u_s = south(uc, row(3, 0))
        u_nw = north(u_w, row(2, 0))
        vc = v_ref[r]
        v_wc, v_ec = col(1)
        v_e = east(vc, v_ec)
        v_w = west(vc, v_wc)
        v_n = north(vc, row(0, 1))
        v_s = south(vc, row(3, 1))
        v_se = south(v_e, row(4, 1))

        def tracer(ref, centre, field, wcol, ecol):
            east_side = east(centre, ecol)
            west_side = west(centre, wcol)
            north_side = north(centre, row(0, field))
            south_side = south(centre, row(3, field))
            flux_east = mask_east * (
                uc * (centre + east_side) * 0.5 - lateral_diff * (east_side - centre)
            )
            flux_west = mask_west * (
                u_w * (west_side + centre) * 0.5 - lateral_diff * (centre - west_side)
            )
            flux_north = mask_north * (
                vc * (centre + north_side) * 0.5 - lateral_diff * (north_side - centre)
            )
            flux_south = mask_south * (
                v_s * (south_side + centre) * 0.5 - lateral_diff * (centre - south_side)
            )
            tendency = (
                flux_west - flux_east + (flux_south - flux_north) + column(ref, centre)
            )
            return w * (centre + time_step * tendency)

        temp_ref[r] = tracer(t_ref, tc, 2, t_wc, t_ec)
        salt_ref[r] = tracer(s_ref, sc, 3, s_wc, s_ec)

        corner_ne = w * w_e * w_n * w_ne
        corner_se = w_s * w_se * w * w_e
        corner_nw = w_w * w * w_nw * w_n
        half_e = (uc + u_e) * 0.5
        cell_east = w_e * (half_e * half_e - lateral_diff * (u_e - uc))
        half_w = (u_w + uc) * 0.5
        cell_west = w * (half_w * half_w - lateral_diff * (uc - u_w))
        product_ne = (vc + v_e) * 0.5 * (uc + u_n) * 0.5
        product_se = (v_s + v_se) * 0.5 * (u_s + uc) * 0.5
        product_nw = (u_w + u_nw) * 0.5 * (v_w + vc) * 0.5
        shear_north = corner_ne * (product_ne - lateral_diff * (u_n - uc))
        shear_south = corner_se * (product_se - lateral_diff * (uc - u_s))
        north_mean = (vc + v_e + v_s + v_se) * 0.25
        east_tend = (
            cell_west
            - cell_east
            + (shear_south - shear_north)
            + cor_t * north_mean
            - pressure_coef * (p_e - pres)
            + column(u_ref, uc)
            - drag_coef * bottom * uc
        )
        east_ref[r] = mask_east * (uc + time_step * east_tend)
        half_n = (vc + v_n) * 0.5
        cell_north = w_n * (half_n * half_n - lateral_diff * (v_n - vc))
        half_s = (v_s + vc) * 0.5
        cell_south = w * (half_s * half_s - lateral_diff * (vc - v_s))
        stress_east = corner_ne * (product_ne - lateral_diff * (v_e - vc))
        stress_west = corner_nw * (product_nw - lateral_diff * (vc - v_w))
        east_mean = (uc + u_w + u_n + u_nw) * 0.25
        north_tend = (
            stress_west
            - stress_east
            + (cell_south - cell_north)
            - cor_v * east_mean
            - pressure_coef * (p_n - pres)
            + column(v_ref, vc)
            - drag_coef * bottom * vc
        )
        north_ref[r] = mask_north * (vc + time_step * north_tend)
        return pres, pres_e, pres_n

    init = (p_ref[...], pe_ref[...], pn_ref[...])
    pres, pres_e, pres_n = lax.fori_loop(0, chunk, body, init)
    p_ref[...] = pres
    pe_ref[...] = pres_e
    pn_ref[...] = pres_n


def per_device(
    eastbound_current,
    poleward_current,
    warmth_excess,
    saltiness_excess,
    water_indicator,
    column_layer_count,
):
    inputs = (
        eastbound_current,
        poleward_current,
        warmth_excess,
        saltiness_excess,
        water_indicator,
    )

    levels, rows, cols = eastbound_current.shape
    fields = len(inputs)
    chunk = 8 if levels % 8 == 0 else levels
    row_block = pl.BlockSpec((fields, chunk, cols), lambda c: (0, c, 0))
    col_block = pl.BlockSpec((fields, rows, levels), lambda c: (0, 0, 0))
    top, bottom, west_col, east_col = pl.pallas_call(
        edge_kernel,
        grid=(levels // chunk,),
        in_specs=[pl.BlockSpec((chunk, rows, cols), lambda c: (c, 0, 0))] * fields,
        out_specs=(row_block, row_block, col_block, col_block),
        out_shape=(
            jax.ShapeDtypeStruct((fields, levels, cols), jnp.float32),
            jax.ShapeDtypeStruct((fields, levels, cols), jnp.float32),
            jax.ShapeDtypeStruct((fields, rows, levels), jnp.float32),
            jax.ShapeDtypeStruct((fields, rows, levels), jnp.float32),
        ),
    )(*inputs)

    def east_of(a, b, na, nl):
        return (a, (b + 1) % nl)

    def west_of(a, b, na, nl):
        return (a, (b - 1) % nl)

    def north_of(a, b, na, nl):
        return (a + 1, b) if a + 1 < na else None

    def south_of(a, b, na, nl):
        return (a - 1, b) if a > 0 else None

    def mirror(a, b, na, nl):
        return (a, nl - 1 - b) if a == na - 1 else None

    halo_south = shift(top, north_of)
    halo_north = shift(bottom, south_of)
    fold_row = shift(top, mirror)
    sign = jnp.array([-1.0, -1.0, 1.0, 1.0, 1.0], dtype=jnp.float32)[:, None, None]
    is_top = lax.axis_index("lat") == lax.axis_size("lat") - 1
    halo_north = jnp.where(is_top, sign * fold_row[:, :, ::-1], halo_north)
    pad = jnp.zeros((fields, 6, levels), jnp.float32)
    west_tall = jnp.concatenate(
        [west_col, halo_south[:, None, :, 0], halo_north[:, None, :, 0], pad], axis=1
    )
    east_tall = jnp.concatenate(
        [east_col, halo_south[:, None, :, -1], halo_north[:, None, :, -1], pad], axis=1
    )
    halo_west = shift(east_tall, east_of).reshape(-1, levels)
    halo_east = shift(west_tall, west_of).reshape(-1, levels)

    row_start = lax.axis_index("lat") * rows
    total_rows = rows * lax.axis_size("lat")
    row_index = (row_start + jnp.arange(rows, dtype=jnp.int32)).astype(jnp.float32)[:, None]
    coriolis_t = coriolis_max * (2.0 * (row_index + 0.5) / total_rows - 1.0)
    coriolis_v = coriolis_max * (2.0 * (row_index + 1.0) / total_rows - 1.0)
    coriolis = jnp.broadcast_to(jnp.stack([coriolis_t, coriolis_v]), (2, rows, cols))

    block = jax.ShapeDtypeStruct((levels, rows, cols), jnp.float32)
    main = pl.BlockSpec((chunk, rows, cols), lambda c: (c, 0, 0))
    above = pl.BlockSpec((1, rows, cols), lambda c: (jnp.maximum(c * chunk - 1, 0), 0, 0))
    below = pl.BlockSpec(
        (1, rows, cols), lambda c: (jnp.minimum(c * chunk + chunk, levels - 1), 0, 0)
    )

    def whole(shape):
        return pl.BlockSpec(shape, lambda c: (0,) * len(shape))

    halo_row = pl.BlockSpec((fields, chunk, cols), lambda c: (0, c, 0))
    return pl.pallas_call(
        stencil_kernel,
        grid=(levels // chunk,),
        in_specs=[whole((2, rows, cols))]
        + [main] * fields
        + [above] * fields
        + [below] * fields
        + [whole((rows, cols)), halo_row, halo_row, whole(halo_west.shape), whole(halo_east.shape)],
        out_specs=(main, main, main, main),
        out_shape=(block, block, block, block),
        scratch_shapes=[
            pltpu.VMEM((rows, cols), jnp.float32),
            pltpu.VMEM((rows, cols), jnp.float32),
            pltpu.VMEM((1, cols), jnp.float32),
        ],
    )(
        coriolis,
        *inputs,
        *inputs,
        *inputs,
        column_layer_count,
        halo_north,
        halo_south,
        halo_west,
        halo_east,
    )


def solution(mesh):
    placed = (
        P(None, "lat", "lon"),
        P(None, "lat", "lon"),
        P(None, "lat", "lon"),
        P(None, "lat", "lon"),
        P(None, "lat", "lon"),
        P("lat", "lon"),
    )
    return jax.shard_map(
        per_device,
        mesh=mesh,
        in_specs=placed,
        out_specs=(
            P(None, "lat", "lon"),
            P(None, "lat", "lon"),
            P(None, "lat", "lon"),
            P(None, "lat", "lon"),
        ),
        check_vma=False,
    )
```

```python
import jax
import jax.numpy as jnp
from jax import lax
from jax.experimental import pallas as pl
from jax.experimental.pallas import tpu as pltpu
from jax.sharding import PartitionSpec as P

time_step = 0.2
lateral_diff = 0.1
vertical_diff = 0.5
pressure_coef = 0.1
drag_coef = 2.0
coriolis_max = 1.0
level_depth = 100.0
thermal_expand = 0.1655
haline_contract = 0.76554
cabbel_temp = 0.05952
cabbel_salt = 0.00054914
cabbel_mixed = 0.0024341
thermo_temp = 0.0001497
thermo_salt = 1.109e-05


def view_at(field, lat_step, lon_step):
    rows = field.shape[1] - 2
    cols = field.shape[2] - 2
    return field[:, 1 + lat_step : 1 + lat_step + rows, 1 + lon_step : 1 + lon_step + cols]


def column_flux(centre, mixing):
    between = -vertical_diff * mixing * (centre[1:] - centre[:-1])
    surface = jnp.zeros_like(centre[:1])
    above = jnp.concatenate([surface, between], axis=0)
    below = jnp.concatenate([between, surface], axis=0)
    return above - below


def advance(extended, column_layer_count, row_start, total_rows):
    eastward = extended[0]
    northward = extended[1]
    temper = extended[2]
    saline = extended[3]
    wet = extended[4]
    levels = extended.shape[1]
    rows = extended.shape[2] - 2
    level_index = jnp.arange(levels, dtype=jnp.int32)[:, None, None]
    wet_here = view_at(wet, 0, 0)
    mask_east = wet_here * view_at(wet, 0, 1)
    mask_west = view_at(wet, 0, -1) * wet_here
    mask_north = wet_here * view_at(wet, 1, 0)
    mask_south = view_at(wet, -1, 0) * wet_here
    mixing = (
        wet_here[:-1]
        * wet_here[1:]
        * (level_index[1:] < column_layer_count[None]).astype(jnp.float32)
    )
    bottom = (level_index == column_layer_count[None] - 1).astype(jnp.float32)
    depth = (level_index.astype(jnp.float32) + 0.5) * level_depth
    density = (
        -thermal_expand * (1.0 + 0.5 * cabbel_temp * temper + thermo_temp * depth) * temper
        + haline_contract * (1.0 - 0.5 * cabbel_salt * saline - thermo_salt * depth) * saline
        - cabbel_mixed * temper * saline
    )
    pressure = jnp.cumsum(wet * density, axis=0)
    row_index = (row_start + jnp.arange(rows, dtype=jnp.int32)).astype(jnp.float32)[None, :, None]
    coriolis_t = coriolis_max * (2.0 * (row_index + 0.5) / total_rows - 1.0)
    coriolis_v = coriolis_max * (2.0 * (row_index + 1.0) / total_rows - 1.0)

    def tracer(field):
        centre = view_at(field, 0, 0)
        east_side = view_at(field, 0, 1)
        west_side = view_at(field, 0, -1)
        north_side = view_at(field, 1, 0)
        south_side = view_at(field, -1, 0)
        flux_east = mask_east * (
            view_at(eastward, 0, 0) * (centre + east_side) * 0.5
            - lateral_diff * (east_side - centre)
        )
        flux_west = mask_west * (
            view_at(eastward, 0, -1) * (west_side + centre) * 0.5
            - lateral_diff * (centre - west_side)
        )
        flux_north = mask_north * (
            view_at(northward, 0, 0) * (centre + north_side) * 0.5
            - lateral_diff * (north_side - centre)
        )
        flux_south = mask_south * (
            view_at(northward, -1, 0) * (south_side + centre) * 0.5
            - lateral_diff * (centre - south_side)
        )
        tendency = flux_west - flux_east + (flux_south - flux_north) + column_flux(centre, mixing)
        return wet_here * (centre + time_step * tendency)

    east_here = view_at(eastward, 0, 0)
    north_here = view_at(northward, 0, 0)
    corner_ne = wet_here * view_at(wet, 0, 1) * view_at(wet, 1, 0) * view_at(wet, 1, 1)
    corner_se = view_at(wet, -1, 0) * view_at(wet, -1, 1) * wet_here * view_at(wet, 0, 1)
    corner_nw = view_at(wet, 0, -1) * wet_here * view_at(wet, 1, -1) * view_at(wet, 1, 0)
    cell_east = view_at(wet, 0, 1) * (
        ((east_here + view_at(eastward, 0, 1)) * 0.5) ** 2
        - lateral_diff * (view_at(eastward, 0, 1) - east_here)
    )
    cell_west = wet_here * (
        ((view_at(eastward, 0, -1) + east_here) * 0.5) ** 2
        - lateral_diff * (east_here - view_at(eastward, 0, -1))
    )
    product_ne = (
        (north_here + view_at(northward, 0, 1)) * 0.5 * (east_here + view_at(eastward, 1, 0)) * 0.5
    )
    product_se = (
        (view_at(northward, -1, 0) + view_at(northward, -1, 1))
        * 0.5
        * (view_at(eastward, -1, 0) + east_here)
        * 0.5
    )
    product_nw = (
        (view_at(eastward, 0, -1) + view_at(eastward, 1, -1))
        * 0.5
        * (view_at(northward, 0, -1) + north_here)
        * 0.5
    )
    shear_north = corner_ne * (product_ne - lateral_diff * (view_at(eastward, 1, 0) - east_here))
    shear_south = corner_se * (product_se - lateral_diff * (east_here - view_at(eastward, -1, 0)))
    north_mean = (
        north_here
        + view_at(northward, 0, 1)
        + view_at(northward, -1, 0)
        + view_at(northward, -1, 1)
    ) * 0.25
    east_tend = (
        cell_west
        - cell_east
        + (shear_south - shear_north)
        + coriolis_t * north_mean
        - pressure_coef * (view_at(pressure, 0, 1) - view_at(pressure, 0, 0))
        + column_flux(east_here, mixing)
        - drag_coef * bottom * east_here
    )
    east_next = mask_east * (east_here + time_step * east_tend)
    cell_north = view_at(wet, 1, 0) * (
        ((north_here + view_at(northward, 1, 0)) * 0.5) ** 2
        - lateral_diff * (view_at(northward, 1, 0) - north_here)
    )
    cell_south = wet_here * (
        ((view_at(northward, -1, 0) + north_here) * 0.5) ** 2
        - lateral_diff * (north_here - view_at(northward, -1, 0))
    )
    stress_east = corner_ne * (product_ne - lateral_diff * (view_at(northward, 0, 1) - north_here))
    stress_west = corner_nw * (product_nw - lateral_diff * (north_here - view_at(northward, 0, -1)))
    east_mean = (
        east_here + view_at(eastward, 0, -1) + view_at(eastward, 1, 0) + view_at(eastward, 1, -1)
    ) * 0.25
    north_tend = (
        stress_west
        - stress_east
        + (cell_south - cell_north)
        - coriolis_v * east_mean
        - pressure_coef * (view_at(pressure, 1, 0) - view_at(pressure, 0, 0))
        + column_flux(north_here, mixing)
        - drag_coef * bottom * north_here
    )
    north_next = mask_north * (north_here + time_step * north_tend)
    return (east_next, north_next, tracer(temper), tracer(saline))


def shift(value, mapping):
    lat_size = lax.axis_size("lat")
    lon_size = lax.axis_size("lon")
    pairs = []
    for a in range(lat_size):
        for b in range(lon_size):
            target = mapping(a, b, lat_size, lon_size)
            if target is not None:
                pairs.append((b * lat_size + a, target[1] * lat_size + target[0]))
    return lax.ppermute(value, ("lon", "lat"), pairs)


def edge_kernel(*refs):
    fields = len(refs) - 4
    sources = refs[:fields]
    top_ref, bottom_ref, west_ref, east_ref = refs[fields:]
    chunk, rows, cols = sources[0].shape
    levels = west_ref.shape[2]
    step = pl.program_id(0)
    lane = lax.broadcasted_iota(jnp.int32, (rows, levels), 1)

    @pl.when(step == 0)
    def _():
        west_ref[...] = jnp.zeros(west_ref.shape, jnp.float32)
        east_ref[...] = jnp.zeros(east_ref.shape, jnp.float32)

    for field, source in enumerate(sources):
        west = west_ref[field]
        east = east_ref[field]
        for r in range(chunk):
            x = source[r].astype(jnp.float32)
            top_ref[field, r : r + 1, :] = x[rows - 1 : rows, :]
            bottom_ref[field, r : r + 1, :] = x[0:1, :]
            here = lane == step * chunk + r
            west = jnp.where(here, x[:, 0:1], west)
            east = jnp.where(here, x[:, cols - 1 : cols], east)
        west_ref[field] = west
        east_ref[field] = east


def stencil_kernel(
    cor_ref, u_ref, v_ref, t_ref, s_ref, wet_ref, ua_ref, va_ref, ta_ref, sa_ref, wa_ref,
    ub_ref, vb_ref, tb_ref, sb_ref, wb_ref, clc_ref, rn_ref, rs_ref, tw_ref, te_ref,
    east_ref, north_ref, temp_ref, salt_ref, p_ref, pe_ref, pn_ref,
):
    chunk, rows, cols = u_ref.shape
    levels = tw_ref.shape[2]
    step = pl.program_id(0)
    near = {
        id(u_ref): (ua_ref, ub_ref),
        id(v_ref): (va_ref, vb_ref),
        id(t_ref): (ta_ref, tb_ref),
        id(s_ref): (sa_ref, sb_ref),
        id(wet_ref): (wa_ref, wb_ref),
    }

    def level(ref, r, offset):
        above, below = near[id(ref)]
        if offset < 0:
            return jnp.where(r == 0, above[0], ref[jnp.maximum(r - 1, 0)])
        return jnp.where(r == chunk - 1, below[0], ref[jnp.minimum(r + 1, chunk - 1)])

    @pl.when(step == 0)
    def _():
        p_ref[...] = jnp.zeros(p_ref.shape, jnp.float32)
        pe_ref[...] = jnp.zeros(pe_ref.shape, jnp.float32)
        pn_ref[...] = jnp.zeros(pn_ref.shape, jnp.float32)

    fields = 5
    lane = lax.broadcasted_iota(jnp.int32, (rows, cols), 1)
    sub = lax.broadcasted_iota(jnp.int32, (rows, cols), 0)
    at_east = lane == cols - 1
    at_west = lane == 0
    at_north = sub == rows - 1
    at_south = sub == 0
    row_lane = lax.broadcasted_iota(jnp.int32, (1, cols), 1)
    row_east = row_lane == cols - 1
    row_west = row_lane == 0
    pick_lane = lax.broadcasted_iota(jnp.int32, tw_ref.shape[1:], 1)
    cor_t = cor_ref[0]
    cor_v = cor_ref[1]
    count = clc_ref[...]

    def east(x, col):
        return jnp.where(at_east, col, pltpu.roll(x, cols - 1, 1))

    def west(x, col):
        return jnp.where(at_west, col, pltpu.roll(x, 1, 1))

    def north(x, row):
        return jnp.where(at_north, row, pltpu.roll(x, rows - 1, 0))

    def south(x, row):
        return jnp.where(at_south, row, pltpu.roll(x, 1, 0))

    def body(r, carry):
        pres, pres_e, pres_n = carry
        k = step * chunk + r

        spread = {}

        def tall(field):
            if field not in spread:
                spread[field] = tuple(
                    jnp.broadcast_to(
                        jnp.sum(jnp.where(pick_lane == k, ref[field], 0.0), axis=1, keepdims=True),
                        (ref.shape[1], cols),
                    )
                    for ref in (tw_ref, te_ref)
                )
            return spread[field]

        def row(variant, field):
            west_t, east_t = tall(field)
            if variant == 0:
                return rn_ref[field, pl.ds(r, 1), :]
            if variant == 3:
                return rs_ref[field, pl.ds(r, 1), :]
            if variant == 1:
                return jnp.where(row_east, east_t[rows + 1 : rows + 2], pltpu.roll(row(0, field), cols - 1, 1))
            if variant == 2:
                return jnp.where(row_west, west_t[rows + 1 : rows + 2], pltpu.roll(row(0, field), 1, 1))
            return jnp.where(row_east, east_t[rows : rows + 1], pltpu.roll(row(3, field), cols - 1, 1))

        def col(field):
            west_t, east_t = tall(field)
            return west_t[0:rows], east_t[0:rows]

        w = wet_ref[r].astype(jnp.float32)
        w_above = level(wet_ref, r, -1).astype(jnp.float32)
        w_below = level(wet_ref, r, 1).astype(jnp.float32)
        w_wc, w_ec = col(4)
        w_e = east(w, w_ec)
        w_w = west(w, w_wc)
        w_n = north(w, row(0, 4))
        w_s = south(w, row(3, 4))
        w_ne = north(w_e, row(1, 4))
        w_se = south(w_e, row(4, 4))
        w_nw = north(w_w, row(2, 4))
        mask_east = w * w_e
        mask_west = w_w * w
        mask_north = w * w_n
        mask_south = w_s * w
        mix_below = jnp.where(
            k < levels - 1, w * w_below * (k + 1 < count).astype(jnp.float32), 0.0
        )
        mix_above = jnp.where(k > 0, w_above * w * (k < count).astype(jnp.float32), 0.0)
        bottom = (k == count - 1).astype(jnp.float32)

        def column(ref, centre):
            upper = level(ref, r, -1)
            lower = level(ref, r, 1)
            above = -vertical_diff * mix_above * (centre - upper)
            below = -vertical_diff * mix_below * (lower - centre)
            return above - below

        depth = (k.astype(jnp.float32) + 0.5) * level_depth

        def density(temper, saline):
            return (
                -thermal_expand * (1.0 + 0.5 * cabbel_temp * temper + thermo_temp * depth) * temper
                + haline_contract * (1.0 - 0.5 * cabbel_salt * saline - thermo_salt * depth) * saline
                - cabbel_mixed * temper * saline
            )

        tc = t_ref[r]
        sc = s_ref[r]
        t_wc, t_ec = col(2)
        s_wc, s_ec = col(3)
        pres = pres + w * density(tc, sc)
        pres_e = pres_e + w_ec * density(t_ec, s_ec)
        pres_n = pres_n + row(0, 4) * density(row(0, 2), row(0, 3))
        p_e = east(pres, pres_e)
        p_n = north(pres, pres_n)

        uc = u_ref[r]
        u_wc, u_ec = col(0)
        u_e = east(uc, u_ec)
        u_w = west(uc, u_wc)
        u_n = north(uc, row(0, 0))
        u_s = south(uc, row(3, 0))
        u_nw = north(u_w, row(2, 0))
        vc = v_ref[r]
        v_wc, v_ec = col(1)
        v_e = east(vc, v_ec)
        v_w = west(vc, v_wc)
        v_n = north(vc, row(0, 1))
        v_s = south(vc, row(3, 1))
        v_se = south(v_e, row(4, 1))

        def tracer(ref, centre, field, wcol, ecol):
            east_side = east(centre, ecol)
            west_side = west(centre, wcol)
            north_side = north(centre, row(0, field))
            south_side = south(centre, row(3, field))
            flux_east = mask_east * (
                uc * (centre + east_side) * 0.5 - lateral_diff * (east_side - centre)
            )
            flux_west = mask_west * (
                u_w * (west_side + centre) * 0.5 - lateral_diff * (centre - west_side)
            )
            flux_north = mask_north * (
                vc * (centre + north_side) * 0.5 - lateral_diff * (north_side - centre)
            )
            flux_south = mask_south * (
                v_s * (south_side + centre) * 0.5 - lateral_diff * (centre - south_side)
            )
            tendency = (
                flux_west - flux_east + (flux_south - flux_north) + column(ref, centre)
            )
            return w * (centre + time_step * tendency)

        temp_ref[r] = tracer(t_ref, tc, 2, t_wc, t_ec)
        salt_ref[r] = tracer(s_ref, sc, 3, s_wc, s_ec)

        corner_ne = w * w_e * w_n * w_ne
        corner_se = w_s * w_se * w * w_e
        corner_nw = w_w * w * w_nw * w_n
        half_e = (uc + u_e) * 0.5
        cell_east = w_e * (half_e * half_e - lateral_diff * (u_e - uc))
        half_w = (u_w + uc) * 0.5
        cell_west = w * (half_w * half_w - lateral_diff * (uc - u_w))
        product_ne = (vc + v_e) * 0.5 * (uc + u_n) * 0.5
        product_se = (v_s + v_se) * 0.5 * (u_s + uc) * 0.5
        product_nw = (u_w + u_nw) * 0.5 * (v_w + vc) * 0.5
        shear_north = corner_ne * (product_ne - lateral_diff * (u_n - uc))
        shear_south = corner_se * (product_se - lateral_diff * (uc - u_s))
        north_mean = (vc + v_e + v_s + v_se) * 0.25
        east_tend = (
            cell_west
            - cell_east
            + (shear_south - shear_north)
            + cor_t * north_mean
            - pressure_coef * (p_e - pres)
            + column(u_ref, uc)
            - drag_coef * bottom * uc
        )
        east_ref[r] = mask_east * (uc + time_step * east_tend)
        half_n = (vc + v_n) * 0.5
        cell_north = w_n * (half_n * half_n - lateral_diff * (v_n - vc))
        half_s = (v_s + vc) * 0.5
        cell_south = w * (half_s * half_s - lateral_diff * (vc - v_s))
        stress_east = corner_ne * (product_ne - lateral_diff * (v_e - vc))
        stress_west = corner_nw * (product_nw - lateral_diff * (vc - v_w))
        east_mean = (uc + u_w + u_n + u_nw) * 0.25
        north_tend = (
            stress_west
            - stress_east
            + (cell_south - cell_north)
            - cor_v * east_mean
            - pressure_coef * (p_n - pres)
            + column(v_ref, vc)
            - drag_coef * bottom * vc
        )
        north_ref[r] = mask_north * (vc + time_step * north_tend)
        return pres, pres_e, pres_n

    init = (p_ref[...], pe_ref[...], pn_ref[...])
    pres, pres_e, pres_n = lax.fori_loop(0, chunk, body, init)
    p_ref[...] = pres
    pe_ref[...] = pres_e
    pn_ref[...] = pres_n


def per_device(
    eastbound_current,
    poleward_current,
    warmth_excess,
    saltiness_excess,
    water_indicator,
    column_layer_count,
):
    inputs = (
        eastbound_current,
        poleward_current,
        warmth_excess,
        saltiness_excess,
        water_indicator,
    )

    levels, rows, cols = eastbound_current.shape
    fields = len(inputs)
    chunk = 8 if levels % 8 == 0 else levels
    row_block = pl.BlockSpec((fields, chunk, cols), lambda c: (0, c, 0))
    col_block = pl.BlockSpec((fields, rows, levels), lambda c: (0, 0, 0))
    top, bottom, west_col, east_col = pl.pallas_call(
        edge_kernel,
        grid=(levels // chunk,),
        in_specs=[pl.BlockSpec((chunk, rows, cols), lambda c: (c, 0, 0))] * fields,
        out_specs=(row_block, row_block, col_block, col_block),
        out_shape=(
            jax.ShapeDtypeStruct((fields, levels, cols), jnp.float32),
            jax.ShapeDtypeStruct((fields, levels, cols), jnp.float32),
            jax.ShapeDtypeStruct((fields, rows, levels), jnp.float32),
            jax.ShapeDtypeStruct((fields, rows, levels), jnp.float32),
        ),
    )(*inputs)

    def east_of(a, b, na, nl):
        return (a, (b + 1) % nl)

    def west_of(a, b, na, nl):
        return (a, (b - 1) % nl)

    def north_of(a, b, na, nl):
        return (a + 1, b) if a + 1 < na else None

    def south_of(a, b, na, nl):
        return (a - 1, b) if a > 0 else None

    def mirror(a, b, na, nl):
        return (a, nl - 1 - b) if a == na - 1 else None

    halo_south = shift(top, north_of)
    halo_north = shift(bottom, south_of)
    fold_row = shift(top, mirror)
    sign = jnp.array([-1.0, -1.0, 1.0, 1.0, 1.0], dtype=jnp.float32)[:, None, None]
    is_top = lax.axis_index("lat") == lax.axis_size("lat") - 1
    halo_north = jnp.where(is_top, sign * fold_row[:, :, ::-1], halo_north)
    pad = jnp.zeros((fields, 6, levels), jnp.float32)
    west_tall = jnp.concatenate(
        [west_col, halo_south[:, None, :, 0], halo_north[:, None, :, 0], pad], axis=1
    )
    east_tall = jnp.concatenate(
        [east_col, halo_south[:, None, :, -1], halo_north[:, None, :, -1], pad], axis=1
    )
    halo_west = shift(east_tall, east_of)
    halo_east = shift(west_tall, west_of)

    row_start = lax.axis_index("lat") * rows
    total_rows = rows * lax.axis_size("lat")
    row_index = (row_start + jnp.arange(rows, dtype=jnp.int32)).astype(jnp.float32)[:, None]
    coriolis_t = coriolis_max * (2.0 * (row_index + 0.5) / total_rows - 1.0)
    coriolis_v = coriolis_max * (2.0 * (row_index + 1.0) / total_rows - 1.0)
    coriolis = jnp.broadcast_to(jnp.stack([coriolis_t, coriolis_v]), (2, rows, cols))

    block = jax.ShapeDtypeStruct((levels, rows, cols), jnp.float32)
    main = pl.BlockSpec((chunk, rows, cols), lambda c: (c, 0, 0))
    above = pl.BlockSpec((1, rows, cols), lambda c: (jnp.maximum(c * chunk - 1, 0), 0, 0))
    below = pl.BlockSpec(
        (1, rows, cols), lambda c: (jnp.minimum(c * chunk + chunk, levels - 1), 0, 0)
    )

    def whole(shape):
        return pl.BlockSpec(shape, lambda c: (0,) * len(shape))

    halo_row = pl.BlockSpec((fields, chunk, cols), lambda c: (0, c, 0))
    return pl.pallas_call(
        stencil_kernel,
        grid=(levels // chunk,),
        in_specs=[whole((2, rows, cols))]
        + [main] * fields
        + [above] * fields
        + [below] * fields
        + [whole((rows, cols)), halo_row, halo_row, whole(halo_west.shape), whole(halo_east.shape)],
        out_specs=(main, main, main, main),
        out_shape=(block, block, block, block),
        scratch_shapes=[
            pltpu.VMEM((rows, cols), jnp.float32),
            pltpu.VMEM((rows, cols), jnp.float32),
            pltpu.VMEM((1, cols), jnp.float32),
        ],
    )(
        coriolis,
        *inputs,
        *inputs,
        *inputs,
        column_layer_count,
        halo_north,
        halo_south,
        halo_west,
        halo_east,
    )


def solution(mesh):
    placed = (
        P(None, "lat", "lon"),
        P(None, "lat", "lon"),
        P(None, "lat", "lon"),
        P(None, "lat", "lon"),
        P(None, "lat", "lon"),
        P("lat", "lon"),
    )
    return jax.shard_map(
        per_device,
        mesh=mesh,
        in_specs=placed,
        out_specs=(
            P(None, "lat", "lon"),
            P(None, "lat", "lon"),
            P(None, "lat", "lon"),
            P(None, "lat", "lon"),
        ),
        check_vma=False,
    )
```

```python
import jax
import jax.numpy as jnp
from jax import lax
from jax.experimental import pallas as pl
from jax.experimental.pallas import tpu as pltpu
from jax.sharding import PartitionSpec as P

time_step = 0.2
lateral_diff = 0.1
vertical_diff = 0.5
pressure_coef = 0.1
drag_coef = 2.0
coriolis_max = 1.0
level_depth = 100.0
thermal_expand = 0.1655
haline_contract = 0.76554
cabbel_temp = 0.05952
cabbel_salt = 0.00054914
cabbel_mixed = 0.0024341
thermo_temp = 0.0001497
thermo_salt = 1.109e-05


def view_at(field, lat_step, lon_step):
    rows = field.shape[1] - 2
    cols = field.shape[2] - 2
    return field[:, 1 + lat_step : 1 + lat_step + rows, 1 + lon_step : 1 + lon_step + cols]


def column_flux(centre, mixing):
    between = -vertical_diff * mixing * (centre[1:] - centre[:-1])
    surface = jnp.zeros_like(centre[:1])
    above = jnp.concatenate([surface, between], axis=0)
    below = jnp.concatenate([between, surface], axis=0)
    return above - below


def advance(extended, column_layer_count, row_start, total_rows):
    eastward = extended[0]
    northward = extended[1]
    temper = extended[2]
    saline = extended[3]
    wet = extended[4]
    levels = extended.shape[1]
    rows = extended.shape[2] - 2
    level_index = jnp.arange(levels, dtype=jnp.int32)[:, None, None]
    wet_here = view_at(wet, 0, 0)
    mask_east = wet_here * view_at(wet, 0, 1)
    mask_west = view_at(wet, 0, -1) * wet_here
    mask_north = wet_here * view_at(wet, 1, 0)
    mask_south = view_at(wet, -1, 0) * wet_here
    mixing = (
        wet_here[:-1]
        * wet_here[1:]
        * (level_index[1:] < column_layer_count[None]).astype(jnp.float32)
    )
    bottom = (level_index == column_layer_count[None] - 1).astype(jnp.float32)
    depth = (level_index.astype(jnp.float32) + 0.5) * level_depth
    density = (
        -thermal_expand * (1.0 + 0.5 * cabbel_temp * temper + thermo_temp * depth) * temper
        + haline_contract * (1.0 - 0.5 * cabbel_salt * saline - thermo_salt * depth) * saline
        - cabbel_mixed * temper * saline
    )
    pressure = jnp.cumsum(wet * density, axis=0)
    row_index = (row_start + jnp.arange(rows, dtype=jnp.int32)).astype(jnp.float32)[None, :, None]
    coriolis_t = coriolis_max * (2.0 * (row_index + 0.5) / total_rows - 1.0)
    coriolis_v = coriolis_max * (2.0 * (row_index + 1.0) / total_rows - 1.0)

    def tracer(field):
        centre = view_at(field, 0, 0)
        east_side = view_at(field, 0, 1)
        west_side = view_at(field, 0, -1)
        north_side = view_at(field, 1, 0)
        south_side = view_at(field, -1, 0)
        flux_east = mask_east * (
            view_at(eastward, 0, 0) * (centre + east_side) * 0.5
            - lateral_diff * (east_side - centre)
        )
        flux_west = mask_west * (
            view_at(eastward, 0, -1) * (west_side + centre) * 0.5
            - lateral_diff * (centre - west_side)
        )
        flux_north = mask_north * (
            view_at(northward, 0, 0) * (centre + north_side) * 0.5
            - lateral_diff * (north_side - centre)
        )
        flux_south = mask_south * (
            view_at(northward, -1, 0) * (south_side + centre) * 0.5
            - lateral_diff * (centre - south_side)
        )
        tendency = flux_west - flux_east + (flux_south - flux_north) + column_flux(centre, mixing)
        return wet_here * (centre + time_step * tendency)

    east_here = view_at(eastward, 0, 0)
    north_here = view_at(northward, 0, 0)
    corner_ne = wet_here * view_at(wet, 0, 1) * view_at(wet, 1, 0) * view_at(wet, 1, 1)
    corner_se = view_at(wet, -1, 0) * view_at(wet, -1, 1) * wet_here * view_at(wet, 0, 1)
    corner_nw = view_at(wet, 0, -1) * wet_here * view_at(wet, 1, -1) * view_at(wet, 1, 0)
    cell_east = view_at(wet, 0, 1) * (
        ((east_here + view_at(eastward, 0, 1)) * 0.5) ** 2
        - lateral_diff * (view_at(eastward, 0, 1) - east_here)
    )
    cell_west = wet_here * (
        ((view_at(eastward, 0, -1) + east_here) * 0.5) ** 2
        - lateral_diff * (east_here - view_at(eastward, 0, -1))
    )
    product_ne = (
        (north_here + view_at(northward, 0, 1)) * 0.5 * (east_here + view_at(eastward, 1, 0)) * 0.5
    )
    product_se = (
        (view_at(northward, -1, 0) + view_at(northward, -1, 1))
        * 0.5
        * (view_at(eastward, -1, 0) + east_here)
        * 0.5
    )
    product_nw = (
        (view_at(eastward, 0, -1) + view_at(eastward, 1, -1))
        * 0.5
        * (view_at(northward, 0, -1) + north_here)
        * 0.5
    )
    shear_north = corner_ne * (product_ne - lateral_diff * (view_at(eastward, 1, 0) - east_here))
    shear_south = corner_se * (product_se - lateral_diff * (east_here - view_at(eastward, -1, 0)))
    north_mean = (
        north_here
        + view_at(northward, 0, 1)
        + view_at(northward, -1, 0)
        + view_at(northward, -1, 1)
    ) * 0.25
    east_tend = (
        cell_west
        - cell_east
        + (shear_south - shear_north)
        + coriolis_t * north_mean
        - pressure_coef * (view_at(pressure, 0, 1) - view_at(pressure, 0, 0))
        + column_flux(east_here, mixing)
        - drag_coef * bottom * east_here
    )
    east_next = mask_east * (east_here + time_step * east_tend)
    cell_north = view_at(wet, 1, 0) * (
        ((north_here + view_at(northward, 1, 0)) * 0.5) ** 2
        - lateral_diff * (view_at(northward, 1, 0) - north_here)
    )
    cell_south = wet_here * (
        ((view_at(northward, -1, 0) + north_here) * 0.5) ** 2
        - lateral_diff * (north_here - view_at(northward, -1, 0))
    )
    stress_east = corner_ne * (product_ne - lateral_diff * (view_at(northward, 0, 1) - north_here))
    stress_west = corner_nw * (product_nw - lateral_diff * (north_here - view_at(northward, 0, -1)))
    east_mean = (
        east_here + view_at(eastward, 0, -1) + view_at(eastward, 1, 0) + view_at(eastward, 1, -1)
    ) * 0.25
    north_tend = (
        stress_west
        - stress_east
        + (cell_south - cell_north)
        - coriolis_v * east_mean
        - pressure_coef * (view_at(pressure, 1, 0) - view_at(pressure, 0, 0))
        + column_flux(north_here, mixing)
        - drag_coef * bottom * north_here
    )
    north_next = mask_north * (north_here + time_step * north_tend)
    return (east_next, north_next, tracer(temper), tracer(saline))


def shift(value, mapping):
    lat_size = lax.axis_size("lat")
    lon_size = lax.axis_size("lon")
    pairs = []
    for a in range(lat_size):
        for b in range(lon_size):
            target = mapping(a, b, lat_size, lon_size)
            if target is not None:
                pairs.append((b * lat_size + a, target[1] * lat_size + target[0]))
    return lax.ppermute(value, ("lon", "lat"), pairs)


def edge_kernel(*refs):
    fields = len(refs) - 4
    sources = refs[:fields]
    top_ref, bottom_ref, west_ref, east_ref = refs[fields:]
    chunk, rows, cols = sources[0].shape
    levels = west_ref.shape[2]
    step = pl.program_id(0)
    lane = lax.broadcasted_iota(jnp.int32, (rows, levels), 1)

    @pl.when(step == 0)
    def _():
        west_ref[...] = jnp.zeros(west_ref.shape, jnp.float32)
        east_ref[...] = jnp.zeros(east_ref.shape, jnp.float32)

    for field, source in enumerate(sources):
        west = west_ref[field]
        east = east_ref[field]
        for r in range(chunk):
            x = source[r].astype(jnp.float32)
            top_ref[field, r : r + 1, :] = x[rows - 1 : rows, :]
            bottom_ref[field, r : r + 1, :] = x[0:1, :]
            here = lane == step * chunk + r
            west = jnp.where(here, x[:, 0:1], west)
            east = jnp.where(here, x[:, cols - 1 : cols], east)
        west_ref[field] = west
        east_ref[field] = east


def stencil_kernel(
    cor_ref, u_ref, v_ref, t_ref, s_ref, wet_ref, ua_ref, va_ref, ta_ref, sa_ref, wa_ref,
    ub_ref, vb_ref, tb_ref, sb_ref, wb_ref, clc_ref, rn_ref, rs_ref, tw_ref, te_ref,
    east_ref, north_ref, temp_ref, salt_ref, p_ref, pe_ref, pn_ref,
):
    chunk, rows, cols = u_ref.shape
    levels = tw_ref.shape[2]
    step = pl.program_id(0)
    near = {
        id(u_ref): (ua_ref, ub_ref),
        id(v_ref): (va_ref, vb_ref),
        id(t_ref): (ta_ref, tb_ref),
        id(s_ref): (sa_ref, sb_ref),
        id(wet_ref): (wa_ref, wb_ref),
    }

    def level(ref, r, offset):
        above, below = near[id(ref)]
        if offset < 0:
            return jnp.where(r == 0, above[0], ref[jnp.maximum(r - 1, 0)])
        return jnp.where(r == chunk - 1, below[0], ref[jnp.minimum(r + 1, chunk - 1)])

    @pl.when(step == 0)
    def _():
        p_ref[...] = jnp.zeros(p_ref.shape, jnp.float32)
        pe_ref[...] = jnp.zeros(pe_ref.shape, jnp.float32)
        pn_ref[...] = jnp.zeros(pn_ref.shape, jnp.float32)

    fields = 5
    lane = lax.broadcasted_iota(jnp.int32, (rows, cols), 1)
    sub = lax.broadcasted_iota(jnp.int32, (rows, cols), 0)
    at_east = lane == cols - 1
    at_west = lane == 0
    at_north = sub == rows - 1
    at_south = sub == 0
    row_lane = lax.broadcasted_iota(jnp.int32, (1, cols), 1)
    row_east = row_lane == cols - 1
    row_west = row_lane == 0
    pick_lane = lax.broadcasted_iota(jnp.int32, tw_ref.shape[1:], 1)
    cor_t = cor_ref[0]
    cor_v = cor_ref[1]
    count = clc_ref[...]

    def east(x, col):
        return jnp.where(at_east, col, pltpu.roll(x, cols - 1, 1))

    def west(x, col):
        return jnp.where(at_west, col, pltpu.roll(x, 1, 1))

    def north(x, row):
        return jnp.where(at_north, row, pltpu.roll(x, rows - 1, 0))

    def south(x, row):
        return jnp.where(at_south, row, pltpu.roll(x, 1, 0))

    def body(r, carry):
        pres, pres_e, pres_n = carry
        k = step * chunk + r

        spread = {}

        def tall(field):
            if field not in spread:
                spread[field] = tuple(
                    jnp.sum(jnp.where(pick_lane == k, ref[field], 0.0), axis=1, keepdims=True)
                    for ref in (tw_ref, te_ref)
                )
            return spread[field]

        def row(variant, field):
            west_t, east_t = tall(field)
            if variant == 0:
                return rn_ref[field, pl.ds(r, 1), :]
            if variant == 3:
                return rs_ref[field, pl.ds(r, 1), :]
            if variant == 1:
                return jnp.where(row_east, east_t[rows + 1 : rows + 2], pltpu.roll(row(0, field), cols - 1, 1))
            if variant == 2:
                return jnp.where(row_west, west_t[rows + 1 : rows + 2], pltpu.roll(row(0, field), 1, 1))
            return jnp.where(row_east, east_t[rows : rows + 1], pltpu.roll(row(3, field), cols - 1, 1))

        def col(field):
            west_t, east_t = tall(field)
            return west_t[0:rows], east_t[0:rows]

        w = wet_ref[r].astype(jnp.float32)
        w_above = level(wet_ref, r, -1).astype(jnp.float32)
        w_below = level(wet_ref, r, 1).astype(jnp.float32)
        w_wc, w_ec = col(4)
        w_e = east(w, w_ec)
        w_w = west(w, w_wc)
        w_n = north(w, row(0, 4))
        w_s = south(w, row(3, 4))
        w_ne = north(w_e, row(1, 4))
        w_se = south(w_e, row(4, 4))
        w_nw = north(w_w, row(2, 4))
        mask_east = w * w_e
        mask_west = w_w * w
        mask_north = w * w_n
        mask_south = w_s * w
        mix_below = jnp.where(
            k < levels - 1, w * w_below * (k + 1 < count).astype(jnp.float32), 0.0
        )
        mix_above = jnp.where(k > 0, w_above * w * (k < count).astype(jnp.float32), 0.0)
        bottom = (k == count - 1).astype(jnp.float32)

        def column(ref, centre):
            upper = level(ref, r, -1)
            lower = level(ref, r, 1)
            above = -vertical_diff * mix_above * (centre - upper)
            below = -vertical_diff * mix_below * (lower - centre)
            return above - below

        depth = (k.astype(jnp.float32) + 0.5) * level_depth

        def density(temper, saline):
            return (
                -thermal_expand * (1.0 + 0.5 * cabbel_temp * temper + thermo_temp * depth) * temper
                + haline_contract * (1.0 - 0.5 * cabbel_salt * saline - thermo_salt * depth) * saline
                - cabbel_mixed * temper * saline
            )

        tc = t_ref[r]
        sc = s_ref[r]
        t_wc, t_ec = col(2)
        s_wc, s_ec = col(3)
        pres = pres + w * density(tc, sc)
        pres_e = pres_e + w_ec * density(t_ec, s_ec)
        pres_n = pres_n + row(0, 4) * density(row(0, 2), row(0, 3))
        p_e = east(pres, pres_e)
        p_n = north(pres, pres_n)

        uc = u_ref[r]
        u_wc, u_ec = col(0)
        u_e = east(uc, u_ec)
        u_w = west(uc, u_wc)
        u_n = north(uc, row(0, 0))
        u_s = south(uc, row(3, 0))
        u_nw = north(u_w, row(2, 0))
        vc = v_ref[r]
        v_wc, v_ec = col(1)
        v_e = east(vc, v_ec)
        v_w = west(vc, v_wc)
        v_n = north(vc, row(0, 1))
        v_s = south(vc, row(3, 1))
        v_se = south(v_e, row(4, 1))

        def tracer(ref, centre, field, wcol, ecol):
            east_side = east(centre, ecol)
            west_side = west(centre, wcol)
            north_side = north(centre, row(0, field))
            south_side = south(centre, row(3, field))
            flux_east = mask_east * (
                uc * (centre + east_side) * 0.5 - lateral_diff * (east_side - centre)
            )
            flux_west = mask_west * (
                u_w * (west_side + centre) * 0.5 - lateral_diff * (centre - west_side)
            )
            flux_north = mask_north * (
                vc * (centre + north_side) * 0.5 - lateral_diff * (north_side - centre)
            )
            flux_south = mask_south * (
                v_s * (south_side + centre) * 0.5 - lateral_diff * (centre - south_side)
            )
            tendency = (
                flux_west - flux_east + (flux_south - flux_north) + column(ref, centre)
            )
            return w * (centre + time_step * tendency)

        temp_ref[r] = tracer(t_ref, tc, 2, t_wc, t_ec)
        salt_ref[r] = tracer(s_ref, sc, 3, s_wc, s_ec)

        corner_ne = w * w_e * w_n * w_ne
        corner_se = w_s * w_se * w * w_e
        corner_nw = w_w * w * w_nw * w_n
        half_e = (uc + u_e) * 0.5
        cell_east = w_e * (half_e * half_e - lateral_diff * (u_e - uc))
        half_w = (u_w + uc) * 0.5
        cell_west = w * (half_w * half_w - lateral_diff * (uc - u_w))
        product_ne = (vc + v_e) * 0.5 * (uc + u_n) * 0.5
        product_se = (v_s + v_se) * 0.5 * (u_s + uc) * 0.5
        product_nw = (u_w + u_nw) * 0.5 * (v_w + vc) * 0.5
        shear_north = corner_ne * (product_ne - lateral_diff * (u_n - uc))
        shear_south = corner_se * (product_se - lateral_diff * (uc - u_s))
        north_mean = (vc + v_e + v_s + v_se) * 0.25
        east_tend = (
            cell_west
            - cell_east
            + (shear_south - shear_north)
            + cor_t * north_mean
            - pressure_coef * (p_e - pres)
            + column(u_ref, uc)
            - drag_coef * bottom * uc
        )
        east_ref[r] = mask_east * (uc + time_step * east_tend)
        half_n = (vc + v_n) * 0.5
        cell_north = w_n * (half_n * half_n - lateral_diff * (v_n - vc))
        half_s = (v_s + vc) * 0.5
        cell_south = w * (half_s * half_s - lateral_diff * (vc - v_s))
        stress_east = corner_ne * (product_ne - lateral_diff * (v_e - vc))
        stress_west = corner_nw * (product_nw - lateral_diff * (vc - v_w))
        east_mean = (uc + u_w + u_n + u_nw) * 0.25
        north_tend = (
            stress_west
            - stress_east
            + (cell_south - cell_north)
            - cor_v * east_mean
            - pressure_coef * (p_n - pres)
            + column(v_ref, vc)
            - drag_coef * bottom * vc
        )
        north_ref[r] = mask_north * (vc + time_step * north_tend)
        return pres, pres_e, pres_n

    init = (p_ref[...], pe_ref[...], pn_ref[...])
    pres, pres_e, pres_n = lax.fori_loop(0, chunk, body, init)
    p_ref[...] = pres
    pe_ref[...] = pres_e
    pn_ref[...] = pres_n


def per_device(
    eastbound_current,
    poleward_current,
    warmth_excess,
    saltiness_excess,
    water_indicator,
    column_layer_count,
):
    inputs = (
        eastbound_current,
        poleward_current,
        warmth_excess,
        saltiness_excess,
        water_indicator,
    )

    levels, rows, cols = eastbound_current.shape
    fields = len(inputs)
    chunk = 8 if levels % 8 == 0 else levels
    row_block = pl.BlockSpec((fields, chunk, cols), lambda c: (0, c, 0))
    col_block = pl.BlockSpec((fields, rows, levels), lambda c: (0, 0, 0))
    top, bottom, west_col, east_col = pl.pallas_call(
        edge_kernel,
        grid=(levels // chunk,),
        in_specs=[pl.BlockSpec((chunk, rows, cols), lambda c: (c, 0, 0))] * fields,
        out_specs=(row_block, row_block, col_block, col_block),
        out_shape=(
            jax.ShapeDtypeStruct((fields, levels, cols), jnp.float32),
            jax.ShapeDtypeStruct((fields, levels, cols), jnp.float32),
            jax.ShapeDtypeStruct((fields, rows, levels), jnp.float32),
            jax.ShapeDtypeStruct((fields, rows, levels), jnp.float32),
        ),
    )(*inputs)

    def east_of(a, b, na, nl):
        return (a, (b + 1) % nl)

    def west_of(a, b, na, nl):
        return (a, (b - 1) % nl)

    def north_of(a, b, na, nl):
        return (a + 1, b) if a + 1 < na else None

    def south_of(a, b, na, nl):
        return (a - 1, b) if a > 0 else None

    def mirror(a, b, na, nl):
        return (a, nl - 1 - b) if a == na - 1 else None

    halo_south = shift(top, north_of)
    halo_north = shift(bottom, south_of)
    fold_row = shift(top, mirror)
    sign = jnp.array([-1.0, -1.0, 1.0, 1.0, 1.0], dtype=jnp.float32)[:, None, None]
    is_top = lax.axis_index("lat") == lax.axis_size("lat") - 1
    halo_north = jnp.where(is_top, sign * fold_row[:, :, ::-1], halo_north)
    pad = jnp.zeros((fields, 6, levels), jnp.float32)
    west_tall = jnp.concatenate(
        [west_col, halo_south[:, None, :, 0], halo_north[:, None, :, 0], pad], axis=1
    )
    east_tall = jnp.concatenate(
        [east_col, halo_south[:, None, :, -1], halo_north[:, None, :, -1], pad], axis=1
    )
    halo_west = shift(east_tall, east_of)
    halo_east = shift(west_tall, west_of)

    row_start = lax.axis_index("lat") * rows
    total_rows = rows * lax.axis_size("lat")
    row_index = (row_start + jnp.arange(rows, dtype=jnp.int32)).astype(jnp.float32)[:, None]
    coriolis_t = coriolis_max * (2.0 * (row_index + 0.5) / total_rows - 1.0)
    coriolis_v = coriolis_max * (2.0 * (row_index + 1.0) / total_rows - 1.0)
    coriolis = jnp.broadcast_to(jnp.stack([coriolis_t, coriolis_v]), (2, rows, cols))

    block = jax.ShapeDtypeStruct((levels, rows, cols), jnp.float32)
    main = pl.BlockSpec((chunk, rows, cols), lambda c: (c, 0, 0))
    above = pl.BlockSpec((1, rows, cols), lambda c: (jnp.maximum(c * chunk - 1, 0), 0, 0))
    below = pl.BlockSpec(
        (1, rows, cols), lambda c: (jnp.minimum(c * chunk + chunk, levels - 1), 0, 0)
    )

    def whole(shape):
        return pl.BlockSpec(shape, lambda c: (0,) * len(shape))

    halo_row = pl.BlockSpec((fields, chunk, cols), lambda c: (0, c, 0))
    return pl.pallas_call(
        stencil_kernel,
        grid=(levels // chunk,),
        in_specs=[whole((2, rows, cols))]
        + [main] * fields
        + [above] * fields
        + [below] * fields
        + [whole((rows, cols)), halo_row, halo_row, whole(halo_west.shape), whole(halo_east.shape)],
        out_specs=(main, main, main, main),
        out_shape=(block, block, block, block),
        scratch_shapes=[
            pltpu.VMEM((rows, cols), jnp.float32),
            pltpu.VMEM((rows, 1), jnp.float32),
            pltpu.VMEM((1, cols), jnp.float32),
        ],
    )(
        coriolis,
        *inputs,
        *inputs,
        *inputs,
        column_layer_count,
        halo_north,
        halo_south,
        halo_west,
        halo_east,
    )


def solution(mesh):
    placed = (
        P(None, "lat", "lon"),
        P(None, "lat", "lon"),
        P(None, "lat", "lon"),
        P(None, "lat", "lon"),
        P(None, "lat", "lon"),
        P("lat", "lon"),
    )
    return jax.shard_map(
        per_device,
        mesh=mesh,
        in_specs=placed,
        out_specs=(
            P(None, "lat", "lon"),
            P(None, "lat", "lon"),
            P(None, "lat", "lon"),
            P(None, "lat", "lon"),
        ),
        check_vma=False,
    )
```

```python
import jax
import jax.numpy as jnp
from jax import lax
from jax.experimental import pallas as pl
from jax.experimental.pallas import tpu as pltpu
from jax.sharding import PartitionSpec as P

time_step = 0.2
lateral_diff = 0.1
vertical_diff = 0.5
pressure_coef = 0.1
drag_coef = 2.0
coriolis_max = 1.0
level_depth = 100.0
thermal_expand = 0.1655
haline_contract = 0.76554
cabbel_temp = 0.05952
cabbel_salt = 0.00054914
cabbel_mixed = 0.0024341
thermo_temp = 0.0001497
thermo_salt = 1.109e-05


def view_at(field, lat_step, lon_step):
    rows = field.shape[1] - 2
    cols = field.shape[2] - 2
    return field[:, 1 + lat_step : 1 + lat_step + rows, 1 + lon_step : 1 + lon_step + cols]


def column_flux(centre, mixing):
    between = -vertical_diff * mixing * (centre[1:] - centre[:-1])
    surface = jnp.zeros_like(centre[:1])
    above = jnp.concatenate([surface, between], axis=0)
    below = jnp.concatenate([between, surface], axis=0)
    return above - below


def advance(extended, column_layer_count, row_start, total_rows):
    eastward = extended[0]
    northward = extended[1]
    temper = extended[2]
    saline = extended[3]
    wet = extended[4]
    levels = extended.shape[1]
    rows = extended.shape[2] - 2
    level_index = jnp.arange(levels, dtype=jnp.int32)[:, None, None]
    wet_here = view_at(wet, 0, 0)
    mask_east = wet_here * view_at(wet, 0, 1)
    mask_west = view_at(wet, 0, -1) * wet_here
    mask_north = wet_here * view_at(wet, 1, 0)
    mask_south = view_at(wet, -1, 0) * wet_here
    mixing = (
        wet_here[:-1]
        * wet_here[1:]
        * (level_index[1:] < column_layer_count[None]).astype(jnp.float32)
    )
    bottom = (level_index == column_layer_count[None] - 1).astype(jnp.float32)
    depth = (level_index.astype(jnp.float32) + 0.5) * level_depth
    density = (
        -thermal_expand * (1.0 + 0.5 * cabbel_temp * temper + thermo_temp * depth) * temper
        + haline_contract * (1.0 - 0.5 * cabbel_salt * saline - thermo_salt * depth) * saline
        - cabbel_mixed * temper * saline
    )
    pressure = jnp.cumsum(wet * density, axis=0)
    row_index = (row_start + jnp.arange(rows, dtype=jnp.int32)).astype(jnp.float32)[None, :, None]
    coriolis_t = coriolis_max * (2.0 * (row_index + 0.5) / total_rows - 1.0)
    coriolis_v = coriolis_max * (2.0 * (row_index + 1.0) / total_rows - 1.0)

    def tracer(field):
        centre = view_at(field, 0, 0)
        east_side = view_at(field, 0, 1)
        west_side = view_at(field, 0, -1)
        north_side = view_at(field, 1, 0)
        south_side = view_at(field, -1, 0)
        flux_east = mask_east * (
            view_at(eastward, 0, 0) * (centre + east_side) * 0.5
            - lateral_diff * (east_side - centre)
        )
        flux_west = mask_west * (
            view_at(eastward, 0, -1) * (west_side + centre) * 0.5
            - lateral_diff * (centre - west_side)
        )
        flux_north = mask_north * (
            view_at(northward, 0, 0) * (centre + north_side) * 0.5
            - lateral_diff * (north_side - centre)
        )
        flux_south = mask_south * (
            view_at(northward, -1, 0) * (south_side + centre) * 0.5
            - lateral_diff * (centre - south_side)
        )
        tendency = flux_west - flux_east + (flux_south - flux_north) + column_flux(centre, mixing)
        return wet_here * (centre + time_step * tendency)

    east_here = view_at(eastward, 0, 0)
    north_here = view_at(northward, 0, 0)
    corner_ne = wet_here * view_at(wet, 0, 1) * view_at(wet, 1, 0) * view_at(wet, 1, 1)
    corner_se = view_at(wet, -1, 0) * view_at(wet, -1, 1) * wet_here * view_at(wet, 0, 1)
    corner_nw = view_at(wet, 0, -1) * wet_here * view_at(wet, 1, -1) * view_at(wet, 1, 0)
    cell_east = view_at(wet, 0, 1) * (
        ((east_here + view_at(eastward, 0, 1)) * 0.5) ** 2
        - lateral_diff * (view_at(eastward, 0, 1) - east_here)
    )
    cell_west = wet_here * (
        ((view_at(eastward, 0, -1) + east_here) * 0.5) ** 2
        - lateral_diff * (east_here - view_at(eastward, 0, -1))
    )
    product_ne = (
        (north_here + view_at(northward, 0, 1)) * 0.5 * (east_here + view_at(eastward, 1, 0)) * 0.5
    )
    product_se = (
        (view_at(northward, -1, 0) + view_at(northward, -1, 1))
        * 0.5
        * (view_at(eastward, -1, 0) + east_here)
        * 0.5
    )
    product_nw = (
        (view_at(eastward, 0, -1) + view_at(eastward, 1, -1))
        * 0.5
        * (view_at(northward, 0, -1) + north_here)
        * 0.5
    )
    shear_north = corner_ne * (product_ne - lateral_diff * (view_at(eastward, 1, 0) - east_here))
    shear_south = corner_se * (product_se - lateral_diff * (east_here - view_at(eastward, -1, 0)))
    north_mean = (
        north_here
        + view_at(northward, 0, 1)
        + view_at(northward, -1, 0)
        + view_at(northward, -1, 1)
    ) * 0.25
    east_tend = (
        cell_west
        - cell_east
        + (shear_south - shear_north)
        + coriolis_t * north_mean
        - pressure_coef * (view_at(pressure, 0, 1) - view_at(pressure, 0, 0))
        + column_flux(east_here, mixing)
        - drag_coef * bottom * east_here
    )
    east_next = mask_east * (east_here + time_step * east_tend)
    cell_north = view_at(wet, 1, 0) * (
        ((north_here + view_at(northward, 1, 0)) * 0.5) ** 2
        - lateral_diff * (view_at(northward, 1, 0) - north_here)
    )
    cell_south = wet_here * (
        ((view_at(northward, -1, 0) + north_here) * 0.5) ** 2
        - lateral_diff * (north_here - view_at(northward, -1, 0))
    )
    stress_east = corner_ne * (product_ne - lateral_diff * (view_at(northward, 0, 1) - north_here))
    stress_west = corner_nw * (product_nw - lateral_diff * (north_here - view_at(northward, 0, -1)))
    east_mean = (
        east_here + view_at(eastward, 0, -1) + view_at(eastward, 1, 0) + view_at(eastward, 1, -1)
    ) * 0.25
    north_tend = (
        stress_west
        - stress_east
        + (cell_south - cell_north)
        - coriolis_v * east_mean
        - pressure_coef * (view_at(pressure, 1, 0) - view_at(pressure, 0, 0))
        + column_flux(north_here, mixing)
        - drag_coef * bottom * north_here
    )
    north_next = mask_north * (north_here + time_step * north_tend)
    return (east_next, north_next, tracer(temper), tracer(saline))


def shift(value, mapping):
    lat_size = lax.axis_size("lat")
    lon_size = lax.axis_size("lon")
    pairs = []
    for a in range(lat_size):
        for b in range(lon_size):
            target = mapping(a, b, lat_size, lon_size)
            if target is not None:
                pairs.append((b * lat_size + a, target[1] * lat_size + target[0]))
    return lax.ppermute(value, ("lon", "lat"), pairs)


def edge_kernel(*refs):
    fields = len(refs) - 4
    sources = refs[:fields]
    top_ref, bottom_ref, west_ref, east_ref = refs[fields:]
    chunk, rows, cols = sources[0].shape
    levels = west_ref.shape[2]
    step = pl.program_id(0)
    lane = lax.broadcasted_iota(jnp.int32, (rows, levels), 1)

    @pl.when(step == 0)
    def _():
        west_ref[...] = jnp.zeros(west_ref.shape, jnp.float32)
        east_ref[...] = jnp.zeros(east_ref.shape, jnp.float32)

    for field, source in enumerate(sources):
        west = west_ref[field]
        east = east_ref[field]
        for r in range(chunk):
            x = source[r].astype(jnp.float32)
            top_ref[field, r : r + 1, :] = x[rows - 1 : rows, :]
            bottom_ref[field, r : r + 1, :] = x[0:1, :]
            here = lane == step * chunk + r
            west = jnp.where(here, x[:, 0:1], west)
            east = jnp.where(here, x[:, cols - 1 : cols], east)
        west_ref[field] = west
        east_ref[field] = east


def stencil_kernel(
    cor_ref, u_ref, v_ref, t_ref, s_ref, wet_ref, ua_ref, va_ref, ta_ref, sa_ref, wa_ref,
    ub_ref, vb_ref, tb_ref, sb_ref, wb_ref, clc_ref, rn_ref, rs_ref, tw_ref, te_ref,
    east_ref, north_ref, temp_ref, salt_ref, p_ref, pe_ref, pn_ref,
):
    chunk, rows, cols = u_ref.shape
    levels = tw_ref.shape[2]
    step = pl.program_id(0)
    near = {
        id(u_ref): (ua_ref, ub_ref),
        id(v_ref): (va_ref, vb_ref),
        id(t_ref): (ta_ref, tb_ref),
        id(s_ref): (sa_ref, sb_ref),
        id(wet_ref): (wa_ref, wb_ref),
    }

    def level(ref, r, offset):
        above, below = near[id(ref)]
        if offset < 0:
            return jnp.where(r == 0, above[0], ref[jnp.maximum(r - 1, 0)])
        return jnp.where(r == chunk - 1, below[0], ref[jnp.minimum(r + 1, chunk - 1)])

    @pl.when(step == 0)
    def _():
        p_ref[...] = jnp.zeros(p_ref.shape, jnp.float32)
        pe_ref[...] = jnp.zeros(pe_ref.shape, jnp.float32)
        pn_ref[...] = jnp.zeros(pn_ref.shape, jnp.float32)

    fields = 5
    lane = lax.broadcasted_iota(jnp.int32, (rows, cols), 1)
    sub = lax.broadcasted_iota(jnp.int32, (rows, cols), 0)
    at_east = lane == cols - 1
    at_west = lane == 0
    at_north = sub == rows - 1
    at_south = sub == 0
    row_lane = lax.broadcasted_iota(jnp.int32, (1, cols), 1)
    row_east = row_lane == cols - 1
    row_west = row_lane == 0
    pick_lane = lax.broadcasted_iota(jnp.int32, tw_ref.shape[1:], 1)
    cor_t = cor_ref[0]
    cor_v = cor_ref[1]
    count = clc_ref[...]

    def east(x, col):
        return jnp.where(at_east, col, pltpu.roll(x, cols - 1, 1))

    def west(x, col):
        return jnp.where(at_west, col, pltpu.roll(x, 1, 1))

    def north(x, row):
        return jnp.where(at_north, row, pltpu.roll(x, rows - 1, 0))

    def south(x, row):
        return jnp.where(at_south, row, pltpu.roll(x, 1, 0))

    def body(r, carry):
        pres, pres_e, pres_n = carry
        k = step * chunk + r

        spread = {}

        def tall(field):
            if field not in spread:
                spread[field] = tuple(
                    jnp.broadcast_to(
                        jnp.sum(jnp.where(pick_lane == k, ref[field], 0.0), axis=1, keepdims=True),
                        (ref.shape[1], cols),
                    )
                    for ref in (tw_ref, te_ref)
                )
            return spread[field]

        def row(variant, field):
            west_t, east_t = tall(field)
            if variant == 0:
                return rn_ref[field, pl.ds(r, 1), :]
            if variant == 3:
                return rs_ref[field, pl.ds(r, 1), :]
            if variant == 1:
                return jnp.where(row_east, east_t[rows + 1 : rows + 2], pltpu.roll(row(0, field), cols - 1, 1))
            if variant == 2:
                return jnp.where(row_west, west_t[rows + 1 : rows + 2], pltpu.roll(row(0, field), 1, 1))
            return jnp.where(row_east, east_t[rows : rows + 1], pltpu.roll(row(3, field), cols - 1, 1))

        def col(field):
            west_t, east_t = tall(field)
            return west_t[0:rows], east_t[0:rows]

        w = wet_ref[r].astype(jnp.float32)
        w_above = level(wet_ref, r, -1).astype(jnp.float32)
        w_below = level(wet_ref, r, 1).astype(jnp.float32)
        w_wc, w_ec = col(4)
        w_e = east(w, w_ec)
        w_w = west(w, w_wc)
        w_n = north(w, row(0, 4))
        w_s = south(w, row(3, 4))
        w_ne = north(w_e, row(1, 4))
        w_se = south(w_e, row(4, 4))
        w_nw = north(w_w, row(2, 4))
        mask_east = w * w_e
        mask_west = w_w * w
        mask_north = w * w_n
        mask_south = w_s * w
        mix_below = jnp.where(
            k < levels - 1, w * w_below * (k + 1 < count).astype(jnp.float32), 0.0
        )
        mix_above = jnp.where(k > 0, w_above * w * (k < count).astype(jnp.float32), 0.0)
        bottom = (k == count - 1).astype(jnp.float32)

        def column(ref, centre):
            upper = level(ref, r, -1)
            lower = level(ref, r, 1)
            above = -vertical_diff * mix_above * (centre - upper)
            below = -vertical_diff * mix_below * (lower - centre)
            return above - below

        depth = (k.astype(jnp.float32) + 0.5) * level_depth

        def density(temper, saline):
            return (
                -thermal_expand * (1.0 + 0.5 * cabbel_temp * temper + thermo_temp * depth) * temper
                + haline_contract * (1.0 - 0.5 * cabbel_salt * saline - thermo_salt * depth) * saline
                - cabbel_mixed * temper * saline
            )

        tc = t_ref[r]
        sc = s_ref[r]
        t_wc, t_ec = col(2)
        s_wc, s_ec = col(3)
        pres = pres + w * density(tc, sc)
        pres_e = pres_e + w_ec * density(t_ec, s_ec)
        pres_n = pres_n + row(0, 4) * density(row(0, 2), row(0, 3))
        p_e = east(pres, pres_e)
        p_n = north(pres, pres_n)

        uc = u_ref[r]
        u_wc, u_ec = col(0)
        u_e = east(uc, u_ec)
        u_w = west(uc, u_wc)
        u_n = north(uc, row(0, 0))
        u_s = south(uc, row(3, 0))
        u_nw = north(u_w, row(2, 0))
        vc = v_ref[r]
        v_wc, v_ec = col(1)
        v_e = east(vc, v_ec)
        v_w = west(vc, v_wc)
        v_n = north(vc, row(0, 1))
        v_s = south(vc, row(3, 1))
        v_se = south(v_e, row(4, 1))

        def tracer(ref, centre, field, wcol, ecol):
            east_side = east(centre, ecol)
            west_side = west(centre, wcol)
            north_side = north(centre, row(0, field))
            south_side = south(centre, row(3, field))
            flux_east = mask_east * (
                uc * (centre + east_side) * 0.5 - lateral_diff * (east_side - centre)
            )
            flux_west = mask_west * (
                u_w * (west_side + centre) * 0.5 - lateral_diff * (centre - west_side)
            )
            flux_north = mask_north * (
                vc * (centre + north_side) * 0.5 - lateral_diff * (north_side - centre)
            )
            flux_south = mask_south * (
                v_s * (south_side + centre) * 0.5 - lateral_diff * (centre - south_side)
            )
            tendency = (
                flux_west - flux_east + (flux_south - flux_north) + column(ref, centre)
            )
            return w * (centre + time_step * tendency)

        temp_ref[r] = tracer(t_ref, tc, 2, t_wc, t_ec)
        salt_ref[r] = tracer(s_ref, sc, 3, s_wc, s_ec)

        corner_ne = w * w_e * w_n * w_ne
        corner_se = w_s * w_se * w * w_e
        corner_nw = w_w * w * w_nw * w_n
        half_e = (uc + u_e) * 0.5
        cell_east = w_e * (half_e * half_e - lateral_diff * (u_e - uc))
        half_w = (u_w + uc) * 0.5
        cell_west = w * (half_w * half_w - lateral_diff * (uc - u_w))
        product_ne = (vc + v_e) * 0.5 * (uc + u_n) * 0.5
        product_se = (v_s + v_se) * 0.5 * (u_s + uc) * 0.5
        product_nw = (u_w + u_nw) * 0.5 * (v_w + vc) * 0.5
        shear_north = corner_ne * (product_ne - lateral_diff * (u_n - uc))
        shear_south = corner_se * (product_se - lateral_diff * (uc - u_s))
        north_mean = (vc + v_e + v_s + v_se) * 0.25
        east_tend = (
            cell_west
            - cell_east
            + (shear_south - shear_north)
            + cor_t * north_mean
            - pressure_coef * (p_e - pres)
            + column(u_ref, uc)
            - drag_coef * bottom * uc
        )
        east_ref[r] = mask_east * (uc + time_step * east_tend)
        half_n = (vc + v_n) * 0.5
        cell_north = w_n * (half_n * half_n - lateral_diff * (v_n - vc))
        half_s = (v_s + vc) * 0.5
        cell_south = w * (half_s * half_s - lateral_diff * (vc - v_s))
        stress_east = corner_ne * (product_ne - lateral_diff * (v_e - vc))
        stress_west = corner_nw * (product_nw - lateral_diff * (vc - v_w))
        east_mean = (uc + u_w + u_n + u_nw) * 0.25
        north_tend = (
            stress_west
            - stress_east
            + (cell_south - cell_north)
            - cor_v * east_mean
            - pressure_coef * (p_n - pres)
            + column(v_ref, vc)
            - drag_coef * bottom * vc
        )
        north_ref[r] = mask_north * (vc + time_step * north_tend)
        return pres, pres_e, pres_n

    init = (p_ref[...], pe_ref[...], pn_ref[...])
    pres, pres_e, pres_n = lax.fori_loop(0, chunk, body, init)
    p_ref[...] = pres
    pe_ref[...] = pres_e
    pn_ref[...] = pres_n


def per_device(
    eastbound_current,
    poleward_current,
    warmth_excess,
    saltiness_excess,
    water_indicator,
    column_layer_count,
):
    inputs = (
        eastbound_current,
        poleward_current,
        warmth_excess,
        saltiness_excess,
        water_indicator,
    )

    levels, rows, cols = eastbound_current.shape
    fields = len(inputs)
    chunk = 8 if levels % 8 == 0 else levels
    row_block = pl.BlockSpec((fields, chunk, cols), lambda c: (0, c, 0))
    col_block = pl.BlockSpec((fields, rows, levels), lambda c: (0, 0, 0))
    top, bottom, west_col, east_col = pl.pallas_call(
        edge_kernel,
        grid=(levels // chunk,),
        in_specs=[pl.BlockSpec((chunk, rows, cols), lambda c: (c, 0, 0))] * fields,
        out_specs=(row_block, row_block, col_block, col_block),
        out_shape=(
            jax.ShapeDtypeStruct((fields, levels, cols), jnp.float32),
            jax.ShapeDtypeStruct((fields, levels, cols), jnp.float32),
            jax.ShapeDtypeStruct((fields, rows, levels), jnp.float32),
            jax.ShapeDtypeStruct((fields, rows, levels), jnp.float32),
        ),
    )(*inputs)

    def east_of(a, b, na, nl):
        return (a, (b + 1) % nl)

    def west_of(a, b, na, nl):
        return (a, (b - 1) % nl)

    def north_of(a, b, na, nl):
        return (a + 1, b) if a + 1 < na else None

    def south_of(a, b, na, nl):
        return (a - 1, b) if a > 0 else None

    def mirror(a, b, na, nl):
        return (a, nl - 1 - b) if a == na - 1 else None

    halo_south = shift(top, north_of)
    halo_north = shift(bottom, south_of)
    fold_row = shift(top, mirror)
    sign = jnp.array([-1.0, -1.0, 1.0, 1.0, 1.0], dtype=jnp.float32)[:, None, None]
    is_top = lax.axis_index("lat") == lax.axis_size("lat") - 1
    halo_north = jnp.where(is_top, sign * fold_row[:, :, ::-1], halo_north)
    pad = jnp.zeros((fields, 6, levels), jnp.float32)
    west_tall = jnp.concatenate(
        [west_col, halo_south[:, None, :, 0], halo_north[:, None, :, 0], pad], axis=1
    )
    east_tall = jnp.concatenate(
        [east_col, halo_south[:, None, :, -1], halo_north[:, None, :, -1], pad], axis=1
    )
    halo_west = shift(east_tall, east_of)
    halo_east = shift(west_tall, west_of)

    row_start = lax.axis_index("lat") * rows
    total_rows = rows * lax.axis_size("lat")
    row_index = (row_start + jnp.arange(rows, dtype=jnp.int32)).astype(jnp.float32)[:, None]
    coriolis_t = coriolis_max * (2.0 * (row_index + 0.5) / total_rows - 1.0)
    coriolis_v = coriolis_max * (2.0 * (row_index + 1.0) / total_rows - 1.0)
    coriolis = jnp.stack([coriolis_t, coriolis_v])

    block = jax.ShapeDtypeStruct((levels, rows, cols), jnp.float32)
    main = pl.BlockSpec((chunk, rows, cols), lambda c: (c, 0, 0))
    above = pl.BlockSpec((1, rows, cols), lambda c: (jnp.maximum(c * chunk - 1, 0), 0, 0))
    below = pl.BlockSpec(
        (1, rows, cols), lambda c: (jnp.minimum(c * chunk + chunk, levels - 1), 0, 0)
    )

    def whole(shape):
        return pl.BlockSpec(shape, lambda c: (0,) * len(shape))

    halo_row = pl.BlockSpec((fields, chunk, cols), lambda c: (0, c, 0))
    return pl.pallas_call(
        stencil_kernel,
        grid=(levels // chunk,),
        in_specs=[whole((2, rows, 1))]
        + [main] * fields
        + [above] * fields
        + [below] * fields
        + [whole((rows, cols)), halo_row, halo_row, whole(halo_west.shape), whole(halo_east.shape)],
        out_specs=(main, main, main, main),
        out_shape=(block, block, block, block),
        scratch_shapes=[
            pltpu.VMEM((rows, cols), jnp.float32),
            pltpu.VMEM((rows, cols), jnp.float32),
            pltpu.VMEM((1, cols), jnp.float32),
        ],
    )(
        coriolis,
        *inputs,
        *inputs,
        *inputs,
        column_layer_count,
        halo_north,
        halo_south,
        halo_west,
        halo_east,
    )


def solution(mesh):
    placed = (
        P(None, "lat", "lon"),
        P(None, "lat", "lon"),
        P(None, "lat", "lon"),
        P(None, "lat", "lon"),
        P(None, "lat", "lon"),
        P("lat", "lon"),
    )
    return jax.shard_map(
        per_device,
        mesh=mesh,
        in_specs=placed,
        out_specs=(
            P(None, "lat", "lon"),
            P(None, "lat", "lon"),
            P(None, "lat", "lon"),
            P(None, "lat", "lon"),
        ),
        check_vma=False,
    )
```

```python
import jax
import jax.numpy as jnp
from jax import lax
from jax.experimental import pallas as pl
from jax.experimental.pallas import tpu as pltpu
from jax.sharding import PartitionSpec as P

time_step = 0.2
lateral_diff = 0.1
vertical_diff = 0.5
pressure_coef = 0.1
drag_coef = 2.0
coriolis_max = 1.0
level_depth = 100.0
thermal_expand = 0.1655
haline_contract = 0.76554
cabbel_temp = 0.05952
cabbel_salt = 0.00054914
cabbel_mixed = 0.0024341
thermo_temp = 0.0001497
thermo_salt = 1.109e-05


def view_at(field, lat_step, lon_step):
    rows = field.shape[1] - 2
    cols = field.shape[2] - 2
    return field[:, 1 + lat_step : 1 + lat_step + rows, 1 + lon_step : 1 + lon_step + cols]


def column_flux(centre, mixing):
    between = -vertical_diff * mixing * (centre[1:] - centre[:-1])
    surface = jnp.zeros_like(centre[:1])
    above = jnp.concatenate([surface, between], axis=0)
    below = jnp.concatenate([between, surface], axis=0)
    return above - below


def advance(extended, column_layer_count, row_start, total_rows):
    eastward = extended[0]
    northward = extended[1]
    temper = extended[2]
    saline = extended[3]
    wet = extended[4]
    levels = extended.shape[1]
    rows = extended.shape[2] - 2
    level_index = jnp.arange(levels, dtype=jnp.int32)[:, None, None]
    wet_here = view_at(wet, 0, 0)
    mask_east = wet_here * view_at(wet, 0, 1)
    mask_west = view_at(wet, 0, -1) * wet_here
    mask_north = wet_here * view_at(wet, 1, 0)
    mask_south = view_at(wet, -1, 0) * wet_here
    mixing = (
        wet_here[:-1]
        * wet_here[1:]
        * (level_index[1:] < column_layer_count[None]).astype(jnp.float32)
    )
    bottom = (level_index == column_layer_count[None] - 1).astype(jnp.float32)
    depth = (level_index.astype(jnp.float32) + 0.5) * level_depth
    density = (
        -thermal_expand * (1.0 + 0.5 * cabbel_temp * temper + thermo_temp * depth) * temper
        + haline_contract * (1.0 - 0.5 * cabbel_salt * saline - thermo_salt * depth) * saline
        - cabbel_mixed * temper * saline
    )
    pressure = jnp.cumsum(wet * density, axis=0)
    row_index = (row_start + jnp.arange(rows, dtype=jnp.int32)).astype(jnp.float32)[None, :, None]
    coriolis_t = coriolis_max * (2.0 * (row_index + 0.5) / total_rows - 1.0)
    coriolis_v = coriolis_max * (2.0 * (row_index + 1.0) / total_rows - 1.0)

    def tracer(field):
        centre = view_at(field, 0, 0)
        east_side = view_at(field, 0, 1)
        west_side = view_at(field, 0, -1)
        north_side = view_at(field, 1, 0)
        south_side = view_at(field, -1, 0)
        flux_east = mask_east * (
            view_at(eastward, 0, 0) * (centre + east_side) * 0.5
            - lateral_diff * (east_side - centre)
        )
        flux_west = mask_west * (
            view_at(eastward, 0, -1) * (west_side + centre) * 0.5
            - lateral_diff * (centre - west_side)
        )
        flux_north = mask_north * (
            view_at(northward, 0, 0) * (centre + north_side) * 0.5
            - lateral_diff * (north_side - centre)
        )
        flux_south = mask_south * (
            view_at(northward, -1, 0) * (south_side + centre) * 0.5
            - lateral_diff * (centre - south_side)
        )
        tendency = flux_west - flux_east + (flux_south - flux_north) + column_flux(centre, mixing)
        return wet_here * (centre + time_step * tendency)

    east_here = view_at(eastward, 0, 0)
    north_here = view_at(northward, 0, 0)
    corner_ne = wet_here * view_at(wet, 0, 1) * view_at(wet, 1, 0) * view_at(wet, 1, 1)
    corner_se = view_at(wet, -1, 0) * view_at(wet, -1, 1) * wet_here * view_at(wet, 0, 1)
    corner_nw = view_at(wet, 0, -1) * wet_here * view_at(wet, 1, -1) * view_at(wet, 1, 0)
    cell_east = view_at(wet, 0, 1) * (
        ((east_here + view_at(eastward, 0, 1)) * 0.5) ** 2
        - lateral_diff * (view_at(eastward, 0, 1) - east_here)
    )
    cell_west = wet_here * (
        ((view_at(eastward, 0, -1) + east_here) * 0.5) ** 2
        - lateral_diff * (east_here - view_at(eastward, 0, -1))
    )
    product_ne = (
        (north_here + view_at(northward, 0, 1)) * 0.5 * (east_here + view_at(eastward, 1, 0)) * 0.5
    )
    product_se = (
        (view_at(northward, -1, 0) + view_at(northward, -1, 1))
        * 0.5
        * (view_at(eastward, -1, 0) + east_here)
        * 0.5
    )
    product_nw = (
        (view_at(eastward, 0, -1) + view_at(eastward, 1, -1))
        * 0.5
        * (view_at(northward, 0, -1) + north_here)
        * 0.5
    )
    shear_north = corner_ne * (product_ne - lateral_diff * (view_at(eastward, 1, 0) - east_here))
    shear_south = corner_se * (product_se - lateral_diff * (east_here - view_at(eastward, -1, 0)))
    north_mean = (
        north_here
        + view_at(northward, 0, 1)
        + view_at(northward, -1, 0)
        + view_at(northward, -1, 1)
    ) * 0.25
    east_tend = (
        cell_west
        - cell_east
        + (shear_south - shear_north)
        + coriolis_t * north_mean
        - pressure_coef * (view_at(pressure, 0, 1) - view_at(pressure, 0, 0))
        + column_flux(east_here, mixing)
        - drag_coef * bottom * east_here
    )
    east_next = mask_east * (east_here + time_step * east_tend)
    cell_north = view_at(wet, 1, 0) * (
        ((north_here + view_at(northward, 1, 0)) * 0.5) ** 2
        - lateral_diff * (view_at(northward, 1, 0) - north_here)
    )
    cell_south = wet_here * (
        ((view_at(northward, -1, 0) + north_here) * 0.5) ** 2
        - lateral_diff * (north_here - view_at(northward, -1, 0))
    )
    stress_east = corner_ne * (product_ne - lateral_diff * (view_at(northward, 0, 1) - north_here))
    stress_west = corner_nw * (product_nw - lateral_diff * (north_here - view_at(northward, 0, -1)))
    east_mean = (
        east_here + view_at(eastward, 0, -1) + view_at(eastward, 1, 0) + view_at(eastward, 1, -1)
    ) * 0.25
    north_tend = (
        stress_west
        - stress_east
        + (cell_south - cell_north)
        - coriolis_v * east_mean
        - pressure_coef * (view_at(pressure, 1, 0) - view_at(pressure, 0, 0))
        + column_flux(north_here, mixing)
        - drag_coef * bottom * north_here
    )
    north_next = mask_north * (north_here + time_step * north_tend)
    return (east_next, north_next, tracer(temper), tracer(saline))


def shift(value, mapping):
    lat_size = lax.axis_size("lat")
    lon_size = lax.axis_size("lon")
    pairs = []
    for a in range(lat_size):
        for b in range(lon_size):
            target = mapping(a, b, lat_size, lon_size)
            if target is not None:
                pairs.append((b * lat_size + a, target[1] * lat_size + target[0]))
    return lax.ppermute(value, ("lon", "lat"), pairs)


def row_kernel(*refs):
    fields = (len(refs) - 2) // 2
    lows = refs[:fields]
    highs = refs[fields : 2 * fields]
    top_ref, bottom_ref = refs[2 * fields :]
    chunk, tile, cols = lows[0].shape
    for field in range(fields):
        for r in range(chunk):
            top_ref[field, r : r + 1, :] = highs[field][r][tile - 1 : tile, :].astype(jnp.float32)
            bottom_ref[field, r : r + 1, :] = lows[field][r][0:1, :].astype(jnp.float32)


def edge_kernel(*refs):
    fields = len(refs) - 2
    sources = refs[:fields]
    west_ref, east_ref = refs[fields:]
    chunk, rows, cols = sources[0].shape
    levels = west_ref.shape[2]
    step = pl.program_id(0)
    lane = lax.broadcasted_iota(jnp.int32, (rows, levels), 1)

    @pl.when(step == 0)
    def _():
        west_ref[...] = jnp.zeros(west_ref.shape, jnp.float32)
        east_ref[...] = jnp.zeros(east_ref.shape, jnp.float32)

    for field, source in enumerate(sources):
        west = west_ref[field]
        east = east_ref[field]
        for r in range(chunk):
            x = source[r].astype(jnp.float32)
            here = lane == step * chunk + r
            west = jnp.where(here, x[:, 0:1], west)
            east = jnp.where(here, x[:, cols - 1 : cols], east)
        west_ref[field] = west
        east_ref[field] = east


def stencil_kernel(
    cor_ref, u_ref, v_ref, t_ref, s_ref, wet_ref, ua_ref, va_ref, ta_ref, sa_ref, wa_ref,
    ub_ref, vb_ref, tb_ref, sb_ref, wb_ref, clc_ref, rn_ref, rs_ref, tw_ref, te_ref,
    east_ref, north_ref, temp_ref, salt_ref, p_ref, pe_ref, pn_ref,
):
    chunk, rows, cols = u_ref.shape
    levels = tw_ref.shape[2]
    step = pl.program_id(0)
    near = {
        id(u_ref): (ua_ref, ub_ref),
        id(v_ref): (va_ref, vb_ref),
        id(t_ref): (ta_ref, tb_ref),
        id(s_ref): (sa_ref, sb_ref),
        id(wet_ref): (wa_ref, wb_ref),
    }

    def level(ref, r, offset):
        above, below = near[id(ref)]
        if offset < 0:
            return jnp.where(r == 0, above[0], ref[jnp.maximum(r - 1, 0)])
        return jnp.where(r == chunk - 1, below[0], ref[jnp.minimum(r + 1, chunk - 1)])

    @pl.when(step == 0)
    def _():
        p_ref[...] = jnp.zeros(p_ref.shape, jnp.float32)
        pe_ref[...] = jnp.zeros(pe_ref.shape, jnp.float32)
        pn_ref[...] = jnp.zeros(pn_ref.shape, jnp.float32)

    fields = 5
    lane = lax.broadcasted_iota(jnp.int32, (rows, cols), 1)
    sub = lax.broadcasted_iota(jnp.int32, (rows, cols), 0)
    at_east = lane == cols - 1
    at_west = lane == 0
    at_north = sub == rows - 1
    at_south = sub == 0
    row_lane = lax.broadcasted_iota(jnp.int32, (1, cols), 1)
    row_east = row_lane == cols - 1
    row_west = row_lane == 0
    pick_lane = lax.broadcasted_iota(jnp.int32, tw_ref.shape[1:], 1)
    cor_t = cor_ref[0]
    cor_v = cor_ref[1]
    count = clc_ref[...]

    def east(x, col):
        return jnp.where(at_east, col, pltpu.roll(x, cols - 1, 1))

    def west(x, col):
        return jnp.where(at_west, col, pltpu.roll(x, 1, 1))

    def north(x, row):
        return jnp.where(at_north, row, pltpu.roll(x, rows - 1, 0))

    def south(x, row):
        return jnp.where(at_south, row, pltpu.roll(x, 1, 0))

    def body(r, carry):
        pres, pres_e, pres_n = carry
        k = step * chunk + r

        spread = {}

        def tall(field):
            if field not in spread:
                spread[field] = tuple(
                    jnp.broadcast_to(
                        jnp.sum(jnp.where(pick_lane == k, ref[field], 0.0), axis=1, keepdims=True),
                        (ref.shape[1], cols),
                    )
                    for ref in (tw_ref, te_ref)
                )
            return spread[field]

        def row(variant, field):
            west_t, east_t = tall(field)
            if variant == 0:
                return rn_ref[field, pl.ds(r, 1), :]
            if variant == 3:
                return rs_ref[field, pl.ds(r, 1), :]
            if variant == 1:
                return jnp.where(row_east, east_t[rows + 1 : rows + 2], pltpu.roll(row(0, field), cols - 1, 1))
            if variant == 2:
                return jnp.where(row_west, west_t[rows + 1 : rows + 2], pltpu.roll(row(0, field), 1, 1))
            return jnp.where(row_east, east_t[rows : rows + 1], pltpu.roll(row(3, field), cols - 1, 1))

        def col(field):
            west_t, east_t = tall(field)
            return west_t[0:rows], east_t[0:rows]

        w = wet_ref[r].astype(jnp.float32)
        w_above = level(wet_ref, r, -1).astype(jnp.float32)
        w_below = level(wet_ref, r, 1).astype(jnp.float32)
        w_wc, w_ec = col(4)
        w_e = east(w, w_ec)
        w_w = west(w, w_wc)
        w_n = north(w, row(0, 4))
        w_s = south(w, row(3, 4))
        w_ne = north(w_e, row(1, 4))
        w_se = south(w_e, row(4, 4))
        w_nw = north(w_w, row(2, 4))
        mask_east = w * w_e
        mask_west = w_w * w
        mask_north = w * w_n
        mask_south = w_s * w
        mix_below = jnp.where(
            k < levels - 1, w * w_below * (k + 1 < count).astype(jnp.float32), 0.0
        )
        mix_above = jnp.where(k > 0, w_above * w * (k < count).astype(jnp.float32), 0.0)
        bottom = (k == count - 1).astype(jnp.float32)

        def column(ref, centre):
            upper = level(ref, r, -1)
            lower = level(ref, r, 1)
            above = -vertical_diff * mix_above * (centre - upper)
            below = -vertical_diff * mix_below * (lower - centre)
            return above - below

        depth = (k.astype(jnp.float32) + 0.5) * level_depth

        def density(temper, saline):
            return (
                -thermal_expand * (1.0 + 0.5 * cabbel_temp * temper + thermo_temp * depth) * temper
                + haline_contract * (1.0 - 0.5 * cabbel_salt * saline - thermo_salt * depth) * saline
                - cabbel_mixed * temper * saline
            )

        tc = t_ref[r]
        sc = s_ref[r]
        t_wc, t_ec = col(2)
        s_wc, s_ec = col(3)
        pres = pres + w * density(tc, sc)
        pres_e = pres_e + w_ec * density(t_ec, s_ec)
        pres_n = pres_n + row(0, 4) * density(row(0, 2), row(0, 3))
        p_e = east(pres, pres_e)
        p_n = north(pres, pres_n)

        uc = u_ref[r]
        u_wc, u_ec = col(0)
        u_e = east(uc, u_ec)
        u_w = west(uc, u_wc)
        u_n = north(uc, row(0, 0))
        u_s = south(uc, row(3, 0))
        u_nw = north(u_w, row(2, 0))
        vc = v_ref[r]
        v_wc, v_ec = col(1)
        v_e = east(vc, v_ec)
        v_w = west(vc, v_wc)
        v_n = north(vc, row(0, 1))
        v_s = south(vc, row(3, 1))
        v_se = south(v_e, row(4, 1))

        def tracer(ref, centre, field, wcol, ecol):
            east_side = east(centre, ecol)
            west_side = west(centre, wcol)
            north_side = north(centre, row(0, field))
            south_side = south(centre, row(3, field))
            flux_east = mask_east * (
                uc * (centre + east_side) * 0.5 - lateral_diff * (east_side - centre)
            )
            flux_west = mask_west * (
                u_w * (west_side + centre) * 0.5 - lateral_diff * (centre - west_side)
            )
            flux_north = mask_north * (
                vc * (centre + north_side) * 0.5 - lateral_diff * (north_side - centre)
            )
            flux_south = mask_south * (
                v_s * (south_side + centre) * 0.5 - lateral_diff * (centre - south_side)
            )
            tendency = (
                flux_west - flux_east + (flux_south - flux_north) + column(ref, centre)
            )
            return w * (centre + time_step * tendency)

        temp_ref[r] = tracer(t_ref, tc, 2, t_wc, t_ec)
        salt_ref[r] = tracer(s_ref, sc, 3, s_wc, s_ec)

        corner_ne = w * w_e * w_n * w_ne
        corner_se = w_s * w_se * w * w_e
        corner_nw = w_w * w * w_nw * w_n
        half_e = (uc + u_e) * 0.5
        cell_east = w_e * (half_e * half_e - lateral_diff * (u_e - uc))
        half_w = (u_w + uc) * 0.5
        cell_west = w * (half_w * half_w - lateral_diff * (uc - u_w))
        product_ne = (vc + v_e) * 0.5 * (uc + u_n) * 0.5
        product_se = (v_s + v_se) * 0.5 * (u_s + uc) * 0.5
        product_nw = (u_w + u_nw) * 0.5 * (v_w + vc) * 0.5
        shear_north = corner_ne * (product_ne - lateral_diff * (u_n - uc))
        shear_south = corner_se * (product_se - lateral_diff * (uc - u_s))
        north_mean = (vc + v_e + v_s + v_se) * 0.25
        east_tend = (
            cell_west
            - cell_east
            + (shear_south - shear_north)
            + cor_t * north_mean
            - pressure_coef * (p_e - pres)
            + column(u_ref, uc)
            - drag_coef * bottom * uc
        )
        east_ref[r] = mask_east * (uc + time_step * east_tend)
        half_n = (vc + v_n) * 0.5
        cell_north = w_n * (half_n * half_n - lateral_diff * (v_n - vc))
        half_s = (v_s + vc) * 0.5
        cell_south = w * (half_s * half_s - lateral_diff * (vc - v_s))
        stress_east = corner_ne * (product_ne - lateral_diff * (v_e - vc))
        stress_west = corner_nw * (product_nw - lateral_diff * (vc - v_w))
        east_mean = (uc + u_w + u_n + u_nw) * 0.25
        north_tend = (
            stress_west
            - stress_east
            + (cell_south - cell_north)
            - cor_v * east_mean
            - pressure_coef * (p_n - pres)
            + column(v_ref, vc)
            - drag_coef * bottom * vc
        )
        north_ref[r] = mask_north * (vc + time_step * north_tend)
        return pres, pres_e, pres_n

    init = (p_ref[...], pe_ref[...], pn_ref[...])
    pres, pres_e, pres_n = lax.fori_loop(0, chunk, body, init)
    p_ref[...] = pres
    pe_ref[...] = pres_e
    pn_ref[...] = pres_n


def per_device(
    eastbound_current,
    poleward_current,
    warmth_excess,
    saltiness_excess,
    water_indicator,
    column_layer_count,
):
    inputs = (
        eastbound_current,
        poleward_current,
        warmth_excess,
        saltiness_excess,
        water_indicator,
    )

    levels, rows, cols = eastbound_current.shape
    fields = len(inputs)
    chunk = 8 if levels % 8 == 0 else levels
    row_block = pl.BlockSpec((fields, chunk, cols), lambda c: (0, c, 0))
    col_block = pl.BlockSpec((fields, rows, levels), lambda c: (0, 0, 0))
    tile = 8
    top, bottom = pl.pallas_call(
        row_kernel,
        grid=(levels // chunk,),
        in_specs=[pl.BlockSpec((chunk, tile, cols), lambda c: (c, 0, 0))] * fields
        + [pl.BlockSpec((chunk, tile, cols), lambda c: (c, rows // tile - 1, 0))] * fields,
        out_specs=(row_block, row_block),
        out_shape=(
            jax.ShapeDtypeStruct((fields, levels, cols), jnp.float32),
            jax.ShapeDtypeStruct((fields, levels, cols), jnp.float32),
        ),
    )(*inputs, *inputs)
    west_col, east_col = pl.pallas_call(
        edge_kernel,
        grid=(levels // chunk,),
        in_specs=[pl.BlockSpec((chunk, rows, cols), lambda c: (c, 0, 0))] * fields,
        out_specs=(col_block, col_block),
        out_shape=(
            jax.ShapeDtypeStruct((fields, rows, levels), jnp.float32),
            jax.ShapeDtypeStruct((fields, rows, levels), jnp.float32),
        ),
    )(*inputs)

    def east_of(a, b, na, nl):
        return (a, (b + 1) % nl)

    def west_of(a, b, na, nl):
        return (a, (b - 1) % nl)

    def north_of(a, b, na, nl):
        return (a + 1, b) if a + 1 < na else None

    def south_of(a, b, na, nl):
        return (a - 1, b) if a > 0 else None

    def mirror(a, b, na, nl):
        return (a, nl - 1 - b) if a == na - 1 else None

    halo_south = shift(top, north_of)
    halo_north = shift(bottom, south_of)
    fold_row = shift(top, mirror)
    sign = jnp.array([-1.0, -1.0, 1.0, 1.0, 1.0], dtype=jnp.float32)[:, None, None]
    is_top = lax.axis_index("lat") == lax.axis_size("lat") - 1
    halo_north = jnp.where(is_top, sign * fold_row[:, :, ::-1], halo_north)
    pad = jnp.zeros((fields, 6, levels), jnp.float32)
    west_tall = jnp.concatenate(
        [west_col, halo_south[:, None, :, 0], halo_north[:, None, :, 0], pad], axis=1
    )
    east_tall = jnp.concatenate(
        [east_col, halo_south[:, None, :, -1], halo_north[:, None, :, -1], pad], axis=1
    )
    halo_west = shift(east_tall, east_of)
    halo_east = shift(west_tall, west_of)

    row_start = lax.axis_index("lat") * rows
    total_rows = rows * lax.axis_size("lat")
    row_index = (row_start + jnp.arange(rows, dtype=jnp.int32)).astype(jnp.float32)[:, None]
    coriolis_t = coriolis_max * (2.0 * (row_index + 0.5) / total_rows - 1.0)
    coriolis_v = coriolis_max * (2.0 * (row_index + 1.0) / total_rows - 1.0)
    coriolis = jnp.broadcast_to(jnp.stack([coriolis_t, coriolis_v]), (2, rows, cols))

    block = jax.ShapeDtypeStruct((levels, rows, cols), jnp.float32)
    main = pl.BlockSpec((chunk, rows, cols), lambda c: (c, 0, 0))
    above = pl.BlockSpec((1, rows, cols), lambda c: (jnp.maximum(c * chunk - 1, 0), 0, 0))
    below = pl.BlockSpec(
        (1, rows, cols), lambda c: (jnp.minimum(c * chunk + chunk, levels - 1), 0, 0)
    )

    def whole(shape):
        return pl.BlockSpec(shape, lambda c: (0,) * len(shape))

    halo_row = pl.BlockSpec((fields, chunk, cols), lambda c: (0, c, 0))
    return pl.pallas_call(
        stencil_kernel,
        grid=(levels // chunk,),
        in_specs=[whole((2, rows, cols))]
        + [main] * fields
        + [above] * fields
        + [below] * fields
        + [whole((rows, cols)), halo_row, halo_row, whole(halo_west.shape), whole(halo_east.shape)],
        out_specs=(main, main, main, main),
        out_shape=(block, block, block, block),
        scratch_shapes=[
            pltpu.VMEM((rows, cols), jnp.float32),
            pltpu.VMEM((rows, cols), jnp.float32),
            pltpu.VMEM((1, cols), jnp.float32),
        ],
    )(
        coriolis,
        *inputs,
        *inputs,
        *inputs,
        column_layer_count,
        halo_north,
        halo_south,
        halo_west,
        halo_east,
    )


def solution(mesh):
    placed = (
        P(None, "lat", "lon"),
        P(None, "lat", "lon"),
        P(None, "lat", "lon"),
        P(None, "lat", "lon"),
        P(None, "lat", "lon"),
        P("lat", "lon"),
    )
    return jax.shard_map(
        per_device,
        mesh=mesh,
        in_specs=placed,
        out_specs=(
            P(None, "lat", "lon"),
            P(None, "lat", "lon"),
            P(None, "lat", "lon"),
            P(None, "lat", "lon"),
        ),
        check_vma=False,
    )
```

```python
import jax
import jax.numpy as jnp
from jax import lax
from jax.experimental import pallas as pl
from jax.experimental.pallas import tpu as pltpu
from jax.sharding import PartitionSpec as P

time_step = 0.2
lateral_diff = 0.1
vertical_diff = 0.5
pressure_coef = 0.1
drag_coef = 2.0
coriolis_max = 1.0
level_depth = 100.0
thermal_expand = 0.1655
haline_contract = 0.76554
cabbel_temp = 0.05952
cabbel_salt = 0.00054914
cabbel_mixed = 0.0024341
thermo_temp = 0.0001497
thermo_salt = 1.109e-05


def view_at(field, lat_step, lon_step):
    rows = field.shape[1] - 2
    cols = field.shape[2] - 2
    return field[:, 1 + lat_step : 1 + lat_step + rows, 1 + lon_step : 1 + lon_step + cols]


def column_flux(centre, mixing):
    between = -vertical_diff * mixing * (centre[1:] - centre[:-1])
    surface = jnp.zeros_like(centre[:1])
    above = jnp.concatenate([surface, between], axis=0)
    below = jnp.concatenate([between, surface], axis=0)
    return above - below


def advance(extended, column_layer_count, row_start, total_rows):
    eastward = extended[0]
    northward = extended[1]
    temper = extended[2]
    saline = extended[3]
    wet = extended[4]
    levels = extended.shape[1]
    rows = extended.shape[2] - 2
    level_index = jnp.arange(levels, dtype=jnp.int32)[:, None, None]
    wet_here = view_at(wet, 0, 0)
    mask_east = wet_here * view_at(wet, 0, 1)
    mask_west = view_at(wet, 0, -1) * wet_here
    mask_north = wet_here * view_at(wet, 1, 0)
    mask_south = view_at(wet, -1, 0) * wet_here
    mixing = (
        wet_here[:-1]
        * wet_here[1:]
        * (level_index[1:] < column_layer_count[None]).astype(jnp.float32)
    )
    bottom = (level_index == column_layer_count[None] - 1).astype(jnp.float32)
    depth = (level_index.astype(jnp.float32) + 0.5) * level_depth
    density = (
        -thermal_expand * (1.0 + 0.5 * cabbel_temp * temper + thermo_temp * depth) * temper
        + haline_contract * (1.0 - 0.5 * cabbel_salt * saline - thermo_salt * depth) * saline
        - cabbel_mixed * temper * saline
    )
    pressure = jnp.cumsum(wet * density, axis=0)
    row_index = (row_start + jnp.arange(rows, dtype=jnp.int32)).astype(jnp.float32)[None, :, None]
    coriolis_t = coriolis_max * (2.0 * (row_index + 0.5) / total_rows - 1.0)
    coriolis_v = coriolis_max * (2.0 * (row_index + 1.0) / total_rows - 1.0)

    def tracer(field):
        centre = view_at(field, 0, 0)
        east_side = view_at(field, 0, 1)
        west_side = view_at(field, 0, -1)
        north_side = view_at(field, 1, 0)
        south_side = view_at(field, -1, 0)
        flux_east = mask_east * (
            view_at(eastward, 0, 0) * (centre + east_side) * 0.5
            - lateral_diff * (east_side - centre)
        )
        flux_west = mask_west * (
            view_at(eastward, 0, -1) * (west_side + centre) * 0.5
            - lateral_diff * (centre - west_side)
        )
        flux_north = mask_north * (
            view_at(northward, 0, 0) * (centre + north_side) * 0.5
            - lateral_diff * (north_side - centre)
        )
        flux_south = mask_south * (
            view_at(northward, -1, 0) * (south_side + centre) * 0.5
            - lateral_diff * (centre - south_side)
        )
        tendency = flux_west - flux_east + (flux_south - flux_north) + column_flux(centre, mixing)
        return wet_here * (centre + time_step * tendency)

    east_here = view_at(eastward, 0, 0)
    north_here = view_at(northward, 0, 0)
    corner_ne = wet_here * view_at(wet, 0, 1) * view_at(wet, 1, 0) * view_at(wet, 1, 1)
    corner_se = view_at(wet, -1, 0) * view_at(wet, -1, 1) * wet_here * view_at(wet, 0, 1)
    corner_nw = view_at(wet, 0, -1) * wet_here * view_at(wet, 1, -1) * view_at(wet, 1, 0)
    cell_east = view_at(wet, 0, 1) * (
        ((east_here + view_at(eastward, 0, 1)) * 0.5) ** 2
        - lateral_diff * (view_at(eastward, 0, 1) - east_here)
    )
    cell_west = wet_here * (
        ((view_at(eastward, 0, -1) + east_here) * 0.5) ** 2
        - lateral_diff * (east_here - view_at(eastward, 0, -1))
    )
    product_ne = (
        (north_here + view_at(northward, 0, 1)) * 0.5 * (east_here + view_at(eastward, 1, 0)) * 0.5
    )
    product_se = (
        (view_at(northward, -1, 0) + view_at(northward, -1, 1))
        * 0.5
        * (view_at(eastward, -1, 0) + east_here)
        * 0.5
    )
    product_nw = (
        (view_at(eastward, 0, -1) + view_at(eastward, 1, -1))
        * 0.5
        * (view_at(northward, 0, -1) + north_here)
        * 0.5
    )
    shear_north = corner_ne * (product_ne - lateral_diff * (view_at(eastward, 1, 0) - east_here))
    shear_south = corner_se * (product_se - lateral_diff * (east_here - view_at(eastward, -1, 0)))
    north_mean = (
        north_here
        + view_at(northward, 0, 1)
        + view_at(northward, -1, 0)
        + view_at(northward, -1, 1)
    ) * 0.25
    east_tend = (
        cell_west
        - cell_east
        + (shear_south - shear_north)
        + coriolis_t * north_mean
        - pressure_coef * (view_at(pressure, 0, 1) - view_at(pressure, 0, 0))
        + column_flux(east_here, mixing)
        - drag_coef * bottom * east_here
    )
    east_next = mask_east * (east_here + time_step * east_tend)
    cell_north = view_at(wet, 1, 0) * (
        ((north_here + view_at(northward, 1, 0)) * 0.5) ** 2
        - lateral_diff * (view_at(northward, 1, 0) - north_here)
    )
    cell_south = wet_here * (
        ((view_at(northward, -1, 0) + north_here) * 0.5) ** 2
        - lateral_diff * (north_here - view_at(northward, -1, 0))
    )
    stress_east = corner_ne * (product_ne - lateral_diff * (view_at(northward, 0, 1) - north_here))
    stress_west = corner_nw * (product_nw - lateral_diff * (north_here - view_at(northward, 0, -1)))
    east_mean = (
        east_here + view_at(eastward, 0, -1) + view_at(eastward, 1, 0) + view_at(eastward, 1, -1)
    ) * 0.25
    north_tend = (
        stress_west
        - stress_east
        + (cell_south - cell_north)
        - coriolis_v * east_mean
        - pressure_coef * (view_at(pressure, 1, 0) - view_at(pressure, 0, 0))
        + column_flux(north_here, mixing)
        - drag_coef * bottom * north_here
    )
    north_next = mask_north * (north_here + time_step * north_tend)
    return (east_next, north_next, tracer(temper), tracer(saline))


def shift(value, mapping):
    lat_size = lax.axis_size("lat")
    lon_size = lax.axis_size("lon")
    pairs = []
    for a in range(lat_size):
        for b in range(lon_size):
            target = mapping(a, b, lat_size, lon_size)
            if target is not None:
                pairs.append((b * lat_size + a, target[1] * lat_size + target[0]))
    return lax.ppermute(value, ("lon", "lat"), pairs)


def row_kernel(*refs):
    fields = (len(refs) - 2) // 2
    lows = refs[:fields]
    highs = refs[fields : 2 * fields]
    top_ref, bottom_ref = refs[2 * fields :]
    chunk, tile, cols = lows[0].shape
    for field in range(fields):
        for r in range(chunk):
            top_ref[field, r : r + 1, :] = highs[field][r][tile - 1 : tile, :].astype(jnp.float32)
            bottom_ref[field, r : r + 1, :] = lows[field][r][0:1, :].astype(jnp.float32)


def edge_kernel(*refs):
    fields = len(refs) - 2
    sources = refs[:fields]
    west_ref, east_ref = refs[fields:]
    chunk, rows, cols = sources[0].shape
    levels = west_ref.shape[2]
    step = pl.program_id(0)
    lane = lax.broadcasted_iota(jnp.int32, (rows, levels), 1)

    @pl.when(step == 0)
    def _():
        west_ref[...] = jnp.zeros(west_ref.shape, jnp.float32)
        east_ref[...] = jnp.zeros(east_ref.shape, jnp.float32)

    for field, source in enumerate(sources):
        west = west_ref[field]
        east = east_ref[field]
        for r in range(chunk):
            x = source[r].astype(jnp.float32)
            here = lane == step * chunk + r
            west = jnp.where(here, x[:, 0:1], west)
            east = jnp.where(here, x[:, cols - 1 : cols], east)
        west_ref[field] = west
        east_ref[field] = east


def stencil_kernel(
    cor_ref, u_ref, v_ref, t_ref, s_ref, wet_ref, ua_ref, va_ref, ta_ref, sa_ref, wa_ref,
    ub_ref, vb_ref, tb_ref, sb_ref, wb_ref, clc_ref, rn_ref, rs_ref, tw_ref, te_ref,
    east_ref, north_ref, temp_ref, salt_ref, p_ref, pe_ref, pn_ref,
):
    chunk, rows, cols = u_ref.shape
    levels = tw_ref.shape[2]
    step = pl.program_id(0)
    near = {
        id(u_ref): (ua_ref, ub_ref),
        id(v_ref): (va_ref, vb_ref),
        id(t_ref): (ta_ref, tb_ref),
        id(s_ref): (sa_ref, sb_ref),
        id(wet_ref): (wa_ref, wb_ref),
    }

    def level(ref, r, offset):
        above, below = near[id(ref)]
        if offset < 0:
            return jnp.where(r == 0, above[0], ref[jnp.maximum(r - 1, 0)])
        return jnp.where(r == chunk - 1, below[0], ref[jnp.minimum(r + 1, chunk - 1)])

    @pl.when(step == 0)
    def _():
        p_ref[...] = jnp.zeros(p_ref.shape, jnp.float32)
        pe_ref[...] = jnp.zeros(pe_ref.shape, jnp.float32)
        pn_ref[...] = jnp.zeros(pn_ref.shape, jnp.float32)

    fields = 5
    lane = lax.broadcasted_iota(jnp.int32, (rows, cols), 1)
    sub = lax.broadcasted_iota(jnp.int32, (rows, cols), 0)
    at_east = lane == cols - 1
    at_west = lane == 0
    at_north = sub == rows - 1
    at_south = sub == 0
    row_lane = lax.broadcasted_iota(jnp.int32, (1, cols), 1)
    row_east = row_lane == cols - 1
    row_west = row_lane == 0
    pick_lane = lax.broadcasted_iota(jnp.int32, tw_ref.shape[1:], 1)
    cor_t = cor_ref[0]
    cor_v = cor_ref[1]
    count = clc_ref[...]

    def east(x, col):
        return jnp.where(at_east, col, pltpu.roll(x, cols - 1, 1))

    def west(x, col):
        return jnp.where(at_west, col, pltpu.roll(x, 1, 1))

    def north(x, row):
        return jnp.where(at_north, row, pltpu.roll(x, rows - 1, 0))

    def south(x, row):
        return jnp.where(at_south, row, pltpu.roll(x, 1, 0))

    def body(r, carry):
        pres, pres_e, pres_n = carry
        k = step * chunk + r

        spread = {}

        def tall(field):
            if field not in spread:
                spread[field] = tuple(
                    jnp.broadcast_to(
                        jnp.sum(jnp.where(pick_lane == k, ref[field], 0.0), axis=1, keepdims=True),
                        (ref.shape[1], cols),
                    )
                    for ref in (tw_ref, te_ref)
                )
            return spread[field]

        def row(variant, field):
            west_t, east_t = tall(field)
            if variant == 0:
                return rn_ref[field, pl.ds(r, 1), :]
            if variant == 3:
                return rs_ref[field, pl.ds(r, 1), :]
            if variant == 1:
                return jnp.where(row_east, east_t[rows + 1 : rows + 2], pltpu.roll(row(0, field), cols - 1, 1))
            if variant == 2:
                return jnp.where(row_west, west_t[rows + 1 : rows + 2], pltpu.roll(row(0, field), 1, 1))
            return jnp.where(row_east, east_t[rows : rows + 1], pltpu.roll(row(3, field), cols - 1, 1))

        def col(field):
            west_t, east_t = tall(field)
            return west_t[0:rows], east_t[0:rows]

        w = wet_ref[r].astype(jnp.float32)
        w_above = level(wet_ref, r, -1).astype(jnp.float32)
        w_below = level(wet_ref, r, 1).astype(jnp.float32)
        w_wc, w_ec = col(4)
        w_e = east(w, w_ec)
        w_w = west(w, w_wc)
        w_n = north(w, row(0, 4))
        w_s = south(w, row(3, 4))
        w_ne = north(w_e, row(1, 4))
        w_se = south(w_e, row(4, 4))
        w_nw = north(w_w, row(2, 4))
        mask_east = w * w_e
        mask_west = w_w * w
        mask_north = w * w_n
        mask_south = w_s * w
        mix_below = jnp.where(
            k < levels - 1, w * w_below * (k + 1 < count).astype(jnp.float32), 0.0
        )
        mix_above = jnp.where(k > 0, w_above * w * (k < count).astype(jnp.float32), 0.0)
        bottom = (k == count - 1).astype(jnp.float32)

        def column(ref, centre):
            upper = level(ref, r, -1)
            lower = level(ref, r, 1)
            above = -vertical_diff * mix_above * (centre - upper)
            below = -vertical_diff * mix_below * (lower - centre)
            return above - below

        depth = (k.astype(jnp.float32) + 0.5) * level_depth

        def density(temper, saline):
            return (
                -thermal_expand * (1.0 + 0.5 * cabbel_temp * temper + thermo_temp * depth) * temper
                + haline_contract * (1.0 - 0.5 * cabbel_salt * saline - thermo_salt * depth) * saline
                - cabbel_mixed * temper * saline
            )

        tc = t_ref[r]
        sc = s_ref[r]
        t_wc, t_ec = col(2)
        s_wc, s_ec = col(3)
        pres = pres + w * density(tc, sc)
        pres_e = pres_e + w_ec * density(t_ec, s_ec)
        pres_n = pres_n + row(0, 4) * density(row(0, 2), row(0, 3))
        p_e = east(pres, pres_e)
        p_n = north(pres, pres_n)

        uc = u_ref[r]
        u_wc, u_ec = col(0)
        u_e = east(uc, u_ec)
        u_w = west(uc, u_wc)
        u_n = north(uc, row(0, 0))
        u_s = south(uc, row(3, 0))
        u_nw = north(u_w, row(2, 0))
        vc = v_ref[r]
        v_wc, v_ec = col(1)
        v_e = east(vc, v_ec)
        v_w = west(vc, v_wc)
        v_n = north(vc, row(0, 1))
        v_s = south(vc, row(3, 1))
        v_se = south(v_e, row(4, 1))

        def tracer(ref, centre, field, wcol, ecol):
            east_side = east(centre, ecol)
            west_side = west(centre, wcol)
            north_side = north(centre, row(0, field))
            south_side = south(centre, row(3, field))
            flux_east = mask_east * (
                uc * (centre + east_side) * 0.5 - lateral_diff * (east_side - centre)
            )
            flux_west = mask_west * (
                u_w * (west_side + centre) * 0.5 - lateral_diff * (centre - west_side)
            )
            flux_north = mask_north * (
                vc * (centre + north_side) * 0.5 - lateral_diff * (north_side - centre)
            )
            flux_south = mask_south * (
                v_s * (south_side + centre) * 0.5 - lateral_diff * (centre - south_side)
            )
            tendency = (
                flux_west - flux_east + (flux_south - flux_north) + column(ref, centre)
            )
            return w * (centre + time_step * tendency)

        temp_ref[r] = tracer(t_ref, tc, 2, t_wc, t_ec)
        salt_ref[r] = tracer(s_ref, sc, 3, s_wc, s_ec)

        corner_ne = w * w_e * w_n * w_ne
        corner_se = w_s * w_se * w * w_e
        corner_nw = w_w * w * w_nw * w_n
        half_e = (uc + u_e) * 0.5
        cell_east = w_e * (half_e * half_e - lateral_diff * (u_e - uc))
        half_w = (u_w + uc) * 0.5
        cell_west = w * (half_w * half_w - lateral_diff * (uc - u_w))
        product_ne = (vc + v_e) * 0.5 * (uc + u_n) * 0.5
        product_se = (v_s + v_se) * 0.5 * (u_s + uc) * 0.5
        product_nw = (u_w + u_nw) * 0.5 * (v_w + vc) * 0.5
        shear_north = corner_ne * (product_ne - lateral_diff * (u_n - uc))
        shear_south = corner_se * (product_se - lateral_diff * (uc - u_s))
        north_mean = (vc + v_e + v_s + v_se) * 0.25
        east_tend = (
            cell_west
            - cell_east
            + (shear_south - shear_north)
            + cor_t * north_mean
            - pressure_coef * (p_e - pres)
            + column(u_ref, uc)
            - drag_coef * bottom * uc
        )
        east_ref[r] = mask_east * (uc + time_step * east_tend)
        half_n = (vc + v_n) * 0.5
        cell_north = w_n * (half_n * half_n - lateral_diff * (v_n - vc))
        half_s = (v_s + vc) * 0.5
        cell_south = w * (half_s * half_s - lateral_diff * (vc - v_s))
        stress_east = corner_ne * (product_ne - lateral_diff * (v_e - vc))
        stress_west = corner_nw * (product_nw - lateral_diff * (vc - v_w))
        east_mean = (uc + u_w + u_n + u_nw) * 0.25
        north_tend = (
            stress_west
            - stress_east
            + (cell_south - cell_north)
            - cor_v * east_mean
            - pressure_coef * (p_n - pres)
            + column(v_ref, vc)
            - drag_coef * bottom * vc
        )
        north_ref[r] = mask_north * (vc + time_step * north_tend)
        return pres, pres_e, pres_n

    init = (p_ref[...], pe_ref[...], pn_ref[...])
    pres, pres_e, pres_n = lax.fori_loop(0, chunk, body, init)
    p_ref[...] = pres
    pe_ref[...] = pres_e
    pn_ref[...] = pres_n


def per_device(
    eastbound_current,
    poleward_current,
    warmth_excess,
    saltiness_excess,
    water_indicator,
    column_layer_count,
):
    inputs = (
        eastbound_current,
        poleward_current,
        warmth_excess,
        saltiness_excess,
        water_indicator,
    )

    levels, rows, cols = eastbound_current.shape
    fields = len(inputs)
    chunk = 8 if levels % 8 == 0 else levels
    row_block = pl.BlockSpec((fields, chunk, cols), lambda c: (0, c, 0))
    col_block = pl.BlockSpec((fields, rows, levels), lambda c: (0, 0, 0))
    tile = 8
    top, bottom = pl.pallas_call(
        row_kernel,
        grid=(1,),
        in_specs=[pl.BlockSpec((levels, tile, cols), lambda c: (0, 0, 0))] * fields
        + [pl.BlockSpec((levels, tile, cols), lambda c: (0, rows // tile - 1, 0))] * fields,
        out_specs=(
            pl.BlockSpec((fields, levels, cols), lambda c: (0, 0, 0)),
            pl.BlockSpec((fields, levels, cols), lambda c: (0, 0, 0)),
        ),
        out_shape=(
            jax.ShapeDtypeStruct((fields, levels, cols), jnp.float32),
            jax.ShapeDtypeStruct((fields, levels, cols), jnp.float32),
        ),
    )(*inputs, *inputs)
    west_col, east_col = pl.pallas_call(
        edge_kernel,
        grid=(levels // chunk,),
        in_specs=[pl.BlockSpec((chunk, rows, cols), lambda c: (c, 0, 0))] * fields,
        out_specs=(col_block, col_block),
        out_shape=(
            jax.ShapeDtypeStruct((fields, rows, levels), jnp.float32),
            jax.ShapeDtypeStruct((fields, rows, levels), jnp.float32),
        ),
    )(*inputs)

    def east_of(a, b, na, nl):
        return (a, (b + 1) % nl)

    def west_of(a, b, na, nl):
        return (a, (b - 1) % nl)

    def north_of(a, b, na, nl):
        return (a + 1, b) if a + 1 < na else None

    def south_of(a, b, na, nl):
        return (a - 1, b) if a > 0 else None

    def mirror(a, b, na, nl):
        return (a, nl - 1 - b) if a == na - 1 else None

    halo_south = shift(top, north_of)
    halo_north = shift(bottom, south_of)
    fold_row = shift(top, mirror)
    sign = jnp.array([-1.0, -1.0, 1.0, 1.0, 1.0], dtype=jnp.float32)[:, None, None]
    is_top = lax.axis_index("lat") == lax.axis_size("lat") - 1
    halo_north = jnp.where(is_top, sign * fold_row[:, :, ::-1], halo_north)
    pad = jnp.zeros((fields, 6, levels), jnp.float32)
    west_tall = jnp.concatenate(
        [west_col, halo_south[:, None, :, 0], halo_north[:, None, :, 0], pad], axis=1
    )
    east_tall = jnp.concatenate(
        [east_col, halo_south[:, None, :, -1], halo_north[:, None, :, -1], pad], axis=1
    )
    halo_west = shift(east_tall, east_of)
    halo_east = shift(west_tall, west_of)

    row_start = lax.axis_index("lat") * rows
    total_rows = rows * lax.axis_size("lat")
    row_index = (row_start + jnp.arange(rows, dtype=jnp.int32)).astype(jnp.float32)[:, None]
    coriolis_t = coriolis_max * (2.0 * (row_index + 0.5) / total_rows - 1.0)
    coriolis_v = coriolis_max * (2.0 * (row_index + 1.0) / total_rows - 1.0)
    coriolis = jnp.broadcast_to(jnp.stack([coriolis_t, coriolis_v]), (2, rows, cols))

    block = jax.ShapeDtypeStruct((levels, rows, cols), jnp.float32)
    main = pl.BlockSpec((chunk, rows, cols), lambda c: (c, 0, 0))
    above = pl.BlockSpec((1, rows, cols), lambda c: (jnp.maximum(c * chunk - 1, 0), 0, 0))
    below = pl.BlockSpec(
        (1, rows, cols), lambda c: (jnp.minimum(c * chunk + chunk, levels - 1), 0, 0)
    )

    def whole(shape):
        return pl.BlockSpec(shape, lambda c: (0,) * len(shape))

    halo_row = pl.BlockSpec((fields, chunk, cols), lambda c: (0, c, 0))
    return pl.pallas_call(
        stencil_kernel,
        grid=(levels // chunk,),
        in_specs=[whole((2, rows, cols))]
        + [main] * fields
        + [above] * fields
        + [below] * fields
        + [whole((rows, cols)), halo_row, halo_row, whole(halo_west.shape), whole(halo_east.shape)],
        out_specs=(main, main, main, main),
        out_shape=(block, block, block, block),
        scratch_shapes=[
            pltpu.VMEM((rows, cols), jnp.float32),
            pltpu.VMEM((rows, cols), jnp.float32),
            pltpu.VMEM((1, cols), jnp.float32),
        ],
    )(
        coriolis,
        *inputs,
        *inputs,
        *inputs,
        column_layer_count,
        halo_north,
        halo_south,
        halo_west,
        halo_east,
    )


def solution(mesh):
    placed = (
        P(None, "lat", "lon"),
        P(None, "lat", "lon"),
        P(None, "lat", "lon"),
        P(None, "lat", "lon"),
        P(None, "lat", "lon"),
        P("lat", "lon"),
    )
    return jax.shard_map(
        per_device,
        mesh=mesh,
        in_specs=placed,
        out_specs=(
            P(None, "lat", "lon"),
            P(None, "lat", "lon"),
            P(None, "lat", "lon"),
            P(None, "lat", "lon"),
        ),
        check_vma=False,
    )
```

```python
import jax
import jax.numpy as jnp
from jax import lax
from jax.experimental import pallas as pl
from jax.experimental.pallas import tpu as pltpu
from jax.sharding import PartitionSpec as P

time_step = 0.2
lateral_diff = 0.1
vertical_diff = 0.5
pressure_coef = 0.1
drag_coef = 2.0
coriolis_max = 1.0
level_depth = 100.0
thermal_expand = 0.1655
haline_contract = 0.76554
cabbel_temp = 0.05952
cabbel_salt = 0.00054914
cabbel_mixed = 0.0024341
thermo_temp = 0.0001497
thermo_salt = 1.109e-05


def view_at(field, lat_step, lon_step):
    rows = field.shape[1] - 2
    cols = field.shape[2] - 2
    return field[:, 1 + lat_step : 1 + lat_step + rows, 1 + lon_step : 1 + lon_step + cols]


def column_flux(centre, mixing):
    between = -vertical_diff * mixing * (centre[1:] - centre[:-1])
    surface = jnp.zeros_like(centre[:1])
    above = jnp.concatenate([surface, between], axis=0)
    below = jnp.concatenate([between, surface], axis=0)
    return above - below


def advance(extended, column_layer_count, row_start, total_rows):
    eastward = extended[0]
    northward = extended[1]
    temper = extended[2]
    saline = extended[3]
    wet = extended[4]
    levels = extended.shape[1]
    rows = extended.shape[2] - 2
    level_index = jnp.arange(levels, dtype=jnp.int32)[:, None, None]
    wet_here = view_at(wet, 0, 0)
    mask_east = wet_here * view_at(wet, 0, 1)
    mask_west = view_at(wet, 0, -1) * wet_here
    mask_north = wet_here * view_at(wet, 1, 0)
    mask_south = view_at(wet, -1, 0) * wet_here
    mixing = (
        wet_here[:-1]
        * wet_here[1:]
        * (level_index[1:] < column_layer_count[None]).astype(jnp.float32)
    )
    bottom = (level_index == column_layer_count[None] - 1).astype(jnp.float32)
    depth = (level_index.astype(jnp.float32) + 0.5) * level_depth
    density = (
        -thermal_expand * (1.0 + 0.5 * cabbel_temp * temper + thermo_temp * depth) * temper
        + haline_contract * (1.0 - 0.5 * cabbel_salt * saline - thermo_salt * depth) * saline
        - cabbel_mixed * temper * saline
    )
    pressure = jnp.cumsum(wet * density, axis=0)
    row_index = (row_start + jnp.arange(rows, dtype=jnp.int32)).astype(jnp.float32)[None, :, None]
    coriolis_t = coriolis_max * (2.0 * (row_index + 0.5) / total_rows - 1.0)
    coriolis_v = coriolis_max * (2.0 * (row_index + 1.0) / total_rows - 1.0)

    def tracer(field):
        centre = view_at(field, 0, 0)
        east_side = view_at(field, 0, 1)
        west_side = view_at(field, 0, -1)
        north_side = view_at(field, 1, 0)
        south_side = view_at(field, -1, 0)
        flux_east = mask_east * (
            view_at(eastward, 0, 0) * (centre + east_side) * 0.5
            - lateral_diff * (east_side - centre)
        )
        flux_west = mask_west * (
            view_at(eastward, 0, -1) * (west_side + centre) * 0.5
            - lateral_diff * (centre - west_side)
        )
        flux_north = mask_north * (
            view_at(northward, 0, 0) * (centre + north_side) * 0.5
            - lateral_diff * (north_side - centre)
        )
        flux_south = mask_south * (
            view_at(northward, -1, 0) * (south_side + centre) * 0.5
            - lateral_diff * (centre - south_side)
        )
        tendency = flux_west - flux_east + (flux_south - flux_north) + column_flux(centre, mixing)
        return wet_here * (centre + time_step * tendency)

    east_here = view_at(eastward, 0, 0)
    north_here = view_at(northward, 0, 0)
    corner_ne = wet_here * view_at(wet, 0, 1) * view_at(wet, 1, 0) * view_at(wet, 1, 1)
    corner_se = view_at(wet, -1, 0) * view_at(wet, -1, 1) * wet_here * view_at(wet, 0, 1)
    corner_nw = view_at(wet, 0, -1) * wet_here * view_at(wet, 1, -1) * view_at(wet, 1, 0)
    cell_east = view_at(wet, 0, 1) * (
        ((east_here + view_at(eastward, 0, 1)) * 0.5) ** 2
        - lateral_diff * (view_at(eastward, 0, 1) - east_here)
    )
    cell_west = wet_here * (
        ((view_at(eastward, 0, -1) + east_here) * 0.5) ** 2
        - lateral_diff * (east_here - view_at(eastward, 0, -1))
    )
    product_ne = (
        (north_here + view_at(northward, 0, 1)) * 0.5 * (east_here + view_at(eastward, 1, 0)) * 0.5
    )
    product_se = (
        (view_at(northward, -1, 0) + view_at(northward, -1, 1))
        * 0.5
        * (view_at(eastward, -1, 0) + east_here)
        * 0.5
    )
    product_nw = (
        (view_at(eastward, 0, -1) + view_at(eastward, 1, -1))
        * 0.5
        * (view_at(northward, 0, -1) + north_here)
        * 0.5
    )
    shear_north = corner_ne * (product_ne - lateral_diff * (view_at(eastward, 1, 0) - east_here))
    shear_south = corner_se * (product_se - lateral_diff * (east_here - view_at(eastward, -1, 0)))
    north_mean = (
        north_here
        + view_at(northward, 0, 1)
        + view_at(northward, -1, 0)
        + view_at(northward, -1, 1)
    ) * 0.25
    east_tend = (
        cell_west
        - cell_east
        + (shear_south - shear_north)
        + coriolis_t * north_mean
        - pressure_coef * (view_at(pressure, 0, 1) - view_at(pressure, 0, 0))
        + column_flux(east_here, mixing)
        - drag_coef * bottom * east_here
    )
    east_next = mask_east * (east_here + time_step * east_tend)
    cell_north = view_at(wet, 1, 0) * (
        ((north_here + view_at(northward, 1, 0)) * 0.5) ** 2
        - lateral_diff * (view_at(northward, 1, 0) - north_here)
    )
    cell_south = wet_here * (
        ((view_at(northward, -1, 0) + north_here) * 0.5) ** 2
        - lateral_diff * (north_here - view_at(northward, -1, 0))
    )
    stress_east = corner_ne * (product_ne - lateral_diff * (view_at(northward, 0, 1) - north_here))
    stress_west = corner_nw * (product_nw - lateral_diff * (north_here - view_at(northward, 0, -1)))
    east_mean = (
        east_here + view_at(eastward, 0, -1) + view_at(eastward, 1, 0) + view_at(eastward, 1, -1)
    ) * 0.25
    north_tend = (
        stress_west
        - stress_east
        + (cell_south - cell_north)
        - coriolis_v * east_mean
        - pressure_coef * (view_at(pressure, 1, 0) - view_at(pressure, 0, 0))
        + column_flux(north_here, mixing)
        - drag_coef * bottom * north_here
    )
    north_next = mask_north * (north_here + time_step * north_tend)
    return (east_next, north_next, tracer(temper), tracer(saline))


def shift(value, mapping):
    lat_size = lax.axis_size("lat")
    lon_size = lax.axis_size("lon")
    pairs = []
    for a in range(lat_size):
        for b in range(lon_size):
            target = mapping(a, b, lat_size, lon_size)
            if target is not None:
                pairs.append((b * lat_size + a, target[1] * lat_size + target[0]))
    return lax.ppermute(value, ("lon", "lat"), pairs)


def row_kernel(*refs):
    fields = (len(refs) - 2) // 2
    lows = refs[:fields]
    highs = refs[fields : 2 * fields]
    top_ref, bottom_ref = refs[2 * fields :]
    chunk, tile, cols = lows[0].shape
    for field in range(fields):
        for r in range(chunk):
            top_ref[field, r : r + 1, :] = highs[field][r][tile - 1 : tile, :].astype(jnp.float32)
            bottom_ref[field, r : r + 1, :] = lows[field][r][0:1, :].astype(jnp.float32)


def edge_kernel(*refs):
    fields = len(refs) - 2
    sources = refs[:fields]
    west_ref, east_ref = refs[fields:]
    chunk, rows, cols = sources[0].shape
    levels = west_ref.shape[2]
    step = pl.program_id(0)
    lane = lax.broadcasted_iota(jnp.int32, (rows, levels), 1)

    @pl.when(step == 0)
    def _():
        west_ref[...] = jnp.zeros(west_ref.shape, jnp.float32)
        east_ref[...] = jnp.zeros(east_ref.shape, jnp.float32)

    for field, source in enumerate(sources):
        west = west_ref[field]
        east = east_ref[field]
        for r in range(chunk):
            x = source[r].astype(jnp.float32)
            here = lane == step * chunk + r
            west = jnp.where(here, x[:, 0:1], west)
            east = jnp.where(here, x[:, cols - 1 : cols], east)
        west_ref[field] = west
        east_ref[field] = east


def stencil_kernel(
    top_ref, cor_ref, u_ref, v_ref, t_ref, s_ref, wet_ref, ua_ref, va_ref, ta_ref, sa_ref, wa_ref,
    ub_ref, vb_ref, tb_ref, sb_ref, wb_ref, clc_ref, hn_ref, fold_ref, rs_ref, tw_ref, te_ref,
    east_ref, north_ref, temp_ref, salt_ref, p_ref, pe_ref, pn_ref, rn_ref,
):
    chunk, rows, cols = u_ref.shape
    levels = tw_ref.shape[2]
    step = pl.program_id(0)
    near = {
        id(u_ref): (ua_ref, ub_ref),
        id(v_ref): (va_ref, vb_ref),
        id(t_ref): (ta_ref, tb_ref),
        id(s_ref): (sa_ref, sb_ref),
        id(wet_ref): (wa_ref, wb_ref),
    }

    def level(ref, r, offset):
        above, below = near[id(ref)]
        if offset < 0:
            return jnp.where(r == 0, above[0], ref[jnp.maximum(r - 1, 0)])
        return jnp.where(r == chunk - 1, below[0], ref[jnp.minimum(r + 1, chunk - 1)])

    @pl.when(step == 0)
    def _():
        p_ref[...] = jnp.zeros(p_ref.shape, jnp.float32)
        pe_ref[...] = jnp.zeros(pe_ref.shape, jnp.float32)
        pn_ref[...] = jnp.zeros(pn_ref.shape, jnp.float32)

    fields = 5
    lane = lax.broadcasted_iota(jnp.int32, (rows, cols), 1)
    sub = lax.broadcasted_iota(jnp.int32, (rows, cols), 0)
    at_east = lane == cols - 1
    at_west = lane == 0
    at_north = sub == rows - 1
    at_south = sub == 0
    row_lane = lax.broadcasted_iota(jnp.int32, (1, cols), 1)
    row_east = row_lane == cols - 1
    row_west = row_lane == 0
    pick_lane = lax.broadcasted_iota(jnp.int32, tw_ref.shape[1:], 1)
    flip = (
        lax.broadcasted_iota(jnp.int32, (cols, cols), 0)
        + lax.broadcasted_iota(jnp.int32, (cols, cols), 1)
        == cols - 1
    ).astype(jnp.float32)
    for field in range(rn_ref.shape[0]):
        mirrored = jnp.dot(
            fold_ref[field],
            flip,
            precision=lax.Precision.HIGHEST,
            preferred_element_type=jnp.float32,
        )
        sign = -1.0 if field < 2 else 1.0
        rn_ref[field] = jnp.where(top_ref[0] == 1, sign * mirrored, hn_ref[field])
    cor_t = cor_ref[0]
    cor_v = cor_ref[1]
    count = clc_ref[...]

    def east(x, col):
        return jnp.where(at_east, col, pltpu.roll(x, cols - 1, 1))

    def west(x, col):
        return jnp.where(at_west, col, pltpu.roll(x, 1, 1))

    def north(x, row):
        return jnp.where(at_north, row, pltpu.roll(x, rows - 1, 0))

    def south(x, row):
        return jnp.where(at_south, row, pltpu.roll(x, 1, 0))

    def body(r, carry):
        pres, pres_e, pres_n = carry
        k = step * chunk + r

        spread = {}

        def tall(field):
            if field not in spread:
                spread[field] = tuple(
                    jnp.broadcast_to(
                        jnp.sum(jnp.where(pick_lane == k, ref[field], 0.0), axis=1, keepdims=True),
                        (ref.shape[1], cols),
                    )
                    for ref in (tw_ref, te_ref)
                )
            return spread[field]

        def row(variant, field):
            west_t, east_t = tall(field)
            if variant == 0:
                return rn_ref[field, pl.ds(r, 1), :]
            if variant == 3:
                return rs_ref[field, pl.ds(r, 1), :]
            if variant == 1:
                return jnp.where(row_east, east_t[rows + 1 : rows + 2], pltpu.roll(row(0, field), cols - 1, 1))
            if variant == 2:
                return jnp.where(row_west, west_t[rows + 1 : rows + 2], pltpu.roll(row(0, field), 1, 1))
            return jnp.where(row_east, east_t[rows : rows + 1], pltpu.roll(row(3, field), cols - 1, 1))

        def col(field):
            west_t, east_t = tall(field)
            return west_t[0:rows], east_t[0:rows]

        w = wet_ref[r].astype(jnp.float32)
        w_above = level(wet_ref, r, -1).astype(jnp.float32)
        w_below = level(wet_ref, r, 1).astype(jnp.float32)
        w_wc, w_ec = col(4)
        w_e = east(w, w_ec)
        w_w = west(w, w_wc)
        w_n = north(w, row(0, 4))
        w_s = south(w, row(3, 4))
        w_ne = north(w_e, row(1, 4))
        w_se = south(w_e, row(4, 4))
        w_nw = north(w_w, row(2, 4))
        mask_east = w * w_e
        mask_west = w_w * w
        mask_north = w * w_n
        mask_south = w_s * w
        mix_below = jnp.where(
            k < levels - 1, w * w_below * (k + 1 < count).astype(jnp.float32), 0.0
        )
        mix_above = jnp.where(k > 0, w_above * w * (k < count).astype(jnp.float32), 0.0)
        bottom = (k == count - 1).astype(jnp.float32)

        def column(ref, centre):
            upper = level(ref, r, -1)
            lower = level(ref, r, 1)
            above = -vertical_diff * mix_above * (centre - upper)
            below = -vertical_diff * mix_below * (lower - centre)
            return above - below

        depth = (k.astype(jnp.float32) + 0.5) * level_depth

        def density(temper, saline):
            return (
                -thermal_expand * (1.0 + 0.5 * cabbel_temp * temper + thermo_temp * depth) * temper
                + haline_contract * (1.0 - 0.5 * cabbel_salt * saline - thermo_salt * depth) * saline
                - cabbel_mixed * temper * saline
            )

        tc = t_ref[r]
        sc = s_ref[r]
        t_wc, t_ec = col(2)
        s_wc, s_ec = col(3)
        pres = pres + w * density(tc, sc)
        pres_e = pres_e + w_ec * density(t_ec, s_ec)
        pres_n = pres_n + row(0, 4) * density(row(0, 2), row(0, 3))
        p_e = east(pres, pres_e)
        p_n = north(pres, pres_n)

        uc = u_ref[r]
        u_wc, u_ec = col(0)
        u_e = east(uc, u_ec)
        u_w = west(uc, u_wc)
        u_n = north(uc, row(0, 0))
        u_s = south(uc, row(3, 0))
        u_nw = north(u_w, row(2, 0))
        vc = v_ref[r]
        v_wc, v_ec = col(1)
        v_e = east(vc, v_ec)
        v_w = west(vc, v_wc)
        v_n = north(vc, row(0, 1))
        v_s = south(vc, row(3, 1))
        v_se = south(v_e, row(4, 1))

        def tracer(ref, centre, field, wcol, ecol):
            east_side = east(centre, ecol)
            west_side = west(centre, wcol)
            north_side = north(centre, row(0, field))
            south_side = south(centre, row(3, field))
            flux_east = mask_east * (
                uc * (centre + east_side) * 0.5 - lateral_diff * (east_side - centre)
            )
            flux_west = mask_west * (
                u_w * (west_side + centre) * 0.5 - lateral_diff * (centre - west_side)
            )
            flux_north = mask_north * (
                vc * (centre + north_side) * 0.5 - lateral_diff * (north_side - centre)
            )
            flux_south = mask_south * (
                v_s * (south_side + centre) * 0.5 - lateral_diff * (centre - south_side)
            )
            tendency = (
                flux_west - flux_east + (flux_south - flux_north) + column(ref, centre)
            )
            return w * (centre + time_step * tendency)

        temp_ref[r] = tracer(t_ref, tc, 2, t_wc, t_ec)
        salt_ref[r] = tracer(s_ref, sc, 3, s_wc, s_ec)

        corner_ne = w * w_e * w_n * w_ne
        corner_se = w_s * w_se * w * w_e
        corner_nw = w_w * w * w_nw * w_n
        half_e = (uc + u_e) * 0.5
        cell_east = w_e * (half_e * half_e - lateral_diff * (u_e - uc))
        half_w = (u_w + uc) * 0.5
        cell_west = w * (half_w * half_w - lateral_diff * (uc - u_w))
        product_ne = (vc + v_e) * 0.5 * (uc + u_n) * 0.5
        product_se = (v_s + v_se) * 0.5 * (u_s + uc) * 0.5
        product_nw = (u_w + u_nw) * 0.5 * (v_w + vc) * 0.5
        shear_north = corner_ne * (product_ne - lateral_diff * (u_n - uc))
        shear_south = corner_se * (product_se - lateral_diff * (uc - u_s))
        north_mean = (vc + v_e + v_s + v_se) * 0.25
        east_tend = (
            cell_west
            - cell_east
            + (shear_south - shear_north)
            + cor_t * north_mean
            - pressure_coef * (p_e - pres)
            + column(u_ref, uc)
            - drag_coef * bottom * uc
        )
        east_ref[r] = mask_east * (uc + time_step * east_tend)
        half_n = (vc + v_n) * 0.5
        cell_north = w_n * (half_n * half_n - lateral_diff * (v_n - vc))
        half_s = (v_s + vc) * 0.5
        cell_south = w * (half_s * half_s - lateral_diff * (vc - v_s))
        stress_east = corner_ne * (product_ne - lateral_diff * (v_e - vc))
        stress_west = corner_nw * (product_nw - lateral_diff * (vc - v_w))
        east_mean = (uc + u_w + u_n + u_nw) * 0.25
        north_tend = (
            stress_west
            - stress_east
            + (cell_south - cell_north)
            - cor_v * east_mean
            - pressure_coef * (p_n - pres)
            + column(v_ref, vc)
            - drag_coef * bottom * vc
        )
        north_ref[r] = mask_north * (vc + time_step * north_tend)
        return pres, pres_e, pres_n

    init = (p_ref[...], pe_ref[...], pn_ref[...])
    pres, pres_e, pres_n = lax.fori_loop(0, chunk, body, init)
    p_ref[...] = pres
    pe_ref[...] = pres_e
    pn_ref[...] = pres_n


def per_device(
    eastbound_current,
    poleward_current,
    warmth_excess,
    saltiness_excess,
    water_indicator,
    column_layer_count,
):
    inputs = (
        eastbound_current,
        poleward_current,
        warmth_excess,
        saltiness_excess,
        water_indicator,
    )

    levels, rows, cols = eastbound_current.shape
    fields = len(inputs)
    chunk = 8 if levels % 8 == 0 else levels
    row_block = pl.BlockSpec((fields, chunk, cols), lambda c: (0, c, 0))
    col_block = pl.BlockSpec((fields, rows, levels), lambda c: (0, 0, 0))
    tile = 8
    top, bottom = pl.pallas_call(
        row_kernel,
        grid=(1,),
        in_specs=[pl.BlockSpec((levels, tile, cols), lambda c: (0, 0, 0))] * fields
        + [pl.BlockSpec((levels, tile, cols), lambda c: (0, rows // tile - 1, 0))] * fields,
        out_specs=(
            pl.BlockSpec((fields, levels, cols), lambda c: (0, 0, 0)),
            pl.BlockSpec((fields, levels, cols), lambda c: (0, 0, 0)),
        ),
        out_shape=(
            jax.ShapeDtypeStruct((fields, levels, cols), jnp.float32),
            jax.ShapeDtypeStruct((fields, levels, cols), jnp.float32),
        ),
    )(*inputs, *inputs)
    west_col, east_col = pl.pallas_call(
        edge_kernel,
        grid=(levels // chunk,),
        in_specs=[pl.BlockSpec((chunk, rows, cols), lambda c: (c, 0, 0))] * fields,
        out_specs=(col_block, col_block),
        out_shape=(
            jax.ShapeDtypeStruct((fields, rows, levels), jnp.float32),
            jax.ShapeDtypeStruct((fields, rows, levels), jnp.float32),
        ),
    )(*inputs)

    def east_of(a, b, na, nl):
        return (a, (b + 1) % nl)

    def west_of(a, b, na, nl):
        return (a, (b - 1) % nl)

    def north_of(a, b, na, nl):
        return (a + 1, b) if a + 1 < na else None

    def south_of(a, b, na, nl):
        return (a - 1, b) if a > 0 else None

    def mirror(a, b, na, nl):
        return (a, nl - 1 - b) if a == na - 1 else None

    halo_south = shift(top, north_of)
    halo_north = shift(bottom, south_of)
    fold_row = shift(top, mirror)
    sign = jnp.array([-1.0, -1.0, 1.0, 1.0, 1.0], dtype=jnp.float32)[:, None, None]
    is_top = lax.axis_index("lat") == lax.axis_size("lat") - 1
    north_first = jnp.where(is_top, sign[:, :, 0] * fold_row[:, :, -1], halo_north[:, :, 0])
    north_last = jnp.where(is_top, sign[:, :, 0] * fold_row[:, :, 0], halo_north[:, :, -1])
    pad = jnp.zeros((fields, 6, levels), jnp.float32)
    west_tall = jnp.concatenate(
        [west_col, halo_south[:, None, :, 0], north_first[:, None, :], pad], axis=1
    )
    east_tall = jnp.concatenate(
        [east_col, halo_south[:, None, :, -1], north_last[:, None, :], pad], axis=1
    )
    halo_west = shift(east_tall, east_of)
    halo_east = shift(west_tall, west_of)

    row_start = lax.axis_index("lat") * rows
    total_rows = rows * lax.axis_size("lat")
    row_index = (row_start + jnp.arange(rows, dtype=jnp.int32)).astype(jnp.float32)[:, None]
    coriolis_t = coriolis_max * (2.0 * (row_index + 0.5) / total_rows - 1.0)
    coriolis_v = coriolis_max * (2.0 * (row_index + 1.0) / total_rows - 1.0)
    coriolis = jnp.broadcast_to(jnp.stack([coriolis_t, coriolis_v]), (2, rows, cols))

    block = jax.ShapeDtypeStruct((levels, rows, cols), jnp.float32)
    main = pl.BlockSpec((chunk, rows, cols), lambda c: (c, 0, 0))
    above = pl.BlockSpec((1, rows, cols), lambda c: (jnp.maximum(c * chunk - 1, 0), 0, 0))
    below = pl.BlockSpec(
        (1, rows, cols), lambda c: (jnp.minimum(c * chunk + chunk, levels - 1), 0, 0)
    )

    def whole(shape):
        return pl.BlockSpec(shape, lambda c: (0,) * len(shape))

    halo_row = pl.BlockSpec((fields, chunk, cols), lambda c: (0, c, 0))
    return pl.pallas_call(
        stencil_kernel,
        grid=(levels // chunk,),
        in_specs=[pl.BlockSpec(memory_space=pltpu.SMEM), whole((2, rows, cols))]
        + [main] * fields
        + [above] * fields
        + [below] * fields
        + [whole((rows, cols)), halo_row, halo_row, halo_row, whole(halo_west.shape)]
        + [whole(halo_east.shape)],
        out_specs=(main, main, main, main),
        out_shape=(block, block, block, block),
        scratch_shapes=[
            pltpu.VMEM((rows, cols), jnp.float32),
            pltpu.VMEM((rows, cols), jnp.float32),
            pltpu.VMEM((1, cols), jnp.float32),
            pltpu.VMEM((fields, chunk, cols), jnp.float32),
        ],
    )(
        is_top.astype(jnp.int32).reshape(1),
        coriolis,
        *inputs,
        *inputs,
        *inputs,
        column_layer_count,
        halo_north,
        fold_row,
        halo_south,
        halo_west,
        halo_east,
    )


def solution(mesh):
    placed = (
        P(None, "lat", "lon"),
        P(None, "lat", "lon"),
        P(None, "lat", "lon"),
        P(None, "lat", "lon"),
        P(None, "lat", "lon"),
        P("lat", "lon"),
    )
    return jax.shard_map(
        per_device,
        mesh=mesh,
        in_specs=placed,
        out_specs=(
            P(None, "lat", "lon"),
            P(None, "lat", "lon"),
            P(None, "lat", "lon"),
            P(None, "lat", "lon"),
        ),
        check_vma=False,
    )
```

```python
import functools

import jax
import jax.numpy as jnp
from jax import lax
from jax.experimental import pallas as pl
from jax.experimental.pallas import tpu as pltpu
from jax.sharding import PartitionSpec as P

time_step = 0.2
lateral_diff = 0.1
vertical_diff = 0.5
pressure_coef = 0.1
drag_coef = 2.0
coriolis_max = 1.0
level_depth = 100.0
thermal_expand = 0.1655
haline_contract = 0.76554
cabbel_temp = 0.05952
cabbel_salt = 0.00054914
cabbel_mixed = 0.0024341
thermo_temp = 0.0001497
thermo_salt = 1.109e-05


def view_at(field, lat_step, lon_step):
    rows = field.shape[1] - 2
    cols = field.shape[2] - 2
    return field[:, 1 + lat_step : 1 + lat_step + rows, 1 + lon_step : 1 + lon_step + cols]


def column_flux(centre, mixing):
    between = -vertical_diff * mixing * (centre[1:] - centre[:-1])
    surface = jnp.zeros_like(centre[:1])
    above = jnp.concatenate([surface, between], axis=0)
    below = jnp.concatenate([between, surface], axis=0)
    return above - below


def advance(extended, column_layer_count, row_start, total_rows):
    eastward = extended[0]
    northward = extended[1]
    temper = extended[2]
    saline = extended[3]
    wet = extended[4]
    levels = extended.shape[1]
    rows = extended.shape[2] - 2
    level_index = jnp.arange(levels, dtype=jnp.int32)[:, None, None]
    wet_here = view_at(wet, 0, 0)
    mask_east = wet_here * view_at(wet, 0, 1)
    mask_west = view_at(wet, 0, -1) * wet_here
    mask_north = wet_here * view_at(wet, 1, 0)
    mask_south = view_at(wet, -1, 0) * wet_here
    mixing = (
        wet_here[:-1]
        * wet_here[1:]
        * (level_index[1:] < column_layer_count[None]).astype(jnp.float32)
    )
    bottom = (level_index == column_layer_count[None] - 1).astype(jnp.float32)
    depth = (level_index.astype(jnp.float32) + 0.5) * level_depth
    density = (
        -thermal_expand * (1.0 + 0.5 * cabbel_temp * temper + thermo_temp * depth) * temper
        + haline_contract * (1.0 - 0.5 * cabbel_salt * saline - thermo_salt * depth) * saline
        - cabbel_mixed * temper * saline
    )
    pressure = jnp.cumsum(wet * density, axis=0)
    row_index = (row_start + jnp.arange(rows, dtype=jnp.int32)).astype(jnp.float32)[None, :, None]
    coriolis_t = coriolis_max * (2.0 * (row_index + 0.5) / total_rows - 1.0)
    coriolis_v = coriolis_max * (2.0 * (row_index + 1.0) / total_rows - 1.0)

    def tracer(field):
        centre = view_at(field, 0, 0)
        east_side = view_at(field, 0, 1)
        west_side = view_at(field, 0, -1)
        north_side = view_at(field, 1, 0)
        south_side = view_at(field, -1, 0)
        flux_east = mask_east * (
            view_at(eastward, 0, 0) * (centre + east_side) * 0.5
            - lateral_diff * (east_side - centre)
        )
        flux_west = mask_west * (
            view_at(eastward, 0, -1) * (west_side + centre) * 0.5
            - lateral_diff * (centre - west_side)
        )
        flux_north = mask_north * (
            view_at(northward, 0, 0) * (centre + north_side) * 0.5
            - lateral_diff * (north_side - centre)
        )
        flux_south = mask_south * (
            view_at(northward, -1, 0) * (south_side + centre) * 0.5
            - lateral_diff * (centre - south_side)
        )
        tendency = flux_west - flux_east + (flux_south - flux_north) + column_flux(centre, mixing)
        return wet_here * (centre + time_step * tendency)

    east_here = view_at(eastward, 0, 0)
    north_here = view_at(northward, 0, 0)
    corner_ne = wet_here * view_at(wet, 0, 1) * view_at(wet, 1, 0) * view_at(wet, 1, 1)
    corner_se = view_at(wet, -1, 0) * view_at(wet, -1, 1) * wet_here * view_at(wet, 0, 1)
    corner_nw = view_at(wet, 0, -1) * wet_here * view_at(wet, 1, -1) * view_at(wet, 1, 0)
    cell_east = view_at(wet, 0, 1) * (
        ((east_here + view_at(eastward, 0, 1)) * 0.5) ** 2
        - lateral_diff * (view_at(eastward, 0, 1) - east_here)
    )
    cell_west = wet_here * (
        ((view_at(eastward, 0, -1) + east_here) * 0.5) ** 2
        - lateral_diff * (east_here - view_at(eastward, 0, -1))
    )
    product_ne = (
        (north_here + view_at(northward, 0, 1)) * 0.5 * (east_here + view_at(eastward, 1, 0)) * 0.5
    )
    product_se = (
        (view_at(northward, -1, 0) + view_at(northward, -1, 1))
        * 0.5
        * (view_at(eastward, -1, 0) + east_here)
        * 0.5
    )
    product_nw = (
        (view_at(eastward, 0, -1) + view_at(eastward, 1, -1))
        * 0.5
        * (view_at(northward, 0, -1) + north_here)
        * 0.5
    )
    shear_north = corner_ne * (product_ne - lateral_diff * (view_at(eastward, 1, 0) - east_here))
    shear_south = corner_se * (product_se - lateral_diff * (east_here - view_at(eastward, -1, 0)))
    north_mean = (
        north_here
        + view_at(northward, 0, 1)
        + view_at(northward, -1, 0)
        + view_at(northward, -1, 1)
    ) * 0.25
    east_tend = (
        cell_west
        - cell_east
        + (shear_south - shear_north)
        + coriolis_t * north_mean
        - pressure_coef * (view_at(pressure, 0, 1) - view_at(pressure, 0, 0))
        + column_flux(east_here, mixing)
        - drag_coef * bottom * east_here
    )
    east_next = mask_east * (east_here + time_step * east_tend)
    cell_north = view_at(wet, 1, 0) * (
        ((north_here + view_at(northward, 1, 0)) * 0.5) ** 2
        - lateral_diff * (view_at(northward, 1, 0) - north_here)
    )
    cell_south = wet_here * (
        ((view_at(northward, -1, 0) + north_here) * 0.5) ** 2
        - lateral_diff * (north_here - view_at(northward, -1, 0))
    )
    stress_east = corner_ne * (product_ne - lateral_diff * (view_at(northward, 0, 1) - north_here))
    stress_west = corner_nw * (product_nw - lateral_diff * (north_here - view_at(northward, 0, -1)))
    east_mean = (
        east_here + view_at(eastward, 0, -1) + view_at(eastward, 1, 0) + view_at(eastward, 1, -1)
    ) * 0.25
    north_tend = (
        stress_west
        - stress_east
        + (cell_south - cell_north)
        - coriolis_v * east_mean
        - pressure_coef * (view_at(pressure, 1, 0) - view_at(pressure, 0, 0))
        + column_flux(north_here, mixing)
        - drag_coef * bottom * north_here
    )
    north_next = mask_north * (north_here + time_step * north_tend)
    return (east_next, north_next, tracer(temper), tracer(saline))


def shift(value, mapping):
    lat_size = lax.axis_size("lat")
    lon_size = lax.axis_size("lon")
    pairs = []
    for a in range(lat_size):
        for b in range(lon_size):
            target = mapping(a, b, lat_size, lon_size)
            if target is not None:
                pairs.append((b * lat_size + a, target[1] * lat_size + target[0]))
    return lax.ppermute(value, ("lon", "lat"), pairs)


def row_kernel(*refs):
    fields = (len(refs) - 2) // 2
    lows = refs[:fields]
    highs = refs[fields : 2 * fields]
    top_ref, bottom_ref = refs[2 * fields :]
    chunk, tile, cols = lows[0].shape
    for field in range(fields):
        for r in range(chunk):
            top_ref[field, r : r + 1, :] = highs[field][r][tile - 1 : tile, :].astype(jnp.float32)
            bottom_ref[field, r : r + 1, :] = lows[field][r][0:1, :].astype(jnp.float32)


def edge_kernel(*refs):
    fields = len(refs) - 2
    sources = refs[:fields]
    west_ref, east_ref = refs[fields:]
    chunk, rows, cols = sources[0].shape
    levels = west_ref.shape[2]
    step = pl.program_id(0)
    lane = lax.broadcasted_iota(jnp.int32, (rows, levels), 1)

    @pl.when(step == 0)
    def _():
        west_ref[...] = jnp.zeros(west_ref.shape, jnp.float32)
        east_ref[...] = jnp.zeros(east_ref.shape, jnp.float32)

    for field, source in enumerate(sources):
        west = west_ref[field]
        east = east_ref[field]
        for r in range(chunk):
            x = source[r].astype(jnp.float32)
            here = lane == step * chunk + r
            west = jnp.where(here, x[:, 0:1], west)
            east = jnp.where(here, x[:, cols - 1 : cols], east)
        west_ref[field] = west
        east_ref[field] = east


def stencil_kernel(
    meta_ref, u_ref, v_ref, t_ref, s_ref, wet_ref, ua_ref, va_ref, ta_ref, sa_ref, wa_ref,
    ub_ref, vb_ref, tb_ref, sb_ref, wb_ref, clc_ref, rn_ref, rs_ref, tw_ref, te_ref,
    east_ref, north_ref, temp_ref, salt_ref, p_ref, pe_ref, pn_ref, *, total_rows,
):
    chunk, rows, cols = u_ref.shape
    levels = tw_ref.shape[2]
    step = pl.program_id(0)
    near = {
        id(u_ref): (ua_ref, ub_ref),
        id(v_ref): (va_ref, vb_ref),
        id(t_ref): (ta_ref, tb_ref),
        id(s_ref): (sa_ref, sb_ref),
        id(wet_ref): (wa_ref, wb_ref),
    }

    def level(ref, r, offset):
        above, below = near[id(ref)]
        if offset < 0:
            return jnp.where(r == 0, above[0], ref[jnp.maximum(r - 1, 0)])
        return jnp.where(r == chunk - 1, below[0], ref[jnp.minimum(r + 1, chunk - 1)])

    @pl.when(step == 0)
    def _():
        p_ref[...] = jnp.zeros(p_ref.shape, jnp.float32)
        pe_ref[...] = jnp.zeros(pe_ref.shape, jnp.float32)
        pn_ref[...] = jnp.zeros(pn_ref.shape, jnp.float32)

    fields = 5
    lane = lax.broadcasted_iota(jnp.int32, (rows, cols), 1)
    sub = lax.broadcasted_iota(jnp.int32, (rows, cols), 0)
    at_east = lane == cols - 1
    at_west = lane == 0
    at_north = sub == rows - 1
    at_south = sub == 0
    row_lane = lax.broadcasted_iota(jnp.int32, (1, cols), 1)
    row_east = row_lane == cols - 1
    row_west = row_lane == 0
    pick_lane = lax.broadcasted_iota(jnp.int32, tw_ref.shape[1:], 1)
    row_index = (meta_ref[0] * rows + sub).astype(jnp.float32)

    def per_total(x):
        if total_rows & (total_rows - 1) == 0:
            return x * (1.0 / total_rows)
        return x / total_rows

    cor_t = coriolis_max * (per_total(2.0 * (row_index + 0.5)) - 1.0)
    cor_v = coriolis_max * (per_total(2.0 * (row_index + 1.0)) - 1.0)
    count = clc_ref[...]

    def east(x, col):
        return jnp.where(at_east, col, pltpu.roll(x, cols - 1, 1))

    def west(x, col):
        return jnp.where(at_west, col, pltpu.roll(x, 1, 1))

    def north(x, row):
        return jnp.where(at_north, row, pltpu.roll(x, rows - 1, 0))

    def south(x, row):
        return jnp.where(at_south, row, pltpu.roll(x, 1, 0))

    def body(r, carry):
        pres, pres_e, pres_n = carry
        k = step * chunk + r

        spread = {}

        def tall(field):
            if field not in spread:
                spread[field] = tuple(
                    jnp.broadcast_to(
                        jnp.sum(jnp.where(pick_lane == k, ref[field], 0.0), axis=1, keepdims=True),
                        (ref.shape[1], cols),
                    )
                    for ref in (tw_ref, te_ref)
                )
            return spread[field]

        def row(variant, field):
            west_t, east_t = tall(field)
            if variant == 0:
                return rn_ref[field, pl.ds(r, 1), :]
            if variant == 3:
                return rs_ref[field, pl.ds(r, 1), :]
            if variant == 1:
                return jnp.where(row_east, east_t[rows + 1 : rows + 2], pltpu.roll(row(0, field), cols - 1, 1))
            if variant == 2:
                return jnp.where(row_west, west_t[rows + 1 : rows + 2], pltpu.roll(row(0, field), 1, 1))
            return jnp.where(row_east, east_t[rows : rows + 1], pltpu.roll(row(3, field), cols - 1, 1))

        def col(field):
            west_t, east_t = tall(field)
            return west_t[0:rows], east_t[0:rows]

        w = wet_ref[r].astype(jnp.float32)
        w_above = level(wet_ref, r, -1).astype(jnp.float32)
        w_below = level(wet_ref, r, 1).astype(jnp.float32)
        w_wc, w_ec = col(4)
        w_e = east(w, w_ec)
        w_w = west(w, w_wc)
        w_n = north(w, row(0, 4))
        w_s = south(w, row(3, 4))
        w_ne = north(w_e, row(1, 4))
        w_se = south(w_e, row(4, 4))
        w_nw = north(w_w, row(2, 4))
        mask_east = w * w_e
        mask_west = w_w * w
        mask_north = w * w_n
        mask_south = w_s * w
        mix_below = jnp.where(
            k < levels - 1, w * w_below * (k + 1 < count).astype(jnp.float32), 0.0
        )
        mix_above = jnp.where(k > 0, w_above * w * (k < count).astype(jnp.float32), 0.0)
        bottom = (k == count - 1).astype(jnp.float32)

        def column(ref, centre):
            upper = level(ref, r, -1)
            lower = level(ref, r, 1)
            above = -vertical_diff * mix_above * (centre - upper)
            below = -vertical_diff * mix_below * (lower - centre)
            return above - below

        depth = (k.astype(jnp.float32) + 0.5) * level_depth

        def density(temper, saline):
            return (
                -thermal_expand * (1.0 + 0.5 * cabbel_temp * temper + thermo_temp * depth) * temper
                + haline_contract * (1.0 - 0.5 * cabbel_salt * saline - thermo_salt * depth) * saline
                - cabbel_mixed * temper * saline
            )

        tc = t_ref[r]
        sc = s_ref[r]
        t_wc, t_ec = col(2)
        s_wc, s_ec = col(3)
        pres = pres + w * density(tc, sc)
        pres_e = pres_e + w_ec * density(t_ec, s_ec)
        pres_n = pres_n + row(0, 4) * density(row(0, 2), row(0, 3))
        p_e = east(pres, pres_e)
        p_n = north(pres, pres_n)

        uc = u_ref[r]
        u_wc, u_ec = col(0)
        u_e = east(uc, u_ec)
        u_w = west(uc, u_wc)
        u_n = north(uc, row(0, 0))
        u_s = south(uc, row(3, 0))
        u_nw = north(u_w, row(2, 0))
        vc = v_ref[r]
        v_wc, v_ec = col(1)
        v_e = east(vc, v_ec)
        v_w = west(vc, v_wc)
        v_n = north(vc, row(0, 1))
        v_s = south(vc, row(3, 1))
        v_se = south(v_e, row(4, 1))

        def tracer(ref, centre, field, wcol, ecol):
            east_side = east(centre, ecol)
            west_side = west(centre, wcol)
            north_side = north(centre, row(0, field))
            south_side = south(centre, row(3, field))
            flux_east = mask_east * (
                uc * (centre + east_side) * 0.5 - lateral_diff * (east_side - centre)
            )
            flux_west = mask_west * (
                u_w * (west_side + centre) * 0.5 - lateral_diff * (centre - west_side)
            )
            flux_north = mask_north * (
                vc * (centre + north_side) * 0.5 - lateral_diff * (north_side - centre)
            )
            flux_south = mask_south * (
                v_s * (south_side + centre) * 0.5 - lateral_diff * (centre - south_side)
            )
            tendency = (
                flux_west - flux_east + (flux_south - flux_north) + column(ref, centre)
            )
            return w * (centre + time_step * tendency)

        temp_ref[r] = tracer(t_ref, tc, 2, t_wc, t_ec)
        salt_ref[r] = tracer(s_ref, sc, 3, s_wc, s_ec)

        corner_ne = w * w_e * w_n * w_ne
        corner_se = w_s * w_se * w * w_e
        corner_nw = w_w * w * w_nw * w_n
        half_e = (uc + u_e) * 0.5
        cell_east = w_e * (half_e * half_e - lateral_diff * (u_e - uc))
        half_w = (u_w + uc) * 0.5
        cell_west = w * (half_w * half_w - lateral_diff * (uc - u_w))
        product_ne = (vc + v_e) * 0.5 * (uc + u_n) * 0.5
        product_se = (v_s + v_se) * 0.5 * (u_s + uc) * 0.5
        product_nw = (u_w + u_nw) * 0.5 * (v_w + vc) * 0.5
        shear_north = corner_ne * (product_ne - lateral_diff * (u_n - uc))
        shear_south = corner_se * (product_se - lateral_diff * (uc - u_s))
        north_mean = (vc + v_e + v_s + v_se) * 0.25
        east_tend = (
            cell_west
            - cell_east
            + (shear_south - shear_north)
            + cor_t * north_mean
            - pressure_coef * (p_e - pres)
            + column(u_ref, uc)
            - drag_coef * bottom * uc
        )
        east_ref[r] = mask_east * (uc + time_step * east_tend)
        half_n = (vc + v_n) * 0.5
        cell_north = w_n * (half_n * half_n - lateral_diff * (v_n - vc))
        half_s = (v_s + vc) * 0.5
        cell_south = w * (half_s * half_s - lateral_diff * (vc - v_s))
        stress_east = corner_ne * (product_ne - lateral_diff * (v_e - vc))
        stress_west = corner_nw * (product_nw - lateral_diff * (vc - v_w))
        east_mean = (uc + u_w + u_n + u_nw) * 0.25
        north_tend = (
            stress_west
            - stress_east
            + (cell_south - cell_north)
            - cor_v * east_mean
            - pressure_coef * (p_n - pres)
            + column(v_ref, vc)
            - drag_coef * bottom * vc
        )
        north_ref[r] = mask_north * (vc + time_step * north_tend)
        return pres, pres_e, pres_n

    init = (p_ref[...], pe_ref[...], pn_ref[...])
    pres, pres_e, pres_n = lax.fori_loop(0, chunk, body, init)
    p_ref[...] = pres
    pe_ref[...] = pres_e
    pn_ref[...] = pres_n


def per_device(
    eastbound_current,
    poleward_current,
    warmth_excess,
    saltiness_excess,
    water_indicator,
    column_layer_count,
):
    inputs = (
        eastbound_current,
        poleward_current,
        warmth_excess,
        saltiness_excess,
        water_indicator,
    )

    levels, rows, cols = eastbound_current.shape
    fields = len(inputs)
    chunk = 8 if levels % 8 == 0 else levels
    row_block = pl.BlockSpec((fields, chunk, cols), lambda c: (0, c, 0))
    col_block = pl.BlockSpec((fields, rows, levels), lambda c: (0, 0, 0))
    tile = 8
    top, bottom = pl.pallas_call(
        row_kernel,
        grid=(1,),
        in_specs=[pl.BlockSpec((levels, tile, cols), lambda c: (0, 0, 0))] * fields
        + [pl.BlockSpec((levels, tile, cols), lambda c: (0, rows // tile - 1, 0))] * fields,
        out_specs=(
            pl.BlockSpec((fields, levels, cols), lambda c: (0, 0, 0)),
            pl.BlockSpec((fields, levels, cols), lambda c: (0, 0, 0)),
        ),
        out_shape=(
            jax.ShapeDtypeStruct((fields, levels, cols), jnp.float32),
            jax.ShapeDtypeStruct((fields, levels, cols), jnp.float32),
        ),
    )(*inputs, *inputs)
    west_col, east_col = pl.pallas_call(
        edge_kernel,
        grid=(levels // chunk,),
        in_specs=[pl.BlockSpec((chunk, rows, cols), lambda c: (c, 0, 0))] * fields,
        out_specs=(col_block, col_block),
        out_shape=(
            jax.ShapeDtypeStruct((fields, rows, levels), jnp.float32),
            jax.ShapeDtypeStruct((fields, rows, levels), jnp.float32),
        ),
    )(*inputs)

    def east_of(a, b, na, nl):
        return (a, (b + 1) % nl)

    def west_of(a, b, na, nl):
        return (a, (b - 1) % nl)

    def north_of(a, b, na, nl):
        return (a + 1, b) if a + 1 < na else None

    def south_of(a, b, na, nl):
        return (a - 1, b) if a > 0 else None

    def mirror(a, b, na, nl):
        return (a, nl - 1 - b) if a == na - 1 else None

    halo_south = shift(top, north_of)
    halo_north = shift(bottom, south_of)
    fold_row = shift(top, mirror)
    sign = jnp.array([-1.0, -1.0, 1.0, 1.0, 1.0], dtype=jnp.float32)[:, None, None]
    is_top = lax.axis_index("lat") == lax.axis_size("lat") - 1
    halo_north = jnp.where(is_top, sign * fold_row[:, :, ::-1], halo_north)
    pad = jnp.zeros((fields, 6, levels), jnp.float32)
    west_tall = jnp.concatenate(
        [west_col, halo_south[:, None, :, 0], halo_north[:, None, :, 0], pad], axis=1
    )
    east_tall = jnp.concatenate(
        [east_col, halo_south[:, None, :, -1], halo_north[:, None, :, -1], pad], axis=1
    )
    halo_west = shift(east_tall, east_of)
    halo_east = shift(west_tall, west_of)

    row_start = lax.axis_index("lat") * rows
    total_rows = rows * lax.axis_size("lat")
    row_index = (row_start + jnp.arange(rows, dtype=jnp.int32)).astype(jnp.float32)[:, None]
    coriolis_t = coriolis_max * (2.0 * (row_index + 0.5) / total_rows - 1.0)
    coriolis_v = coriolis_max * (2.0 * (row_index + 1.0) / total_rows - 1.0)
    meta = lax.axis_index("lat").reshape(1)

    block = jax.ShapeDtypeStruct((levels, rows, cols), jnp.float32)
    main = pl.BlockSpec((chunk, rows, cols), lambda c: (c, 0, 0))
    above = pl.BlockSpec((1, rows, cols), lambda c: (jnp.maximum(c * chunk - 1, 0), 0, 0))
    below = pl.BlockSpec(
        (1, rows, cols), lambda c: (jnp.minimum(c * chunk + chunk, levels - 1), 0, 0)
    )

    def whole(shape):
        return pl.BlockSpec(shape, lambda c: (0,) * len(shape))

    halo_row = pl.BlockSpec((fields, chunk, cols), lambda c: (0, c, 0))
    return pl.pallas_call(
        functools.partial(stencil_kernel, total_rows=total_rows),
        grid=(levels // chunk,),
        in_specs=[pl.BlockSpec(memory_space=pltpu.SMEM)]
        + [main] * fields
        + [above] * fields
        + [below] * fields
        + [whole((rows, cols)), halo_row, halo_row, whole(halo_west.shape), whole(halo_east.shape)],
        out_specs=(main, main, main, main),
        out_shape=(block, block, block, block),
        scratch_shapes=[
            pltpu.VMEM((rows, cols), jnp.float32),
            pltpu.VMEM((rows, cols), jnp.float32),
            pltpu.VMEM((1, cols), jnp.float32),
        ],
    )(
        meta.astype(jnp.int32),
        *inputs,
        *inputs,
        *inputs,
        column_layer_count,
        halo_north,
        halo_south,
        halo_west,
        halo_east,
    )


def solution(mesh):
    placed = (
        P(None, "lat", "lon"),
        P(None, "lat", "lon"),
        P(None, "lat", "lon"),
        P(None, "lat", "lon"),
        P(None, "lat", "lon"),
        P("lat", "lon"),
    )
    return jax.shard_map(
        per_device,
        mesh=mesh,
        in_specs=placed,
        out_specs=(
            P(None, "lat", "lon"),
            P(None, "lat", "lon"),
            P(None, "lat", "lon"),
            P(None, "lat", "lon"),
        ),
        check_vma=False,
    )
```

```python
import functools

import jax
import jax.numpy as jnp
from jax import lax
from jax.experimental import pallas as pl
from jax.experimental.pallas import tpu as pltpu
from jax.sharding import PartitionSpec as P

time_step = 0.2
lateral_diff = 0.1
vertical_diff = 0.5
pressure_coef = 0.1
drag_coef = 2.0
coriolis_max = 1.0
level_depth = 100.0
thermal_expand = 0.1655
haline_contract = 0.76554
cabbel_temp = 0.05952
cabbel_salt = 0.00054914
cabbel_mixed = 0.0024341
thermo_temp = 0.0001497
thermo_salt = 1.109e-05


def view_at(field, lat_step, lon_step):
    rows = field.shape[1] - 2
    cols = field.shape[2] - 2
    return field[:, 1 + lat_step : 1 + lat_step + rows, 1 + lon_step : 1 + lon_step + cols]


def column_flux(centre, mixing):
    between = -vertical_diff * mixing * (centre[1:] - centre[:-1])
    surface = jnp.zeros_like(centre[:1])
    above = jnp.concatenate([surface, between], axis=0)
    below = jnp.concatenate([between, surface], axis=0)
    return above - below


def advance(extended, column_layer_count, row_start, total_rows):
    eastward = extended[0]
    northward = extended[1]
    temper = extended[2]
    saline = extended[3]
    wet = extended[4]
    levels = extended.shape[1]
    rows = extended.shape[2] - 2
    level_index = jnp.arange(levels, dtype=jnp.int32)[:, None, None]
    wet_here = view_at(wet, 0, 0)
    mask_east = wet_here * view_at(wet, 0, 1)
    mask_west = view_at(wet, 0, -1) * wet_here
    mask_north = wet_here * view_at(wet, 1, 0)
    mask_south = view_at(wet, -1, 0) * wet_here
    mixing = (
        wet_here[:-1]
        * wet_here[1:]
        * (level_index[1:] < column_layer_count[None]).astype(jnp.float32)
    )
    bottom = (level_index == column_layer_count[None] - 1).astype(jnp.float32)
    depth = (level_index.astype(jnp.float32) + 0.5) * level_depth
    density = (
        -thermal_expand * (1.0 + 0.5 * cabbel_temp * temper + thermo_temp * depth) * temper
        + haline_contract * (1.0 - 0.5 * cabbel_salt * saline - thermo_salt * depth) * saline
        - cabbel_mixed * temper * saline
    )
    pressure = jnp.cumsum(wet * density, axis=0)
    row_index = (row_start + jnp.arange(rows, dtype=jnp.int32)).astype(jnp.float32)[None, :, None]
    coriolis_t = coriolis_max * (2.0 * (row_index + 0.5) / total_rows - 1.0)
    coriolis_v = coriolis_max * (2.0 * (row_index + 1.0) / total_rows - 1.0)

    def tracer(field):
        centre = view_at(field, 0, 0)
        east_side = view_at(field, 0, 1)
        west_side = view_at(field, 0, -1)
        north_side = view_at(field, 1, 0)
        south_side = view_at(field, -1, 0)
        flux_east = mask_east * (
            view_at(eastward, 0, 0) * (centre + east_side) * 0.5
            - lateral_diff * (east_side - centre)
        )
        flux_west = mask_west * (
            view_at(eastward, 0, -1) * (west_side + centre) * 0.5
            - lateral_diff * (centre - west_side)
        )
        flux_north = mask_north * (
            view_at(northward, 0, 0) * (centre + north_side) * 0.5
            - lateral_diff * (north_side - centre)
        )
        flux_south = mask_south * (
            view_at(northward, -1, 0) * (south_side + centre) * 0.5
            - lateral_diff * (centre - south_side)
        )
        tendency = flux_west - flux_east + (flux_south - flux_north) + column_flux(centre, mixing)
        return wet_here * (centre + time_step * tendency)

    east_here = view_at(eastward, 0, 0)
    north_here = view_at(northward, 0, 0)
    corner_ne = wet_here * view_at(wet, 0, 1) * view_at(wet, 1, 0) * view_at(wet, 1, 1)
    corner_se = view_at(wet, -1, 0) * view_at(wet, -1, 1) * wet_here * view_at(wet, 0, 1)
    corner_nw = view_at(wet, 0, -1) * wet_here * view_at(wet, 1, -1) * view_at(wet, 1, 0)
    cell_east = view_at(wet, 0, 1) * (
        ((east_here + view_at(eastward, 0, 1)) * 0.5) ** 2
        - lateral_diff * (view_at(eastward, 0, 1) - east_here)
    )
    cell_west = wet_here * (
        ((view_at(eastward, 0, -1) + east_here) * 0.5) ** 2
        - lateral_diff * (east_here - view_at(eastward, 0, -1))
    )
    product_ne = (
        (north_here + view_at(northward, 0, 1)) * 0.5 * (east_here + view_at(eastward, 1, 0)) * 0.5
    )
    product_se = (
        (view_at(northward, -1, 0) + view_at(northward, -1, 1))
        * 0.5
        * (view_at(eastward, -1, 0) + east_here)
        * 0.5
    )
    product_nw = (
        (view_at(eastward, 0, -1) + view_at(eastward, 1, -1))
        * 0.5
        * (view_at(northward, 0, -1) + north_here)
        * 0.5
    )
    shear_north = corner_ne * (product_ne - lateral_diff * (view_at(eastward, 1, 0) - east_here))
    shear_south = corner_se * (product_se - lateral_diff * (east_here - view_at(eastward, -1, 0)))
    north_mean = (
        north_here
        + view_at(northward, 0, 1)
        + view_at(northward, -1, 0)
        + view_at(northward, -1, 1)
    ) * 0.25
    east_tend = (
        cell_west
        - cell_east
        + (shear_south - shear_north)
        + coriolis_t * north_mean
        - pressure_coef * (view_at(pressure, 0, 1) - view_at(pressure, 0, 0))
        + column_flux(east_here, mixing)
        - drag_coef * bottom * east_here
    )
    east_next = mask_east * (east_here + time_step * east_tend)
    cell_north = view_at(wet, 1, 0) * (
        ((north_here + view_at(northward, 1, 0)) * 0.5) ** 2
        - lateral_diff * (view_at(northward, 1, 0) - north_here)
    )
    cell_south = wet_here * (
        ((view_at(northward, -1, 0) + north_here) * 0.5) ** 2
        - lateral_diff * (north_here - view_at(northward, -1, 0))
    )
    stress_east = corner_ne * (product_ne - lateral_diff * (view_at(northward, 0, 1) - north_here))
    stress_west = corner_nw * (product_nw - lateral_diff * (north_here - view_at(northward, 0, -1)))
    east_mean = (
        east_here + view_at(eastward, 0, -1) + view_at(eastward, 1, 0) + view_at(eastward, 1, -1)
    ) * 0.25
    north_tend = (
        stress_west
        - stress_east
        + (cell_south - cell_north)
        - coriolis_v * east_mean
        - pressure_coef * (view_at(pressure, 1, 0) - view_at(pressure, 0, 0))
        + column_flux(north_here, mixing)
        - drag_coef * bottom * north_here
    )
    north_next = mask_north * (north_here + time_step * north_tend)
    return (east_next, north_next, tracer(temper), tracer(saline))


def shift(value, mapping):
    lat_size = lax.axis_size("lat")
    lon_size = lax.axis_size("lon")
    pairs = []
    for a in range(lat_size):
        for b in range(lon_size):
            target = mapping(a, b, lat_size, lon_size)
            if target is not None:
                pairs.append((b * lat_size + a, target[1] * lat_size + target[0]))
    return lax.ppermute(value, ("lon", "lat"), pairs)


def row_kernel(*refs):
    fields = (len(refs) - 2) // 2
    lows = refs[:fields]
    highs = refs[fields : 2 * fields]
    top_ref, bottom_ref = refs[2 * fields :]
    chunk, tile, cols = lows[0].shape
    for field in range(fields):
        for r in range(chunk):
            top_ref[field, r : r + 1, :] = highs[field][r][tile - 1 : tile, :].astype(jnp.float32)
            bottom_ref[field, r : r + 1, :] = lows[field][r][0:1, :].astype(jnp.float32)


def edge_kernel(*refs):
    fields = len(refs) - 2
    sources = refs[:fields]
    west_ref, east_ref = refs[fields:]
    chunk, rows, cols = sources[0].shape
    levels = west_ref.shape[2]
    step = pl.program_id(0)
    lane = lax.broadcasted_iota(jnp.int32, (rows, levels), 1)

    @pl.when(step == 0)
    def _():
        west_ref[...] = jnp.zeros(west_ref.shape, jnp.float32)
        east_ref[...] = jnp.zeros(east_ref.shape, jnp.float32)

    for field, source in enumerate(sources):
        west = west_ref[field]
        east = east_ref[field]
        for r in range(chunk):
            x = source[r].astype(jnp.float32)
            here = lane == step * chunk + r
            west = jnp.where(here, x[:, 0:1], west)
            east = jnp.where(here, x[:, cols - 1 : cols], east)
        west_ref[field] = west
        east_ref[field] = east


def stencil_kernel(
    meta_ref, u_ref, v_ref, t_ref, s_ref, wet_ref, ua_ref, va_ref, ta_ref, sa_ref, wa_ref,
    ub_ref, vb_ref, tb_ref, sb_ref, wb_ref, clc_ref, rn_ref, rs_ref, tw_ref, te_ref,
    east_ref, north_ref, temp_ref, salt_ref, p_ref, pe_ref, pn_ref, *, total_rows,
):
    chunk, rows, cols = u_ref.shape
    levels = tw_ref.shape[2]
    step = pl.program_id(0)
    near = {
        id(u_ref): (ua_ref, ub_ref),
        id(v_ref): (va_ref, vb_ref),
        id(t_ref): (ta_ref, tb_ref),
        id(s_ref): (sa_ref, sb_ref),
        id(wet_ref): (wa_ref, wb_ref),
    }

    def level(ref, r, offset):
        above, below = near[id(ref)]
        if offset < 0:
            return jnp.where(r == 0, above[0], ref[jnp.maximum(r - 1, 0)])
        return jnp.where(r == chunk - 1, below[0], ref[jnp.minimum(r + 1, chunk - 1)])

    @pl.when(step == 0)
    def _():
        p_ref[...] = jnp.zeros(p_ref.shape, jnp.float32)
        pe_ref[...] = jnp.zeros(pe_ref.shape, jnp.float32)
        pn_ref[...] = jnp.zeros(pn_ref.shape, jnp.float32)

    fields = 5
    lane = lax.broadcasted_iota(jnp.int32, (rows, cols), 1)
    sub = lax.broadcasted_iota(jnp.int32, (rows, cols), 0)
    at_east = lane == cols - 1
    at_west = lane == 0
    at_north = sub == rows - 1
    at_south = sub == 0
    row_lane = lax.broadcasted_iota(jnp.int32, (1, cols), 1)
    row_east = row_lane == cols - 1
    row_west = row_lane == 0
    pick_lane = lax.broadcasted_iota(jnp.int32, tw_ref.shape[1:], 1)
    row_index = (meta_ref[0] * rows + sub).astype(jnp.float32)

    def per_total(x):
        if total_rows & (total_rows - 1) == 0:
            return x * (1.0 / total_rows)
        return x / total_rows

    cor_t = coriolis_max * (per_total(2.0 * (row_index + 0.5)) - 1.0)
    cor_v = coriolis_max * (per_total(2.0 * (row_index + 1.0)) - 1.0)
    count = clc_ref[...]

    def east(x, col):
        return jnp.where(at_east, col, pltpu.roll(x, cols - 1, 1))

    def west(x, col):
        return jnp.where(at_west, col, pltpu.roll(x, 1, 1))

    def north(x, row):
        return jnp.where(at_north, row, pltpu.roll(x, rows - 1, 0))

    def south(x, row):
        return jnp.where(at_south, row, pltpu.roll(x, 1, 0))

    def body(r, carry):
        pres, pres_e, pres_n = carry
        k = step * chunk + r

        spread = {}

        def tall(field):
            if field not in spread:
                spread[field] = tuple(
                    jnp.broadcast_to(
                        jnp.sum(jnp.where(pick_lane == k, ref[field], 0.0), axis=1, keepdims=True),
                        (ref.shape[1], cols),
                    )
                    for ref in (tw_ref, te_ref)
                )
            return spread[field]

        def row(variant, field):
            west_t, east_t = tall(field)
            if variant == 0:
                return rn_ref[field, pl.ds(r, 1), :]
            if variant == 3:
                return rs_ref[field, pl.ds(r, 1), :]
            if variant == 1:
                return jnp.where(row_east, east_t[rows + 1 : rows + 2], pltpu.roll(row(0, field), cols - 1, 1))
            if variant == 2:
                return jnp.where(row_west, west_t[rows + 1 : rows + 2], pltpu.roll(row(0, field), 1, 1))
            return jnp.where(row_east, east_t[rows : rows + 1], pltpu.roll(row(3, field), cols - 1, 1))

        def col(field):
            west_t, east_t = tall(field)
            return west_t[0:rows], east_t[0:rows]

        w = wet_ref[r].astype(jnp.float32)
        w_above = level(wet_ref, r, -1).astype(jnp.float32)
        w_below = level(wet_ref, r, 1).astype(jnp.float32)
        w_wc, w_ec = col(4)
        w_e = east(w, w_ec)
        w_w = west(w, w_wc)
        w_n = north(w, row(0, 4))
        w_s = south(w, row(3, 4))
        w_ne = north(w_e, row(1, 4))
        w_se = south(w_e, row(4, 4))
        w_nw = north(w_w, row(2, 4))
        mask_east = w * w_e
        mask_west = w_w * w
        mask_north = w * w_n
        mask_south = w_s * w
        mix_below = jnp.where(
            k < levels - 1, w * w_below * (k + 1 < count).astype(jnp.float32), 0.0
        )
        mix_above = jnp.where(k > 0, w_above * w * (k < count).astype(jnp.float32), 0.0)
        bottom = (k == count - 1).astype(jnp.float32)

        def column(ref, centre):
            upper = level(ref, r, -1)
            lower = level(ref, r, 1)
            above = -vertical_diff * mix_above * (centre - upper)
            below = -vertical_diff * mix_below * (lower - centre)
            return above - below

        depth = (k.astype(jnp.float32) + 0.5) * level_depth

        def density(temper, saline):
            return (
                -thermal_expand * (1.0 + 0.5 * cabbel_temp * temper + thermo_temp * depth) * temper
                + haline_contract * (1.0 - 0.5 * cabbel_salt * saline - thermo_salt * depth) * saline
                - cabbel_mixed * temper * saline
            )

        tc = t_ref[r]
        sc = s_ref[r]
        t_wc, t_ec = col(2)
        s_wc, s_ec = col(3)
        pres = pres + w * density(tc, sc)
        pres_e = pres_e + w_ec * density(t_ec, s_ec)
        pres_n = pres_n + row(0, 4) * density(row(0, 2), row(0, 3))
        p_e = east(pres, pres_e)
        p_n = north(pres, pres_n)

        uc = u_ref[r]
        u_wc, u_ec = col(0)
        u_e = east(uc, u_ec)
        u_w = west(uc, u_wc)
        u_n = north(uc, row(0, 0))
        u_s = south(uc, row(3, 0))
        u_nw = north(u_w, row(2, 0))
        vc = v_ref[r]
        v_wc, v_ec = col(1)
        v_e = east(vc, v_ec)
        v_w = west(vc, v_wc)
        v_n = north(vc, row(0, 1))
        v_s = south(vc, row(3, 1))
        v_se = south(v_e, row(4, 1))

        def tracer(ref, centre, field, wcol, ecol):
            east_side = east(centre, ecol)
            west_side = west(centre, wcol)
            north_side = north(centre, row(0, field))
            south_side = south(centre, row(3, field))
            flux_east = mask_east * (
                uc * (centre + east_side) * 0.5 - lateral_diff * (east_side - centre)
            )
            flux_west = mask_west * (
                u_w * (west_side + centre) * 0.5 - lateral_diff * (centre - west_side)
            )
            flux_north = mask_north * (
                vc * (centre + north_side) * 0.5 - lateral_diff * (north_side - centre)
            )
            flux_south = mask_south * (
                v_s * (south_side + centre) * 0.5 - lateral_diff * (centre - south_side)
            )
            tendency = (
                flux_west - flux_east + (flux_south - flux_north) + column(ref, centre)
            )
            return w * (centre + time_step * tendency)

        temp_ref[r] = tracer(t_ref, tc, 2, t_wc, t_ec)
        salt_ref[r] = tracer(s_ref, sc, 3, s_wc, s_ec)

        corner_ne = w * w_e * w_n * w_ne
        corner_se = w_s * w_se * w * w_e
        corner_nw = w_w * w * w_nw * w_n
        half_e = (uc + u_e) * 0.5
        cell_east = w_e * (half_e * half_e - lateral_diff * (u_e - uc))
        half_w = (u_w + uc) * 0.5
        cell_west = w * (half_w * half_w - lateral_diff * (uc - u_w))
        product_ne = (vc + v_e) * 0.5 * (uc + u_n) * 0.5
        product_se = (v_s + v_se) * 0.5 * (u_s + uc) * 0.5
        product_nw = (u_w + u_nw) * 0.5 * (v_w + vc) * 0.5
        shear_north = corner_ne * (product_ne - lateral_diff * (u_n - uc))
        shear_south = corner_se * (product_se - lateral_diff * (uc - u_s))
        north_mean = (vc + v_e + v_s + v_se) * 0.25
        east_tend = (
            cell_west
            - cell_east
            + (shear_south - shear_north)
            + cor_t * north_mean
            - pressure_coef * (p_e - pres)
            + column(u_ref, uc)
            - drag_coef * bottom * uc
        )
        east_ref[r] = mask_east * (uc + time_step * east_tend)
        half_n = (vc + v_n) * 0.5
        cell_north = w_n * (half_n * half_n - lateral_diff * (v_n - vc))
        half_s = (v_s + vc) * 0.5
        cell_south = w * (half_s * half_s - lateral_diff * (vc - v_s))
        stress_east = corner_ne * (product_ne - lateral_diff * (v_e - vc))
        stress_west = corner_nw * (product_nw - lateral_diff * (vc - v_w))
        east_mean = (uc + u_w + u_n + u_nw) * 0.25
        north_tend = (
            stress_west
            - stress_east
            + (cell_south - cell_north)
            - cor_v * east_mean
            - pressure_coef * (p_n - pres)
            + column(v_ref, vc)
            - drag_coef * bottom * vc
        )
        north_ref[r] = mask_north * (vc + time_step * north_tend)
        return pres, pres_e, pres_n

    init = (p_ref[...], pe_ref[...], pn_ref[...])
    pres, pres_e, pres_n = lax.fori_loop(0, chunk, body, init)
    p_ref[...] = pres
    pe_ref[...] = pres_e
    pn_ref[...] = pres_n


def per_device(
    eastbound_current,
    poleward_current,
    warmth_excess,
    saltiness_excess,
    water_indicator,
    column_layer_count,
):
    inputs = (
        eastbound_current,
        poleward_current,
        warmth_excess,
        saltiness_excess,
        water_indicator,
    )

    levels, rows, cols = eastbound_current.shape
    fields = len(inputs)
    chunk = 8 if levels % 8 == 0 else levels
    row_block = pl.BlockSpec((fields, chunk, cols), lambda c: (0, c, 0))
    col_block = pl.BlockSpec((fields, rows, levels), lambda c: (0, 0, 0))
    tile = 8
    top, bottom = pl.pallas_call(
        row_kernel,
        grid=(1,),
        in_specs=[pl.BlockSpec((levels, tile, cols), lambda c: (0, 0, 0))] * fields
        + [pl.BlockSpec((levels, tile, cols), lambda c: (0, rows // tile - 1, 0))] * fields,
        out_specs=(
            pl.BlockSpec((fields, levels, cols), lambda c: (0, 0, 0)),
            pl.BlockSpec((fields, levels, cols), lambda c: (0, 0, 0)),
        ),
        out_shape=(
            jax.ShapeDtypeStruct((fields, levels, cols), jnp.float32),
            jax.ShapeDtypeStruct((fields, levels, cols), jnp.float32),
        ),
    )(*inputs, *inputs)
    west_col, east_col = pl.pallas_call(
        edge_kernel,
        grid=(levels // chunk,),
        in_specs=[pl.BlockSpec((chunk, rows, cols), lambda c: (c, 0, 0))] * fields,
        out_specs=(col_block, col_block),
        out_shape=(
            jax.ShapeDtypeStruct((fields, rows, levels), jnp.float32),
            jax.ShapeDtypeStruct((fields, rows, levels), jnp.float32),
        ),
    )(*inputs)

    def east_of(a, b, na, nl):
        return (a, (b + 1) % nl)

    def west_of(a, b, na, nl):
        return (a, (b - 1) % nl)

    def north_of(a, b, na, nl):
        return (a + 1, b) if a + 1 < na else None

    def south_of(a, b, na, nl):
        return (a - 1, b) if a > 0 else None

    def mirror(a, b, na, nl):
        return (a, nl - 1 - b) if a == na - 1 else None

    halo_south = shift(top, north_of)
    halo_north = shift(bottom, south_of)
    fold_row = shift(top, mirror)
    sign = jnp.array([-1.0, -1.0, 1.0, 1.0, 1.0], dtype=jnp.float32)[:, None, None]
    is_top = lax.axis_index("lat") == lax.axis_size("lat") - 1
    flip = (jnp.arange(cols)[:, None] + jnp.arange(cols)[None, :] == cols - 1).astype(jnp.float32)
    mirrored = jnp.dot(fold_row, flip, precision=lax.Precision.HIGHEST)
    halo_north = jnp.where(is_top, sign * mirrored, halo_north)
    pad = jnp.zeros((fields, 6, levels), jnp.float32)
    west_tall = jnp.concatenate(
        [west_col, halo_south[:, None, :, 0], halo_north[:, None, :, 0], pad], axis=1
    )
    east_tall = jnp.concatenate(
        [east_col, halo_south[:, None, :, -1], halo_north[:, None, :, -1], pad], axis=1
    )
    halo_west = shift(east_tall, east_of)
    halo_east = shift(west_tall, west_of)

    row_start = lax.axis_index("lat") * rows
    total_rows = rows * lax.axis_size("lat")
    row_index = (row_start + jnp.arange(rows, dtype=jnp.int32)).astype(jnp.float32)[:, None]
    coriolis_t = coriolis_max * (2.0 * (row_index + 0.5) / total_rows - 1.0)
    coriolis_v = coriolis_max * (2.0 * (row_index + 1.0) / total_rows - 1.0)
    meta = lax.axis_index("lat").reshape(1)

    block = jax.ShapeDtypeStruct((levels, rows, cols), jnp.float32)
    main = pl.BlockSpec((chunk, rows, cols), lambda c: (c, 0, 0))
    above = pl.BlockSpec((1, rows, cols), lambda c: (jnp.maximum(c * chunk - 1, 0), 0, 0))
    below = pl.BlockSpec(
        (1, rows, cols), lambda c: (jnp.minimum(c * chunk + chunk, levels - 1), 0, 0)
    )

    def whole(shape):
        return pl.BlockSpec(shape, lambda c: (0,) * len(shape))

    halo_row = pl.BlockSpec((fields, chunk, cols), lambda c: (0, c, 0))
    return pl.pallas_call(
        functools.partial(stencil_kernel, total_rows=total_rows),
        grid=(levels // chunk,),
        in_specs=[pl.BlockSpec(memory_space=pltpu.SMEM)]
        + [main] * fields
        + [above] * fields
        + [below] * fields
        + [whole((rows, cols)), halo_row, halo_row, whole(halo_west.shape), whole(halo_east.shape)],
        out_specs=(main, main, main, main),
        out_shape=(block, block, block, block),
        scratch_shapes=[
            pltpu.VMEM((rows, cols), jnp.float32),
            pltpu.VMEM((rows, cols), jnp.float32),
            pltpu.VMEM((1, cols), jnp.float32),
        ],
    )(
        meta.astype(jnp.int32),
        *inputs,
        *inputs,
        *inputs,
        column_layer_count,
        halo_north,
        halo_south,
        halo_west,
        halo_east,
    )


def solution(mesh):
    placed = (
        P(None, "lat", "lon"),
        P(None, "lat", "lon"),
        P(None, "lat", "lon"),
        P(None, "lat", "lon"),
        P(None, "lat", "lon"),
        P("lat", "lon"),
    )
    return jax.shard_map(
        per_device,
        mesh=mesh,
        in_specs=placed,
        out_specs=(
            P(None, "lat", "lon"),
            P(None, "lat", "lon"),
            P(None, "lat", "lon"),
            P(None, "lat", "lon"),
        ),
        check_vma=False,
    )
```

```python
import functools

import jax
import jax.numpy as jnp
from jax import lax
from jax.experimental import pallas as pl
from jax.experimental.pallas import tpu as pltpu
from jax.sharding import PartitionSpec as P

time_step = 0.2
lateral_diff = 0.1
vertical_diff = 0.5
pressure_coef = 0.1
drag_coef = 2.0
coriolis_max = 1.0
level_depth = 100.0
thermal_expand = 0.1655
haline_contract = 0.76554
cabbel_temp = 0.05952
cabbel_salt = 0.00054914
cabbel_mixed = 0.0024341
thermo_temp = 0.0001497
thermo_salt = 1.109e-05


def view_at(field, lat_step, lon_step):
    rows = field.shape[1] - 2
    cols = field.shape[2] - 2
    return field[:, 1 + lat_step : 1 + lat_step + rows, 1 + lon_step : 1 + lon_step + cols]


def column_flux(centre, mixing):
    between = -vertical_diff * mixing * (centre[1:] - centre[:-1])
    surface = jnp.zeros_like(centre[:1])
    above = jnp.concatenate([surface, between], axis=0)
    below = jnp.concatenate([between, surface], axis=0)
    return above - below


def advance(extended, column_layer_count, row_start, total_rows):
    eastward = extended[0]
    northward = extended[1]
    temper = extended[2]
    saline = extended[3]
    wet = extended[4]
    levels = extended.shape[1]
    rows = extended.shape[2] - 2
    level_index = jnp.arange(levels, dtype=jnp.int32)[:, None, None]
    wet_here = view_at(wet, 0, 0)
    mask_east = wet_here * view_at(wet, 0, 1)
    mask_west = view_at(wet, 0, -1) * wet_here
    mask_north = wet_here * view_at(wet, 1, 0)
    mask_south = view_at(wet, -1, 0) * wet_here
    mixing = (
        wet_here[:-1]
        * wet_here[1:]
        * (level_index[1:] < column_layer_count[None]).astype(jnp.float32)
    )
    bottom = (level_index == column_layer_count[None] - 1).astype(jnp.float32)
    depth = (level_index.astype(jnp.float32) + 0.5) * level_depth
    density = (
        -thermal_expand * (1.0 + 0.5 * cabbel_temp * temper + thermo_temp * depth) * temper
        + haline_contract * (1.0 - 0.5 * cabbel_salt * saline - thermo_salt * depth) * saline
        - cabbel_mixed * temper * saline
    )
    pressure = jnp.cumsum(wet * density, axis=0)
    row_index = (row_start + jnp.arange(rows, dtype=jnp.int32)).astype(jnp.float32)[None, :, None]
    coriolis_t = coriolis_max * (2.0 * (row_index + 0.5) / total_rows - 1.0)
    coriolis_v = coriolis_max * (2.0 * (row_index + 1.0) / total_rows - 1.0)

    def tracer(field):
        centre = view_at(field, 0, 0)
        east_side = view_at(field, 0, 1)
        west_side = view_at(field, 0, -1)
        north_side = view_at(field, 1, 0)
        south_side = view_at(field, -1, 0)
        flux_east = mask_east * (
            view_at(eastward, 0, 0) * (centre + east_side) * 0.5
            - lateral_diff * (east_side - centre)
        )
        flux_west = mask_west * (
            view_at(eastward, 0, -1) * (west_side + centre) * 0.5
            - lateral_diff * (centre - west_side)
        )
        flux_north = mask_north * (
            view_at(northward, 0, 0) * (centre + north_side) * 0.5
            - lateral_diff * (north_side - centre)
        )
        flux_south = mask_south * (
            view_at(northward, -1, 0) * (south_side + centre) * 0.5
            - lateral_diff * (centre - south_side)
        )
        tendency = flux_west - flux_east + (flux_south - flux_north) + column_flux(centre, mixing)
        return wet_here * (centre + time_step * tendency)

    east_here = view_at(eastward, 0, 0)
    north_here = view_at(northward, 0, 0)
    corner_ne = wet_here * view_at(wet, 0, 1) * view_at(wet, 1, 0) * view_at(wet, 1, 1)
    corner_se = view_at(wet, -1, 0) * view_at(wet, -1, 1) * wet_here * view_at(wet, 0, 1)
    corner_nw = view_at(wet, 0, -1) * wet_here * view_at(wet, 1, -1) * view_at(wet, 1, 0)
    cell_east = view_at(wet, 0, 1) * (
        ((east_here + view_at(eastward, 0, 1)) * 0.5) ** 2
        - lateral_diff * (view_at(eastward, 0, 1) - east_here)
    )
    cell_west = wet_here * (
        ((view_at(eastward, 0, -1) + east_here) * 0.5) ** 2
        - lateral_diff * (east_here - view_at(eastward, 0, -1))
    )
    product_ne = (
        (north_here + view_at(northward, 0, 1)) * 0.5 * (east_here + view_at(eastward, 1, 0)) * 0.5
    )
    product_se = (
        (view_at(northward, -1, 0) + view_at(northward, -1, 1))
        * 0.5
        * (view_at(eastward, -1, 0) + east_here)
        * 0.5
    )
    product_nw = (
        (view_at(eastward, 0, -1) + view_at(eastward, 1, -1))
        * 0.5
        * (view_at(northward, 0, -1) + north_here)
        * 0.5
    )
    shear_north = corner_ne * (product_ne - lateral_diff * (view_at(eastward, 1, 0) - east_here))
    shear_south = corner_se * (product_se - lateral_diff * (east_here - view_at(eastward, -1, 0)))
    north_mean = (
        north_here
        + view_at(northward, 0, 1)
        + view_at(northward, -1, 0)
        + view_at(northward, -1, 1)
    ) * 0.25
    east_tend = (
        cell_west
        - cell_east
        + (shear_south - shear_north)
        + coriolis_t * north_mean
        - pressure_coef * (view_at(pressure, 0, 1) - view_at(pressure, 0, 0))
        + column_flux(east_here, mixing)
        - drag_coef * bottom * east_here
    )
    east_next = mask_east * (east_here + time_step * east_tend)
    cell_north = view_at(wet, 1, 0) * (
        ((north_here + view_at(northward, 1, 0)) * 0.5) ** 2
        - lateral_diff * (view_at(northward, 1, 0) - north_here)
    )
    cell_south = wet_here * (
        ((view_at(northward, -1, 0) + north_here) * 0.5) ** 2
        - lateral_diff * (north_here - view_at(northward, -1, 0))
    )
    stress_east = corner_ne * (product_ne - lateral_diff * (view_at(northward, 0, 1) - north_here))
    stress_west = corner_nw * (product_nw - lateral_diff * (north_here - view_at(northward, 0, -1)))
    east_mean = (
        east_here + view_at(eastward, 0, -1) + view_at(eastward, 1, 0) + view_at(eastward, 1, -1)
    ) * 0.25
    north_tend = (
        stress_west
        - stress_east
        + (cell_south - cell_north)
        - coriolis_v * east_mean
        - pressure_coef * (view_at(pressure, 1, 0) - view_at(pressure, 0, 0))
        + column_flux(north_here, mixing)
        - drag_coef * bottom * north_here
    )
    north_next = mask_north * (north_here + time_step * north_tend)
    return (east_next, north_next, tracer(temper), tracer(saline))


def shift(value, mapping):
    lat_size = lax.axis_size("lat")
    lon_size = lax.axis_size("lon")
    pairs = []
    for a in range(lat_size):
        for b in range(lon_size):
            target = mapping(a, b, lat_size, lon_size)
            if target is not None:
                pairs.append((b * lat_size + a, target[1] * lat_size + target[0]))
    return lax.ppermute(value, ("lon", "lat"), pairs)


def row_kernel(*refs):
    fields = (len(refs) - 2) // 2
    lows = refs[:fields]
    highs = refs[fields : 2 * fields]
    top_ref, bottom_ref = refs[2 * fields :]
    chunk, tile, cols = lows[0].shape
    for field in range(fields):
        for r in range(chunk):
            top_ref[field, r : r + 1, :] = highs[field][r][tile - 1 : tile, :].astype(jnp.float32)
            bottom_ref[field, r : r + 1, :] = lows[field][r][0:1, :].astype(jnp.float32)


def edge_kernel(*refs):
    fields = len(refs) - 2
    sources = refs[:fields]
    west_ref, east_ref = refs[fields:]
    chunk, rows, cols = sources[0].shape
    levels = west_ref.shape[2]
    step = pl.program_id(0)
    lane = lax.broadcasted_iota(jnp.int32, (rows, levels), 1)

    @pl.when(step == 0)
    def _():
        west_ref[...] = jnp.zeros(west_ref.shape, jnp.float32)
        east_ref[...] = jnp.zeros(east_ref.shape, jnp.float32)

    for field, source in enumerate(sources):
        west = west_ref[field]
        east = east_ref[field]
        for r in range(chunk):
            x = source[r].astype(jnp.float32)
            here = lane == step * chunk + r
            west = jnp.where(here, x[:, 0:1], west)
            east = jnp.where(here, x[:, cols - 1 : cols], east)
        west_ref[field] = west
        east_ref[field] = east


def stencil_kernel(
    meta_ref, u_ref, v_ref, t_ref, s_ref, wet_ref, ua_ref, va_ref, ta_ref, sa_ref, wa_ref,
    ub_ref, vb_ref, tb_ref, sb_ref, wb_ref, clc_ref, rn_ref, rs_ref, tw_ref, te_ref,
    east_ref, north_ref, temp_ref, salt_ref, p_ref, pe_ref, pn_ref, pm_ref, *, total_rows,
):
    chunk, rows, cols = u_ref.shape
    levels = tw_ref.shape[2]
    step = pl.program_id(0)
    near = {
        id(u_ref): (ua_ref, ub_ref),
        id(v_ref): (va_ref, vb_ref),
        id(t_ref): (ta_ref, tb_ref),
        id(s_ref): (sa_ref, sb_ref),
        id(wet_ref): (wa_ref, wb_ref),
    }

    def level(ref, r, offset):
        above, below = near[id(ref)]
        if offset < 0:
            return jnp.where(r == 0, above[0], ref[jnp.maximum(r - 1, 0)])
        return jnp.where(r == chunk - 1, below[0], ref[jnp.minimum(r + 1, chunk - 1)])

    @pl.when(step == 0)
    def _():
        p_ref[...] = jnp.zeros(p_ref.shape, jnp.float32)
        pe_ref[...] = jnp.zeros(pe_ref.shape, jnp.float32)
        pn_ref[...] = jnp.zeros(pn_ref.shape, jnp.float32)
        pm_ref[...] = jnp.zeros(pm_ref.shape, jnp.float32)

    fields = 5
    lane = lax.broadcasted_iota(jnp.int32, (rows, cols), 1)
    sub = lax.broadcasted_iota(jnp.int32, (rows, cols), 0)
    at_east = lane == cols - 1
    at_west = lane == 0
    at_north = sub == rows - 1
    at_south = sub == 0
    row_lane = lax.broadcasted_iota(jnp.int32, (1, cols), 1)
    row_east = row_lane == cols - 1
    row_west = row_lane == 0
    pick_lane = lax.broadcasted_iota(jnp.int32, tw_ref.shape[1:], 1)
    row_index = (meta_ref[0] * rows + sub).astype(jnp.float32)

    def per_total(x):
        if total_rows & (total_rows - 1) == 0:
            return x * (1.0 / total_rows)
        return x / total_rows

    cor_t = coriolis_max * (per_total(2.0 * (row_index + 0.5)) - 1.0)
    cor_v = coriolis_max * (per_total(2.0 * (row_index + 1.0)) - 1.0)
    count = clc_ref[...]

    def east(x, col):
        return jnp.where(at_east, col, pltpu.roll(x, cols - 1, 1))

    def west(x, col):
        return jnp.where(at_west, col, pltpu.roll(x, 1, 1))

    def north(x, row):
        return jnp.where(at_north, row, pltpu.roll(x, rows - 1, 0))

    def south(x, row):
        return jnp.where(at_south, row, pltpu.roll(x, 1, 0))

    def body(r, carry):
        pres, pres_e, pres_n, mix_above = carry
        k = step * chunk + r

        spread = {}

        def tall(field):
            if field not in spread:
                spread[field] = tuple(
                    jnp.broadcast_to(
                        jnp.sum(jnp.where(pick_lane == k, ref[field], 0.0), axis=1, keepdims=True),
                        (ref.shape[1], cols),
                    )
                    for ref in (tw_ref, te_ref)
                )
            return spread[field]

        def row(variant, field):
            west_t, east_t = tall(field)
            if variant == 0:
                return rn_ref[field, pl.ds(r, 1), :]
            if variant == 3:
                return rs_ref[field, pl.ds(r, 1), :]
            if variant == 1:
                return jnp.where(row_east, east_t[rows + 1 : rows + 2], pltpu.roll(row(0, field), cols - 1, 1))
            if variant == 2:
                return jnp.where(row_west, west_t[rows + 1 : rows + 2], pltpu.roll(row(0, field), 1, 1))
            return jnp.where(row_east, east_t[rows : rows + 1], pltpu.roll(row(3, field), cols - 1, 1))

        def col(field):
            west_t, east_t = tall(field)
            return west_t[0:rows], east_t[0:rows]

        w = wet_ref[r].astype(jnp.float32)
        w_below = level(wet_ref, r, 1).astype(jnp.float32)
        w_wc, w_ec = col(4)
        w_e = east(w, w_ec)
        w_w = west(w, w_wc)
        w_n = north(w, row(0, 4))
        w_s = south(w, row(3, 4))
        w_ne = north(w_e, row(1, 4))
        w_se = south(w_e, row(4, 4))
        w_nw = north(w_w, row(2, 4))
        mask_east = w * w_e
        mask_west = w_w * w
        mask_north = w * w_n
        mask_south = w_s * w
        mix_below = jnp.where(
            k < levels - 1, w * w_below * (k + 1 < count).astype(jnp.float32), 0.0
        )
        bottom = (k == count - 1).astype(jnp.float32)

        def column(ref, centre):
            upper = level(ref, r, -1)
            lower = level(ref, r, 1)
            above = -vertical_diff * mix_above * (centre - upper)
            below = -vertical_diff * mix_below * (lower - centre)
            return above - below

        depth = (k.astype(jnp.float32) + 0.5) * level_depth

        def density(temper, saline):
            return (
                -thermal_expand * (1.0 + 0.5 * cabbel_temp * temper + thermo_temp * depth) * temper
                + haline_contract * (1.0 - 0.5 * cabbel_salt * saline - thermo_salt * depth) * saline
                - cabbel_mixed * temper * saline
            )

        tc = t_ref[r]
        sc = s_ref[r]
        t_wc, t_ec = col(2)
        s_wc, s_ec = col(3)
        pres = pres + w * density(tc, sc)
        pres_e = pres_e + w_ec * density(t_ec, s_ec)
        pres_n = pres_n + row(0, 4) * density(row(0, 2), row(0, 3))
        p_e = east(pres, pres_e)
        p_n = north(pres, pres_n)

        uc = u_ref[r]
        u_wc, u_ec = col(0)
        u_e = east(uc, u_ec)
        u_w = west(uc, u_wc)
        u_n = north(uc, row(0, 0))
        u_s = south(uc, row(3, 0))
        u_nw = north(u_w, row(2, 0))
        vc = v_ref[r]
        v_wc, v_ec = col(1)
        v_e = east(vc, v_ec)
        v_w = west(vc, v_wc)
        v_n = north(vc, row(0, 1))
        v_s = south(vc, row(3, 1))
        v_se = south(v_e, row(4, 1))

        def tracer(ref, centre, field, wcol, ecol):
            east_side = east(centre, ecol)
            west_side = west(centre, wcol)
            north_side = north(centre, row(0, field))
            south_side = south(centre, row(3, field))
            flux_east = mask_east * (
                uc * (centre + east_side) * 0.5 - lateral_diff * (east_side - centre)
            )
            flux_west = mask_west * (
                u_w * (west_side + centre) * 0.5 - lateral_diff * (centre - west_side)
            )
            flux_north = mask_north * (
                vc * (centre + north_side) * 0.5 - lateral_diff * (north_side - centre)
            )
            flux_south = mask_south * (
                v_s * (south_side + centre) * 0.5 - lateral_diff * (centre - south_side)
            )
            tendency = (
                flux_west - flux_east + (flux_south - flux_north) + column(ref, centre)
            )
            return w * (centre + time_step * tendency)

        temp_ref[r] = tracer(t_ref, tc, 2, t_wc, t_ec)
        salt_ref[r] = tracer(s_ref, sc, 3, s_wc, s_ec)

        corner_ne = w * w_e * w_n * w_ne
        corner_se = w_s * w_se * w * w_e
        corner_nw = w_w * w * w_nw * w_n
        half_e = (uc + u_e) * 0.5
        cell_east = w_e * (half_e * half_e - lateral_diff * (u_e - uc))
        half_w = (u_w + uc) * 0.5
        cell_west = w * (half_w * half_w - lateral_diff * (uc - u_w))
        product_ne = (vc + v_e) * 0.5 * (uc + u_n) * 0.5
        product_se = (v_s + v_se) * 0.5 * (u_s + uc) * 0.5
        product_nw = (u_w + u_nw) * 0.5 * (v_w + vc) * 0.5
        shear_north = corner_ne * (product_ne - lateral_diff * (u_n - uc))
        shear_south = corner_se * (product_se - lateral_diff * (uc - u_s))
        north_mean = (vc + v_e + v_s + v_se) * 0.25
        east_tend = (
            cell_west
            - cell_east
            + (shear_south - shear_north)
            + cor_t * north_mean
            - pressure_coef * (p_e - pres)
            + column(u_ref, uc)
            - drag_coef * bottom * uc
        )
        east_ref[r] = mask_east * (uc + time_step * east_tend)
        half_n = (vc + v_n) * 0.5
        cell_north = w_n * (half_n * half_n - lateral_diff * (v_n - vc))
        half_s = (v_s + vc) * 0.5
        cell_south = w * (half_s * half_s - lateral_diff * (vc - v_s))
        stress_east = corner_ne * (product_ne - lateral_diff * (v_e - vc))
        stress_west = corner_nw * (product_nw - lateral_diff * (vc - v_w))
        east_mean = (uc + u_w + u_n + u_nw) * 0.25
        north_tend = (
            stress_west
            - stress_east
            + (cell_south - cell_north)
            - cor_v * east_mean
            - pressure_coef * (p_n - pres)
            + column(v_ref, vc)
            - drag_coef * bottom * vc
        )
        north_ref[r] = mask_north * (vc + time_step * north_tend)
        return pres, pres_e, pres_n, mix_below

    init = (p_ref[...], pe_ref[...], pn_ref[...], pm_ref[...])
    pres, pres_e, pres_n, mix_last = lax.fori_loop(0, chunk, body, init)
    pm_ref[...] = mix_last
    p_ref[...] = pres
    pe_ref[...] = pres_e
    pn_ref[...] = pres_n


def per_device(
    eastbound_current,
    poleward_current,
    warmth_excess,
    saltiness_excess,
    water_indicator,
    column_layer_count,
):
    inputs = (
        eastbound_current,
        poleward_current,
        warmth_excess,
        saltiness_excess,
        water_indicator,
    )

    levels, rows, cols = eastbound_current.shape
    fields = len(inputs)
    chunk = 8 if levels % 8 == 0 else levels
    row_block = pl.BlockSpec((fields, chunk, cols), lambda c: (0, c, 0))
    col_block = pl.BlockSpec((fields, rows, levels), lambda c: (0, 0, 0))
    tile = 8
    top, bottom = pl.pallas_call(
        row_kernel,
        grid=(1,),
        in_specs=[pl.BlockSpec((levels, tile, cols), lambda c: (0, 0, 0))] * fields
        + [pl.BlockSpec((levels, tile, cols), lambda c: (0, rows // tile - 1, 0))] * fields,
        out_specs=(
            pl.BlockSpec((fields, levels, cols), lambda c: (0, 0, 0)),
            pl.BlockSpec((fields, levels, cols), lambda c: (0, 0, 0)),
        ),
        out_shape=(
            jax.ShapeDtypeStruct((fields, levels, cols), jnp.float32),
            jax.ShapeDtypeStruct((fields, levels, cols), jnp.float32),
        ),
    )(*inputs, *inputs)
    west_col, east_col = pl.pallas_call(
        edge_kernel,
        grid=(levels // chunk,),
        in_specs=[pl.BlockSpec((chunk, rows, cols), lambda c: (c, 0, 0))] * fields,
        out_specs=(col_block, col_block),
        out_shape=(
            jax.ShapeDtypeStruct((fields, rows, levels), jnp.float32),
            jax.ShapeDtypeStruct((fields, rows, levels), jnp.float32),
        ),
    )(*inputs)

    def east_of(a, b, na, nl):
        return (a, (b + 1) % nl)

    def west_of(a, b, na, nl):
        return (a, (b - 1) % nl)

    def north_of(a, b, na, nl):
        return (a + 1, b) if a + 1 < na else None

    def south_of(a, b, na, nl):
        return (a - 1, b) if a > 0 else None

    def mirror(a, b, na, nl):
        return (a, nl - 1 - b) if a == na - 1 else None

    halo_south = shift(top, north_of)
    halo_north = shift(bottom, south_of)
    fold_row = shift(top, mirror)
    sign = jnp.array([-1.0, -1.0, 1.0, 1.0, 1.0], dtype=jnp.float32)[:, None, None]
    is_top = lax.axis_index("lat") == lax.axis_size("lat") - 1
    flip = (jnp.arange(cols)[:, None] + jnp.arange(cols)[None, :] == cols - 1).astype(jnp.float32)
    mirrored = jnp.dot(fold_row, flip, precision=lax.Precision.HIGHEST)
    halo_north = jnp.where(is_top, sign * mirrored, halo_north)
    pad = jnp.zeros((fields, 6, levels), jnp.float32)
    west_tall = jnp.concatenate(
        [west_col, halo_south[:, None, :, 0], halo_north[:, None, :, 0], pad], axis=1
    )
    east_tall = jnp.concatenate(
        [east_col, halo_south[:, None, :, -1], halo_north[:, None, :, -1], pad], axis=1
    )
    halo_west = shift(east_tall, east_of)
    halo_east = shift(west_tall, west_of)

    row_start = lax.axis_index("lat") * rows
    total_rows = rows * lax.axis_size("lat")
    row_index = (row_start + jnp.arange(rows, dtype=jnp.int32)).astype(jnp.float32)[:, None]
    coriolis_t = coriolis_max * (2.0 * (row_index + 0.5) / total_rows - 1.0)
    coriolis_v = coriolis_max * (2.0 * (row_index + 1.0) / total_rows - 1.0)
    meta = lax.axis_index("lat").reshape(1)

    block = jax.ShapeDtypeStruct((levels, rows, cols), jnp.float32)
    main = pl.BlockSpec((chunk, rows, cols), lambda c: (c, 0, 0))
    above = pl.BlockSpec((1, rows, cols), lambda c: (jnp.maximum(c * chunk - 1, 0), 0, 0))
    below = pl.BlockSpec(
        (1, rows, cols), lambda c: (jnp.minimum(c * chunk + chunk, levels - 1), 0, 0)
    )

    def whole(shape):
        return pl.BlockSpec(shape, lambda c: (0,) * len(shape))

    halo_row = pl.BlockSpec((fields, chunk, cols), lambda c: (0, c, 0))
    return pl.pallas_call(
        functools.partial(stencil_kernel, total_rows=total_rows),
        grid=(levels // chunk,),
        in_specs=[pl.BlockSpec(memory_space=pltpu.SMEM)]
        + [main] * fields
        + [above] * fields
        + [below] * fields
        + [whole((rows, cols)), halo_row, halo_row, whole(halo_west.shape), whole(halo_east.shape)],
        out_specs=(main, main, main, main),
        out_shape=(block, block, block, block),
        scratch_shapes=[
            pltpu.VMEM((rows, cols), jnp.float32),
            pltpu.VMEM((rows, cols), jnp.float32),
            pltpu.VMEM((1, cols), jnp.float32),
            pltpu.VMEM((rows, cols), jnp.float32),
        ],
    )(
        meta.astype(jnp.int32),
        *inputs,
        *inputs,
        *inputs,
        column_layer_count,
        halo_north,
        halo_south,
        halo_west,
        halo_east,
    )


def solution(mesh):
    placed = (
        P(None, "lat", "lon"),
        P(None, "lat", "lon"),
        P(None, "lat", "lon"),
        P(None, "lat", "lon"),
        P(None, "lat", "lon"),
        P("lat", "lon"),
    )
    return jax.shard_map(
        per_device,
        mesh=mesh,
        in_specs=placed,
        out_specs=(
            P(None, "lat", "lon"),
            P(None, "lat", "lon"),
            P(None, "lat", "lon"),
            P(None, "lat", "lon"),
        ),
        check_vma=False,
    )
```

```python
import functools

import jax
import jax.numpy as jnp
from jax import lax
from jax.experimental import pallas as pl
from jax.experimental.pallas import tpu as pltpu
from jax.sharding import PartitionSpec as P

time_step = 0.2
lateral_diff = 0.1
vertical_diff = 0.5
pressure_coef = 0.1
drag_coef = 2.0
coriolis_max = 1.0
level_depth = 100.0
thermal_expand = 0.1655
haline_contract = 0.76554
cabbel_temp = 0.05952
cabbel_salt = 0.00054914
cabbel_mixed = 0.0024341
thermo_temp = 0.0001497
thermo_salt = 1.109e-05


def view_at(field, lat_step, lon_step):
    rows = field.shape[1] - 2
    cols = field.shape[2] - 2
    return field[:, 1 + lat_step : 1 + lat_step + rows, 1 + lon_step : 1 + lon_step + cols]


def column_flux(centre, mixing):
    between = -vertical_diff * mixing * (centre[1:] - centre[:-1])
    surface = jnp.zeros_like(centre[:1])
    above = jnp.concatenate([surface, between], axis=0)
    below = jnp.concatenate([between, surface], axis=0)
    return above - below


def advance(extended, column_layer_count, row_start, total_rows):
    eastward = extended[0]
    northward = extended[1]
    temper = extended[2]
    saline = extended[3]
    wet = extended[4]
    levels = extended.shape[1]
    rows = extended.shape[2] - 2
    level_index = jnp.arange(levels, dtype=jnp.int32)[:, None, None]
    wet_here = view_at(wet, 0, 0)
    mask_east = wet_here * view_at(wet, 0, 1)
    mask_west = view_at(wet, 0, -1) * wet_here
    mask_north = wet_here * view_at(wet, 1, 0)
    mask_south = view_at(wet, -1, 0) * wet_here
    mixing = (
        wet_here[:-1]
        * wet_here[1:]
        * (level_index[1:] < column_layer_count[None]).astype(jnp.float32)
    )
    bottom = (level_index == column_layer_count[None] - 1).astype(jnp.float32)
    depth = (level_index.astype(jnp.float32) + 0.5) * level_depth
    density = (
        -thermal_expand * (1.0 + 0.5 * cabbel_temp * temper + thermo_temp * depth) * temper
        + haline_contract * (1.0 - 0.5 * cabbel_salt * saline - thermo_salt * depth) * saline
        - cabbel_mixed * temper * saline
    )
    pressure = jnp.cumsum(wet * density, axis=0)
    row_index = (row_start + jnp.arange(rows, dtype=jnp.int32)).astype(jnp.float32)[None, :, None]
    coriolis_t = coriolis_max * (2.0 * (row_index + 0.5) / total_rows - 1.0)
    coriolis_v = coriolis_max * (2.0 * (row_index + 1.0) / total_rows - 1.0)

    def tracer(field):
        centre = view_at(field, 0, 0)
        east_side = view_at(field, 0, 1)
        west_side = view_at(field, 0, -1)
        north_side = view_at(field, 1, 0)
        south_side = view_at(field, -1, 0)
        flux_east = mask_east * (
            view_at(eastward, 0, 0) * (centre + east_side) * 0.5
            - lateral_diff * (east_side - centre)
        )
        flux_west = mask_west * (
            view_at(eastward, 0, -1) * (west_side + centre) * 0.5
            - lateral_diff * (centre - west_side)
        )
        flux_north = mask_north * (
            view_at(northward, 0, 0) * (centre + north_side) * 0.5
            - lateral_diff * (north_side - centre)
        )
        flux_south = mask_south * (
            view_at(northward, -1, 0) * (south_side + centre) * 0.5
            - lateral_diff * (centre - south_side)
        )
        tendency = flux_west - flux_east + (flux_south - flux_north) + column_flux(centre, mixing)
        return wet_here * (centre + time_step * tendency)

    east_here = view_at(eastward, 0, 0)
    north_here = view_at(northward, 0, 0)
    corner_ne = wet_here * view_at(wet, 0, 1) * view_at(wet, 1, 0) * view_at(wet, 1, 1)
    corner_se = view_at(wet, -1, 0) * view_at(wet, -1, 1) * wet_here * view_at(wet, 0, 1)
    corner_nw = view_at(wet, 0, -1) * wet_here * view_at(wet, 1, -1) * view_at(wet, 1, 0)
    cell_east = view_at(wet, 0, 1) * (
        ((east_here + view_at(eastward, 0, 1)) * 0.5) ** 2
        - lateral_diff * (view_at(eastward, 0, 1) - east_here)
    )
    cell_west = wet_here * (
        ((view_at(eastward, 0, -1) + east_here) * 0.5) ** 2
        - lateral_diff * (east_here - view_at(eastward, 0, -1))
    )
    product_ne = (
        (north_here + view_at(northward, 0, 1)) * 0.5 * (east_here + view_at(eastward, 1, 0)) * 0.5
    )
    product_se = (
        (view_at(northward, -1, 0) + view_at(northward, -1, 1))
        * 0.5
        * (view_at(eastward, -1, 0) + east_here)
        * 0.5
    )
    product_nw = (
        (view_at(eastward, 0, -1) + view_at(eastward, 1, -1))
        * 0.5
        * (view_at(northward, 0, -1) + north_here)
        * 0.5
    )
    shear_north = corner_ne * (product_ne - lateral_diff * (view_at(eastward, 1, 0) - east_here))
    shear_south = corner_se * (product_se - lateral_diff * (east_here - view_at(eastward, -1, 0)))
    north_mean = (
        north_here
        + view_at(northward, 0, 1)
        + view_at(northward, -1, 0)
        + view_at(northward, -1, 1)
    ) * 0.25
    east_tend = (
        cell_west
        - cell_east
        + (shear_south - shear_north)
        + coriolis_t * north_mean
        - pressure_coef * (view_at(pressure, 0, 1) - view_at(pressure, 0, 0))
        + column_flux(east_here, mixing)
        - drag_coef * bottom * east_here
    )
    east_next = mask_east * (east_here + time_step * east_tend)
    cell_north = view_at(wet, 1, 0) * (
        ((north_here + view_at(northward, 1, 0)) * 0.5) ** 2
        - lateral_diff * (view_at(northward, 1, 0) - north_here)
    )
    cell_south = wet_here * (
        ((view_at(northward, -1, 0) + north_here) * 0.5) ** 2
        - lateral_diff * (north_here - view_at(northward, -1, 0))
    )
    stress_east = corner_ne * (product_ne - lateral_diff * (view_at(northward, 0, 1) - north_here))
    stress_west = corner_nw * (product_nw - lateral_diff * (north_here - view_at(northward, 0, -1)))
    east_mean = (
        east_here + view_at(eastward, 0, -1) + view_at(eastward, 1, 0) + view_at(eastward, 1, -1)
    ) * 0.25
    north_tend = (
        stress_west
        - stress_east
        + (cell_south - cell_north)
        - coriolis_v * east_mean
        - pressure_coef * (view_at(pressure, 1, 0) - view_at(pressure, 0, 0))
        + column_flux(north_here, mixing)
        - drag_coef * bottom * north_here
    )
    north_next = mask_north * (north_here + time_step * north_tend)
    return (east_next, north_next, tracer(temper), tracer(saline))


def shift(value, mapping):
    lat_size = lax.axis_size("lat")
    lon_size = lax.axis_size("lon")
    pairs = []
    for a in range(lat_size):
        for b in range(lon_size):
            target = mapping(a, b, lat_size, lon_size)
            if target is not None:
                pairs.append((b * lat_size + a, target[1] * lat_size + target[0]))
    return lax.ppermute(value, ("lon", "lat"), pairs)


def row_kernel(*refs):
    fields = (len(refs) - 2) // 2
    lows = refs[:fields]
    highs = refs[fields : 2 * fields]
    top_ref, bottom_ref = refs[2 * fields :]
    chunk, tile, cols = lows[0].shape
    for field in range(fields):
        top_ref[field] = highs[field][:, tile - 1, :].astype(jnp.float32)
        bottom_ref[field] = lows[field][:, 0, :].astype(jnp.float32)


def edge_kernel(*refs):
    fields = len(refs) - 2
    sources = refs[:fields]
    west_ref, east_ref = refs[fields:]
    chunk, rows, cols = sources[0].shape
    levels = west_ref.shape[2]
    step = pl.program_id(0)
    lane = lax.broadcasted_iota(jnp.int32, (rows, levels), 1)

    @pl.when(step == 0)
    def _():
        west_ref[...] = jnp.zeros(west_ref.shape, jnp.float32)
        east_ref[...] = jnp.zeros(east_ref.shape, jnp.float32)

    for field, source in enumerate(sources):
        west = west_ref[field]
        east = east_ref[field]
        for r in range(chunk):
            x = source[r].astype(jnp.float32)
            here = lane == step * chunk + r
            west = jnp.where(here, x[:, 0:1], west)
            east = jnp.where(here, x[:, cols - 1 : cols], east)
        west_ref[field] = west
        east_ref[field] = east


def stencil_kernel(
    meta_ref, u_ref, v_ref, t_ref, s_ref, wet_ref, ua_ref, va_ref, ta_ref, sa_ref, wa_ref,
    ub_ref, vb_ref, tb_ref, sb_ref, wb_ref, clc_ref, rn_ref, rs_ref, tw_ref, te_ref,
    east_ref, north_ref, temp_ref, salt_ref, p_ref, pe_ref, pn_ref, *, total_rows,
):
    chunk, rows, cols = u_ref.shape
    levels = tw_ref.shape[2]
    step = pl.program_id(0)
    near = {
        id(u_ref): (ua_ref, ub_ref),
        id(v_ref): (va_ref, vb_ref),
        id(t_ref): (ta_ref, tb_ref),
        id(s_ref): (sa_ref, sb_ref),
        id(wet_ref): (wa_ref, wb_ref),
    }

    def level(ref, r, offset):
        above, below = near[id(ref)]
        if offset < 0:
            return jnp.where(r == 0, above[0], ref[jnp.maximum(r - 1, 0)])
        return jnp.where(r == chunk - 1, below[0], ref[jnp.minimum(r + 1, chunk - 1)])

    @pl.when(step == 0)
    def _():
        p_ref[...] = jnp.zeros(p_ref.shape, jnp.float32)
        pe_ref[...] = jnp.zeros(pe_ref.shape, jnp.float32)
        pn_ref[...] = jnp.zeros(pn_ref.shape, jnp.float32)

    fields = 5
    lane = lax.broadcasted_iota(jnp.int32, (rows, cols), 1)
    sub = lax.broadcasted_iota(jnp.int32, (rows, cols), 0)
    at_east = lane == cols - 1
    at_west = lane == 0
    at_north = sub == rows - 1
    at_south = sub == 0
    row_lane = lax.broadcasted_iota(jnp.int32, (1, cols), 1)
    row_east = row_lane == cols - 1
    row_west = row_lane == 0
    pick_lane = lax.broadcasted_iota(jnp.int32, tw_ref.shape[1:], 1)
    row_index = (meta_ref[0] * rows + sub).astype(jnp.float32)

    def per_total(x):
        if total_rows & (total_rows - 1) == 0:
            return x * (1.0 / total_rows)
        return x / total_rows

    cor_t = coriolis_max * (per_total(2.0 * (row_index + 0.5)) - 1.0)
    cor_v = coriolis_max * (per_total(2.0 * (row_index + 1.0)) - 1.0)
    count = clc_ref[...]

    def east(x, col):
        return jnp.where(at_east, col, pltpu.roll(x, cols - 1, 1))

    def west(x, col):
        return jnp.where(at_west, col, pltpu.roll(x, 1, 1))

    def north(x, row):
        return jnp.where(at_north, row, pltpu.roll(x, rows - 1, 0))

    def south(x, row):
        return jnp.where(at_south, row, pltpu.roll(x, 1, 0))

    def body(r, carry):
        pres, pres_e, pres_n = carry
        k = step * chunk + r

        spread = {}

        def tall(field):
            if field not in spread:
                spread[field] = tuple(
                    jnp.broadcast_to(
                        jnp.sum(jnp.where(pick_lane == k, ref[field], 0.0), axis=1, keepdims=True),
                        (ref.shape[1], cols),
                    )
                    for ref in (tw_ref, te_ref)
                )
            return spread[field]

        def row(variant, field):
            west_t, east_t = tall(field)
            if variant == 0:
                return rn_ref[field, pl.ds(r, 1), :]
            if variant == 3:
                return rs_ref[field, pl.ds(r, 1), :]
            if variant == 1:
                return jnp.where(row_east, east_t[rows + 1 : rows + 2], pltpu.roll(row(0, field), cols - 1, 1))
            if variant == 2:
                return jnp.where(row_west, west_t[rows + 1 : rows + 2], pltpu.roll(row(0, field), 1, 1))
            return jnp.where(row_east, east_t[rows : rows + 1], pltpu.roll(row(3, field), cols - 1, 1))

        def col(field):
            west_t, east_t = tall(field)
            return west_t[0:rows], east_t[0:rows]

        w = wet_ref[r].astype(jnp.float32)
        w_above = level(wet_ref, r, -1).astype(jnp.float32)
        w_below = level(wet_ref, r, 1).astype(jnp.float32)
        w_wc, w_ec = col(4)
        w_e = east(w, w_ec)
        w_w = west(w, w_wc)
        w_n = north(w, row(0, 4))
        w_s = south(w, row(3, 4))
        w_ne = north(w_e, row(1, 4))
        w_se = south(w_e, row(4, 4))
        w_nw = north(w_w, row(2, 4))
        mask_east = w * w_e
        mask_west = w_w * w
        mask_north = w * w_n
        mask_south = w_s * w
        mix_below = jnp.where(
            k < levels - 1, w * w_below * (k + 1 < count).astype(jnp.float32), 0.0
        )
        mix_above = jnp.where(k > 0, w_above * w * (k < count).astype(jnp.float32), 0.0)
        bottom = (k == count - 1).astype(jnp.float32)

        def column(ref, centre):
            upper = level(ref, r, -1)
            lower = level(ref, r, 1)
            above = -vertical_diff * mix_above * (centre - upper)
            below = -vertical_diff * mix_below * (lower - centre)
            return above - below

        depth = (k.astype(jnp.float32) + 0.5) * level_depth

        def density(temper, saline):
            return (
                -thermal_expand * (1.0 + 0.5 * cabbel_temp * temper + thermo_temp * depth) * temper
                + haline_contract * (1.0 - 0.5 * cabbel_salt * saline - thermo_salt * depth) * saline
                - cabbel_mixed * temper * saline
            )

        tc = t_ref[r]
        sc = s_ref[r]
        t_wc, t_ec = col(2)
        s_wc, s_ec = col(3)
        pres = pres + w * density(tc, sc)
        pres_e = pres_e + w_ec * density(t_ec, s_ec)
        pres_n = pres_n + row(0, 4) * density(row(0, 2), row(0, 3))
        p_e = east(pres, pres_e)
        p_n = north(pres, pres_n)

        uc = u_ref[r]
        u_wc, u_ec = col(0)
        u_e = east(uc, u_ec)
        u_w = west(uc, u_wc)
        u_n = north(uc, row(0, 0))
        u_s = south(uc, row(3, 0))
        u_nw = north(u_w, row(2, 0))
        vc = v_ref[r]
        v_wc, v_ec = col(1)
        v_e = east(vc, v_ec)
        v_w = west(vc, v_wc)
        v_n = north(vc, row(0, 1))
        v_s = south(vc, row(3, 1))
        v_se = south(v_e, row(4, 1))

        def tracer(ref, centre, field, wcol, ecol):
            east_side = east(centre, ecol)
            west_side = west(centre, wcol)
            north_side = north(centre, row(0, field))
            south_side = south(centre, row(3, field))
            flux_east = mask_east * (
                uc * (centre + east_side) * 0.5 - lateral_diff * (east_side - centre)
            )
            flux_west = mask_west * (
                u_w * (west_side + centre) * 0.5 - lateral_diff * (centre - west_side)
            )
            flux_north = mask_north * (
                vc * (centre + north_side) * 0.5 - lateral_diff * (north_side - centre)
            )
            flux_south = mask_south * (
                v_s * (south_side + centre) * 0.5 - lateral_diff * (centre - south_side)
            )
            tendency = (
                flux_west - flux_east + (flux_south - flux_north) + column(ref, centre)
            )
            return w * (centre + time_step * tendency)

        temp_ref[r] = tracer(t_ref, tc, 2, t_wc, t_ec)
        salt_ref[r] = tracer(s_ref, sc, 3, s_wc, s_ec)

        corner_ne = w * w_e * w_n * w_ne
        corner_se = w_s * w_se * w * w_e
        corner_nw = w_w * w * w_nw * w_n
        half_e = (uc + u_e) * 0.5
        cell_east = w_e * (half_e * half_e - lateral_diff * (u_e - uc))
        half_w = (u_w + uc) * 0.5
        cell_west = w * (half_w * half_w - lateral_diff * (uc - u_w))
        product_ne = (vc + v_e) * 0.5 * (uc + u_n) * 0.5
        product_se = (v_s + v_se) * 0.5 * (u_s + uc) * 0.5
        product_nw = (u_w + u_nw) * 0.5 * (v_w + vc) * 0.5
        shear_north = corner_ne * (product_ne - lateral_diff * (u_n - uc))
        shear_south = corner_se * (product_se - lateral_diff * (uc - u_s))
        north_mean = (vc + v_e + v_s + v_se) * 0.25
        east_tend = (
            cell_west
            - cell_east
            + (shear_south - shear_north)
            + cor_t * north_mean
            - pressure_coef * (p_e - pres)
            + column(u_ref, uc)
            - drag_coef * bottom * uc
        )
        east_ref[r] = mask_east * (uc + time_step * east_tend)
        half_n = (vc + v_n) * 0.5
        cell_north = w_n * (half_n * half_n - lateral_diff * (v_n - vc))
        half_s = (v_s + vc) * 0.5
        cell_south = w * (half_s * half_s - lateral_diff * (vc - v_s))
        stress_east = corner_ne * (product_ne - lateral_diff * (v_e - vc))
        stress_west = corner_nw * (product_nw - lateral_diff * (vc - v_w))
        east_mean = (uc + u_w + u_n + u_nw) * 0.25
        north_tend = (
            stress_west
            - stress_east
            + (cell_south - cell_north)
            - cor_v * east_mean
            - pressure_coef * (p_n - pres)
            + column(v_ref, vc)
            - drag_coef * bottom * vc
        )
        north_ref[r] = mask_north * (vc + time_step * north_tend)
        return pres, pres_e, pres_n

    init = (p_ref[...], pe_ref[...], pn_ref[...])
    pres, pres_e, pres_n = lax.fori_loop(0, chunk, body, init)
    p_ref[...] = pres
    pe_ref[...] = pres_e
    pn_ref[...] = pres_n


def per_device(
    eastbound_current,
    poleward_current,
    warmth_excess,
    saltiness_excess,
    water_indicator,
    column_layer_count,
):
    inputs = (
        eastbound_current,
        poleward_current,
        warmth_excess,
        saltiness_excess,
        water_indicator,
    )

    levels, rows, cols = eastbound_current.shape
    fields = len(inputs)
    chunk = 8 if levels % 8 == 0 else levels
    row_block = pl.BlockSpec((fields, chunk, cols), lambda c: (0, c, 0))
    col_block = pl.BlockSpec((fields, rows, levels), lambda c: (0, 0, 0))
    tile = 8
    top, bottom = pl.pallas_call(
        row_kernel,
        grid=(1,),
        in_specs=[pl.BlockSpec((levels, tile, cols), lambda c: (0, 0, 0))] * fields
        + [pl.BlockSpec((levels, tile, cols), lambda c: (0, rows // tile - 1, 0))] * fields,
        out_specs=(
            pl.BlockSpec((fields, levels, cols), lambda c: (0, 0, 0)),
            pl.BlockSpec((fields, levels, cols), lambda c: (0, 0, 0)),
        ),
        out_shape=(
            jax.ShapeDtypeStruct((fields, levels, cols), jnp.float32),
            jax.ShapeDtypeStruct((fields, levels, cols), jnp.float32),
        ),
    )(*inputs, *inputs)
    west_col, east_col = pl.pallas_call(
        edge_kernel,
        grid=(levels // chunk,),
        in_specs=[pl.BlockSpec((chunk, rows, cols), lambda c: (c, 0, 0))] * fields,
        out_specs=(col_block, col_block),
        out_shape=(
            jax.ShapeDtypeStruct((fields, rows, levels), jnp.float32),
            jax.ShapeDtypeStruct((fields, rows, levels), jnp.float32),
        ),
    )(*inputs)

    def east_of(a, b, na, nl):
        return (a, (b + 1) % nl)

    def west_of(a, b, na, nl):
        return (a, (b - 1) % nl)

    def north_of(a, b, na, nl):
        return (a + 1, b) if a + 1 < na else None

    def south_of(a, b, na, nl):
        return (a - 1, b) if a > 0 else None

    def mirror(a, b, na, nl):
        return (a, nl - 1 - b) if a == na - 1 else None

    halo_south = shift(top, north_of)
    halo_north = shift(bottom, south_of)
    fold_row = shift(top, mirror)
    sign = jnp.array([-1.0, -1.0, 1.0, 1.0, 1.0], dtype=jnp.float32)[:, None, None]
    is_top = lax.axis_index("lat") == lax.axis_size("lat") - 1
    flip = (jnp.arange(cols)[:, None] + jnp.arange(cols)[None, :] == cols - 1).astype(jnp.float32)
    mirrored = jnp.dot(fold_row, flip, precision=lax.Precision.HIGHEST)
    halo_north = jnp.where(is_top, sign * mirrored, halo_north)
    pad = jnp.zeros((fields, 6, levels), jnp.float32)
    west_tall = jnp.concatenate(
        [west_col, halo_south[:, None, :, 0], halo_north[:, None, :, 0], pad], axis=1
    )
    east_tall = jnp.concatenate(
        [east_col, halo_south[:, None, :, -1], halo_north[:, None, :, -1], pad], axis=1
    )
    halo_west = shift(east_tall, east_of)
    halo_east = shift(west_tall, west_of)

    row_start = lax.axis_index("lat") * rows
    total_rows = rows * lax.axis_size("lat")
    row_index = (row_start + jnp.arange(rows, dtype=jnp.int32)).astype(jnp.float32)[:, None]
    coriolis_t = coriolis_max * (2.0 * (row_index + 0.5) / total_rows - 1.0)
    coriolis_v = coriolis_max * (2.0 * (row_index + 1.0) / total_rows - 1.0)
    meta = lax.axis_index("lat").reshape(1)

    block = jax.ShapeDtypeStruct((levels, rows, cols), jnp.float32)
    main = pl.BlockSpec((chunk, rows, cols), lambda c: (c, 0, 0))
    above = pl.BlockSpec((1, rows, cols), lambda c: (jnp.maximum(c * chunk - 1, 0), 0, 0))
    below = pl.BlockSpec(
        (1, rows, cols), lambda c: (jnp.minimum(c * chunk + chunk, levels - 1), 0, 0)
    )

    def whole(shape):
        return pl.BlockSpec(shape, lambda c: (0,) * len(shape))

    halo_row = pl.BlockSpec((fields, chunk, cols), lambda c: (0, c, 0))
    return pl.pallas_call(
        functools.partial(stencil_kernel, total_rows=total_rows),
        grid=(levels // chunk,),
        in_specs=[pl.BlockSpec(memory_space=pltpu.SMEM)]
        + [main] * fields
        + [above] * fields
        + [below] * fields
        + [whole((rows, cols)), halo_row, halo_row, whole(halo_west.shape), whole(halo_east.shape)],
        out_specs=(main, main, main, main),
        out_shape=(block, block, block, block),
        scratch_shapes=[
            pltpu.VMEM((rows, cols), jnp.float32),
            pltpu.VMEM((rows, cols), jnp.float32),
            pltpu.VMEM((1, cols), jnp.float32),
        ],
    )(
        meta.astype(jnp.int32),
        *inputs,
        *inputs,
        *inputs,
        column_layer_count,
        halo_north,
        halo_south,
        halo_west,
        halo_east,
    )


def solution(mesh):
    placed = (
        P(None, "lat", "lon"),
        P(None, "lat", "lon"),
        P(None, "lat", "lon"),
        P(None, "lat", "lon"),
        P(None, "lat", "lon"),
        P("lat", "lon"),
    )
    return jax.shard_map(
        per_device,
        mesh=mesh,
        in_specs=placed,
        out_specs=(
            P(None, "lat", "lon"),
            P(None, "lat", "lon"),
            P(None, "lat", "lon"),
            P(None, "lat", "lon"),
        ),
        check_vma=False,
    )
```

```python
import functools

import jax
import jax.numpy as jnp
from jax import lax
from jax.experimental import pallas as pl
from jax.experimental.pallas import tpu as pltpu
from jax.sharding import PartitionSpec as P

time_step = 0.2
lateral_diff = 0.1
vertical_diff = 0.5
pressure_coef = 0.1
drag_coef = 2.0
coriolis_max = 1.0
level_depth = 100.0
thermal_expand = 0.1655
haline_contract = 0.76554
cabbel_temp = 0.05952
cabbel_salt = 0.00054914
cabbel_mixed = 0.0024341
thermo_temp = 0.0001497
thermo_salt = 1.109e-05


def view_at(field, lat_step, lon_step):
    rows = field.shape[1] - 2
    cols = field.shape[2] - 2
    return field[:, 1 + lat_step : 1 + lat_step + rows, 1 + lon_step : 1 + lon_step + cols]


def column_flux(centre, mixing):
    between = -vertical_diff * mixing * (centre[1:] - centre[:-1])
    surface = jnp.zeros_like(centre[:1])
    above = jnp.concatenate([surface, between], axis=0)
    below = jnp.concatenate([between, surface], axis=0)
    return above - below


def advance(extended, column_layer_count, row_start, total_rows):
    eastward = extended[0]
    northward = extended[1]
    temper = extended[2]
    saline = extended[3]
    wet = extended[4]
    levels = extended.shape[1]
    rows = extended.shape[2] - 2
    level_index = jnp.arange(levels, dtype=jnp.int32)[:, None, None]
    wet_here = view_at(wet, 0, 0)
    mask_east = wet_here * view_at(wet, 0, 1)
    mask_west = view_at(wet, 0, -1) * wet_here
    mask_north = wet_here * view_at(wet, 1, 0)
    mask_south = view_at(wet, -1, 0) * wet_here
    mixing = (
        wet_here[:-1]
        * wet_here[1:]
        * (level_index[1:] < column_layer_count[None]).astype(jnp.float32)
    )
    bottom = (level_index == column_layer_count[None] - 1).astype(jnp.float32)
    depth = (level_index.astype(jnp.float32) + 0.5) * level_depth
    density = (
        -thermal_expand * (1.0 + 0.5 * cabbel_temp * temper + thermo_temp * depth) * temper
        + haline_contract * (1.0 - 0.5 * cabbel_salt * saline - thermo_salt * depth) * saline
        - cabbel_mixed * temper * saline
    )
    pressure = jnp.cumsum(wet * density, axis=0)
    row_index = (row_start + jnp.arange(rows, dtype=jnp.int32)).astype(jnp.float32)[None, :, None]
    coriolis_t = coriolis_max * (2.0 * (row_index + 0.5) / total_rows - 1.0)
    coriolis_v = coriolis_max * (2.0 * (row_index + 1.0) / total_rows - 1.0)

    def tracer(field):
        centre = view_at(field, 0, 0)
        east_side = view_at(field, 0, 1)
        west_side = view_at(field, 0, -1)
        north_side = view_at(field, 1, 0)
        south_side = view_at(field, -1, 0)
        flux_east = mask_east * (
            view_at(eastward, 0, 0) * (centre + east_side) * 0.5
            - lateral_diff * (east_side - centre)
        )
        flux_west = mask_west * (
            view_at(eastward, 0, -1) * (west_side + centre) * 0.5
            - lateral_diff * (centre - west_side)
        )
        flux_north = mask_north * (
            view_at(northward, 0, 0) * (centre + north_side) * 0.5
            - lateral_diff * (north_side - centre)
        )
        flux_south = mask_south * (
            view_at(northward, -1, 0) * (south_side + centre) * 0.5
            - lateral_diff * (centre - south_side)
        )
        tendency = flux_west - flux_east + (flux_south - flux_north) + column_flux(centre, mixing)
        return wet_here * (centre + time_step * tendency)

    east_here = view_at(eastward, 0, 0)
    north_here = view_at(northward, 0, 0)
    corner_ne = wet_here * view_at(wet, 0, 1) * view_at(wet, 1, 0) * view_at(wet, 1, 1)
    corner_se = view_at(wet, -1, 0) * view_at(wet, -1, 1) * wet_here * view_at(wet, 0, 1)
    corner_nw = view_at(wet, 0, -1) * wet_here * view_at(wet, 1, -1) * view_at(wet, 1, 0)
    cell_east = view_at(wet, 0, 1) * (
        ((east_here + view_at(eastward, 0, 1)) * 0.5) ** 2
        - lateral_diff * (view_at(eastward, 0, 1) - east_here)
    )
    cell_west = wet_here * (
        ((view_at(eastward, 0, -1) + east_here) * 0.5) ** 2
        - lateral_diff * (east_here - view_at(eastward, 0, -1))
    )
    product_ne = (
        (north_here + view_at(northward, 0, 1)) * 0.5 * (east_here + view_at(eastward, 1, 0)) * 0.5
    )
    product_se = (
        (view_at(northward, -1, 0) + view_at(northward, -1, 1))
        * 0.5
        * (view_at(eastward, -1, 0) + east_here)
        * 0.5
    )
    product_nw = (
        (view_at(eastward, 0, -1) + view_at(eastward, 1, -1))
        * 0.5
        * (view_at(northward, 0, -1) + north_here)
        * 0.5
    )
    shear_north = corner_ne * (product_ne - lateral_diff * (view_at(eastward, 1, 0) - east_here))
    shear_south = corner_se * (product_se - lateral_diff * (east_here - view_at(eastward, -1, 0)))
    north_mean = (
        north_here
        + view_at(northward, 0, 1)
        + view_at(northward, -1, 0)
        + view_at(northward, -1, 1)
    ) * 0.25
    east_tend = (
        cell_west
        - cell_east
        + (shear_south - shear_north)
        + coriolis_t * north_mean
        - pressure_coef * (view_at(pressure, 0, 1) - view_at(pressure, 0, 0))
        + column_flux(east_here, mixing)
        - drag_coef * bottom * east_here
    )
    east_next = mask_east * (east_here + time_step * east_tend)
    cell_north = view_at(wet, 1, 0) * (
        ((north_here + view_at(northward, 1, 0)) * 0.5) ** 2
        - lateral_diff * (view_at(northward, 1, 0) - north_here)
    )
    cell_south = wet_here * (
        ((view_at(northward, -1, 0) + north_here) * 0.5) ** 2
        - lateral_diff * (north_here - view_at(northward, -1, 0))
    )
    stress_east = corner_ne * (product_ne - lateral_diff * (view_at(northward, 0, 1) - north_here))
    stress_west = corner_nw * (product_nw - lateral_diff * (north_here - view_at(northward, 0, -1)))
    east_mean = (
        east_here + view_at(eastward, 0, -1) + view_at(eastward, 1, 0) + view_at(eastward, 1, -1)
    ) * 0.25
    north_tend = (
        stress_west
        - stress_east
        + (cell_south - cell_north)
        - coriolis_v * east_mean
        - pressure_coef * (view_at(pressure, 1, 0) - view_at(pressure, 0, 0))
        + column_flux(north_here, mixing)
        - drag_coef * bottom * north_here
    )
    north_next = mask_north * (north_here + time_step * north_tend)
    return (east_next, north_next, tracer(temper), tracer(saline))


def shift(value, mapping):
    lat_size = lax.axis_size("lat")
    lon_size = lax.axis_size("lon")
    pairs = []
    for a in range(lat_size):
        for b in range(lon_size):
            target = mapping(a, b, lat_size, lon_size)
            if target is not None:
                pairs.append((b * lat_size + a, target[1] * lat_size + target[0]))
    return lax.ppermute(value, ("lon", "lat"), pairs)


def row_kernel(*refs):
    fields = (len(refs) - 2) // 2
    lows = refs[:fields]
    highs = refs[fields : 2 * fields]
    top_ref, bottom_ref = refs[2 * fields :]
    chunk, tile, cols = lows[0].shape
    for field in range(fields):
        for r in range(chunk):
            top_ref[field, r : r + 1, :] = highs[field][r][tile - 1 : tile, :].astype(jnp.float32)
            bottom_ref[field, r : r + 1, :] = lows[field][r][0:1, :].astype(jnp.float32)


def edge_kernel(*refs):
    fields = len(refs) - 2
    sources = refs[:fields]
    west_ref, east_ref = refs[fields:]
    chunk, rows, cols = sources[0].shape
    levels = west_ref.shape[2]
    step = pl.program_id(0)
    lane = lax.broadcasted_iota(jnp.int32, (rows, levels), 1)

    @pl.when(step == 0)
    def _():
        west_ref[...] = jnp.zeros(west_ref.shape, jnp.float32)
        east_ref[...] = jnp.zeros(east_ref.shape, jnp.float32)

    for field, source in enumerate(sources):
        west = west_ref[field]
        east = east_ref[field]
        for r in range(chunk):
            x = source[r].astype(jnp.float32)
            here = lane == step * chunk + r
            west = jnp.where(here, x[:, 0:1], west)
            east = jnp.where(here, x[:, cols - 1 : cols], east)
        west_ref[field] = west
        east_ref[field] = east


def stencil_kernel(
    meta_ref, u_ref, v_ref, t_ref, s_ref, wet_ref, ua_ref, va_ref, ta_ref, sa_ref, wa_ref,
    ub_ref, vb_ref, tb_ref, sb_ref, wb_ref, clc_ref, rn_ref, rs_ref, tw_ref, te_ref,
    east_ref, north_ref, temp_ref, salt_ref, p_ref, pe_ref, pn_ref, *, total_rows,
):
    chunk, rows, cols = u_ref.shape
    levels = tw_ref.shape[2]
    step = pl.program_id(0)
    near = {
        id(u_ref): (ua_ref, ub_ref),
        id(v_ref): (va_ref, vb_ref),
        id(t_ref): (ta_ref, tb_ref),
        id(s_ref): (sa_ref, sb_ref),
        id(wet_ref): (wa_ref, wb_ref),
    }

    def level(ref, r, offset):
        above, below = near[id(ref)]
        if offset < 0:
            return jnp.where(r == 0, above[0], ref[jnp.maximum(r - 1, 0)])
        return jnp.where(r == chunk - 1, below[0], ref[jnp.minimum(r + 1, chunk - 1)])

    @pl.when(step == 0)
    def _():
        p_ref[...] = jnp.zeros(p_ref.shape, jnp.float32)
        pe_ref[...] = jnp.zeros(pe_ref.shape, jnp.float32)
        pn_ref[...] = jnp.zeros(pn_ref.shape, jnp.float32)

    fields = 5
    lane = lax.broadcasted_iota(jnp.int32, (rows, cols), 1)
    sub = lax.broadcasted_iota(jnp.int32, (rows, cols), 0)
    at_east = lane == cols - 1
    at_west = lane == 0
    at_north = sub == rows - 1
    at_south = sub == 0
    row_lane = lax.broadcasted_iota(jnp.int32, (1, cols), 1)
    row_east = row_lane == cols - 1
    row_west = row_lane == 0
    pick_lane = lax.broadcasted_iota(jnp.int32, tw_ref.shape[1:], 1)
    row_index = (meta_ref[0] * rows + sub).astype(jnp.float32)

    def per_total(x):
        if total_rows & (total_rows - 1) == 0:
            return x * (1.0 / total_rows)
        return x / total_rows

    cor_t = coriolis_max * (per_total(2.0 * (row_index + 0.5)) - 1.0)
    cor_v = coriolis_max * (per_total(2.0 * (row_index + 1.0)) - 1.0)
    count = clc_ref[...]

    def east(x, col):
        return jnp.where(at_east, col, pltpu.roll(x, cols - 1, 1))

    def west(x, col):
        return jnp.where(at_west, col, pltpu.roll(x, 1, 1))

    def north(x, row):
        return jnp.where(at_north, row, pltpu.roll(x, rows - 1, 0))

    def south(x, row):
        return jnp.where(at_south, row, pltpu.roll(x, 1, 0))

    def body(r, carry):
        pres, pres_e, pres_n = carry
        k = step * chunk + r

        spread = {}

        def tall(field):
            if field not in spread:
                spread[field] = tuple(
                    jnp.broadcast_to(
                        jnp.sum(jnp.where(pick_lane == k, ref[field], 0.0), axis=1, keepdims=True),
                        (ref.shape[1], cols),
                    )
                    for ref in (tw_ref, te_ref)
                )
            return spread[field]

        def row(variant, field):
            west_t, east_t = tall(field)
            if variant == 0:
                return rn_ref[field, pl.ds(r, 1), :]
            if variant == 3:
                return rs_ref[field, pl.ds(r, 1), :]
            if variant == 1:
                return jnp.where(row_east, east_t[rows + 1 : rows + 2], pltpu.roll(row(0, field), cols - 1, 1))
            if variant == 2:
                return jnp.where(row_west, west_t[rows + 1 : rows + 2], pltpu.roll(row(0, field), 1, 1))
            return jnp.where(row_east, east_t[rows : rows + 1], pltpu.roll(row(3, field), cols - 1, 1))

        def col(field):
            west_t, east_t = tall(field)
            return west_t[0:rows], east_t[0:rows]

        w = wet_ref[r].astype(jnp.float32)
        w_above = level(wet_ref, r, -1).astype(jnp.float32)
        w_below = level(wet_ref, r, 1).astype(jnp.float32)
        w_wc, w_ec = col(4)
        w_e = east(w, w_ec)
        w_w = west(w, w_wc)
        w_n = north(w, row(0, 4))
        w_s = south(w, row(3, 4))
        w_ne = north(w_e, row(1, 4))
        w_se = south(w_e, row(4, 4))
        w_nw = north(w_w, row(2, 4))
        mask_east = w * w_e
        mask_west = w_w * w
        mask_north = w * w_n
        mask_south = w_s * w
        mix_below = jnp.where(
            k < levels - 1, w * w_below * (k + 1 < count).astype(jnp.float32), 0.0
        )
        mix_above = jnp.where(k > 0, w_above * w * (k < count).astype(jnp.float32), 0.0)
        bottom = (k == count - 1).astype(jnp.float32)

        def column(ref, centre):
            upper = level(ref, r, -1)
            lower = level(ref, r, 1)
            above = -vertical_diff * mix_above * (centre - upper)
            below = -vertical_diff * mix_below * (lower - centre)
            return above - below

        depth = (k.astype(jnp.float32) + 0.5) * level_depth

        def density(temper, saline):
            return (
                -thermal_expand * (1.0 + 0.5 * cabbel_temp * temper + thermo_temp * depth) * temper
                + haline_contract * (1.0 - 0.5 * cabbel_salt * saline - thermo_salt * depth) * saline
                - cabbel_mixed * temper * saline
            )

        tc = t_ref[r]
        sc = s_ref[r]
        t_wc, t_ec = col(2)
        s_wc, s_ec = col(3)
        pres = pres + w * density(tc, sc)
        pres_e = pres_e + w_ec * density(t_ec, s_ec)
        pres_n = pres_n + row(0, 4) * density(row(0, 2), row(0, 3))
        p_e = east(pres, pres_e)
        p_n = north(pres, pres_n)

        uc = u_ref[r]
        u_wc, u_ec = col(0)
        u_e = east(uc, u_ec)
        u_w = west(uc, u_wc)
        u_n = north(uc, row(0, 0))
        u_s = south(uc, row(3, 0))
        u_nw = north(u_w, row(2, 0))
        vc = v_ref[r]
        v_wc, v_ec = col(1)
        v_e = east(vc, v_ec)
        v_w = west(vc, v_wc)
        v_n = north(vc, row(0, 1))
        v_s = south(vc, row(3, 1))
        v_se = south(v_e, row(4, 1))

        def tracer(ref, centre, field, wcol, ecol):
            east_side = east(centre, ecol)
            west_side = west(centre, wcol)
            north_side = north(centre, row(0, field))
            south_side = south(centre, row(3, field))
            flux_east = mask_east * (
                uc * (centre + east_side) * 0.5 - lateral_diff * (east_side - centre)
            )
            flux_west = mask_west * (
                u_w * (west_side + centre) * 0.5 - lateral_diff * (centre - west_side)
            )
            flux_north = mask_north * (
                vc * (centre + north_side) * 0.5 - lateral_diff * (north_side - centre)
            )
            flux_south = mask_south * (
                v_s * (south_side + centre) * 0.5 - lateral_diff * (centre - south_side)
            )
            tendency = (
                flux_west - flux_east + (flux_south - flux_north) + column(ref, centre)
            )
            return w * (centre + time_step * tendency)

        temp_ref[r] = tracer(t_ref, tc, 2, t_wc, t_ec)
        salt_ref[r] = tracer(s_ref, sc, 3, s_wc, s_ec)

        corner_ne = w * w_e * w_n * w_ne
        corner_se = w_s * w_se * w * w_e
        corner_nw = w_w * w * w_nw * w_n
        half_e = (uc + u_e) * 0.5
        cell_east = w_e * (half_e * half_e - lateral_diff * (u_e - uc))
        half_w = (u_w + uc) * 0.5
        cell_west = w * (half_w * half_w - lateral_diff * (uc - u_w))
        product_ne = (vc + v_e) * 0.5 * (uc + u_n) * 0.5
        product_se = (v_s + v_se) * 0.5 * (u_s + uc) * 0.5
        product_nw = (u_w + u_nw) * 0.5 * (v_w + vc) * 0.5
        shear_north = corner_ne * (product_ne - lateral_diff * (u_n - uc))
        shear_south = corner_se * (product_se - lateral_diff * (uc - u_s))
        north_mean = (vc + v_e + v_s + v_se) * 0.25
        east_tend = (
            cell_west
            - cell_east
            + (shear_south - shear_north)
            + cor_t * north_mean
            - pressure_coef * (p_e - pres)
            + column(u_ref, uc)
            - drag_coef * bottom * uc
        )
        east_ref[r] = mask_east * (uc + time_step * east_tend)
        half_n = (vc + v_n) * 0.5
        cell_north = w_n * (half_n * half_n - lateral_diff * (v_n - vc))
        half_s = (v_s + vc) * 0.5
        cell_south = w * (half_s * half_s - lateral_diff * (vc - v_s))
        stress_east = corner_ne * (product_ne - lateral_diff * (v_e - vc))
        stress_west = corner_nw * (product_nw - lateral_diff * (vc - v_w))
        east_mean = (uc + u_w + u_n + u_nw) * 0.25
        north_tend = (
            stress_west
            - stress_east
            + (cell_south - cell_north)
            - cor_v * east_mean
            - pressure_coef * (p_n - pres)
            + column(v_ref, vc)
            - drag_coef * bottom * vc
        )
        north_ref[r] = mask_north * (vc + time_step * north_tend)
        return pres, pres_e, pres_n

    init = (p_ref[...], pe_ref[...], pn_ref[...])
    pres, pres_e, pres_n = lax.fori_loop(0, chunk, body, init, unroll=2)
    p_ref[...] = pres
    pe_ref[...] = pres_e
    pn_ref[...] = pres_n


def per_device(
    eastbound_current,
    poleward_current,
    warmth_excess,
    saltiness_excess,
    water_indicator,
    column_layer_count,
):
    inputs = (
        eastbound_current,
        poleward_current,
        warmth_excess,
        saltiness_excess,
        water_indicator,
    )

    levels, rows, cols = eastbound_current.shape
    fields = len(inputs)
    chunk = 8 if levels % 8 == 0 else levels
    row_block = pl.BlockSpec((fields, chunk, cols), lambda c: (0, c, 0))
    col_block = pl.BlockSpec((fields, rows, levels), lambda c: (0, 0, 0))
    tile = 8
    top, bottom = pl.pallas_call(
        row_kernel,
        grid=(1,),
        in_specs=[pl.BlockSpec((levels, tile, cols), lambda c: (0, 0, 0))] * fields
        + [pl.BlockSpec((levels, tile, cols), lambda c: (0, rows // tile - 1, 0))] * fields,
        out_specs=(
            pl.BlockSpec((fields, levels, cols), lambda c: (0, 0, 0)),
            pl.BlockSpec((fields, levels, cols), lambda c: (0, 0, 0)),
        ),
        out_shape=(
            jax.ShapeDtypeStruct((fields, levels, cols), jnp.float32),
            jax.ShapeDtypeStruct((fields, levels, cols), jnp.float32),
        ),
    )(*inputs, *inputs)
    west_col, east_col = pl.pallas_call(
        edge_kernel,
        grid=(levels // chunk,),
        in_specs=[pl.BlockSpec((chunk, rows, cols), lambda c: (c, 0, 0))] * fields,
        out_specs=(col_block, col_block),
        out_shape=(
            jax.ShapeDtypeStruct((fields, rows, levels), jnp.float32),
            jax.ShapeDtypeStruct((fields, rows, levels), jnp.float32),
        ),
    )(*inputs)

    def east_of(a, b, na, nl):
        return (a, (b + 1) % nl)

    def west_of(a, b, na, nl):
        return (a, (b - 1) % nl)

    def north_of(a, b, na, nl):
        return (a + 1, b) if a + 1 < na else None

    def south_of(a, b, na, nl):
        return (a - 1, b) if a > 0 else None

    def mirror(a, b, na, nl):
        return (a, nl - 1 - b) if a == na - 1 else None

    halo_south = shift(top, north_of)
    halo_north = shift(bottom, south_of)
    fold_row = shift(top, mirror)
    sign = jnp.array([-1.0, -1.0, 1.0, 1.0, 1.0], dtype=jnp.float32)[:, None, None]
    is_top = lax.axis_index("lat") == lax.axis_size("lat") - 1
    flip = (jnp.arange(cols)[:, None] + jnp.arange(cols)[None, :] == cols - 1).astype(jnp.float32)
    mirrored = jnp.dot(fold_row, flip, precision=lax.Precision.HIGHEST)
    halo_north = jnp.where(is_top, sign * mirrored, halo_north)
    pad = jnp.zeros((fields, 6, levels), jnp.float32)
    west_tall = jnp.concatenate(
        [west_col, halo_south[:, None, :, 0], halo_north[:, None, :, 0], pad], axis=1
    )
    east_tall = jnp.concatenate(
        [east_col, halo_south[:, None, :, -1], halo_north[:, None, :, -1], pad], axis=1
    )
    halo_west = shift(east_tall, east_of)
    halo_east = shift(west_tall, west_of)

    row_start = lax.axis_index("lat") * rows
    total_rows = rows * lax.axis_size("lat")
    row_index = (row_start + jnp.arange(rows, dtype=jnp.int32)).astype(jnp.float32)[:, None]
    coriolis_t = coriolis_max * (2.0 * (row_index + 0.5) / total_rows - 1.0)
    coriolis_v = coriolis_max * (2.0 * (row_index + 1.0) / total_rows - 1.0)
    meta = lax.axis_index("lat").reshape(1)

    block = jax.ShapeDtypeStruct((levels, rows, cols), jnp.float32)
    main = pl.BlockSpec((chunk, rows, cols), lambda c: (c, 0, 0))
    above = pl.BlockSpec((1, rows, cols), lambda c: (jnp.maximum(c * chunk - 1, 0), 0, 0))
    below = pl.BlockSpec(
        (1, rows, cols), lambda c: (jnp.minimum(c * chunk + chunk, levels - 1), 0, 0)
    )

    def whole(shape):
        return pl.BlockSpec(shape, lambda c: (0,) * len(shape))

    halo_row = pl.BlockSpec((fields, chunk, cols), lambda c: (0, c, 0))
    return pl.pallas_call(
        functools.partial(stencil_kernel, total_rows=total_rows),
        grid=(levels // chunk,),
        in_specs=[pl.BlockSpec(memory_space=pltpu.SMEM)]
        + [main] * fields
        + [above] * fields
        + [below] * fields
        + [whole((rows, cols)), halo_row, halo_row, whole(halo_west.shape), whole(halo_east.shape)],
        out_specs=(main, main, main, main),
        out_shape=(block, block, block, block),
        scratch_shapes=[
            pltpu.VMEM((rows, cols), jnp.float32),
            pltpu.VMEM((rows, cols), jnp.float32),
            pltpu.VMEM((1, cols), jnp.float32),
        ],
    )(
        meta.astype(jnp.int32),
        *inputs,
        *inputs,
        *inputs,
        column_layer_count,
        halo_north,
        halo_south,
        halo_west,
        halo_east,
    )


def solution(mesh):
    placed = (
        P(None, "lat", "lon"),
        P(None, "lat", "lon"),
        P(None, "lat", "lon"),
        P(None, "lat", "lon"),
        P(None, "lat", "lon"),
        P("lat", "lon"),
    )
    return jax.shard_map(
        per_device,
        mesh=mesh,
        in_specs=placed,
        out_specs=(
            P(None, "lat", "lon"),
            P(None, "lat", "lon"),
            P(None, "lat", "lon"),
            P(None, "lat", "lon"),
        ),
        check_vma=False,
    )
```
